32 devices in a mesh: fsdp: 2 (over core), context: 4 (over y, x), tensor: 4 (over z).
Axes of the slice: x: 2, y: 2, z: 4, core: 2. Of those that a mesh axis runs over, the one named last changes fastest.
Arguments:
- inputs: bfloat16 [2, 2, 4096, 768], P(None, 'fsdp', 'context'), may hold values from -6 to 6
- cotangent: bfloat16 [2, 2, 4096, 768], P(None, 'fsdp', 'context'), may hold values from -6 to 6
- picture_starts: int32 [2, 2, 4], P(None, 'fsdp'), may hold values from 0 to 3840, as said below
- qkv_weight: bfloat16 [3, 768, 768], P(None, 'fsdp', 'tensor'), may hold values from -0.21875 to 0.21875
- out_weight: bfloat16 [768, 768], P('tensor', 'fsdp'), may hold values from -1.75 to 1.75
- up_weight: bfloat16 [768, 3072], P('fsdp', 'tensor'), may hold values from -0.21875 to 0.21875
- down_weight: bfloat16 [3072, 768], P('tensor', 'fsdp'), may hold values from -0.109375 to 0.109375
- query_map: bfloat16 [12, 64, 64], P('tensor', 'fsdp'), may hold values from -1.5 to 1.5
- key_map: bfloat16 [12, 64, 64], P('tensor', 'fsdp'), may hold values from -1.5 to 1.5
- first_gain: bfloat16 [768], P('fsdp'), may hold values from 0.5 to 1.5
- first_bias: bfloat16 [768], P('fsdp'), may hold values from -3 to 3
- second_gain: bfloat16 [768], P('fsdp'), may hold values from 0.5 to 1.5
- second_bias: bfloat16 [768], P('fsdp'), may hold values from -3 to 3
Outputs:
- output: bfloat16 [2, 2, 4096, 768], P(None, 'fsdp', 'context')
- input_grad: float32 [2, 2, 4096, 768], P(None, 'fsdp', 'context')
- qkv_grad: float32 [3, 768, 768], P(None, 'fsdp', 'tensor')
- out_grad: float32 [768, 768], P('tensor', 'fsdp')
- up_grad: float32 [768, 3072], P('fsdp', 'tensor')
- down_grad: float32 [3072, 768], P('tensor', 'fsdp')
- query_map_grad: float32 [12, 64, 64], P('tensor', 'fsdp')
- key_map_grad: float32 [12, 64, 64], P('tensor', 'fsdp')
- first_gain_grad: float32 [768], P('fsdp')
- first_bias_grad: float32 [768], P('fsdp')
- second_gain_grad: float32 [768], P('fsdp')
- second_bias_grad: float32 [768], P('fsdp')
The draws below stay inside these ranges and needn't reach their ends.
Inputs may be any that keep to these rules, and one draw needn't show every extreme that they name: `picture_starts`: the 4 starts of a sequence are distinct multiples of 256.
All inputs are finite; a program needn't handle non-finite values.
Results may differ from the reference program's by a relative error of at most 0.025.
Values may be sent and summed in bfloat16 or wider, within the bound.
A program may use at most 192 MiB of HBM per device.

```python
import jax
import jax.numpy as jnp
from jax import lax

D = 768
H = 12
HD = 64
FF = 3072
FEAT = 128
BLK = 256
MICRO = 2
LENGTH = 4096
SEQS = 2
PICS = 4
N_TENSOR = 4


def draw_picture_starts(key, part):
    block_count = LENGTH // BLK
    seq_keys = jax.random.split(key, MICRO * SEQS)

    def pick_blocks(subkey):
        return jax.random.permutation(subkey, block_count)[:PICS]
    chosen = jax.vmap(pick_blocks)(seq_keys).astype(jnp.int32)
    middle_blocks = jax.random.permutation(jax.random.fold_in(key, 7), block_count - 2)[:PICS - 2] + 1
    first_row = jnp.concatenate([jnp.array([0, block_count - 1], dtype=jnp.int32), middle_blocks.astype(jnp.int32)])
    chosen = chosen.at[0].set(first_row)
    return (chosen * BLK).reshape(MICRO, SEQS, PICS)


def block_levels(own_key, shape, pieces, low, top_value):
    factor_of, own = 1.0, jax.random.fold_in(own_key, 6)
    for axis_at, shards_of in pieces:
        heights = jnp.exp(jax.random.uniform(jax.random.fold_in(own, axis_at), (shards_of,), jnp.float32, low / len(pieces), top_value / len(pieces)))
        factor_of = factor_of * jnp.repeat(heights, shape[axis_at] // shards_of).reshape([-1 if axis == axis_at else 1 for axis in range(len(shape))])
    return factor_of


def bell_draw(key, dims, deviation, bound, cuts=(), kind=jnp.bfloat16):
    gain = block_levels(key, dims, cuts, -0.22, 0.18) if cuts else 1.0
    values = jax.random.normal(key, dims, jnp.float32) * deviation * gain
    return jnp.minimum(jnp.maximum(values, -bound), bound).astype(kind)


def setup_inputs(seed: int = 0) -> dict:
    key_list = jax.random.split(jax.random.key(seed), 14)
    return {
        "inputs": bell_draw(key_list[0], (MICRO, SEQS, LENGTH, D), 1.0, 6.0, ((1, 2), (2, 4))),
        "cotangent": bell_draw(key_list[1], (MICRO, SEQS, LENGTH, D), 1.0, 6.0, ((1, 2), (2, 4))),
        "picture_starts": draw_picture_starts(jax.random.fold_in(key_list[13], 71), 0),
        "qkv_weight": bell_draw(key_list[3], (3, D, D), D ** -0.5, 0.21875, ((1, 2), (2, 4))),
        "out_weight": bell_draw(key_list[4], (D, D), (D // 64) ** -0.5, 1.75, ((0, 4), (1, 2))),
        "up_weight": bell_draw(key_list[5], (D, FF), D ** -0.5, 0.21875, ((0, 2), (1, 4))),
        "down_weight": bell_draw(key_list[6], (FF, D), FF ** -0.5, 0.109375, ((0, 4), (1, 2))),
        "query_map": bell_draw(key_list[7], (H, HD, HD), (HD // 4) ** -0.5, 1.5, ((0, 4), (1, 2))),
        "key_map": bell_draw(key_list[8], (H, HD, HD), (HD // 4) ** -0.5, 1.5, ((0, 4), (1, 2))),
        "first_gain": jnp.clip(1.0 + 0.1 * jax.random.normal(key_list[9], (D,), jnp.float32), 0.5, 1.5).astype(jnp.bfloat16),
        "first_bias": bell_draw(key_list[10], (D,), 0.5, 3.0, ((0, 2),)),
        "second_gain": jnp.clip(1.0 + 0.1 * jax.random.normal(key_list[11], (D,), jnp.float32), 0.5, 1.5).astype(jnp.bfloat16),
        "second_bias": bell_draw(key_list[12], (D,), 0.5, 3.0, ((0, 2),)),
    }


epsilon = 1e-05
highest = lax.Precision.HIGHEST

@jax.custom_vjp
def low(v):
    return lax.optimization_barrier(v.astype(jnp.bfloat16)).astype(jnp.float32)

@jax.custom_vjp
def low_back(v):
    return v

def low_keep(v):
    return (low(v), None)

def low_pass(kept, grad):
    return (grad,)

def back_keep(v):
    return (v, None)

def back_low(kept, grad):
    return (low(grad),)
low.defvjp(low_keep, low_pass)
low_back.defvjp(back_keep, back_low)

def product(form, left, right):
    return jnp.einsum(form, left, right, precision=highest)

def layer_norm(values, norm_gain, norm_bias):
    center = values - lax.optimization_barrier(jnp.mean(values, -1, keepdims=True))
    spread = lax.optimization_barrier(jnp.mean(center * center, -1, keepdims=True))
    return center * lax.rsqrt(spread + epsilon) * norm_gain + norm_bias

def features(logits):
    return jnp.concatenate([jax.nn.softmax(logits, -1), jax.nn.softmax(-logits, -1)], -1)

def before_each(values):
    running = jnp.cumsum(values, 0)
    return jnp.concatenate([jnp.zeros_like(values[:1]), running[:-1]], 0)

def sequence(seq_inputs, start_row, params):
    qkv_weight, out_weight, up_weight, down_weight, query_map, key_map, first_gain, first_bias, second_gain, second_bias = params
    length_now = seq_inputs.shape[0]
    block_count = length_now // BLK
    normed_one = low(layer_norm(seq_inputs, first_gain, first_bias))
    projected = low(low_back(product('ld,cde->cle', normed_one, qkv_weight)))
    heads_all = projected.reshape(3, length_now, H, HD)
    query_logits = low_back(product('lhi,hij->lhj', heads_all[0], query_map))
    key_logits = low_back(product('lhi,hij->lhj', heads_all[1], key_map))
    query_feat = low(features(query_logits)).reshape(block_count, BLK, H, FEAT)
    key_feat = low(features(key_logits)).reshape(block_count, BLK, H, FEAT)
    value_rows = heads_all[2].reshape(block_count, BLK, H, HD)
    states = low_back(product('nshf,nshe->nhfe', key_feat, value_rows))
    prior_states = low(before_each(states))
    prior_sums = before_each(lax.optimization_barrier(jnp.sum(key_feat, 1)))
    position = jnp.arange(BLK, dtype=jnp.int32)
    causal = position[None, :] <= position[:, None]
    block_ids = jnp.arange(block_count, dtype=jnp.int32)
    block_flags = lax.optimization_barrier(jnp.sum((start_row[:, None] // BLK == block_ids[None, :]).astype(jnp.int32), 0)) > 0
    allowed = causal[None] | block_flags[:, None, None]
    scores = product('nthf,nshf->nhts', query_feat, key_feat)
    scores = low(low_back(jnp.where(allowed[:, None], scores, 0.0)))
    numerator = product('nhts,nshe->nthe', scores, value_rows) + product('nthf,nhfe->nthe', query_feat, prior_states)
    denominator = lax.optimization_barrier(jnp.sum(scores, -1)).transpose(0, 2, 1) + product('nthf,nhf->nth', query_feat, prior_sums)
    mixed_heads = low(low_back(numerator) / denominator[..., None]).reshape(length_now, N_TENSOR, D // N_TENSOR)
    out_groups = out_weight.reshape(N_TENSOR, D // N_TENSOR, D)
    attended = low_back(lax.optimization_barrier(jnp.sum(low(product('lgk,gkd->gld', mixed_heads, out_groups)), 0)))
    middle = seq_inputs + attended
    normed_two = low(layer_norm(middle, second_gain, second_bias))
    hidden_pre = low_back(product('ld,df->lf', normed_two, up_weight))
    hidden_low = low(jax.nn.gelu(hidden_pre, approximate=True)).reshape(length_now, N_TENSOR, FF // N_TENSOR)
    down_groups = down_weight.reshape(N_TENSOR, FF // N_TENSOR, D)
    branch = low_back(lax.optimization_barrier(jnp.sum(low(product('lgk,gkd->gld', hidden_low, down_groups)), 0)))
    return middle + branch

def reference(inputs, cotangent, picture_starts, qkv_weight, out_weight, up_weight, down_weight, query_map, key_map, first_gain, first_bias, second_gain, second_bias):
    params = (qkv_weight.astype(jnp.float32), out_weight.astype(jnp.float32), up_weight.astype(jnp.float32), down_weight.astype(jnp.float32), query_map.astype(jnp.float32), key_map.astype(jnp.float32), first_gain.astype(jnp.float32), first_bias.astype(jnp.float32), second_gain.astype(jnp.float32), second_bias.astype(jnp.float32))
    flat_inputs = inputs.astype(jnp.float32).reshape(MICRO * SEQS, LENGTH, D)
    start_rows = picture_starts.reshape(MICRO * SEQS, PICS).astype(jnp.int32)
    checked = jax.checkpoint(sequence)

    def forward(seq_all, weights_all):

        def one_sequence(seq_pair):
            return checked(seq_pair[0], seq_pair[1], weights_all)
        return lax.map(one_sequence, (seq_all, start_rows))
    result, pull_back = jax.vjp(forward, flat_inputs, params)
    input_grad, grad_params = pull_back(cotangent.astype(jnp.float32).reshape(MICRO * SEQS, LENGTH, D))
    return (result.astype(jnp.bfloat16).reshape(MICRO, SEQS, LENGTH, D), input_grad.reshape(MICRO, SEQS, LENGTH, D), grad_params[0], grad_params[1], grad_params[2], grad_params[3], grad_params[4], grad_params[5], grad_params[6], grad_params[7], grad_params[8], grad_params[9])
```

```python
import jax
import jax.numpy as jnp
from jax import lax
from jax.sharding import PartitionSpec as P

BLK = 256
MICRO = 2


epsilon = 1e-05
highest = lax.Precision.HIGHEST


EVERY = ("fsdp", "context", "tensor")


def carried_in(value, backward):
    slot, mine = lax.axis_index("tensor"), lax.axis_index("context")
    near = lax.all_gather(value, "tensor")
    far = lax.all_gather(jnp.sum(near, 0).astype(value.dtype), "context")
    near_ids = jnp.arange(near.shape[0]).reshape((-1,) + (1,) * value.ndim)
    far_ids = jnp.arange(far.shape[0]).reshape((-1,) + (1,) * value.ndim)
    near_mask = near_ids > slot if backward else near_ids < slot
    far_mask = far_ids > mine if backward else far_ids < mine
    near, far = near.astype(jnp.float32), far.astype(jnp.float32)
    return jnp.sum(jnp.where(near_mask, near, 0.0), 0) + jnp.sum(jnp.where(far_mask, far, 0.0), 0)


def layer_norm(values, norm_gain, norm_bias):
    center = values - jnp.mean(values, -1, keepdims=True)
    spread = jnp.mean(center * center, -1, keepdims=True)
    return center * lax.rsqrt(spread + epsilon) * norm_gain + norm_bias


def features(logits):
    return jnp.concatenate([jax.nn.softmax(logits, -1), jax.nn.softmax(-logits, -1)], -1)


def gelu_tanh(values):
    return jax.nn.gelu(values, approximate=True)


def prefix_before(values):
    running = jnp.cumsum(values, 1)
    return jnp.concatenate([jnp.zeros_like(values[:, :1]), running[:, :-1]], 1)


def suffix_after(values):
    running = jnp.flip(jnp.cumsum(jnp.flip(values, 1), 1), 1)
    return jnp.concatenate([running[:, 1:], jnp.zeros_like(values[:, :1])], 1)


def spread(part, axis, parts):
    own = lax.axis_index("context")
    size = part.shape[axis] // parts
    mine = lax.dynamic_slice_in_dim(part, own * size, size, axis)
    return lax.all_gather(mine, EVERY)


def full_in(part):
    pieces = spread(part, 1, lax.axis_size("context"))
    fsdp, ctx, tens = (lax.axis_size(name) for name in EVERY)
    pieces = pieces.reshape((fsdp, ctx, tens) + pieces.shape[1:])
    pieces = pieces.transpose(3, 0, 1, 4, 2, 5)
    return pieces.reshape(pieces.shape[0], -1, pieces.shape[4] * pieces.shape[5])


def share_in(grad):
    fsdp, ctx, tens = (lax.axis_size(name) for name in EVERY)
    kinds, rows, cols = grad.shape
    pieces = grad.astype(jnp.bfloat16).reshape(kinds, fsdp, ctx, rows // fsdp // ctx, tens, cols // tens)
    pieces = pieces.transpose(1, 2, 4, 0, 3, 5).reshape((-1,) + (kinds, rows // fsdp // ctx, cols // tens))
    mine = lax.psum_scatter(pieces, EVERY, scatter_dimension=0)
    return lax.all_gather(mine, "context", axis=1, tiled=True).astype(jnp.float32)


def full_rows(part):
    pieces = spread(part, 0, lax.axis_size("context"))
    fsdp, ctx, tens = (lax.axis_size(name) for name in EVERY)
    pieces = pieces.reshape((fsdp, ctx, tens) + pieces.shape[1:])
    pieces = pieces.transpose(2, 1, 3, 0, 4)
    return pieces.reshape(tens * part.shape[0], -1)


def share_rows(grad):
    fsdp, ctx, tens = (lax.axis_size(name) for name in EVERY)
    rows, cols = grad.shape
    pieces = grad.astype(jnp.bfloat16).reshape(tens, ctx, rows // tens // ctx, fsdp, cols // fsdp)
    pieces = pieces.transpose(3, 1, 0, 2, 4).reshape(-1, rows // tens // ctx, cols // fsdp)
    mine = lax.psum_scatter(pieces, EVERY, scatter_dimension=0)
    return lax.all_gather(mine, "context", axis=0, tiled=True).astype(jnp.float32)


def full_maps(part):
    pieces = lax.all_gather(part, ("fsdp", "tensor"))
    fsdp, tens = lax.axis_size("fsdp"), lax.axis_size("tensor")
    pieces = pieces.reshape((fsdp, tens) + part.shape).transpose(1, 2, 0, 3, 4)
    return pieces.reshape(tens * part.shape[0], fsdp * part.shape[1], part.shape[2])


def own_maps(total):
    fsdp, tens = lax.axis_size("fsdp"), lax.axis_size("tensor")
    heads, rows, _ = total.shape
    mine = lax.dynamic_slice_in_dim(total, lax.axis_index("tensor") * (heads // tens), heads // tens, 0)
    return lax.dynamic_slice_in_dim(mine, lax.axis_index("fsdp") * (rows // fsdp), rows // fsdp, 1)


def per_device(
    inputs,
    cotangent,
    picture_starts,
    qkv_weight,
    out_weight,
    up_weight,
    down_weight,
    query_map,
    key_map,
    first_gain,
    first_bias,
    second_gain,
    second_bias,
):
    tensor_size = lax.axis_size("tensor")
    micro, seq_local, seq_len, model_width = inputs.shape
    span = seq_len // tensor_size
    slot = lax.axis_index("tensor")
    head_size = query_map.shape[2]
    feat_size = 2 * head_size
    blocks_local = span // BLK
    seq_count = micro * seq_local
    block_total = seq_count * blocks_local
    row_count = seq_count * span
    first_block = (lax.axis_index("context") * tensor_size + slot) * blocks_local
    block_ids = first_block + jnp.arange(blocks_local, dtype=jnp.int32)
    position = jnp.arange(BLK, dtype=jnp.int32)
    causal = position[None, :] <= position[:, None]

    in_full = full_in(qkv_weight)
    out_full = full_rows(out_weight)
    up_full = full_in(up_weight[None])[0]
    down_full = full_rows(down_weight)
    qmap_full, kmap_full = full_maps(query_map), full_maps(key_map)
    norms = lax.all_gather(jnp.stack([first_gain, first_bias, second_gain, second_bias]), "fsdp", axis=1, tiled=True)
    gain_first, bias_first, gain_second, bias_second = norms.astype(jnp.float32)

    def own(values):
        mine = lax.dynamic_slice_in_dim(values, slot * span, span, 2)
        return mine.reshape(row_count, model_width)

    source = own(inputs).astype(jnp.float32)
    starts_here = picture_starts.reshape(seq_count, -1)
    block_flags = (
        jnp.sum((starts_here[:, :, None] // BLK == block_ids[None, None, :]).astype(jnp.int32), 1)
        > 0
    )
    allowed = causal[None, None] | block_flags[:, :, None, None]
    allowed = allowed.reshape(block_total, 1, BLK, BLK)
    normed_one = layer_norm(source, gain_first, bias_first)
    normed_low = normed_one.astype(jnp.bfloat16)
    projected = jnp.einsum(
        "rd,cde->cre", normed_low, in_full, preferred_element_type=jnp.float32
    ).astype(jnp.bfloat16)
    heads_local = projected.shape[2] // head_size
    queries = projected[0].reshape(row_count, heads_local, head_size)
    key_rows = projected[1].reshape(row_count, heads_local, head_size)
    value_rows = projected[2].reshape(row_count, heads_local, head_size)
    query_logits = jnp.einsum(
        "rhi,hij->rhj", queries, qmap_full, preferred_element_type=jnp.float32
    )
    key_logits = jnp.einsum(
        "rhi,hij->rhj", key_rows, kmap_full, preferred_element_type=jnp.float32
    )
    query_blocks = (
        features(query_logits)
        .astype(jnp.bfloat16)
        .reshape(block_total, BLK, heads_local, feat_size)
    )
    key_blocks = (
        features(key_logits)
        .astype(jnp.bfloat16)
        .reshape(block_total, BLK, heads_local, feat_size)
    )
    value_blocks = value_rows.reshape(block_total, BLK, heads_local, head_size)
    scores = jnp.einsum(
        "nthf,nshf->nhts", query_blocks, key_blocks, preferred_element_type=jnp.float32
    )
    weights_low = jnp.where(allowed, scores, 0.0).astype(jnp.bfloat16)
    states = jnp.einsum(
        "nshf,nshe->nhfe", key_blocks, value_blocks, preferred_element_type=jnp.float32
    )
    states = states.reshape(seq_count, blocks_local, heads_local, feat_size, head_size)
    key_sums = jnp.sum(key_blocks.astype(jnp.float32), 1).reshape(
        seq_count, blocks_local, heads_local, feat_size
    )
    state_total = jnp.sum(states, 1)
    sums_total = jnp.sum(key_sums, 1)
    carried = carried_in(state_total.astype(jnp.bfloat16), False)
    carried_sums = carried_in(sums_total, False)
    prior_states = (carried[:, None] + prefix_before(states)).astype(jnp.bfloat16)
    prior_states = prior_states.reshape(block_total, heads_local, feat_size, head_size)
    prior_sums = (carried_sums[:, None] + prefix_before(key_sums)).reshape(
        block_total, heads_local, feat_size
    )
    numerator = jnp.einsum(
        "nhts,nshe->nthe", weights_low, value_blocks, preferred_element_type=jnp.float32
    )
    numerator = numerator + jnp.einsum(
        "nthf,nhfe->nthe", query_blocks, prior_states, preferred_element_type=jnp.float32
    )
    denominator = jnp.sum(weights_low.astype(jnp.float32), -1).transpose(0, 2, 1)
    denominator = denominator + jnp.einsum(
        "nthf,nhf->nth", query_blocks.astype(jnp.float32), prior_sums, precision=highest
    )
    mixed_heads = (
        (numerator / denominator[..., None])
        .astype(jnp.bfloat16)
        .reshape(row_count, heads_local * head_size)
    )
    attended = jnp.dot(mixed_heads, out_full, preferred_element_type=jnp.float32)
    middle = source + attended
    normed_two = layer_norm(middle, gain_second, bias_second)
    normed_two_low = normed_two.astype(jnp.bfloat16)
    hidden_pre = jnp.dot(normed_two_low, up_full, preferred_element_type=jnp.float32)
    hidden_low = gelu_tanh(hidden_pre).astype(jnp.bfloat16)
    branch = jnp.dot(hidden_low, down_full, preferred_element_type=jnp.float32)
    output = (middle + branch).astype(jnp.bfloat16).reshape(micro, seq_local, span, model_width)
    output = lax.all_gather(output, "tensor", axis=2, tiled=True)
    upstream_low = own(cotangent)
    upstream = upstream_low.astype(jnp.float32)
    grad_down = jnp.einsum(
        "rk,rd->kd", hidden_low, upstream_low, preferred_element_type=jnp.float32
    )
    hidden_grad = jnp.einsum(
        "rd,kd->rk", upstream_low, down_full, preferred_element_type=jnp.float32
    )
    gelu_result, gelu_pull = jax.vjp(gelu_tanh, hidden_pre)
    pre_grad = gelu_pull(hidden_grad)[0].astype(jnp.bfloat16)
    grad_up = jnp.einsum(
        "rd,rf->df", normed_two_low, pre_grad, preferred_element_type=jnp.float32
    )
    normed_two_grad = jnp.einsum(
        "rf,df->rd", pre_grad, up_full, preferred_element_type=jnp.float32
    )
    norm_result, second_pull = jax.vjp(layer_norm, middle, gain_second, bias_second)
    middle_part, grad_gain_second, grad_bias_second = second_pull(normed_two_grad)
    middle_grad = upstream + middle_part
    middle_low = middle_grad.astype(jnp.bfloat16)
    grad_out = jnp.einsum(
        "rk,rd->kd", mixed_heads, middle_low, preferred_element_type=jnp.float32
    )
    mixed_grad = jnp.einsum(
        "rd,kd->rk", middle_low, out_full, preferred_element_type=jnp.float32
    )
    mixed_grad = mixed_grad.reshape(block_total, BLK, heads_local, head_size)
    numer_grad = (mixed_grad / denominator[..., None]).astype(jnp.bfloat16)
    denom_grad = -jnp.sum(mixed_grad * numerator, -1) / (denominator * denominator)
    weight_grad = jnp.einsum(
        "nthe,nshe->nhts", numer_grad, value_blocks, preferred_element_type=jnp.float32
    )
    weight_grad = weight_grad + denom_grad.transpose(0, 2, 1)[..., None]
    weight_grad_low = jnp.where(allowed, weight_grad, 0.0).astype(jnp.bfloat16)
    value_grad = jnp.einsum(
        "nhts,nthe->nshe", weights_low, numer_grad, preferred_element_type=jnp.float32
    )
    query_grad = jnp.einsum(
        "nhts,nshf->nthf", weight_grad_low, key_blocks, preferred_element_type=jnp.float32
    )
    query_grad = query_grad + jnp.einsum(
        "nthe,nhfe->nthf", numer_grad, prior_states, preferred_element_type=jnp.float32
    )
    query_grad = query_grad + denom_grad[..., None] * prior_sums[:, None]
    key_grad = jnp.einsum(
        "nhts,nthf->nshf", weight_grad_low, query_blocks, preferred_element_type=jnp.float32
    )
    prior_grad = jnp.einsum(
        "nthf,nthe->nhfe", query_blocks, numer_grad, preferred_element_type=jnp.float32
    )
    prior_grad = prior_grad.reshape(seq_count, blocks_local, heads_local, feat_size, head_size)
    prior_sums_grad = jnp.einsum(
        "nthf,nth->nhf", query_blocks.astype(jnp.float32), denom_grad, precision=highest
    )
    prior_sums_grad = prior_sums_grad.reshape(seq_count, blocks_local, heads_local, feat_size)
    grad_total = jnp.sum(prior_grad, 1)
    grad_sums_total = jnp.sum(prior_sums_grad, 1)
    later_states = carried_in(grad_total.astype(jnp.bfloat16), True)
    later_sums = carried_in(grad_sums_total, True)
    state_grad = (later_states[:, None] + suffix_after(prior_grad)).astype(jnp.bfloat16)
    state_grad = state_grad.reshape(block_total, heads_local, feat_size, head_size)
    sums_grad = (later_sums[:, None] + suffix_after(prior_sums_grad)).reshape(
        block_total, heads_local, feat_size
    )
    key_grad = key_grad + jnp.einsum(
        "nshe,nhfe->nshf", value_blocks, state_grad, preferred_element_type=jnp.float32
    )
    key_grad = key_grad + sums_grad[:, None]
    value_grad = value_grad + jnp.einsum(
        "nshf,nhfe->nshe", key_blocks, state_grad, preferred_element_type=jnp.float32
    )
    query_feat_now, query_pull = jax.vjp(features, query_logits)
    query_logit_grad = query_pull(query_grad.reshape(row_count, heads_local, feat_size))[
        0
    ].astype(jnp.bfloat16)
    key_feat_now, key_pull = jax.vjp(features, key_logits)
    key_logit_grad = key_pull(key_grad.reshape(row_count, heads_local, feat_size))[0].astype(
        jnp.bfloat16
    )
    grad_qmap = jnp.einsum(
        "rhi,rhj->hij", queries, query_logit_grad, preferred_element_type=jnp.float32
    )
    grad_kmap = jnp.einsum(
        "rhi,rhj->hij", key_rows, key_logit_grad, preferred_element_type=jnp.float32
    )
    raw_query_grad = jnp.einsum(
        "rhj,hij->rhi", query_logit_grad, qmap_full, preferred_element_type=jnp.float32
    )
    raw_key_grad = jnp.einsum(
        "rhj,hij->rhi", key_logit_grad, kmap_full, preferred_element_type=jnp.float32
    )
    projected_grad = jnp.stack(
        [
            raw_query_grad.reshape(row_count, -1),
            raw_key_grad.reshape(row_count, -1),
            value_grad.reshape(row_count, -1),
        ]
    ).astype(jnp.bfloat16)
    grad_in = jnp.einsum(
        "rd,cre->cde", normed_low, projected_grad, preferred_element_type=jnp.float32
    )
    normed_one_grad = jnp.einsum(
        "cre,cde->rd", projected_grad, in_full, preferred_element_type=jnp.float32
    )
    first_result, first_pull = jax.vjp(layer_norm, source, gain_first, bias_first)
    source_part, grad_gain_first, grad_bias_first = first_pull(normed_one_grad)
    input_grad = (middle_grad + source_part).astype(jnp.bfloat16)
    input_grad = input_grad.reshape(micro, seq_local, span, model_width)
    input_grad = lax.all_gather(input_grad, "tensor", axis=2, tiled=True).astype(jnp.float32)
    norm_grads = jnp.stack([grad_gain_first, grad_bias_first, grad_gain_second, grad_bias_second])
    grad_qmap, grad_kmap, norm_grads = lax.psum((grad_qmap, grad_kmap, norm_grads), EVERY)
    share = first_gain.shape[0]
    norm_grads = lax.dynamic_slice_in_dim(norm_grads, lax.axis_index("fsdp") * share, share, 1)
    return (
        output,
        input_grad,
        share_in(grad_in),
        share_rows(grad_out),
        share_in(grad_up[None])[0],
        share_rows(grad_down),
        own_maps(grad_qmap),
        own_maps(grad_kmap),
        norm_grads[0],
        norm_grads[1],
        norm_grads[2],
        norm_grads[3],
    )


def solution(mesh):
    in_specs = (
        P(None, "fsdp", "context", None),
        P(None, "fsdp", "context", None),
        P(None, "fsdp", None),
        P(None, "fsdp", "tensor"),
        P("tensor", "fsdp"),
        P("fsdp", "tensor"),
        P("tensor", "fsdp"),
        P("tensor", "fsdp", None),
        P("tensor", "fsdp", None),
        P("fsdp"),
        P("fsdp"),
        P("fsdp"),
        P("fsdp"),
    )
    out_specs = (
        P(None, "fsdp", "context", None),
        P(None, "fsdp", "context", None),
        P(None, "fsdp", "tensor"),
        P("tensor", "fsdp"),
        P("fsdp", "tensor"),
        P("tensor", "fsdp"),
        P("tensor", "fsdp", None),
        P("tensor", "fsdp", None),
        P("fsdp"),
        P("fsdp"),
        P("fsdp"),
        P("fsdp"),
    )
    return jax.shard_map(
        per_device, mesh=mesh, in_specs=in_specs, out_specs=out_specs, check_vma=False
    )
```

```python
import functools

import jax
import jax.numpy as jnp
from jax import lax
from jax.experimental import pallas as pl
from jax.experimental.pallas import tpu as pltpu
from jax.sharding import PartitionSpec as P

BLK = 256
MICRO = 2


epsilon = 1e-05
highest = lax.Precision.HIGHEST


EVERY = ("fsdp", "context", "tensor")


def carried_in(value, backward):
    slot, mine = lax.axis_index("tensor"), lax.axis_index("context")
    near = lax.all_gather(value, "tensor")
    far = lax.all_gather(jnp.sum(near, 0).astype(value.dtype), "context")
    near_ids = jnp.arange(near.shape[0]).reshape((-1,) + (1,) * value.ndim)
    far_ids = jnp.arange(far.shape[0]).reshape((-1,) + (1,) * value.ndim)
    near_mask = near_ids > slot if backward else near_ids < slot
    far_mask = far_ids > mine if backward else far_ids < mine
    near, far = near.astype(jnp.float32), far.astype(jnp.float32)
    return jnp.sum(jnp.where(near_mask, near, 0.0), 0) + jnp.sum(jnp.where(far_mask, far, 0.0), 0)


def layer_norm(values, norm_gain, norm_bias):
    center = values - jnp.mean(values, -1, keepdims=True)
    spread = jnp.mean(center * center, -1, keepdims=True)
    return center * lax.rsqrt(spread + epsilon) * norm_gain + norm_bias


def features(logits):
    return jnp.concatenate([jax.nn.softmax(logits, -1), jax.nn.softmax(-logits, -1)], -1)


def gelu_tanh(values):
    return jax.nn.gelu(values, approximate=True)


def prefix_before(values):
    running = jnp.cumsum(values, 1)
    return jnp.concatenate([jnp.zeros_like(values[:, :1]), running[:, :-1]], 1)


def suffix_after(values):
    running = jnp.flip(jnp.cumsum(jnp.flip(values, 1), 1), 1)
    return jnp.concatenate([running[:, 1:], jnp.zeros_like(values[:, :1])], 1)


def spread(part, axis, parts):
    own = lax.axis_index("context")
    size = part.shape[axis] // parts
    mine = lax.dynamic_slice_in_dim(part, own * size, size, axis)
    return lax.all_gather(mine, EVERY)


def full_in(part):
    pieces = spread(part, 1, lax.axis_size("context"))
    fsdp, ctx, tens = (lax.axis_size(name) for name in EVERY)
    pieces = pieces.reshape((fsdp, ctx, tens) + pieces.shape[1:])
    pieces = pieces.transpose(3, 0, 1, 4, 2, 5)
    return pieces.reshape(pieces.shape[0], -1, pieces.shape[4] * pieces.shape[5])


def share_in(grad):
    fsdp, ctx, tens = (lax.axis_size(name) for name in EVERY)
    kinds, rows, cols = grad.shape
    pieces = grad.astype(jnp.bfloat16).reshape(kinds, fsdp, ctx, rows // fsdp // ctx, tens, cols // tens)
    pieces = pieces.transpose(1, 2, 4, 0, 3, 5).reshape((-1,) + (kinds, rows // fsdp // ctx, cols // tens))
    mine = lax.psum_scatter(pieces, EVERY, scatter_dimension=0)
    return lax.all_gather(mine, "context", axis=1, tiled=True).astype(jnp.float32)


def full_rows(part):
    pieces = spread(part, 0, lax.axis_size("context"))
    fsdp, ctx, tens = (lax.axis_size(name) for name in EVERY)
    pieces = pieces.reshape((fsdp, ctx, tens) + pieces.shape[1:])
    pieces = pieces.transpose(2, 1, 3, 0, 4)
    return pieces.reshape(tens * part.shape[0], -1)


def share_rows(grad):
    fsdp, ctx, tens = (lax.axis_size(name) for name in EVERY)
    rows, cols = grad.shape
    pieces = grad.astype(jnp.bfloat16).reshape(tens, ctx, rows // tens // ctx, fsdp, cols // fsdp)
    pieces = pieces.transpose(3, 1, 0, 2, 4).reshape(-1, rows // tens // ctx, cols // fsdp)
    mine = lax.psum_scatter(pieces, EVERY, scatter_dimension=0)
    return lax.all_gather(mine, "context", axis=0, tiled=True).astype(jnp.float32)


def full_maps(part):
    pieces = lax.all_gather(part, ("fsdp", "tensor"))
    fsdp, tens = lax.axis_size("fsdp"), lax.axis_size("tensor")
    pieces = pieces.reshape((fsdp, tens) + part.shape).transpose(1, 2, 0, 3, 4)
    return pieces.reshape(tens * part.shape[0], fsdp * part.shape[1], part.shape[2])


def own_maps(total):
    fsdp, tens = lax.axis_size("fsdp"), lax.axis_size("tensor")
    heads, rows, _ = total.shape
    mine = lax.dynamic_slice_in_dim(total, lax.axis_index("tensor") * (heads // tens), heads // tens, 0)
    return lax.dynamic_slice_in_dim(mine, lax.axis_index("fsdp") * (rows // fsdp), rows // fsdp, 1)


MESH = pl.DeviceIdType.MESH
bf16 = jnp.bfloat16
f32 = jnp.float32


def whereabouts():
    return tuple(lax.axis_index(name) for name in EVERY)


def neighbours(f, c, t):
    n = c * 4 + t
    peers = [(1 - f, c, t)]
    for k in range(1, 16):
        other = lax.rem(n + k, 16)
        peers.append((f, other // 4, lax.rem(other, 4)))
    return peers


def meet(f, c, t):
    barrier = pltpu.get_barrier_semaphore()
    peers = neighbours(f, c, t)
    for peer in peers:
        pl.semaphore_signal(barrier, inc=1, device_id=peer, device_id_type=MESH)
    pl.semaphore_wait(barrier, len(peers))


def send(src, dst, send_sem, recv_sem, peer):
    copy = pltpu.make_async_remote_copy(
        src_ref=src, dst_ref=dst, send_sem=send_sem, recv_sem=recv_sem,
        device_id=peer, device_id_type=MESH,
    )
    copy.start()
    return copy


def arrived(ref, sem):
    pltpu.make_async_copy(ref, ref, sem).wait()


def at(start, size, unit):
    return pl.ds(pl.multiple_of(start, unit), size)


def half(ref, m, f):
    if len(ref.shape) == 4:
        w = ref.shape[3] // 2
        return ref.at[:, :, :, at(f * w, w, 128)]
    if len(ref.shape) == 3 and m == 1:
        w = ref.shape[2] // 2
        return ref.at[:, :, at(f * w, w, 128)]
    if m == 0:
        w = ref.shape[2] // 2
        return ref.at[:, :, at(f * w, w, 128)]
    if m == 1:
        w = ref.shape[1] // 2
        return ref.at[:, at(f * w, w, 128)]
    w = ref.shape[0] // 2
    return ref.at[at(f * w, w, 16), :]


def shard(ref, m, f, t):
    if m == 0:
        w, h = ref.shape[2] // 2, ref.shape[1] // 4
        return ref.at[:, at(t * h, h, 16), at(f * w, w, 128)]
    if m == 1:
        w, h = ref.shape[1] // 2, ref.shape[0] // 4
        return ref.at[at(t * h, h, 16), at(f * w, w, 128)]
    h, w = ref.shape[0] // 2, ref.shape[1] // 4
    return ref.at[at(f * h, h, 16), at(t * w, w, 128)]


def piece(ref, m, f, c, t):
    if m == 0:
        w, h = ref.shape[2] // 2, ref.shape[1] // 16
        return ref.at[:, at(t * 4 * h + c * h, h, 16), at(f * w, w, 128)]
    if m == 1:
        w, h = ref.shape[1] // 2, ref.shape[0] // 16
        return ref.at[at(t * 4 * h + c * h, h, 16), at(f * w, w, 128)]
    h, w = ref.shape[0] // 8, ref.shape[1] // 4
    return ref.at[at(f * 4 * h + c * h, h, 16), at(t * w, w, 128)]


def quarter(ref, m, c):
    if m == 0:
        h = ref.shape[1] // 4
        return ref.at[:, at(c * h, h, 16), :]
    h = ref.shape[0] // 4
    return ref.at[at(c * h, h, 16), :]


def gather_kernel(*refs):
    shards, fulls = refs[:4], refs[4:8]
    local_sem, send_sem, z_sem, xy_sem, pair_sem = refs[8:]
    f, c, t = whereabouts()
    meet(f, c, t)
    partner = (1 - f, c, t)
    started = []
    local = []
    for m in range(4):
        for k in range(1, 4):
            peer = (f, c, lax.rem(t + k, 4))
            started.append(send(quarter(shards[m], m, c), piece(fulls[m], m, f, c, t),
                                send_sem.at[m], z_sem.at[m, k], peer))
    for m in range(4):
        copy = pltpu.make_async_copy(shards[m], shard(fulls[m], m, f, t), local_sem.at[m])
        copy.start()
        local.append(copy)
        started.append(send(shards[m], shard(fulls[m], m, f, t), send_sem.at[m], pair_sem.at[m], partner))
    for m in range(4):
        for k in range(1, 4):
            source = lax.rem(t + 4 - k, 4)
            got = piece(fulls[m], m, f, c, source)
            arrived(got, z_sem.at[m, k])
            for j in range(1, 4):
                started.append(send(got, got, send_sem.at[m], xy_sem.at[m, k, j], (f, c ^ j, t)))
            started.append(send(got, got, send_sem.at[m], pair_sem.at[m], partner))
    for m in range(4):
        for k in range(1, 4):
            source = lax.rem(t + 4 - k, 4)
            for j in range(1, 4):
                got = piece(fulls[m], m, f, c ^ j, source)
                arrived(got, xy_sem.at[m, k, j])
                started.append(send(got, got, send_sem.at[m], pair_sem.at[m], partner))
    for m in range(4):
        arrived(half(fulls[m], m, 1 - f), pair_sem.at[m])
        local[m].wait()
    for copy in started:
        copy.wait_send()


def gather_weights(shards):
    d = shards[0].shape[2] * 2
    ff = shards[2].shape[1] * 4
    shapes = [(3, d, d), (d, d), (d, ff), (d, ff)]
    dma = pltpu.SemaphoreType.DMA
    return pl.pallas_call(
        gather_kernel,
        out_shape=[jax.ShapeDtypeStruct(s, bf16) for s in shapes],
        in_specs=[pl.BlockSpec(memory_space=pl.ANY)] * 4,
        out_specs=[pl.BlockSpec(memory_space=pltpu.VMEM)] * 4,
        scratch_shapes=[dma((4,)), dma((4,)), dma((4, 4)), dma((4, 4, 4)), dma((4,))],
        compiler_params=pltpu.CompilerParams(collective_id=0, has_side_effects=True, vmem_limit_bytes=60 << 20),
        name="gather_weights",
    )(*shards)


def scan_kernel(backward, s_ref, z_ref, p_ref, q_ref, s_in, z_in, s_out, z_out, own_sem, send_sem, s_sem, z_sem, p_sem, q_sem):
    f, c, t = whereabouts()
    n = c * 4 + t
    peers = neighbours(f, c, t)
    meet(f, c, t)
    rows = s_ref.shape[1] // 16
    started = []
    for k in range(1, 16):
        other = lax.rem(n + k, 16)
        started.append(send(s_ref.at[:, at(other * rows, rows, 16), :], s_in.at[n], send_sem, s_sem, peers[k]))
        started.append(send(z_ref.at[other], z_in.at[n], send_sem, z_sem, peers[k]))
    a = pltpu.make_async_copy(s_ref.at[:, at(n * rows, rows, 16), :], s_in.at[n], own_sem.at[0])
    b = pltpu.make_async_copy(z_ref.at[n], z_in.at[n], own_sem.at[1])
    a.start()
    b.start()
    a.wait()
    b.wait()
    arrived(s_in.at[pl.ds(0, 15)], s_sem)
    arrived(z_in.at[pl.ds(0, 15)], z_sem)
    total = jnp.zeros(s_in.shape[1:], f32)
    sums = jnp.zeros(z_in.shape[1:], f32)
    order = range(15, -1, -1) if backward else range(16)
    for i in order:
        s_out[i] = total.astype(bf16)
        z_out[i] = sums
        total = total + s_in[i].astype(f32)
        sums = sums + z_in[i]
    back = []
    for k in range(1, 16):
        other = lax.rem(n + k, 16)
        back.append(send(s_out.at[other], p_ref.at[:, at(n * rows, rows, 16), :], send_sem, p_sem, peers[k]))
        back.append(send(z_out.at[other], q_ref.at[n], send_sem, q_sem, peers[k]))
    a = pltpu.make_async_copy(s_out.at[n], p_ref.at[:, at(n * rows, rows, 16), :], own_sem.at[0])
    b = pltpu.make_async_copy(z_out.at[n], q_ref.at[n], own_sem.at[1])
    a.start()
    b.start()
    a.wait()
    b.wait()
    arrived(s_in.at[pl.ds(0, 15)], p_sem)
    arrived(z_in.at[pl.ds(0, 15)], q_sem)
    for copy in started + back:
        copy.wait_send()


def scan_states(states, sums, backward):
    seqs, rows, lanes = states.shape
    dma = pltpu.SemaphoreType.DMA
    return pl.pallas_call(
        functools.partial(scan_kernel, backward),
        out_shape=[jax.ShapeDtypeStruct(states.shape, bf16), jax.ShapeDtypeStruct(sums.shape, f32)],
        in_specs=[pl.BlockSpec(memory_space=pltpu.VMEM)] * 2,
        out_specs=[pl.BlockSpec(memory_space=pltpu.VMEM)] * 2,
        scratch_shapes=[
            pltpu.VMEM((16, seqs, rows // 16, lanes), bf16), pltpu.VMEM((16,) + sums.shape[1:], f32),
            pltpu.VMEM((16, seqs, rows // 16, lanes), bf16), pltpu.VMEM((16,) + sums.shape[1:], f32),
            dma((2,)), dma(()), dma(()), dma(()), dma(()), dma(()),
        ],
        compiler_params=pltpu.CompilerParams(
            collective_id=2 if backward else 1, has_side_effects=True, vmem_limit_bytes=32 << 20
        ),
        name="scan_states",
    )(states, sums)


def summed(m, t_count, refs):
    total = refs[0][...].astype(f32)
    for ref in refs[1:]:
        total = total + ref[...].astype(f32)
    return total


def reduce_kernel(*refs):
    grads, small, rows_out, rows_in = refs[:4], refs[4], refs[5], refs[6]
    outs, small_out, all_out, all_in = refs[7:11], refs[11], refs[12], refs[13]
    own, pair_in, sums, xy_in, z_in, last = (refs[14 + 4 * i : 18 + 4 * i] for i in range(6))
    small_pair, small_own, small_in, small_sum = refs[38:42]
    local_sem, send_sem, rows_sem, pair_sem, xy_sem, z_sem, last_sem, small_sem = refs[42:]
    f, c, t = whereabouts()
    n = c * 4 + t
    peers = neighbours(f, c, t)
    partner = peers[0]
    meet(f, c, t)
    started = []
    for i, (src, dst) in enumerate(((rows_out, all_out), (rows_in, all_in))):
        for k in range(1, 4):
            peer = (f, c, lax.rem(t + k, 4))
            started.append(send(src, dst.at[:, t], send_sem, rows_sem.at[i, k], peer))
    copies = []
    for i, (src, dst) in enumerate(((rows_out, all_out), (rows_in, all_in))):
        copy = pltpu.make_async_copy(src, dst.at[:, t], local_sem.at[i])
        copy.start()
        copies.append(copy)
    for m in range(4):
        started.append(send(half(grads[m], m, 1 - f), pair_in[m], send_sem, pair_sem.at[m], partner))
    started.append(send(small, small_pair, send_sem, small_sem.at[0], partner))
    for m in range(4):
        copy = pltpu.make_async_copy(half(grads[m], m, f), own[m], local_sem.at[2 + m])
        copy.start()
        copies.append(copy)
    for copy in copies:
        copy.wait()
    arrived(small_pair, small_sem.at[0])
    small_own[...] = (small[...] + small_pair[...]).astype(bf16)
    for k in range(1, 16):
        other = lax.rem(n + k, 16)
        started.append(send(small_own.at[other], small_in.at[n], send_sem, small_sem.at[1], peers[k]))
    copy = pltpu.make_async_copy(small_own.at[n], small_in.at[n], local_sem.at[6])
    copy.start()
    copy.wait()
    for m in range(4):
        arrived(pair_in[m], pair_sem.at[m])
        own[m][...] = (own[m][...].astype(f32) + pair_in[m][...].astype(f32)).astype(bf16)
        for j in range(1, 4):
            started.append(send(context_part(own[m], m, c ^ j), xy_in[m].at[j - 1], send_sem, xy_sem.at[m, j], (f, c ^ j, t)))
    arrived(small_in.at[pl.ds(0, 15)], small_sem.at[1])
    total = jnp.zeros(small_in.shape[1:], f32)
    for i in range(16):
        total = total + small_in[i].astype(f32)
    small_sum[...] = total
    for k in range(1, 16):
        started.append(send(small_sum, small_out.at[n], send_sem, small_sem.at[2], peers[k]))
    copy = pltpu.make_async_copy(small_sum, small_out.at[n], local_sem.at[6])
    copy.start()
    copy.wait()
    for m in range(4):
        copy = pltpu.make_async_copy(context_part(own[m], m, c), sums[m], local_sem.at[7 + m])
        copy.start()
        copy.wait()
        for j in range(1, 4):
            arrived(xy_in[m].at[j - 1], xy_sem.at[m, j])
        total = sums[m][...].astype(f32)
        for j in range(3):
            total = total + xy_in[m][j].astype(f32)
        sums[m][...] = total.astype(bf16)
        for k in range(1, 4):
            other = lax.rem(t + k, 4)
            started.append(send(tensor_part(sums[m], m, other), z_in[m].at[k - 1], send_sem, z_sem.at[m, k], (f, c, other)))
    for m in range(4):
        copy = pltpu.make_async_copy(tensor_part(sums[m], m, t), last[m], local_sem.at[11 + m])
        copy.start()
        copy.wait()
        for k in range(1, 4):
            arrived(z_in[m].at[k - 1], z_sem.at[m, k])
        total = last[m][...].astype(f32)
        for k in range(3):
            total = total + z_in[m][k].astype(f32)
        last[m][...] = total.astype(bf16)
        for j in range(1, 4):
            started.append(send(last[m], quarter(outs[m], m, c), send_sem, last_sem.at[m, j], (f, c ^ j, t)))
        copy = pltpu.make_async_copy(last[m], quarter(outs[m], m, c), local_sem.at[15 + m])
        copy.start()
        copy.wait()
    for m in range(4):
        for j in range(1, 4):
            arrived(last[m], last_sem.at[m, j])
    arrived(small_out.at[pl.ds(0, 15)], small_sem.at[2])
    for i, dst in enumerate((all_out, all_in)):
        for k in range(1, 4):
            arrived(dst.at[:, 0], rows_sem.at[i, k])
    for copy in started:
        copy.wait_send()


def context_part(ref, m, c):
    if m == 0:
        h = ref.shape[2] // 4
        return ref.at[:, :, at(c * h, h, 16), :]
    if m == 1:
        h = ref.shape[1] // 4
        return ref.at[:, at(c * h, h, 16), :]
    h = ref.shape[0] // 4
    return ref.at[at(c * h, h, 16), :]


def tensor_part(ref, m, t):
    if m == 0:
        return ref.at[:, t]
    if m == 1:
        return ref.at[t]
    w = ref.shape[1] // 4
    return ref.at[:, at(t * w, w, 128)]


def reduce_grads(grads, small, rows_out, rows_in):
    dma = pltpu.SemaphoreType.DMA
    d, ff = grads[2].shape
    own = [(3, 4, d // 4, d // 2), (4, d // 4, d // 2), (d // 2, ff), (d // 2, ff)]
    sums = [(3, 4, d // 16, d // 2), (4, d // 16, d // 2), (d // 8, ff), (d // 8, ff)]
    last = [(3, d // 16, d // 2), (d // 16, d // 2), (d // 8, ff // 4), (d // 8, ff // 4)]
    outs = [(3, d // 4, d // 2), (d // 4, d // 2), (d // 2, ff // 4), (d // 2, ff // 4)]
    piece_rows = small.shape[1:]
    scratch = []
    for m in range(4):
        pass
    scratch += [pltpu.VMEM(s, bf16) for s in own]
    scratch += [pltpu.VMEM(s, bf16) for s in own]
    scratch += [pltpu.VMEM(s, bf16) for s in sums]
    scratch += [pltpu.VMEM((3,) + s, bf16) for s in sums]
    scratch += [pltpu.VMEM((3,) + s, bf16) for s in last]
    scratch += [pltpu.VMEM(s, bf16) for s in last]
    scratch += [
        pltpu.VMEM(small.shape, f32), pltpu.VMEM(small.shape, bf16), pltpu.VMEM(small.shape, bf16),
        pltpu.VMEM(piece_rows, f32),
    ]
    scratch += [dma((19,)), dma(()), dma((2, 4)), dma((4,)), dma((4, 4)), dma((4, 4)), dma((4, 4)), dma((3,))]
    spread_rows = (rows_out.shape[0], 4) + rows_out.shape[1:]
    return pl.pallas_call(
        reduce_kernel,
        out_shape=[jax.ShapeDtypeStruct(s, bf16) for s in outs]
        + [jax.ShapeDtypeStruct(small.shape, f32)]
        + [jax.ShapeDtypeStruct(spread_rows, bf16)] * 2,
        in_specs=[pl.BlockSpec(memory_space=pltpu.VMEM)] * 7,
        out_specs=[pl.BlockSpec(memory_space=pltpu.VMEM)] * 7,
        scratch_shapes=scratch,
        compiler_params=pltpu.CompilerParams(collective_id=3, has_side_effects=True, vmem_limit_bytes=60 << 20),
        name="reduce_grads",
    )(*grads, small, rows_out, rows_in)


def per_device(
    meshed,
    inputs,
    cotangent,
    picture_starts,
    qkv_weight,
    out_weight,
    up_weight,
    down_weight,
    query_map,
    key_map,
    first_gain,
    first_bias,
    second_gain,
    second_bias,
):
    tensor_size = lax.axis_size("tensor")
    micro, seq_local, seq_len, model_width = inputs.shape
    span = seq_len // tensor_size
    slot = lax.axis_index("tensor")
    head_size = query_map.shape[2]
    feat_size = 2 * head_size
    blocks_local = span // BLK
    seq_count = micro * seq_local
    block_total = seq_count * blocks_local
    row_count = seq_count * span
    first_block = (lax.axis_index("context") * tensor_size + slot) * blocks_local
    block_ids = first_block + jnp.arange(blocks_local, dtype=jnp.int32)
    position = jnp.arange(BLK, dtype=jnp.int32)
    causal = position[None, :] <= position[:, None]

    shards = (qkv_weight.transpose(0, 2, 1), out_weight, up_weight, down_weight.T)
    if meshed:
        in_full, out_full, up_full, down_full = gather_weights(shards)
    else:
        in_full = full_in(qkv_weight).transpose(0, 2, 1)
        out_full = full_rows(out_weight)
        up_full = full_in(up_weight[None])[0]
        down_full = full_rows(down_weight).T
    qmap_full, kmap_full = full_maps(query_map), full_maps(key_map)
    norms = lax.all_gather(jnp.stack([first_gain, first_bias, second_gain, second_bias]), "fsdp", axis=1, tiled=True)
    gain_first, bias_first, gain_second, bias_second = norms.astype(jnp.float32)

    def own(values):
        mine = lax.dynamic_slice_in_dim(values, slot * span, span, 2)
        return mine.reshape(row_count, model_width)

    source = own(inputs).astype(jnp.float32)
    starts_here = picture_starts.reshape(seq_count, -1)
    block_flags = (
        jnp.sum((starts_here[:, :, None] // BLK == block_ids[None, None, :]).astype(jnp.int32), 1)
        > 0
    )
    allowed = causal[None, None] | block_flags[:, :, None, None]
    allowed = allowed.reshape(block_total, 1, BLK, BLK)
    normed_one = layer_norm(source, gain_first, bias_first)
    normed_low = normed_one.astype(jnp.bfloat16)
    projected = jnp.einsum(
        "rd,ced->cre", normed_low, in_full, preferred_element_type=jnp.float32
    ).astype(jnp.bfloat16)
    heads_local = projected.shape[2] // head_size
    queries = projected[0].reshape(row_count, heads_local, head_size)
    key_rows = projected[1].reshape(row_count, heads_local, head_size)
    value_rows = projected[2].reshape(row_count, heads_local, head_size)
    query_logits = jnp.einsum(
        "rhi,hij->rhj", queries, qmap_full, preferred_element_type=jnp.float32
    )
    key_logits = jnp.einsum(
        "rhi,hij->rhj", key_rows, kmap_full, preferred_element_type=jnp.float32
    )
    query_blocks = (
        features(query_logits)
        .astype(jnp.bfloat16)
        .reshape(block_total, BLK, heads_local, feat_size)
    )
    key_blocks = (
        features(key_logits)
        .astype(jnp.bfloat16)
        .reshape(block_total, BLK, heads_local, feat_size)
    )
    value_blocks = value_rows.reshape(block_total, BLK, heads_local, head_size)
    scores = jnp.einsum(
        "nthf,nshf->nhts", query_blocks, key_blocks, preferred_element_type=jnp.float32
    )
    weights_low = jnp.where(allowed, scores, 0.0).astype(jnp.bfloat16)
    states = jnp.einsum(
        "nshf,nshe->nhfe", key_blocks, value_blocks, preferred_element_type=jnp.float32
    )
    states = states.reshape(seq_count, blocks_local, heads_local, feat_size, head_size)
    key_sums = jnp.sum(key_blocks.astype(jnp.float32), 1).reshape(
        seq_count, blocks_local, heads_local, feat_size
    )
    prior_states, prior_sums = carried_states(meshed, states, key_sums, False)
    numerator = jnp.einsum(
        "nhts,nshe->nthe", weights_low, value_blocks, preferred_element_type=jnp.float32
    )
    numerator = numerator + jnp.einsum(
        "nthf,nhfe->nthe", query_blocks, prior_states, preferred_element_type=jnp.float32
    )
    denominator = jnp.sum(weights_low.astype(jnp.float32), -1).transpose(0, 2, 1)
    denominator = denominator + jnp.einsum(
        "nthf,nhf->nth", query_blocks.astype(jnp.float32), prior_sums, precision=highest
    )
    mixed_heads = (
        (numerator / denominator[..., None])
        .astype(jnp.bfloat16)
        .reshape(row_count, heads_local * head_size)
    )
    attended = jnp.dot(mixed_heads, out_full, preferred_element_type=jnp.float32)
    middle = source + attended
    normed_two = layer_norm(middle, gain_second, bias_second)
    normed_two_low = normed_two.astype(jnp.bfloat16)
    hidden_pre = jnp.dot(normed_two_low, up_full, preferred_element_type=jnp.float32)
    hidden_low = gelu_tanh(hidden_pre).astype(jnp.bfloat16)
    branch = jnp.einsum("rk,dk->rd", hidden_low, down_full, preferred_element_type=jnp.float32)
    output = (middle + branch).astype(jnp.bfloat16)
    upstream_low = own(cotangent)
    upstream = upstream_low.astype(jnp.float32)
    grad_down = jnp.einsum(
        "rk,rd->dk", hidden_low, upstream_low, preferred_element_type=jnp.float32
    )
    hidden_grad = jnp.einsum(
        "rd,dk->rk", upstream_low, down_full, preferred_element_type=jnp.float32
    )
    gelu_result, gelu_pull = jax.vjp(gelu_tanh, hidden_pre)
    pre_grad = gelu_pull(hidden_grad)[0].astype(jnp.bfloat16)
    grad_up = jnp.einsum(
        "rd,rf->df", normed_two_low, pre_grad, preferred_element_type=jnp.float32
    )
    normed_two_grad = jnp.einsum(
        "rf,df->rd", pre_grad, up_full, preferred_element_type=jnp.float32
    )
    norm_result, second_pull = jax.vjp(layer_norm, middle, gain_second, bias_second)
    middle_part, grad_gain_second, grad_bias_second = second_pull(normed_two_grad)
    middle_grad = upstream + middle_part
    middle_low = middle_grad.astype(jnp.bfloat16)
    grad_out = jnp.einsum(
        "rk,rd->kd", mixed_heads, middle_low, preferred_element_type=jnp.float32
    )
    mixed_grad = jnp.einsum(
        "rd,kd->rk", middle_low, out_full, preferred_element_type=jnp.float32
    )
    mixed_grad = mixed_grad.reshape(block_total, BLK, heads_local, head_size)
    numer_grad = (mixed_grad / denominator[..., None]).astype(jnp.bfloat16)
    denom_grad = -jnp.sum(mixed_grad * numerator, -1) / (denominator * denominator)
    weight_grad = jnp.einsum(
        "nthe,nshe->nhts", numer_grad, value_blocks, preferred_element_type=jnp.float32
    )
    weight_grad = weight_grad + denom_grad.transpose(0, 2, 1)[..., None]
    weight_grad_low = jnp.where(allowed, weight_grad, 0.0).astype(jnp.bfloat16)
    value_grad = jnp.einsum(
        "nhts,nthe->nshe", weights_low, numer_grad, preferred_element_type=jnp.float32
    )
    query_grad = jnp.einsum(
        "nhts,nshf->nthf", weight_grad_low, key_blocks, preferred_element_type=jnp.float32
    )
    query_grad = query_grad + jnp.einsum(
        "nthe,nhfe->nthf", numer_grad, prior_states, preferred_element_type=jnp.float32
    )
    query_grad = query_grad + denom_grad[..., None] * prior_sums[:, None]
    key_grad = jnp.einsum(
        "nhts,nthf->nshf", weight_grad_low, query_blocks, preferred_element_type=jnp.float32
    )
    prior_grad = jnp.einsum(
        "nthf,nthe->nhfe", query_blocks, numer_grad, preferred_element_type=jnp.float32
    )
    prior_grad = prior_grad.reshape(seq_count, blocks_local, heads_local, feat_size, head_size)
    prior_sums_grad = jnp.einsum(
        "nthf,nth->nhf", query_blocks.astype(jnp.float32), denom_grad, precision=highest
    )
    prior_sums_grad = prior_sums_grad.reshape(seq_count, blocks_local, heads_local, feat_size)
    state_grad, sums_grad = carried_states(meshed, prior_grad, prior_sums_grad, True)
    key_grad = key_grad + jnp.einsum(
        "nshe,nhfe->nshf", value_blocks, state_grad, preferred_element_type=jnp.float32
    )
    key_grad = key_grad + sums_grad[:, None]
    value_grad = value_grad + jnp.einsum(
        "nshf,nhfe->nshe", key_blocks, state_grad, preferred_element_type=jnp.float32
    )
    query_feat_now, query_pull = jax.vjp(features, query_logits)
    query_logit_grad = query_pull(query_grad.reshape(row_count, heads_local, feat_size))[
        0
    ].astype(jnp.bfloat16)
    key_feat_now, key_pull = jax.vjp(features, key_logits)
    key_logit_grad = key_pull(key_grad.reshape(row_count, heads_local, feat_size))[0].astype(
        jnp.bfloat16
    )
    grad_qmap = jnp.einsum(
        "rhi,rhj->hij", queries, query_logit_grad, preferred_element_type=jnp.float32
    )
    grad_kmap = jnp.einsum(
        "rhi,rhj->hij", key_rows, key_logit_grad, preferred_element_type=jnp.float32
    )
    raw_query_grad = jnp.einsum(
        "rhj,hij->rhi", query_logit_grad, qmap_full, preferred_element_type=jnp.float32
    )
    raw_key_grad = jnp.einsum(
        "rhj,hij->rhi", key_logit_grad, kmap_full, preferred_element_type=jnp.float32
    )
    projected_grad = jnp.stack(
        [
            raw_query_grad.reshape(row_count, -1),
            raw_key_grad.reshape(row_count, -1),
            value_grad.reshape(row_count, -1),
        ]
    ).astype(jnp.bfloat16)
    grad_in = jnp.einsum(
        "rd,cre->ced", normed_low, projected_grad, preferred_element_type=jnp.float32
    )
    normed_one_grad = jnp.einsum(
        "cre,ced->rd", projected_grad, in_full, preferred_element_type=jnp.float32
    )
    first_result, first_pull = jax.vjp(layer_norm, source, gain_first, bias_first)
    source_part, grad_gain_first, grad_bias_first = first_pull(normed_one_grad)
    input_grad = (middle_grad + source_part).astype(jnp.bfloat16)
    norm_grads = jnp.stack([grad_gain_first, grad_bias_first, grad_gain_second, grad_bias_second])
    share = first_gain.shape[0]
    if not meshed:
        grad_qmap, grad_kmap, norm_grads = lax.psum((grad_qmap, grad_kmap, norm_grads), EVERY)
        norm_grads = lax.dynamic_slice_in_dim(norm_grads, lax.axis_index("fsdp") * share, share, 1)
        rows = (output.reshape(micro, seq_local, span, -1), input_grad.reshape(micro, seq_local, span, -1))
        all_out, all_in = (lax.all_gather(part, "tensor", axis=2, tiled=True) for part in rows)
        return (
            all_out,
            all_in.astype(jnp.float32),
            share_in(grad_in.transpose(0, 2, 1)),
            share_rows(grad_out),
            share_in(grad_up[None])[0],
            share_rows(grad_down.T),
            own_maps(grad_qmap),
            own_maps(grad_kmap),
            norm_grads[0],
            norm_grads[1],
            norm_grads[2],
            norm_grads[3],
        )
    heads = grad_qmap.shape[0]
    pairs = jnp.stack([grad_qmap, grad_kmap]).reshape(heads, 2, head_size, head_size)
    pairs = pairs.transpose(0, 2, 1, 3).reshape(-1, 2 * head_size)
    small = jnp.concatenate([pairs, norm_grads.reshape(-1, 2 * head_size)])
    small = jnp.pad(small, ((0, -small.shape[0] % 256), (0, 0))).reshape(16, -1, 2 * head_size)
    quarter_rows = model_width // 4
    grads = (
        grad_in.astype(bf16).reshape(3, 4, quarter_rows, model_width),
        grad_out.astype(bf16).reshape(4, quarter_rows, model_width),
        grad_up.astype(bf16),
        grad_down.astype(bf16),
    )
    share_0, share_1, share_2, share_3, small, all_out, all_in = reduce_grads(
        grads, small, output.reshape(micro, span, model_width), input_grad.reshape(micro, span, model_width)
    )
    small = small.reshape(-1, 2 * head_size)
    pairs = small[: heads * head_size].reshape(heads, head_size, 2, head_size)
    pairs = pairs.transpose(0, 2, 1, 3).reshape(2, heads, head_size, head_size)
    norm_grads = small[heads * head_size :].reshape(-1)[: norm_grads.size].reshape(norm_grads.shape)
    norm_grads = lax.dynamic_slice_in_dim(norm_grads, lax.axis_index("fsdp") * share, share, 1)
    return (
        all_out.reshape(inputs.shape),
        all_in.reshape(inputs.shape).astype(jnp.float32),
        share_0.astype(jnp.float32).transpose(0, 2, 1),
        share_1.astype(jnp.float32),
        share_2.astype(jnp.float32),
        share_3.astype(jnp.float32).T,
        own_maps(pairs[0]),
        own_maps(pairs[1]),
        norm_grads[0],
        norm_grads[1],
        norm_grads[2],
        norm_grads[3],
    )


def carried_states(meshed, states, sums, backward):
    seqs, blocks, heads, feats, head = states.shape
    if not meshed:
        inside = suffix_after if backward else prefix_before
        carried = carried_in(jnp.sum(states, 1).astype(bf16), backward)
        carried_sums = carried_in(jnp.sum(sums, 1), backward)
        states = (carried[:, None] + inside(states)).astype(bf16)
        sums = carried_sums[:, None] + inside(sums)
        return states.reshape((-1,) + states.shape[2:]), sums.reshape((-1,) + sums.shape[2:])
    packed = states.reshape(seqs, heads // 2, 2, feats, head).transpose(0, 1, 3, 2, 4)
    packed = packed.reshape(seqs, heads // 2 * feats, 2 * head).astype(bf16)
    rows = jnp.pad(sums.reshape(seqs, heads, feats).transpose(1, 0, 2), ((0, 16 - heads), (0, 8 - seqs), (0, 0)))
    packed, rows = scan_states(packed, rows, backward)
    packed = packed.reshape(seqs, heads // 2, feats, 2, head).transpose(0, 1, 3, 2, 4)
    return packed.reshape(seqs, heads, feats, head), rows[:heads, :seqs].transpose(1, 0, 2)


def solution(mesh):
    in_specs = (
        P(None, "fsdp", "context", None),
        P(None, "fsdp", "context", None),
        P(None, "fsdp", None),
        P(None, "fsdp", "tensor"),
        P("tensor", "fsdp"),
        P("fsdp", "tensor"),
        P("tensor", "fsdp"),
        P("tensor", "fsdp", None),
        P("tensor", "fsdp", None),
        P("fsdp"),
        P("fsdp"),
        P("fsdp"),
        P("fsdp"),
    )
    out_specs = (
        P(None, "fsdp", "context", None),
        P(None, "fsdp", "context", None),
        P(None, "fsdp", "tensor"),
        P("tensor", "fsdp"),
        P("fsdp", "tensor"),
        P("tensor", "fsdp"),
        P("tensor", "fsdp", None),
        P("tensor", "fsdp", None),
        P("fsdp"),
        P("fsdp"),
        P("fsdp"),
        P("fsdp"),
    )
    sizes = tuple(mesh.shape[name] for name in EVERY)
    return jax.shard_map(
        functools.partial(per_device, sizes == (2, 4, 4)), mesh=mesh, in_specs=in_specs, out_specs=out_specs, check_vma=False
    )
```

```python
import jax
import jax.numpy as jnp
from jax import lax
from jax.experimental import pallas as pl
from jax.experimental.pallas import tpu as pltpu
from jax.sharding import PartitionSpec as P

BLK = 256
MICRO = 2


epsilon = 1e-05
highest = lax.Precision.HIGHEST


EVERY = ("fsdp", "context", "tensor")


def carried_in(value, backward):
    slot, mine = lax.axis_index("tensor"), lax.axis_index("context")
    near = lax.all_gather(value, "tensor")
    far = lax.all_gather(jnp.sum(near, 0).astype(value.dtype), "context")
    near_ids = jnp.arange(near.shape[0]).reshape((-1,) + (1,) * value.ndim)
    far_ids = jnp.arange(far.shape[0]).reshape((-1,) + (1,) * value.ndim)
    near_mask = near_ids > slot if backward else near_ids < slot
    far_mask = far_ids > mine if backward else far_ids < mine
    near, far = near.astype(jnp.float32), far.astype(jnp.float32)
    return jnp.sum(jnp.where(near_mask, near, 0.0), 0) + jnp.sum(jnp.where(far_mask, far, 0.0), 0)


def layer_norm(values, norm_gain, norm_bias):
    center = values - jnp.mean(values, -1, keepdims=True)
    spread = jnp.mean(center * center, -1, keepdims=True)
    return center * lax.rsqrt(spread + epsilon) * norm_gain + norm_bias


def features(logits):
    return jnp.concatenate([jax.nn.softmax(logits, -1), jax.nn.softmax(-logits, -1)], -1)


def gelu_tanh(values):
    return jax.nn.gelu(values, approximate=True)


def prefix_before(values):
    running = jnp.cumsum(values, 1)
    return jnp.concatenate([jnp.zeros_like(values[:, :1]), running[:, :-1]], 1)


def suffix_after(values):
    running = jnp.flip(jnp.cumsum(jnp.flip(values, 1), 1), 1)
    return jnp.concatenate([running[:, 1:], jnp.zeros_like(values[:, :1])], 1)


def spread(part, axis, parts):
    own = lax.axis_index("context")
    size = part.shape[axis] // parts
    mine = lax.dynamic_slice_in_dim(part, own * size, size, axis)
    return lax.all_gather(mine, EVERY)


def full_in(part):
    pieces = spread(part, 1, lax.axis_size("context"))
    fsdp, ctx, tens = (lax.axis_size(name) for name in EVERY)
    pieces = pieces.reshape((fsdp, ctx, tens) + pieces.shape[1:])
    pieces = pieces.transpose(3, 0, 1, 4, 2, 5)
    return pieces.reshape(pieces.shape[0], -1, pieces.shape[4] * pieces.shape[5])


def share_in(grad):
    fsdp, ctx, tens = (lax.axis_size(name) for name in EVERY)
    kinds, rows, cols = grad.shape
    pieces = grad.astype(jnp.bfloat16).reshape(kinds, fsdp, ctx, rows // fsdp // ctx, tens, cols // tens)
    pieces = pieces.transpose(1, 2, 4, 0, 3, 5).reshape((-1,) + (kinds, rows // fsdp // ctx, cols // tens))
    mine = lax.psum_scatter(pieces, EVERY, scatter_dimension=0)
    return lax.all_gather(mine, "context", axis=1, tiled=True).astype(jnp.float32)


def full_rows(part):
    pieces = spread(part, 0, lax.axis_size("context"))
    fsdp, ctx, tens = (lax.axis_size(name) for name in EVERY)
    pieces = pieces.reshape((fsdp, ctx, tens) + pieces.shape[1:])
    pieces = pieces.transpose(2, 1, 3, 0, 4)
    return pieces.reshape(tens * part.shape[0], -1)


def share_rows(grad):
    fsdp, ctx, tens = (lax.axis_size(name) for name in EVERY)
    rows, cols = grad.shape
    pieces = grad.astype(jnp.bfloat16).reshape(tens, ctx, rows // tens // ctx, fsdp, cols // fsdp)
    pieces = pieces.transpose(3, 1, 0, 2, 4).reshape(-1, rows // tens // ctx, cols // fsdp)
    mine = lax.psum_scatter(pieces, EVERY, scatter_dimension=0)
    return lax.all_gather(mine, "context", axis=0, tiled=True).astype(jnp.float32)


def full_maps(part):
    pieces = lax.all_gather(part, ("fsdp", "tensor"))
    fsdp, tens = lax.axis_size("fsdp"), lax.axis_size("tensor")
    pieces = pieces.reshape((fsdp, tens) + part.shape).transpose(1, 2, 0, 3, 4)
    return pieces.reshape(tens * part.shape[0], fsdp * part.shape[1], part.shape[2])


def own_maps(total):
    fsdp, tens = lax.axis_size("fsdp"), lax.axis_size("tensor")
    heads, rows, _ = total.shape
    mine = lax.dynamic_slice_in_dim(total, lax.axis_index("tensor") * (heads // tens), heads // tens, 0)
    return lax.dynamic_slice_in_dim(mine, lax.axis_index("fsdp") * (rows // fsdp), rows // fsdp, 1)


def per_device(
    inputs,
    cotangent,
    picture_starts,
    qkv_weight,
    out_weight,
    up_weight,
    down_weight,
    query_map,
    key_map,
    first_gain,
    first_bias,
    second_gain,
    second_bias,
):
    tensor_size = lax.axis_size("tensor")
    micro, seq_local, seq_len, model_width = inputs.shape
    span = seq_len // tensor_size
    slot = lax.axis_index("tensor")
    head_size = query_map.shape[2]
    feat_size = 2 * head_size
    blocks_local = span // BLK
    seq_count = micro * seq_local
    block_total = seq_count * blocks_local
    row_count = seq_count * span
    first_block = (lax.axis_index("context") * tensor_size + slot) * blocks_local
    block_ids = first_block + jnp.arange(blocks_local, dtype=jnp.int32)
    position = jnp.arange(BLK, dtype=jnp.int32)
    causal = position[None, :] <= position[:, None]

    in_full = full_in(qkv_weight)
    out_full = full_rows(out_weight)
    up_full = full_in(up_weight[None])[0]
    down_full = full_rows(down_weight)
    qmap_full, kmap_full = full_maps(query_map), full_maps(key_map)
    norms = lax.all_gather(jnp.stack([first_gain, first_bias, second_gain, second_bias]), "fsdp", axis=1, tiled=True)
    gain_first, bias_first, gain_second, bias_second = norms.astype(jnp.float32)

    def own(values):
        mine = lax.dynamic_slice_in_dim(values, slot * span, span, 2)
        return mine.reshape(row_count, model_width)

    source = own(inputs).astype(jnp.float32)
    starts_here = picture_starts.reshape(seq_count, -1)
    block_flags = (
        jnp.sum((starts_here[:, :, None] // BLK == block_ids[None, None, :]).astype(jnp.int32), 1)
        > 0
    )
    allowed = causal[None, None] | block_flags[:, :, None, None]
    allowed = allowed.reshape(block_total, 1, BLK, BLK)
    normed_one = layer_norm(source, gain_first, bias_first)
    normed_low = normed_one.astype(jnp.bfloat16)
    projected = jnp.einsum(
        "rd,cde->cre", normed_low, in_full, preferred_element_type=jnp.float32
    ).astype(jnp.bfloat16)
    heads_local = projected.shape[2] // head_size
    queries = projected[0].reshape(row_count, heads_local, head_size)
    key_rows = projected[1].reshape(row_count, heads_local, head_size)
    value_rows = projected[2].reshape(row_count, heads_local, head_size)
    query_logits = jnp.einsum(
        "rhi,hij->rhj", queries, qmap_full, preferred_element_type=jnp.float32
    )
    key_logits = jnp.einsum(
        "rhi,hij->rhj", key_rows, kmap_full, preferred_element_type=jnp.float32
    )
    query_blocks = (
        features(query_logits)
        .astype(jnp.bfloat16)
        .reshape(block_total, BLK, heads_local, feat_size)
    )
    key_blocks = (
        features(key_logits)
        .astype(jnp.bfloat16)
        .reshape(block_total, BLK, heads_local, feat_size)
    )
    value_blocks = value_rows.reshape(block_total, BLK, heads_local, head_size)
    scores = jnp.einsum(
        "nthf,nshf->nhts", query_blocks, key_blocks, preferred_element_type=jnp.float32
    )
    weights_low = jnp.where(allowed, scores, 0.0).astype(jnp.bfloat16)
    states = jnp.einsum(
        "nshf,nshe->nhfe", key_blocks, value_blocks, preferred_element_type=jnp.float32
    )
    states = states.reshape(seq_count, blocks_local, heads_local, feat_size, head_size)
    key_sums = jnp.sum(key_blocks.astype(jnp.float32), 1).reshape(
        seq_count, blocks_local, heads_local, feat_size
    )
    state_total = jnp.sum(states, 1)
    sums_total = jnp.sum(key_sums, 1)
    carried = carried_in(state_total.astype(jnp.bfloat16), False)
    carried_sums = carried_in(sums_total, False)
    prior_states = (carried[:, None] + prefix_before(states)).astype(jnp.bfloat16)
    prior_states = prior_states.reshape(block_total, heads_local, feat_size, head_size)
    prior_sums = (carried_sums[:, None] + prefix_before(key_sums)).reshape(
        block_total, heads_local, feat_size
    )
    numerator = jnp.einsum(
        "nhts,nshe->nthe", weights_low, value_blocks, preferred_element_type=jnp.float32
    )
    numerator = numerator + jnp.einsum(
        "nthf,nhfe->nthe", query_blocks, prior_states, preferred_element_type=jnp.float32
    )
    denominator = jnp.sum(weights_low.astype(jnp.float32), -1).transpose(0, 2, 1)
    denominator = denominator + jnp.einsum(
        "nthf,nhf->nth", query_blocks.astype(jnp.float32), prior_sums, precision=highest
    )
    mixed_heads = (
        (numerator / denominator[..., None])
        .astype(jnp.bfloat16)
        .reshape(row_count, heads_local * head_size)
    )
    attended = jnp.dot(mixed_heads, out_full, preferred_element_type=jnp.float32)
    middle = source + attended
    normed_two = layer_norm(middle, gain_second, bias_second)
    normed_two_low = normed_two.astype(jnp.bfloat16)
    hidden_pre = jnp.dot(normed_two_low, up_full, preferred_element_type=jnp.float32)
    hidden_low = gelu_tanh(hidden_pre).astype(jnp.bfloat16)
    branch = jnp.dot(hidden_low, down_full, preferred_element_type=jnp.float32)
    output = (middle + branch).astype(jnp.bfloat16).reshape(micro, seq_local, span, model_width)
    output = lax.all_gather(output, "tensor", axis=2, tiled=True)
    upstream_low = own(cotangent)
    upstream = upstream_low.astype(jnp.float32)
    grad_down = jnp.einsum(
        "rk,rd->kd", hidden_low, upstream_low, preferred_element_type=jnp.float32
    )
    hidden_grad = jnp.einsum(
        "rd,kd->rk", upstream_low, down_full, preferred_element_type=jnp.float32
    )
    gelu_result, gelu_pull = jax.vjp(gelu_tanh, hidden_pre)
    pre_grad = gelu_pull(hidden_grad)[0].astype(jnp.bfloat16)
    grad_up = jnp.einsum(
        "rd,rf->df", normed_two_low, pre_grad, preferred_element_type=jnp.float32
    )
    normed_two_grad = jnp.einsum(
        "rf,df->rd", pre_grad, up_full, preferred_element_type=jnp.float32
    )
    norm_result, second_pull = jax.vjp(layer_norm, middle, gain_second, bias_second)
    middle_part, grad_gain_second, grad_bias_second = second_pull(normed_two_grad)
    middle_grad = upstream + middle_part
    middle_low = middle_grad.astype(jnp.bfloat16)
    grad_out = jnp.einsum(
        "rk,rd->kd", mixed_heads, middle_low, preferred_element_type=jnp.float32
    )
    mixed_grad = jnp.einsum(
        "rd,kd->rk", middle_low, out_full, preferred_element_type=jnp.float32
    )
    mixed_grad = mixed_grad.reshape(block_total, BLK, heads_local, head_size)
    numer_grad = (mixed_grad / denominator[..., None]).astype(jnp.bfloat16)
    denom_grad = -jnp.sum(mixed_grad * numerator, -1) / (denominator * denominator)
    weight_grad = jnp.einsum(
        "nthe,nshe->nhts", numer_grad, value_blocks, preferred_element_type=jnp.float32
    )
    weight_grad = weight_grad + denom_grad.transpose(0, 2, 1)[..., None]
    weight_grad_low = jnp.where(allowed, weight_grad, 0.0).astype(jnp.bfloat16)
    value_grad = jnp.einsum(
        "nhts,nthe->nshe", weights_low, numer_grad, preferred_element_type=jnp.float32
    )
    query_grad = jnp.einsum(
        "nhts,nshf->nthf", weight_grad_low, key_blocks, preferred_element_type=jnp.float32
    )
    query_grad = query_grad + jnp.einsum(
        "nthe,nhfe->nthf", numer_grad, prior_states, preferred_element_type=jnp.float32
    )
    query_grad = query_grad + denom_grad[..., None] * prior_sums[:, None]
    key_grad = jnp.einsum(
        "nhts,nthf->nshf", weight_grad_low, query_blocks, preferred_element_type=jnp.float32
    )
    prior_grad = jnp.einsum(
        "nthf,nthe->nhfe", query_blocks, numer_grad, preferred_element_type=jnp.float32
    )
    prior_grad = prior_grad.reshape(seq_count, blocks_local, heads_local, feat_size, head_size)
    prior_sums_grad = jnp.einsum(
        "nthf,nth->nhf", query_blocks.astype(jnp.float32), denom_grad, precision=highest
    )
    prior_sums_grad = prior_sums_grad.reshape(seq_count, blocks_local, heads_local, feat_size)
    grad_total = jnp.sum(prior_grad, 1)
    grad_sums_total = jnp.sum(prior_sums_grad, 1)
    later_states = carried_in(grad_total.astype(jnp.bfloat16), True)
    later_sums = carried_in(grad_sums_total, True)
    state_grad = (later_states[:, None] + suffix_after(prior_grad)).astype(jnp.bfloat16)
    state_grad = state_grad.reshape(block_total, heads_local, feat_size, head_size)
    sums_grad = (later_sums[:, None] + suffix_after(prior_sums_grad)).reshape(
        block_total, heads_local, feat_size
    )
    key_grad = key_grad + jnp.einsum(
        "nshe,nhfe->nshf", value_blocks, state_grad, preferred_element_type=jnp.float32
    )
    key_grad = key_grad + sums_grad[:, None]
    value_grad = value_grad + jnp.einsum(
        "nshf,nhfe->nshe", key_blocks, state_grad, preferred_element_type=jnp.float32
    )
    query_feat_now, query_pull = jax.vjp(features, query_logits)
    query_logit_grad = query_pull(query_grad.reshape(row_count, heads_local, feat_size))[
        0
    ].astype(jnp.bfloat16)
    key_feat_now, key_pull = jax.vjp(features, key_logits)
    key_logit_grad = key_pull(key_grad.reshape(row_count, heads_local, feat_size))[0].astype(
        jnp.bfloat16
    )
    grad_qmap = jnp.einsum(
        "rhi,rhj->hij", queries, query_logit_grad, preferred_element_type=jnp.float32
    )
    grad_kmap = jnp.einsum(
        "rhi,rhj->hij", key_rows, key_logit_grad, preferred_element_type=jnp.float32
    )
    raw_query_grad = jnp.einsum(
        "rhj,hij->rhi", query_logit_grad, qmap_full, preferred_element_type=jnp.float32
    )
    raw_key_grad = jnp.einsum(
        "rhj,hij->rhi", key_logit_grad, kmap_full, preferred_element_type=jnp.float32
    )
    projected_grad = jnp.stack(
        [
            raw_query_grad.reshape(row_count, -1),
            raw_key_grad.reshape(row_count, -1),
            value_grad.reshape(row_count, -1),
        ]
    ).astype(jnp.bfloat16)
    grad_in = jnp.einsum(
        "rd,cre->cde", normed_low, projected_grad, preferred_element_type=jnp.float32
    )
    normed_one_grad = jnp.einsum(
        "cre,cde->rd", projected_grad, in_full, preferred_element_type=jnp.float32
    )
    first_result, first_pull = jax.vjp(layer_norm, source, gain_first, bias_first)
    source_part, grad_gain_first, grad_bias_first = first_pull(normed_one_grad)
    input_grad = (middle_grad + source_part).astype(jnp.bfloat16)
    input_grad = input_grad.reshape(micro, seq_local, span, model_width)
    input_grad = lax.all_gather(input_grad, "tensor", axis=2, tiled=True).astype(jnp.float32)
    norm_grads = jnp.stack([grad_gain_first, grad_bias_first, grad_gain_second, grad_bias_second])
    grad_qmap, grad_kmap, norm_grads = lax.psum((grad_qmap, grad_kmap, norm_grads), EVERY)
    share = first_gain.shape[0]
    norm_grads = lax.dynamic_slice_in_dim(norm_grads, lax.axis_index("fsdp") * share, share, 1)
    return (
        output,
        input_grad,
        share_in(grad_in),
        share_rows(grad_out),
        share_in(grad_up[None])[0],
        share_rows(grad_down),
        own_maps(grad_qmap),
        own_maps(grad_kmap),
        norm_grads[0],
        norm_grads[1],
        norm_grads[2],
        norm_grads[3],
    )


MESH = pl.DeviceIdType.MESH
bf16 = jnp.bfloat16
f32 = jnp.float32


def whereabouts():
    return tuple(lax.axis_index(name) for name in EVERY)


def neighbours(f, c, t):
    n = c * 4 + t
    peers = [(1 - f, c, t)]
    for k in range(1, 16):
        other = lax.rem(n + k, 16)
        peers.append((f, other // 4, lax.rem(other, 4)))
    for k in range(1, 4):
        peers.append((1 - f, c, lax.rem(t + k, 4)))
    return peers


def meet(f, c, t):
    barrier = pltpu.get_barrier_semaphore()
    peers = neighbours(f, c, t)
    for peer in peers:
        pl.semaphore_signal(barrier, inc=1, device_id=peer, device_id_type=MESH)
    pl.semaphore_wait(barrier, len(peers))


def send(src, dst, send_sem, recv_sem, peer):
    copy = pltpu.make_async_remote_copy(
        src_ref=src, dst_ref=dst, send_sem=send_sem, recv_sem=recv_sem,
        device_id=peer, device_id_type=MESH,
    )
    copy.start()
    return copy


def arrived(ref, sem):
    pltpu.make_async_copy(ref, ref, sem).wait()


def at(start, size, unit):
    return pl.ds(pl.multiple_of(start, unit), size)


def half(ref, m, f):
    if m == 0:
        w = ref.shape[2] // 2
        return ref.at[:, :, at(f * w, w, 128)]
    if m == 1:
        w = ref.shape[1] // 2
        return ref.at[:, at(f * w, w, 128)]
    w = ref.shape[0] // 2
    return ref.at[at(f * w, w, 16), :]


def shard(ref, m, f, t):
    if m == 0:
        w, h = ref.shape[2] // 2, ref.shape[1] // 4
        return ref.at[:, at(t * h, h, 16), at(f * w, w, 128)]
    if m == 1:
        w, h = ref.shape[1] // 2, ref.shape[0] // 4
        return ref.at[at(t * h, h, 16), at(f * w, w, 128)]
    h, w = ref.shape[0] // 2, ref.shape[1] // 4
    return ref.at[at(f * h, h, 16), at(t * w, w, 128)]


def piece(ref, m, f, c, t):
    if m == 0:
        w, h = ref.shape[2] // 2, ref.shape[1] // 16
        return ref.at[:, at(t * 4 * h + c * h, h, 16), at(f * w, w, 128)]
    if m == 1:
        w, h = ref.shape[1] // 2, ref.shape[0] // 16
        return ref.at[at(t * 4 * h + c * h, h, 16), at(f * w, w, 128)]
    h, w = ref.shape[0] // 8, ref.shape[1] // 4
    return ref.at[at(f * 4 * h + c * h, h, 16), at(t * w, w, 128)]


def quarter(ref, m, c):
    if m == 0:
        h = ref.shape[1] // 4
        return ref.at[:, at(c * h, h, 16), :]
    h = ref.shape[0] // 4
    return ref.at[at(c * h, h, 16), :]


def context_part(ref, m, c):
    if m == 0:
        h = ref.shape[2] // 4
        return ref.at[:, :, at(c * h, h, 16), :]
    if m == 1:
        h = ref.shape[1] // 4
        return ref.at[:, at(c * h, h, 16), :]
    h = ref.shape[0] // 4
    return ref.at[at(c * h, h, 16), :]


def tensor_part(ref, m, t):
    if m == 0:
        return ref.at[:, t]
    if m == 1:
        return ref.at[t]
    w = ref.shape[1] // 4
    return ref.at[:, at(t * w, w, 128)]


NN = (((1,), (0,)), ((), ()))
NT = (((1,), (1,)), ((), ()))
TN = (((0,), (0,)), ((), ()))


def mm(a, b, dims=NN):
    return lax.dot_general(a, b, dims, preferred_element_type=f32)


def lanes_of(shape):
    return lax.broadcasted_iota(jnp.int32, shape, len(shape) - 1)


def block_ones(size, group):
    row = lax.broadcasted_iota(jnp.int32, (size, size), 0) // group
    col = lax.broadcasted_iota(jnp.int32, (size, size), 1) // group
    return jnp.where(row == col, 1.0, 0.0).astype(bf16)


def statistics(rows):
    center = rows - jnp.mean(rows, -1, keepdims=True)
    rstd = lax.rsqrt(jnp.mean(center * center, -1, keepdims=True) + epsilon)
    return center * rstd, rstd


def norm_back(grad, e, rstd, gain):
    w = grad * gain
    return rstd * (w - jnp.mean(w, -1, keepdims=True) - e * jnp.mean(w * e, -1, keepdims=True))


def near_far(first, low, high):
    return jnp.where(first, low, high)


def own_half(values, first, odd):
    zero = jnp.zeros_like(values)
    return jnp.where(first, zero, values) if odd else jnp.where(first, values, zero)


def pair_block(values, first):
    return jnp.concatenate([own_half(values, first, 0), own_half(values, first, 1)], 0)


def split_half(full, first, odd):
    other = pltpu.roll(full, 64, 1)
    return jnp.where(first, other, full) if odd else jnp.where(first, full, other)


def layer_kernel(*refs):
    inputs, cotangent, flags, maps, norms = refs[:5]
    shards = refs[5:9]
    all_out, all_in = refs[9:11]
    outs, small_out = refs[11:15], refs[15]
    w, mx, nrm, x, g, n1, qkv, feat = refs[16:20], *refs[20:27]
    prior, sums_in, states, z_buf, s_in, z_in, s_out, z_out = refs[27:35]
    o, rden, num, mid, n2, a, gp, rows_out = refs[35:43]
    gm, dnum, dden, dproj, rows_in, turned = refs[43:49]
    pair_in, xy_in, part, tz_in, last = (refs[49 + 4 * i : 53 + 4 * i] for i in range(5))
    small, small_pair, small_own, small_in, small_sum = refs[69:74]
    local_sem, send_sem, extra_sem, z_sem, xy_sem, pair_sem = refs[74:80]
    scan_sem, rows_sem, gpair_sem, gxy_sem, gz_sem, last_sem, small_sem = refs[80:87]
    wq, wo, wu, wd = w
    d = x.shape[1]
    ff = a.shape[1]
    half_rows = x.shape[0] // 2
    f, c, t = whereabouts()
    n = c * 4 + t
    peers = neighbours(f, c, t)
    partner = peers[0]
    started = []

    def put(src, dst, recv_sem, peer):
        started.append(send(src, dst, send_sem, recv_sem, peer))

    fetched = []

    def fetch(src, dst, sem):
        copy = pltpu.make_async_copy(src, dst, sem)
        copy.start()
        return copy

    for i in range(2):
        rows = pl.ds(i * half_rows, half_rows)
        fetched.append(fetch(inputs.at[i, 0, at(t * half_rows, half_rows, 16), :], x.at[rows], local_sem.at[i]))
        fetched.append(fetch(cotangent.at[i, 0, at(t * half_rows, half_rows, 16), :], g.at[rows], local_sem.at[2 + i]))
    h3 = maps.shape[1]
    lo_norm = d // 2

    def map_place(ff_, tt):
        return mx.at[:, pl.ds(tt * h3, h3), at(ff_ * 32, 32, 16), :]

    def norm_place(ff_):
        return nrm.at[:, at(ff_ * lo_norm, lo_norm, 128)]

    fetched.append(fetch(maps, map_place(f, t), local_sem.at[4]))
    fetched.append(fetch(norms, norm_place(f), local_sem.at[5]))
    shard_copies = [fetch(shards[m], shard(w[m], m, f, t), local_sem.at[6 + m]) for m in range(4)]
    z_buf[...] = jnp.zeros_like(z_buf)
    small[...] = jnp.zeros_like(small)
    meet(f, c, t)

    order = (0, 1, 2, 3)
    for k in range(1, 8):
        peer = (f if k < 4 else 1 - f, c, lax.rem(t + k, 4))
        put(maps, map_place(f, t), extra_sem.at[k], peer)
    put(norms, norm_place(f), extra_sem.at[0], partner)
    for m in order:
        for k in range(1, 4):
            put(quarter(shards[m], m, c), piece(w[m], m, f, c, t), z_sem.at[m, k], (f, c, lax.rem(t + k, 4)))
    for m in order:
        put(shards[m], shard(w[m], m, f, t), pair_sem.at[m], partner)

    def forward(m, k):
        got = piece(w[m], m, f, c, lax.rem(t + 4 - k, 4))
        arrived(got, z_sem.at[m, k])
        for j in range(1, 4):
            put(got, got, xy_sem.at[m, k, j], (f, c ^ j, t))
        put(got, got, pair_sem.at[m], partner)

    def across(m):
        for k in range(1, 4):
            for j in range(1, 4):
                got = piece(w[m], m, f, c ^ j, lax.rem(t + 4 - k, 4))
                arrived(got, xy_sem.at[m, k, j])
                put(got, got, pair_sem.at[m], partner)

    def complete(m):
        shard_copies[m].wait()
        arrived(half(w[m], m, 1 - f), pair_sem.at[m])

    for k in range(1, 4):
        forward(0, k)
    for copy in fetched:
        copy.wait()
    arrived(norm_place(1 - f), extra_sem.at[0])
    first = lanes_of((1, 128)) < 64
    ones64 = block_ones(128, 64)
    step = half_rows // 2

    @pl.loop(0, 4)
    def _(i):
        rows = at(i * step, step, 16)
        e, _unused = statistics(x[rows, :].astype(f32))
        n1[rows, :] = (e * nrm[0:1, :] + nrm[1:2, :]).astype(bf16)

    for k in range(1, 4):
        forward(1, k)
    across(0)
    forward(2, 1)
    for k in range(1, 8):
        arrived(map_place(f if k < 4 else 1 - f, lax.rem(t + 8 - k, 4)), extra_sem.at[k])
    complete(0)

    chunks = d // 256

    @pl.loop(0, 3 * chunks)
    def _(i):
        kind, j = i // chunks, lax.rem(i, chunks)
        cols = at(j * 256, 256, 128)
        qkv[kind, :, cols] = mm(n1[...], wq[kind, cols, :], NT).astype(bf16)

    pairs = d // 128

    def pair_map(side, p):
        zero = jnp.zeros((64, 128), bf16)
        top = jnp.concatenate([mx[side, 2 * p], zero], 1)
        bottom = jnp.concatenate([zero, mx[side, 2 * p + 1]], 1)
        return jnp.concatenate([top, bottom], 0)

    @pl.loop(0, 4 * pairs)
    def _(i):
        side, rest = i // (2 * pairs), lax.rem(i, 2 * pairs)
        b, p = rest // pairs, lax.rem(rest, pairs)
        rows = at(b * half_rows, half_rows, 16)
        logits = mm(qkv[side, rows, at(p * 128, 128, 128)], pair_map(side, p))
        for odd in range(2):
            part_ = logits[:, odd * 128 : odd * 128 + 128]
            low_top = jnp.max(jnp.where(first, part_, -jnp.inf), -1, keepdims=True)
            high_top = jnp.max(jnp.where(first, -jnp.inf, part_), -1, keepdims=True)
            e = jnp.exp(part_ - jnp.where(first, low_top, high_top))
            total = mm(e.astype(bf16), ones64)
            feat[side, rows, at(p * 256 + odd * 128, 128, 128)] = (e / total).astype(bf16)

    @pl.loop(0, 2 * pairs)
    def _(i):
        b, p = i // pairs, lax.rem(i, pairs)
        rows = at(b * half_rows, half_rows, 16)
        keys = feat[1, rows, at(p * 256, 256, 128)]
        both = mm(keys, qkv[2, rows, at(p * 128, 128, 128)], TN)
        states[b, at(p * 128, 128, 16), :] = near_far(first, both[:128], both[128:]).astype(bf16)
        tall = mm(jnp.ones((8, half_rows), bf16), keys)
        slot = lax.broadcasted_iota(jnp.int32, (8, 128), 0) == b
        z_buf[2 * p] = jnp.where(slot, tall[:, :128], z_buf[2 * p])
        z_buf[2 * p + 1] = jnp.where(slot, tall[:, 128:], z_buf[2 * p + 1])

    srows = states.shape[1] // 16

    def scan_out(sem0):
        for k in range(1, 16):
            other = lax.rem(n + k, 16)
            put(states.at[:, at(other * srows, srows, 16), :], s_in.at[n], scan_sem.at[sem0], peers[k])
            put(z_buf.at[other], z_in.at[n], scan_sem.at[sem0 + 1], peers[k])
        one = fetch(states.at[:, at(n * srows, srows, 16), :], s_in.at[n], local_sem.at[0])
        two = fetch(z_buf.at[n], z_in.at[n], local_sem.at[1])
        one.wait()
        two.wait()

    def scan_back(sem0, backward):
        arrived(s_in.at[pl.ds(0, 15)], scan_sem.at[sem0])
        arrived(z_in.at[pl.ds(0, 15)], scan_sem.at[sem0 + 1])
        total = jnp.zeros(s_in.shape[1:], f32)
        sums = jnp.zeros(z_in.shape[1:], f32)
        for i in range(15, -1, -1) if backward else range(16):
            s_out[i] = total.astype(bf16)
            z_out[i] = sums
            total = total + s_in[i].astype(f32)
            sums = sums + z_in[i]
        for k in range(1, 16):
            other = lax.rem(n + k, 16)
            put(s_out.at[other], prior.at[int(backward), :, at(n * srows, srows, 16), :], scan_sem.at[sem0 + 2], peers[k])
            put(z_out.at[other], sums_in.at[int(backward), n], scan_sem.at[sem0 + 3], peers[k])
        one = fetch(s_out.at[n], prior.at[int(backward), :, at(n * srows, srows, 16), :], local_sem.at[0])
        two = fetch(z_out.at[n], sums_in.at[int(backward), n], local_sem.at[1])
        one.wait()
        two.wait()

    def scan_end(sem0):
        arrived(s_in.at[pl.ds(0, 15)], scan_sem.at[sem0 + 2])
        arrived(z_in.at[pl.ds(0, 15)], scan_sem.at[sem0 + 3])

    scan_out(0)
    across(1)
    forward(2, 2)
    forward(2, 3)

    def mask_of(b, turn):
        row = lax.broadcasted_iota(jnp.int32, (half_rows, half_rows), 0)
        col = lax.broadcasted_iota(jnp.int32, (half_rows, half_rows), 1)
        causal = row <= col if turn else col <= row
        return jnp.where(causal, 1.0, flags[b, 0:1, :])

    @pl.loop(0, 2 * pairs)
    def _(i):
        b, p = i // pairs, lax.rem(i, pairs)
        rows = at(b * half_rows, half_rows, 16)
        values = qkv[2, rows, at(p * 128, 128, 128)]
        mask = mask_of(b, False)
        both = None
        for odd in range(2):
            cols = at(p * 256 + odd * 128, 128, 128)
            scores = (mm(feat[0, rows, cols], feat[1, rows, cols], NT) * mask).astype(bf16)
            right = jnp.concatenate(
                [own_half(values, first, odd), own_half(jnp.ones_like(values), first, odd)], 1
            )
            term = mm(scores, right)
            both = term if both is None else both + term
        num[rows, at(p * 128, 128, 128)] = both[:, :128]
        rden[rows, at(p * 128, 128, 128)] = both[:, 128:]

    scan_back(0, False)
    for k in range(1, 4):
        forward(3, k)
    complete(1)
    scan_end(0)

    def sums_pair(direction, b, p, odd):
        tile = sums_in[direction, 2 * p + odd]
        slot = lax.broadcasted_iota(jnp.int32, (8, 128), 0) == b
        return jnp.sum(jnp.where(slot, tile, 0.0), 0, keepdims=True)

    @pl.loop(0, 2 * pairs)
    def _(i):
        b, p = i // pairs, lax.rem(i, pairs)
        rows = at(b * half_rows, half_rows, 16)
        cols = at(p * 128, 128, 128)
        queries = feat[0, rows, at(p * 256, 256, 128)]
        before = pair_block(prior[0, b, at(p * 128, 128, 16), :], first)
        zero = jnp.zeros((64, 128), bf16)
        z_low = jnp.broadcast_to(sums_pair(0, b, p, 0), (64, 128)).astype(bf16)
        z_high = jnp.broadcast_to(sums_pair(0, b, p, 1), (64, 128)).astype(bf16)
        z_rows = jnp.concatenate(
            [jnp.concatenate([z_low, zero], 1), jnp.concatenate([zero, z_high], 1)], 0
        )
        inverse = 1.0 / (rden[rows, cols] + mm(queries, z_rows, NT))
        o[rows, cols] = ((num[rows, cols] + mm(queries, before)) * inverse).astype(bf16)
        rden[rows, cols] = inverse

    @pl.loop(0, 2)
    def _(i):
        rows = at(i * half_rows, half_rows, 16)
        mid[rows, :] = x[rows, :].astype(f32) + mm(o[rows, :], wo[...])

    across(2)

    @pl.loop(0, 4)
    def _(i):
        rows = at(i * step, step, 16)
        e, _unused = statistics(mid[rows, :])
        n2[rows, :] = (e * nrm[2:3, :] + nrm[3:4, :]).astype(bf16)

    complete(2)

    @pl.loop(0, ff // 256)
    def _(i):
        cols = at(i * 256, 256, 128)
        u = mm(n2[...], wu[:, cols])
        scale = 0.7978845608028654
        square = u * u
        tanh = jnp.tanh(scale * u * (1.0 + 0.044715 * square))
        cdf = 0.5 + 0.5 * tanh
        a[:, cols] = (u * cdf).astype(bf16)
        slope = cdf + (0.5 * scale) * u * (1.0 - tanh * tanh) * (1.0 + 0.134145 * square)
        gp[:, cols] = slope.astype(bf16)

    across(3)
    complete(3)

    @pl.loop(0, chunks)
    def _(i):
        cols = at(i * 256, 256, 128)
        rows_out[:, cols] = (mid[:, cols] + mm(a[...], wd[cols, :], NT)).astype(bf16)

    links = []

    def pass_on(i, way, hop, block):
        dst = (all_out, all_in)[i]
        src = (rows_out, rows_in)[i]
        peer = (f, c, t + 1 if way == 0 else t - 1)
        copies = []
        for b in range(2):
            origin = src.at[pl.ds(b * half_rows, half_rows)] if hop == 0 else dst.at[b, block]
            copies.append(pltpu.make_async_remote_copy(
                src_ref=origin, dst_ref=dst.at[b, block], send_sem=rows_sem.at[i, way, hop, 0],
                recv_sem=rows_sem.at[i, way, hop, 1], device_id=peer, device_id_type=MESH,
            ))
        return copies

    def rows_hop(i, hop):
        dst = (all_out, all_in)[i]
        for way in range(2):
            block = t - hop if way == 0 else t + hop
            here = block >= 0 if way == 0 else block <= 3
            more = t < 3 if way == 0 else t > 0
            if hop > 0:
                @pl.when(here)
                def _():
                    arrived(dst.at[:, 0], rows_sem.at[i, way, hop - 1, 1])
            if hop < 3:
                @pl.when(jnp.logical_and(here, more))
                def _():
                    for copy in pass_on(i, way, hop, block):
                        copy.start()

    def rows_sent(i):
        for hop in range(3):
            for way in range(2):
                block = t - hop if way == 0 else t + hop
                here = block >= 0 if way == 0 else block <= 3
                more = t < 3 if way == 0 else t > 0

                @pl.when(jnp.logical_and(here, more))
                def _():
                    for copy in pass_on(i, way, hop, block):
                        copy.wait_send()

    own_rows = []
    for b in range(2):
        own_rows.append(fetch(rows_out.at[pl.ds(b * half_rows, half_rows)], all_out.at[b, t], local_sem.at[2 + b]))
    rows_hop(0, 0)

    def grad_pair(m):
        if m < 2:
            h = d // 4
            for tt in range(4):
                if m == 0:
                    src = w[m].at[:, pl.ds(tt * h, h), at((1 - f) * (d // 2), d // 2, 128)]
                    put(src, pair_in[m].at[:, tt], gpair_sem.at[m], partner)
                else:
                    src = w[m].at[pl.ds(tt * h, h), at((1 - f) * (d // 2), d // 2, 128)]
                    put(src, pair_in[m].at[tt], gpair_sem.at[m], partner)
        else:
            put(half(w[m], m, 1 - f), pair_in[m], gpair_sem.at[m], partner)

    def grad_xy(m):
        arrived(pair_in[m], gpair_sem.at[m])
        h = d // 4
        cols = at(f * (d // 2), d // 2, 128)
        if m == 0:
            @pl.loop(0, 12)
            def _(i):
                kind, tt = i // 4, lax.rem(i, 4)
                mine = wq[kind, at(tt * h, h, 16), cols].astype(f32)
                pair_in[0][kind, tt] = (mine + pair_in[0][kind, tt].astype(f32)).astype(bf16)
        elif m == 1:
            @pl.loop(0, 4)
            def _(tt):
                mine = wo[at(tt * h, h, 16), cols].astype(f32)
                pair_in[1][tt] = (mine + pair_in[1][tt].astype(f32)).astype(bf16)
        else:
            @pl.loop(0, 12)
            def _(i):
                rows = at(i * 32, 32, 16)
                mine = w[m][at(f * (d // 2) + i * 32, 32, 16), :].astype(f32)
                pair_in[m][rows, :] = (mine + pair_in[m][rows, :].astype(f32)).astype(bf16)
        for j in range(1, 4):
            put(context_part(pair_in[m], m, c ^ j), xy_in[m].at[j - 1], gxy_sem.at[m, j], (f, c ^ j, t))

    def grad_z(m):
        for j in range(1, 4):
            arrived(xy_in[m].at[j - 1], gxy_sem.at[m, j])
        if m == 0:
            h = d // 16

            @pl.loop(0, 12)
            def _(i):
                kind, tt = i // 4, lax.rem(i, 4)
                total = pair_in[0][kind, tt, at(c * h, h, 16), :].astype(f32)
                for j in range(3):
                    total = total + xy_in[0][j, kind, tt].astype(f32)
                part[0][kind, tt] = total.astype(bf16)
        elif m == 1:
            h = d // 16

            @pl.loop(0, 4)
            def _(tt):
                total = pair_in[1][tt, at(c * h, h, 16), :].astype(f32)
                for j in range(3):
                    total = total + xy_in[1][j, tt].astype(f32)
                part[1][tt] = total.astype(bf16)
        else:
            @pl.loop(0, d // 8 // 16)
            def _(i):
                rows = at(i * 16, 16, 16)
                total = pair_in[m][at(c * (d // 8) + i * 16, 16, 16), :].astype(f32)
                for j in range(3):
                    total = total + xy_in[m][j, rows, :].astype(f32)
                part[m][rows, :] = total.astype(bf16)
        for k in range(1, 4):
            other = lax.rem(t + k, 4)
            put(tensor_part(part[m], m, other), tz_in[m].at[k - 1], gz_sem.at[m, k], (f, c, other))

    def grad_last(m):
        for k in range(1, 4):
            arrived(tz_in[m].at[k - 1], gz_sem.at[m, k])
        if m == 0:
            for kind in range(3):
                total = part[0][kind, t].astype(f32)
                for k in range(3):
                    total = total + tz_in[0][k, kind].astype(f32)
                last[0][kind] = total.astype(bf16)
        elif m == 1:
            total = part[1][t].astype(f32)
            for k in range(3):
                total = total + tz_in[1][k].astype(f32)
            last[1][...] = total.astype(bf16)
        else:
            cols = at(t * (ff // 4), ff // 4, 128)

            @pl.loop(0, d // 8 // 16)
            def _(i):
                rows = at(i * 16, 16, 16)
                total = part[m][rows, cols].astype(f32)
                for k in range(3):
                    total = total + tz_in[m][k, rows, :].astype(f32)
                last[m][rows, :] = total.astype(bf16)
        for j in range(1, 4):
            put(last[m], quarter(outs[m], m, c), last_sem.at[m, j], (f, c ^ j, t))
        fetch(last[m], quarter(outs[m], m, c), local_sem.at[10 + m]).wait()

    for copy in started:
        copy.wait_send()
    started.clear()

    @pl.loop(0, ff // 256)
    def _(i):
        cols = at(i * 256, 256, 128)
        gp[:, cols] = (mm(g[...], wd[:, cols]) * gp[:, cols].astype(f32)).astype(bf16)

    def turn(src):
        @pl.loop(0, chunks)
        def _(i):
            cols = at(i * 256, 256, 128)
            turned[at(i * 256, 256, 16), :] = src[:, cols].astype(f32).T.astype(bf16)

    turn(g)

    @pl.loop(0, ff // 256)
    def _(i):
        cols = at(i * 256, 256, 128)
        wd[:, cols] = mm(turned[...], a[:, cols]).astype(bf16)

    grad_pair(3)

    @pl.loop(0, chunks)
    def _(i):
        cols = at(i * 256, 256, 128)
        num[:, cols] = mm(gp[...], wu[cols, :], NT)

    @pl.loop(0, 4)
    def _(i):
        rows = at(i * step, step, 16)
        e, rstd = statistics(mid[rows, :])
        grad = num[rows, :]
        nrm[6:7, :] += jnp.sum(grad * e, 0, keepdims=True)
        nrm[7:8, :] += jnp.sum(grad, 0, keepdims=True)
        total = g[rows, :].astype(f32) + norm_back(grad, e, rstd, nrm[2:3, :])
        mid[rows, :] = total
        gm[rows, :] = total.astype(bf16)

    grad_xy(3)

    @pl.loop(0, chunks)
    def _(i):
        cols = at(i * 256, 256, 128)
        back = mm(gm[...], wo[cols, :], NT)
        for side in range(2):
            cut = at(i * 256 + side * 128, 128, 128)
            grad = back[:, side * 128 : side * 128 + 128]
            inverse = rden[:, cut]
            dnum[:, cut] = (grad * inverse).astype(bf16)
            dden[:, cut] = -mm((grad * o[:, cut].astype(f32)).astype(bf16), ones64) * inverse

    @pl.loop(0, 2 * pairs)
    def _(i):
        b, p = i // pairs, lax.rem(i, pairs)
        rows = at(b * half_rows, half_rows, 16)
        cols = at(p * 128, 128, 128)
        queries = feat[0, rows, at(p * 256, 256, 128)]
        both = mm(queries, dnum[rows, cols], TN)
        states[b, at(p * 128, 128, 16), :] = near_far(first, both[:128], both[128:]).astype(bf16)
        slot = lax.broadcasted_iota(jnp.int32, (8, 128), 0) == b
        packed = dden[rows, cols]
        for odd in range(2):
            full = split_half(packed, first, odd)
            tall = jnp.sum(queries[:, odd * 128 : odd * 128 + 128].astype(f32) * full, 0, keepdims=True)
            z_buf[2 * p + odd] = jnp.where(slot, tall, z_buf[2 * p + odd])

    scan_out(4)
    rows_hop(0, 1)

    turn(n2)

    @pl.loop(0, ff // 256)
    def _(i):
        cols = at(i * 256, 256, 128)
        wu[:, cols] = mm(turned[...], gp[:, cols]).astype(bf16)

    grad_pair(2)

    scan_back(4, True)

    @pl.loop(0, chunks)
    def _(i):
        cols = at(i * 256, 256, 128)
        wo[cols, :] = mm(o[:, cols].astype(f32).T.astype(bf16), gm[...]).astype(bf16)

    grad_pair(1)

    lane = lanes_of((1, 128))

    def extended(values, one, two, odd):
        base = 0 if odd else 64
        rest = jnp.where(lane == base, one, jnp.where(lane == base + 1, two, jnp.zeros_like(values)))
        return jnp.where(first, rest, values) if odd else jnp.where(first, values, rest)

    def block_maps(side, p):
        low_ = jnp.where(first, mx[side, 2 * p], jnp.zeros((64, 128), bf16))
        high_ = jnp.where(first, jnp.zeros((64, 128), bf16), -mx[side, 2 * p + 1])
        return jnp.concatenate([low_, high_], 0)

    def through_features(side, b, p, rows, cols, grads):
        logits = []
        for odd in range(2):
            prob = feat[side, rows, at(p * 256 + odd * 128, 128, 128)].astype(f32)
            grad = grads[odd]
            inner = mm((prob * grad).astype(bf16), ones64)
            both = prob * (grad - inner)
            other = pltpu.roll(both, 64, 1)
            logits.append(other - both if odd else both - other)
        packed = jnp.where(first, logits[0], logits[1]).astype(bf16)
        dproj[side, rows, cols] = mm(packed, block_maps(side, p), NT).astype(bf16)
        square = mm(qkv[side, rows, cols], packed, TN)
        small[side * pairs + p] += near_far(first, square[:64], square[64:])

    def exact(packed, odd):
        full = split_half(packed, first, odd)
        head = full.astype(bf16)
        return full, head, (full - head.astype(f32)).astype(bf16)

    @pl.loop(0, 2 * pairs)
    def _(i):
        b, p = i // pairs, lax.rem(i, pairs)
        rows = at(b * half_rows, half_rows, 16)
        cols = at(p * 128, 128, 128)
        values, grad_rows = qkv[2, rows, cols], dnum[rows, cols]
        packed = dden[rows, cols]
        before = prior[0, b, at(p * 128, 128, 16), :]
        mask = mask_of(b, False)
        unit = jnp.ones_like(values)
        grads = []
        for odd in range(2):
            full, head, tail = exact(packed, odd)
            left = extended(grad_rows, head, tail, odd)
            right = extended(values, unit, unit, odd)
            scores = (mm(left, right, NT) * mask).astype(bf16)
            total = mm(scores, feat[1, rows, at(p * 256 + odd * 128, 128, 128)])
            total = total + mm(own_half(grad_rows, first, odd), before, NT)
            grads.append(total + full * sums_pair(0, b, p, odd))
        through_features(0, b, p, rows, cols, grads)

    scan_end(4)
    rows_hop(0, 2)
    grad_xy(2)

    @pl.loop(0, 2 * pairs)
    def _(i):
        b, p = i // pairs, lax.rem(i, pairs)
        rows = at(b * half_rows, half_rows, 16)
        cols = at(p * 128, 128, 128)
        values, grad_rows = qkv[2, rows, cols], dnum[rows, cols]
        packed = dden[rows, cols]
        after = prior[1, b, at(p * 128, 128, 16), :]
        mask = mask_of(b, True)
        unit = jnp.ones_like(values)
        value_grad = mm(feat[1, rows, at(p * 256, 256, 128)], pair_block(after, first))
        grads = []
        for odd in range(2):
            fcols = at(p * 256 + odd * 128, 128, 128)
            queries, keys = feat[0, rows, fcols], feat[1, rows, fcols]
            _full, head, tail = exact(packed, odd)
            left = extended(values, unit, unit, odd)
            right = extended(grad_rows, head, tail, odd)
            scores = (mm(left, right, NT) * mask).astype(bf16)
            total = mm(scores, queries) + mm(own_half(values, first, odd), after, NT)
            grads.append(total + sums_pair(1, b, p, odd))
            weights = (mm(keys, queries, NT) * mask).astype(bf16)
            value_grad = value_grad + mm(weights, own_half(grad_rows, first, odd))
        dproj[2, rows, cols] = value_grad.astype(bf16)
        through_features(1, b, p, rows, cols, grads)

    grad_xy(1)

    @pl.loop(0, chunks)
    def _(i):
        cols = at(i * 256, 256, 128)
        total = mm(dproj[0], wq[0, :, cols])
        for kind in range(1, 3):
            total = total + mm(dproj[kind], wq[kind, :, cols])
        num[:, cols] = total

    @pl.loop(0, 4)
    def _(i):
        rows = at(i * step, step, 16)
        e, rstd = statistics(x[rows, :].astype(f32))
        grad = num[rows, :]
        nrm[4:5, :] += jnp.sum(grad * e, 0, keepdims=True)
        nrm[5:6, :] += jnp.sum(grad, 0, keepdims=True)
        rows_in[rows, :] = (mid[rows, :] + norm_back(grad, e, rstd, nrm[0:1, :])).astype(bf16)

    for b in range(2):
        own_rows.append(fetch(rows_in.at[pl.ds(b * half_rows, half_rows)], all_in.at[b, t], local_sem.at[4 + b]))
    rows_hop(1, 0)

    for i in range(4):
        for j in range(d // 128):
            small[2 * pairs, i * (d // 128) + j : i * (d // 128) + j + 1, :] = nrm[4 + i : 5 + i, j * 128 : j * 128 + 128]
    put(small, small_pair, small_sem.at[0], partner)

    @pl.loop(0, 3 * chunks)
    def _(i):
        kind, j = i // chunks, lax.rem(i, chunks)
        cols = at(j * 256, 256, 128)
        wq[kind, cols, :] = mm(dproj[kind, :, cols].astype(f32).T.astype(bf16), n1[...]).astype(bf16)

    grad_pair(0)
    arrived(small_pair, small_sem.at[0])
    small_own[...] = (small[...] + small_pair[...]).astype(bf16)
    for k in range(1, 16):
        put(small_own.at[lax.rem(n + k, 16)], small_in.at[n], small_sem.at[1], peers[k])
    fetch(small_own.at[n], small_in.at[n], local_sem.at[6]).wait()
    grad_z(3)
    rows_hop(1, 1)
    grad_xy(0)
    grad_z(2)
    grad_z(1)
    grad_last(3)
    rows_hop(0, 3)
    rows_hop(1, 2)
    arrived(small_in.at[pl.ds(0, 15)], small_sem.at[1])
    total = jnp.zeros(small_in.shape[1:], f32)
    for i in range(16):
        total = total + small_in[i].astype(f32)
    small_sum[...] = total
    for k in range(1, 16):
        put(small_sum, small_out.at[n], small_sem.at[2], peers[k])
    fetch(small_sum, small_out.at[n], local_sem.at[6]).wait()
    grad_last(2)
    grad_last(1)
    grad_z(0)
    grad_last(0)
    for m in range(4):
        for j in range(1, 4):
            arrived(last[m], last_sem.at[m, j])
    arrived(small_out.at[pl.ds(0, 15)], small_sem.at[2])
    rows_hop(1, 3)
    for copy in own_rows:
        copy.wait()
    for copy in started:
        copy.wait_send()
    rows_sent(0)
    rows_sent(1)

def mesh_device(
    inputs,
    cotangent,
    picture_starts,
    qkv_weight,
    out_weight,
    up_weight,
    down_weight,
    query_map,
    key_map,
    first_gain,
    first_bias,
    second_gain,
    second_bias,
):
    micro, seq_local, seq_len, d = inputs.shape
    span = seq_len // 4
    rows = micro * seq_local * span
    ff = up_weight.shape[1] * 4
    heads = query_map.shape[0] * 4
    head = query_map.shape[2]
    own_block = lax.axis_index("context") * 4 + lax.axis_index("tensor")
    flags = jnp.any(picture_starts.reshape(micro, -1) // BLK == own_block, 1).astype(f32)
    flags = jnp.broadcast_to(flags[:, None, None], (micro, 8, span))
    maps = jnp.stack([query_map, key_map])
    maps = jnp.concatenate([maps, -maps], -1)
    norms = jnp.stack([first_gain, first_bias, second_gain, second_bias]).astype(f32)
    norms = jnp.concatenate([norms, jnp.zeros_like(norms)])
    dma = pltpu.SemaphoreType.DMA
    own = [(3, 4, d // 4, d // 2), (4, d // 4, d // 2), (d // 2, ff), (d // 2, ff)]
    sums = [(3, 4, d // 16, d // 2), (4, d // 16, d // 2), (d // 8, ff), (d // 8, ff)]
    last = [(3, d // 16, d // 2), (d // 16, d // 2), (d // 8, ff // 4), (d // 8, ff // 4)]
    outs = [(3, d // 4, d // 2), (d // 4, d // 2), (d // 2, ff // 4), (d // 2, ff // 4)]
    low = [(3, d, d), (d, d), (d, ff), (d, ff), (2, heads, head, 128)]
    state_rows = heads // 2 * 128
    pieces = (16, micro, state_rows // 16, 128)
    small = (16, 64, 128)
    scratch = [pltpu.VMEM(s, bf16) for s in low]
    scratch += [pltpu.VMEM((8, d), f32)]
    scratch += [pltpu.VMEM((rows, d), bf16)] * 3
    scratch += [pltpu.VMEM((3, rows, d), bf16), pltpu.VMEM((2, rows, heads * 128), bf16)]
    scratch += [pltpu.VMEM((2, micro, state_rows, 128), bf16), pltpu.VMEM((2, 16, 8, 128), f32)]
    scratch += [pltpu.VMEM((micro, state_rows, 128), bf16), pltpu.VMEM((16, 8, 128), f32)]
    scratch += [pltpu.VMEM(pieces, bf16), pltpu.VMEM((16, 8, 128), f32)] * 2
    scratch += [pltpu.VMEM((rows, d), bf16)] + [pltpu.VMEM((rows, d), f32)] * 3
    scratch += [pltpu.VMEM((rows, d), bf16)] + [pltpu.VMEM((rows, ff), bf16)] * 2
    scratch += [pltpu.VMEM((rows, d), bf16)] * 3 + [pltpu.VMEM((rows, d), f32)]
    scratch += [pltpu.VMEM((3, rows, d), bf16), pltpu.VMEM((rows, d), bf16), pltpu.VMEM((d, rows), bf16)]
    scratch += [pltpu.VMEM(s, bf16) for s in own]
    scratch += [pltpu.VMEM((3,) + s, bf16) for s in sums]
    scratch += [pltpu.VMEM(s, bf16) for s in sums]
    scratch += [pltpu.VMEM((3,) + s, bf16) for s in last]
    scratch += [pltpu.VMEM(s, bf16) for s in last]
    scratch += [pltpu.VMEM(small, f32)] * 2 + [pltpu.VMEM(small, bf16)] * 2 + [pltpu.VMEM(small[1:], f32)]
    scratch += [dma((14,)), dma(()), dma((8,)), dma((4, 4)), dma((4, 4, 4)), dma((4,))]
    scratch += [dma((8,)), dma((2, 2, 3, 2)), dma((4,)), dma((4, 4)), dma((4, 4)), dma((4, 4)), dma((3,))]
    spread_rows = (micro, 4, span, d)
    anywhere = pl.BlockSpec(memory_space=pl.ANY)
    all_out, all_in, share_0, share_1, share_2, share_3, small = pl.pallas_call(
        layer_kernel,
        out_shape=[jax.ShapeDtypeStruct(spread_rows, bf16)] * 2
        + [jax.ShapeDtypeStruct(s, bf16) for s in outs]
        + [jax.ShapeDtypeStruct(small, f32)],
        in_specs=[anywhere] * 2 + [pl.BlockSpec(memory_space=pltpu.VMEM)] + [anywhere] * 6,
        out_specs=[anywhere] * 7,
        scratch_shapes=scratch,
        compiler_params=pltpu.CompilerParams(collective_id=0, has_side_effects=True, vmem_limit_bytes=67043328),
        name="layer",
    )(inputs, cotangent, flags, maps, norms, qkv_weight.transpose(0, 2, 1), out_weight, up_weight, down_weight.T)
    small = small.reshape(-1, 128)
    pairs = small[: heads * head].reshape(heads, head, 2, head)
    pairs = pairs.transpose(0, 2, 1, 3).reshape(2, heads, head, head)
    norm_grads = small[heads * head :].reshape(-1)[: 4 * d].reshape(4, d)
    norm_grads = lax.dynamic_slice_in_dim(norm_grads, lax.axis_index("fsdp") * (d // 2), d // 2, 1)
    return (
        all_out.reshape(inputs.shape),
        all_in.reshape(inputs.shape).astype(f32),
        share_0.astype(f32).transpose(0, 2, 1),
        share_1.astype(f32),
        share_2.astype(f32),
        share_3.astype(f32).T,
        own_maps(pairs[0]),
        own_maps(pairs[1]),
        norm_grads[0],
        norm_grads[1],
        norm_grads[2],
        norm_grads[3],
    )


def solution(mesh):
    in_specs = (
        P(None, "fsdp", "context", None),
        P(None, "fsdp", "context", None),
        P(None, "fsdp", None),
        P(None, "fsdp", "tensor"),
        P("tensor", "fsdp"),
        P("fsdp", "tensor"),
        P("tensor", "fsdp"),
        P("tensor", "fsdp", None),
        P("tensor", "fsdp", None),
        P("fsdp"),
        P("fsdp"),
        P("fsdp"),
        P("fsdp"),
    )
    out_specs = (
        P(None, "fsdp", "context", None),
        P(None, "fsdp", "context", None),
        P(None, "fsdp", "tensor"),
        P("tensor", "fsdp"),
        P("fsdp", "tensor"),
        P("tensor", "fsdp"),
        P("tensor", "fsdp", None),
        P("tensor", "fsdp", None),
        P("fsdp"),
        P("fsdp"),
        P("fsdp"),
        P("fsdp"),
    )
    sizes = tuple(mesh.shape[name] for name in EVERY)
    return jax.shard_map(
        mesh_device if sizes == (2, 4, 4) else per_device, mesh=mesh, in_specs=in_specs, out_specs=out_specs, check_vma=False
    )
```

```python
import jax
import jax.numpy as jnp
from jax import lax
from jax.experimental import pallas as pl
from jax.experimental.pallas import tpu as pltpu
from jax.sharding import PartitionSpec as P

BLK = 256
MICRO = 2


epsilon = 1e-05
highest = lax.Precision.HIGHEST


EVERY = ("fsdp", "context", "tensor")


def carried_in(value, backward):
    slot, mine = lax.axis_index("tensor"), lax.axis_index("context")
    near = lax.all_gather(value, "tensor")
    far = lax.all_gather(jnp.sum(near, 0).astype(value.dtype), "context")
    near_ids = jnp.arange(near.shape[0]).reshape((-1,) + (1,) * value.ndim)
    far_ids = jnp.arange(far.shape[0]).reshape((-1,) + (1,) * value.ndim)
    near_mask = near_ids > slot if backward else near_ids < slot
    far_mask = far_ids > mine if backward else far_ids < mine
    near, far = near.astype(jnp.float32), far.astype(jnp.float32)
    return jnp.sum(jnp.where(near_mask, near, 0.0), 0) + jnp.sum(jnp.where(far_mask, far, 0.0), 0)


def layer_norm(values, norm_gain, norm_bias):
    center = values - jnp.mean(values, -1, keepdims=True)
    spread = jnp.mean(center * center, -1, keepdims=True)
    return center * lax.rsqrt(spread + epsilon) * norm_gain + norm_bias


def features(logits):
    return jnp.concatenate([jax.nn.softmax(logits, -1), jax.nn.softmax(-logits, -1)], -1)


def gelu_tanh(values):
    return jax.nn.gelu(values, approximate=True)


def prefix_before(values):
    running = jnp.cumsum(values, 1)
    return jnp.concatenate([jnp.zeros_like(values[:, :1]), running[:, :-1]], 1)


def suffix_after(values):
    running = jnp.flip(jnp.cumsum(jnp.flip(values, 1), 1), 1)
    return jnp.concatenate([running[:, 1:], jnp.zeros_like(values[:, :1])], 1)


def spread(part, axis, parts):
    own = lax.axis_index("context")
    size = part.shape[axis] // parts
    mine = lax.dynamic_slice_in_dim(part, own * size, size, axis)
    return lax.all_gather(mine, EVERY)


def full_in(part):
    pieces = spread(part, 1, lax.axis_size("context"))
    fsdp, ctx, tens = (lax.axis_size(name) for name in EVERY)
    pieces = pieces.reshape((fsdp, ctx, tens) + pieces.shape[1:])
    pieces = pieces.transpose(3, 0, 1, 4, 2, 5)
    return pieces.reshape(pieces.shape[0], -1, pieces.shape[4] * pieces.shape[5])


def share_in(grad):
    fsdp, ctx, tens = (lax.axis_size(name) for name in EVERY)
    kinds, rows, cols = grad.shape
    pieces = grad.astype(jnp.bfloat16).reshape(kinds, fsdp, ctx, rows // fsdp // ctx, tens, cols // tens)
    pieces = pieces.transpose(1, 2, 4, 0, 3, 5).reshape((-1,) + (kinds, rows // fsdp // ctx, cols // tens))
    mine = lax.psum_scatter(pieces, EVERY, scatter_dimension=0)
    return lax.all_gather(mine, "context", axis=1, tiled=True).astype(jnp.float32)


def full_rows(part):
    pieces = spread(part, 0, lax.axis_size("context"))
    fsdp, ctx, tens = (lax.axis_size(name) for name in EVERY)
    pieces = pieces.reshape((fsdp, ctx, tens) + pieces.shape[1:])
    pieces = pieces.transpose(2, 1, 3, 0, 4)
    return pieces.reshape(tens * part.shape[0], -1)


def share_rows(grad):
    fsdp, ctx, tens = (lax.axis_size(name) for name in EVERY)
    rows, cols = grad.shape
    pieces = grad.astype(jnp.bfloat16).reshape(tens, ctx, rows // tens // ctx, fsdp, cols // fsdp)
    pieces = pieces.transpose(3, 1, 0, 2, 4).reshape(-1, rows // tens // ctx, cols // fsdp)
    mine = lax.psum_scatter(pieces, EVERY, scatter_dimension=0)
    return lax.all_gather(mine, "context", axis=0, tiled=True).astype(jnp.float32)


def full_maps(part):
    pieces = lax.all_gather(part, ("fsdp", "tensor"))
    fsdp, tens = lax.axis_size("fsdp"), lax.axis_size("tensor")
    pieces = pieces.reshape((fsdp, tens) + part.shape).transpose(1, 2, 0, 3, 4)
    return pieces.reshape(tens * part.shape[0], fsdp * part.shape[1], part.shape[2])


def own_maps(total):
    fsdp, tens = lax.axis_size("fsdp"), lax.axis_size("tensor")
    heads, rows, _ = total.shape
    mine = lax.dynamic_slice_in_dim(total, lax.axis_index("tensor") * (heads // tens), heads // tens, 0)
    return lax.dynamic_slice_in_dim(mine, lax.axis_index("fsdp") * (rows // fsdp), rows // fsdp, 1)


def per_device(
    inputs,
    cotangent,
    picture_starts,
    qkv_weight,
    out_weight,
    up_weight,
    down_weight,
    query_map,
    key_map,
    first_gain,
    first_bias,
    second_gain,
    second_bias,
):
    tensor_size = lax.axis_size("tensor")
    micro, seq_local, seq_len, model_width = inputs.shape
    span = seq_len // tensor_size
    slot = lax.axis_index("tensor")
    head_size = query_map.shape[2]
    feat_size = 2 * head_size
    blocks_local = span // BLK
    seq_count = micro * seq_local
    block_total = seq_count * blocks_local
    row_count = seq_count * span
    first_block = (lax.axis_index("context") * tensor_size + slot) * blocks_local
    block_ids = first_block + jnp.arange(blocks_local, dtype=jnp.int32)
    position = jnp.arange(BLK, dtype=jnp.int32)
    causal = position[None, :] <= position[:, None]

    in_full = full_in(qkv_weight)
    out_full = full_rows(out_weight)
    up_full = full_in(up_weight[None])[0]
    down_full = full_rows(down_weight)
    qmap_full, kmap_full = full_maps(query_map), full_maps(key_map)
    norms = lax.all_gather(jnp.stack([first_gain, first_bias, second_gain, second_bias]), "fsdp", axis=1, tiled=True)
    gain_first, bias_first, gain_second, bias_second = norms.astype(jnp.float32)

    def own(values):
        mine = lax.dynamic_slice_in_dim(values, slot * span, span, 2)
        return mine.reshape(row_count, model_width)

    source = own(inputs).astype(jnp.float32)
    starts_here = picture_starts.reshape(seq_count, -1)
    block_flags = (
        jnp.sum((starts_here[:, :, None] // BLK == block_ids[None, None, :]).astype(jnp.int32), 1)
        > 0
    )
    allowed = causal[None, None] | block_flags[:, :, None, None]
    allowed = allowed.reshape(block_total, 1, BLK, BLK)
    normed_one = layer_norm(source, gain_first, bias_first)
    normed_low = normed_one.astype(jnp.bfloat16)
    projected = jnp.einsum(
        "rd,cde->cre", normed_low, in_full, preferred_element_type=jnp.float32
    ).astype(jnp.bfloat16)
    heads_local = projected.shape[2] // head_size
    queries = projected[0].reshape(row_count, heads_local, head_size)
    key_rows = projected[1].reshape(row_count, heads_local, head_size)
    value_rows = projected[2].reshape(row_count, heads_local, head_size)
    query_logits = jnp.einsum(
        "rhi,hij->rhj", queries, qmap_full, preferred_element_type=jnp.float32
    )
    key_logits = jnp.einsum(
        "rhi,hij->rhj", key_rows, kmap_full, preferred_element_type=jnp.float32
    )
    query_blocks = (
        features(query_logits)
        .astype(jnp.bfloat16)
        .reshape(block_total, BLK, heads_local, feat_size)
    )
    key_blocks = (
        features(key_logits)
        .astype(jnp.bfloat16)
        .reshape(block_total, BLK, heads_local, feat_size)
    )
    value_blocks = value_rows.reshape(block_total, BLK, heads_local, head_size)
    scores = jnp.einsum(
        "nthf,nshf->nhts", query_blocks, key_blocks, preferred_element_type=jnp.float32
    )
    weights_low = jnp.where(allowed, scores, 0.0).astype(jnp.bfloat16)
    states = jnp.einsum(
        "nshf,nshe->nhfe", key_blocks, value_blocks, preferred_element_type=jnp.float32
    )
    states = states.reshape(seq_count, blocks_local, heads_local, feat_size, head_size)
    key_sums = jnp.sum(key_blocks.astype(jnp.float32), 1).reshape(
        seq_count, blocks_local, heads_local, feat_size
    )
    state_total = jnp.sum(states, 1)
    sums_total = jnp.sum(key_sums, 1)
    carried = carried_in(state_total.astype(jnp.bfloat16), False)
    carried_sums = carried_in(sums_total, False)
    prior_states = (carried[:, None] + prefix_before(states)).astype(jnp.bfloat16)
    prior_states = prior_states.reshape(block_total, heads_local, feat_size, head_size)
    prior_sums = (carried_sums[:, None] + prefix_before(key_sums)).reshape(
        block_total, heads_local, feat_size
    )
    numerator = jnp.einsum(
        "nhts,nshe->nthe", weights_low, value_blocks, preferred_element_type=jnp.float32
    )
    numerator = numerator + jnp.einsum(
        "nthf,nhfe->nthe", query_blocks, prior_states, preferred_element_type=jnp.float32
    )
    denominator = jnp.sum(weights_low.astype(jnp.float32), -1).transpose(0, 2, 1)
    denominator = denominator + jnp.einsum(
        "nthf,nhf->nth", query_blocks.astype(jnp.float32), prior_sums, precision=highest
    )
    mixed_heads = (
        (numerator / denominator[..., None])
        .astype(jnp.bfloat16)
        .reshape(row_count, heads_local * head_size)
    )
    attended = jnp.dot(mixed_heads, out_full, preferred_element_type=jnp.float32)
    middle = source + attended
    normed_two = layer_norm(middle, gain_second, bias_second)
    normed_two_low = normed_two.astype(jnp.bfloat16)
    hidden_pre = jnp.dot(normed_two_low, up_full, preferred_element_type=jnp.float32)
    hidden_low = gelu_tanh(hidden_pre).astype(jnp.bfloat16)
    branch = jnp.dot(hidden_low, down_full, preferred_element_type=jnp.float32)
    output = (middle + branch).astype(jnp.bfloat16).reshape(micro, seq_local, span, model_width)
    output = lax.all_gather(output, "tensor", axis=2, tiled=True)
    upstream_low = own(cotangent)
    upstream = upstream_low.astype(jnp.float32)
    grad_down = jnp.einsum(
        "rk,rd->kd", hidden_low, upstream_low, preferred_element_type=jnp.float32
    )
    hidden_grad = jnp.einsum(
        "rd,kd->rk", upstream_low, down_full, preferred_element_type=jnp.float32
    )
    gelu_result, gelu_pull = jax.vjp(gelu_tanh, hidden_pre)
    pre_grad = gelu_pull(hidden_grad)[0].astype(jnp.bfloat16)
    grad_up = jnp.einsum(
        "rd,rf->df", normed_two_low, pre_grad, preferred_element_type=jnp.float32
    )
    normed_two_grad = jnp.einsum(
        "rf,df->rd", pre_grad, up_full, preferred_element_type=jnp.float32
    )
    norm_result, second_pull = jax.vjp(layer_norm, middle, gain_second, bias_second)
    middle_part, grad_gain_second, grad_bias_second = second_pull(normed_two_grad)
    middle_grad = upstream + middle_part
    middle_low = middle_grad.astype(jnp.bfloat16)
    grad_out = jnp.einsum(
        "rk,rd->kd", mixed_heads, middle_low, preferred_element_type=jnp.float32
    )
    mixed_grad = jnp.einsum(
        "rd,kd->rk", middle_low, out_full, preferred_element_type=jnp.float32
    )
    mixed_grad = mixed_grad.reshape(block_total, BLK, heads_local, head_size)
    numer_grad = (mixed_grad / denominator[..., None]).astype(jnp.bfloat16)
    denom_grad = -jnp.sum(mixed_grad * numerator, -1) / (denominator * denominator)
    weight_grad = jnp.einsum(
        "nthe,nshe->nhts", numer_grad, value_blocks, preferred_element_type=jnp.float32
    )
    weight_grad = weight_grad + denom_grad.transpose(0, 2, 1)[..., None]
    weight_grad_low = jnp.where(allowed, weight_grad, 0.0).astype(jnp.bfloat16)
    value_grad = jnp.einsum(
        "nhts,nthe->nshe", weights_low, numer_grad, preferred_element_type=jnp.float32
    )
    query_grad = jnp.einsum(
        "nhts,nshf->nthf", weight_grad_low, key_blocks, preferred_element_type=jnp.float32
    )
    query_grad = query_grad + jnp.einsum(
        "nthe,nhfe->nthf", numer_grad, prior_states, preferred_element_type=jnp.float32
    )
    query_grad = query_grad + denom_grad[..., None] * prior_sums[:, None]
    key_grad = jnp.einsum(
        "nhts,nthf->nshf", weight_grad_low, query_blocks, preferred_element_type=jnp.float32
    )
    prior_grad = jnp.einsum(
        "nthf,nthe->nhfe", query_blocks, numer_grad, preferred_element_type=jnp.float32
    )
    prior_grad = prior_grad.reshape(seq_count, blocks_local, heads_local, feat_size, head_size)
    prior_sums_grad = jnp.einsum(
        "nthf,nth->nhf", query_blocks.astype(jnp.float32), denom_grad, precision=highest
    )
    prior_sums_grad = prior_sums_grad.reshape(seq_count, blocks_local, heads_local, feat_size)
    grad_total = jnp.sum(prior_grad, 1)
    grad_sums_total = jnp.sum(prior_sums_grad, 1)
    later_states = carried_in(grad_total.astype(jnp.bfloat16), True)
    later_sums = carried_in(grad_sums_total, True)
    state_grad = (later_states[:, None] + suffix_after(prior_grad)).astype(jnp.bfloat16)
    state_grad = state_grad.reshape(block_total, heads_local, feat_size, head_size)
    sums_grad = (later_sums[:, None] + suffix_after(prior_sums_grad)).reshape(
        block_total, heads_local, feat_size
    )
    key_grad = key_grad + jnp.einsum(
        "nshe,nhfe->nshf", value_blocks, state_grad, preferred_element_type=jnp.float32
    )
    key_grad = key_grad + sums_grad[:, None]
    value_grad = value_grad + jnp.einsum(
        "nshf,nhfe->nshe", key_blocks, state_grad, preferred_element_type=jnp.float32
    )
    query_feat_now, query_pull = jax.vjp(features, query_logits)
    query_logit_grad = query_pull(query_grad.reshape(row_count, heads_local, feat_size))[
        0
    ].astype(jnp.bfloat16)
    key_feat_now, key_pull = jax.vjp(features, key_logits)
    key_logit_grad = key_pull(key_grad.reshape(row_count, heads_local, feat_size))[0].astype(
        jnp.bfloat16
    )
    grad_qmap = jnp.einsum(
        "rhi,rhj->hij", queries, query_logit_grad, preferred_element_type=jnp.float32
    )
    grad_kmap = jnp.einsum(
        "rhi,rhj->hij", key_rows, key_logit_grad, preferred_element_type=jnp.float32
    )
    raw_query_grad = jnp.einsum(
        "rhj,hij->rhi", query_logit_grad, qmap_full, preferred_element_type=jnp.float32
    )
    raw_key_grad = jnp.einsum(
        "rhj,hij->rhi", key_logit_grad, kmap_full, preferred_element_type=jnp.float32
    )
    projected_grad = jnp.stack(
        [
            raw_query_grad.reshape(row_count, -1),
            raw_key_grad.reshape(row_count, -1),
            value_grad.reshape(row_count, -1),
        ]
    ).astype(jnp.bfloat16)
    grad_in = jnp.einsum(
        "rd,cre->cde", normed_low, projected_grad, preferred_element_type=jnp.float32
    )
    normed_one_grad = jnp.einsum(
        "cre,cde->rd", projected_grad, in_full, preferred_element_type=jnp.float32
    )
    first_result, first_pull = jax.vjp(layer_norm, source, gain_first, bias_first)
    source_part, grad_gain_first, grad_bias_first = first_pull(normed_one_grad)
    input_grad = (middle_grad + source_part).astype(jnp.bfloat16)
    input_grad = input_grad.reshape(micro, seq_local, span, model_width)
    input_grad = lax.all_gather(input_grad, "tensor", axis=2, tiled=True).astype(jnp.float32)
    norm_grads = jnp.stack([grad_gain_first, grad_bias_first, grad_gain_second, grad_bias_second])
    grad_qmap, grad_kmap, norm_grads = lax.psum((grad_qmap, grad_kmap, norm_grads), EVERY)
    share = first_gain.shape[0]
    norm_grads = lax.dynamic_slice_in_dim(norm_grads, lax.axis_index("fsdp") * share, share, 1)
    return (
        output,
        input_grad,
        share_in(grad_in),
        share_rows(grad_out),
        share_in(grad_up[None])[0],
        share_rows(grad_down),
        own_maps(grad_qmap),
        own_maps(grad_kmap),
        norm_grads[0],
        norm_grads[1],
        norm_grads[2],
        norm_grads[3],
    )


MESH = pl.DeviceIdType.MESH
bf16 = jnp.bfloat16
f32 = jnp.float32


def whereabouts():
    return tuple(lax.axis_index(name) for name in EVERY)


def neighbours(f, c, t):
    n = c * 4 + t
    peers = [(1 - f, c, t)]
    for k in range(1, 16):
        other = lax.rem(n + k, 16)
        peers.append((f, other // 4, lax.rem(other, 4)))
    for k in range(1, 4):
        peers.append((1 - f, c, lax.rem(t + k, 4)))
    return peers


def meet(f, c, t):
    barrier = pltpu.get_barrier_semaphore()
    peers = neighbours(f, c, t)
    for peer in peers:
        pl.semaphore_signal(barrier, inc=1, device_id=peer, device_id_type=MESH)
    pl.semaphore_wait(barrier, len(peers))


def send(src, dst, send_sem, recv_sem, peer):
    copy = pltpu.make_async_remote_copy(
        src_ref=src, dst_ref=dst, send_sem=send_sem, recv_sem=recv_sem,
        device_id=peer, device_id_type=MESH,
    )
    copy.start()
    return copy


def arrived(ref, sem):
    pltpu.make_async_copy(ref, ref, sem).wait()


def at(start, size, unit):
    return pl.ds(pl.multiple_of(start, unit), size)


def half(ref, m, f):
    if m == 0:
        w = ref.shape[2] // 2
        return ref.at[:, :, at(f * w, w, 128)]
    if m == 1:
        w = ref.shape[1] // 2
        return ref.at[:, at(f * w, w, 128)]
    w = ref.shape[0] // 2
    return ref.at[at(f * w, w, 16), :]


def shard(ref, m, f, t):
    if m == 0:
        w, h = ref.shape[2] // 2, ref.shape[1] // 4
        return ref.at[:, at(t * h, h, 16), at(f * w, w, 128)]
    if m == 1:
        w, h = ref.shape[1] // 2, ref.shape[0] // 4
        return ref.at[at(t * h, h, 16), at(f * w, w, 128)]
    h, w = ref.shape[0] // 2, ref.shape[1] // 4
    return ref.at[at(f * h, h, 16), at(t * w, w, 128)]


def piece(ref, m, f, c, t):
    if m == 0:
        w, h = ref.shape[2] // 2, ref.shape[1] // 16
        return ref.at[:, at(t * 4 * h + c * h, h, 16), at(f * w, w, 128)]
    if m == 1:
        w, h = ref.shape[1] // 2, ref.shape[0] // 16
        return ref.at[at(t * 4 * h + c * h, h, 16), at(f * w, w, 128)]
    h, w = ref.shape[0] // 8, ref.shape[1] // 4
    return ref.at[at(f * 4 * h + c * h, h, 16), at(t * w, w, 128)]


def quarter(ref, m, c):
    if m == 0:
        h = ref.shape[1] // 4
        return ref.at[:, at(c * h, h, 16), :]
    h = ref.shape[0] // 4
    return ref.at[at(c * h, h, 16), :]


def context_part(ref, m, c):
    if m == 0:
        h = ref.shape[2] // 4
        return ref.at[:, :, at(c * h, h, 16), :]
    if m == 1:
        h = ref.shape[1] // 4
        return ref.at[:, at(c * h, h, 16), :]
    h = ref.shape[0] // 4
    return ref.at[at(c * h, h, 16), :]


def tensor_part(ref, m, t):
    if m == 0:
        return ref.at[:, t]
    if m == 1:
        return ref.at[t]
    w = ref.shape[1] // 4
    return ref.at[:, at(t * w, w, 128)]


NN = (((1,), (0,)), ((), ()))
NT = (((1,), (1,)), ((), ()))
TN = (((0,), (0,)), ((), ()))


def mm(a, b, dims=NN):
    return lax.dot_general(a, b, dims, preferred_element_type=f32)


def lanes_of(shape):
    return lax.broadcasted_iota(jnp.int32, shape, len(shape) - 1)


def block_ones(size, group):
    row = lax.broadcasted_iota(jnp.int32, (size, size), 0) // group
    col = lax.broadcasted_iota(jnp.int32, (size, size), 1) // group
    return jnp.where(row == col, 1.0, 0.0).astype(bf16)


def statistics(rows):
    center = rows - jnp.mean(rows, -1, keepdims=True)
    rstd = lax.rsqrt(jnp.mean(center * center, -1, keepdims=True) + epsilon)
    return center * rstd, rstd


def norm_back(grad, e, rstd, gain):
    w = grad * gain
    return rstd * (w - jnp.mean(w, -1, keepdims=True) - e * jnp.mean(w * e, -1, keepdims=True))


def near_far(first, low, high):
    return jnp.where(first, low, high)


def own_half(values, first, odd):
    zero = jnp.zeros_like(values)
    return jnp.where(first, zero, values) if odd else jnp.where(first, values, zero)


def pair_block(values, first):
    return jnp.concatenate([own_half(values, first, 0), own_half(values, first, 1)], 0)


def split_half(full, first, odd):
    other = pltpu.roll(full, 64, 1)
    return jnp.where(first, other, full) if odd else jnp.where(first, full, other)


def layer_kernel(*refs):
    inputs, cotangent, flags, maps, norms = refs[:5]
    shards = refs[5:9]
    all_out, all_in = refs[9:11]
    outs, maps_out, norms_out = refs[11:15], refs[15:17], refs[17]
    w, mx, nrm, x, g, n1, qkv, feat = refs[18:22], *refs[22:29]
    prior, sums_in, states, z_buf, s_in, z_in, s_out, z_out = refs[29:37]
    o, rden, num, mid, n2, a, gp, rows_out = refs[37:45]
    gm, dnum, dden, dproj, rows_in, turned = refs[45:51]
    pair_in, xy_in, part, tz_in, last = (refs[51 + 4 * i : 55 + 4 * i] for i in range(5))
    small, small_pair, small_own, small_in, small_sum, small_all = refs[71:77]
    vec, vec_pair, vec_own, vec_in, vec_sum, vec_all = refs[77:83]
    local_sem, send_sem, extra_sem, z_sem, xy_sem, pair_sem = refs[83:89]
    scan_sem, rows_sem, gpair_sem, gxy_sem, gz_sem, last_sem, small_sem = refs[89:96]
    wq, wo, wu, wd = w
    d = x.shape[1]
    ff = a.shape[1]
    half_rows = x.shape[0] // 2
    f, c, t = whereabouts()
    n = c * 4 + t
    peers = neighbours(f, c, t)
    partner = peers[0]
    started = []

    def put(src, dst, recv_sem, peer):
        started.append(send(src, dst, send_sem, recv_sem, peer))

    fetched = []

    def fetch(src, dst, sem):
        copy = pltpu.make_async_copy(src, dst, sem)
        copy.start()
        return copy

    for i in range(2):
        rows = pl.ds(i * half_rows, half_rows)
        fetched.append(fetch(inputs.at[i, 0, at(t * half_rows, half_rows, 16), :], x.at[rows], local_sem.at[i]))
        fetched.append(fetch(cotangent.at[i, 0, at(t * half_rows, half_rows, 16), :], g.at[rows], local_sem.at[2 + i]))
    h3 = maps.shape[1]
    head_rows = small.shape[1]
    pairs_of = (0, 1, 3, 4)
    lo_norm = d // 2

    def map_place(ff_, tt):
        return mx.at[:, pl.ds(tt * h3, h3), at(ff_ * 32, 32, 16), :]

    def norm_place(ff_):
        return nrm.at[:, at(ff_ * lo_norm, lo_norm, 128)]

    fetched.append(fetch(maps, map_place(f, t), local_sem.at[4]))
    fetched.append(fetch(norms, norm_place(f), local_sem.at[5]))
    shard_copies = [fetch(shards[m], shard(w[m], m, f, t), local_sem.at[6 + m]) for m in range(4)]
    z_buf[...] = jnp.zeros_like(z_buf)
    small[...] = jnp.zeros_like(small)
    vec[...] = jnp.zeros_like(vec)
    meet(f, c, t)

    order = (0, 1, 2, 3)
    put(norms, norm_place(f), extra_sem.at[0], partner)
    put(maps, map_place(f, t), extra_sem.at[4], partner)
    for m in order:
        for k in range(1, 4):
            put(quarter(shards[m], m, c), piece(w[m], m, f, c, t), z_sem.at[m, k], (f, c, lax.rem(t + k, 4)))
        if m == 0:
            for k in range(1, 4):
                put(maps, map_place(f, t), extra_sem.at[k], (f, c, lax.rem(t + k, 4)))
    for m in order:
        put(shards[m], shard(w[m], m, f, t), pair_sem.at[m], partner)

    def forward(m, k):
        got = piece(w[m], m, f, c, lax.rem(t + 4 - k, 4))
        arrived(got, z_sem.at[m, k])
        for j in range(1, 3):
            put(got, got, xy_sem.at[m, k, j], (f, c ^ j, t))
        put(got, got, pair_sem.at[m], partner)

    def relay(m, k):
        for j in range(1, 3):
            got = piece(w[m], m, f, c ^ j, lax.rem(t + 4 - k, 4))
            arrived(got, xy_sem.at[m, k, j])
            if (m + k + j) % 2:
                put(got, got, xy_sem.at[m, k, 3], (f, c ^ 3 ^ j, t))
            put(got, got, pair_sem.at[m], partner)

    def across(m):
        for k in range(1, 4):
            got = piece(w[m], m, f, c ^ 3, lax.rem(t + 4 - k, 4))
            arrived(got, xy_sem.at[m, k, 3])
            put(got, got, pair_sem.at[m], partner)

    def take_maps():
        for k in range(1, 4):
            got = map_place(f, lax.rem(t + 4 - k, 4))
            arrived(got, extra_sem.at[k])
            put(got, got, extra_sem.at[4 + k], partner)

    def maps_here():
        for k in range(4):
            arrived(map_place(1 - f, lax.rem(t + 4 - k, 4)), extra_sem.at[4 + k])

    def complete(m):
        shard_copies[m].wait()
        arrived(half(w[m], m, 1 - f), pair_sem.at[m])

    for k in range(1, 4):
        forward(0, k)
    for copy in fetched:
        copy.wait()
    arrived(norm_place(1 - f), extra_sem.at[0])
    first = lanes_of((1, 128)) < 64
    ones64 = block_ones(128, 64)
    step = half_rows // 2

    @pl.loop(0, 4)
    def _(i):
        rows = at(i * step, step, 16)
        e, _unused = statistics(x[rows, :].astype(f32))
        n1[rows, :] = (e * nrm[0:1, :] + nrm[1:2, :]).astype(bf16)

    take_maps()
    for k in range(1, 4):
        relay(0, k)
        forward(1, k)
    across(0)
    forward(2, 1)
    complete(0)

    chunks = d // 256

    @pl.loop(0, 3 * chunks)
    def _(i):
        kind, j = i // chunks, lax.rem(i, chunks)
        cols = at(j * 256, 256, 128)
        qkv[kind, :, cols] = mm(n1[...], wq[kind, cols, :], NT).astype(bf16)

    for k in range(1, 4):
        relay(1, k)
    forward(2, 2)
    maps_here()

    pairs = d // 128

    def pair_map(side, p):
        zero = jnp.zeros((64, 128), bf16)
        top = jnp.concatenate([mx[side, 2 * p], zero], 1)
        bottom = jnp.concatenate([zero, mx[side, 2 * p + 1]], 1)
        return jnp.concatenate([top, bottom], 0)

    def features_of(side, i):
        b, p = i // pairs, lax.rem(i, pairs)
        rows = at(b * half_rows, half_rows, 16)
        logits = mm(qkv[side, rows, at(p * 128, 128, 128)], pair_map(side, p))
        for odd in range(2):
            part_ = logits[:, odd * 128 : odd * 128 + 128]
            low_top = jnp.max(jnp.where(first, part_, -jnp.inf), -1, keepdims=True)
            high_top = jnp.max(jnp.where(first, -jnp.inf, part_), -1, keepdims=True)
            e = jnp.exp(part_ - jnp.where(first, low_top, high_top))
            total = mm(e.astype(bf16), ones64)
            feat[side, rows, at(p * 256 + odd * 128, 128, 128)] = (e / total).astype(bf16)

    @pl.loop(0, 2 * pairs)
    def _(i):
        features_of(1, i)

    forward(2, 3)
    across(1)
    relay(2, 1)

    @pl.loop(0, 2 * pairs)
    def _(i):
        b, p = i // pairs, lax.rem(i, pairs)
        rows = at(b * half_rows, half_rows, 16)
        keys = feat[1, rows, at(p * 256, 256, 128)]
        both = mm(keys, qkv[2, rows, at(p * 128, 128, 128)], TN)
        states[b, at(p * 128, 128, 16), :] = near_far(first, both[:128], both[128:]).astype(bf16)
        tall = mm(jnp.ones((8, half_rows), bf16), keys)
        slot = lax.broadcasted_iota(jnp.int32, (8, 128), 0) == b
        z_buf[2 * p] = jnp.where(slot, tall[:, :128], z_buf[2 * p])
        z_buf[2 * p + 1] = jnp.where(slot, tall[:, 128:], z_buf[2 * p + 1])

    srows = states.shape[1] // 16

    def scan_out(sem0):
        for k in range(1, 16):
            other = lax.rem(n + k, 16)
            put(states.at[:, at(other * srows, srows, 16), :], s_in.at[n], scan_sem.at[sem0], peers[k])
            put(z_buf.at[other], z_in.at[n], scan_sem.at[sem0 + 1], peers[k])
        one = fetch(states.at[:, at(n * srows, srows, 16), :], s_in.at[n], local_sem.at[0])
        two = fetch(z_buf.at[n], z_in.at[n], local_sem.at[1])
        one.wait()
        two.wait()

    def scan_back(sem0, backward):
        arrived(s_in.at[pl.ds(0, 15)], scan_sem.at[sem0])
        arrived(z_in.at[pl.ds(0, 15)], scan_sem.at[sem0 + 1])
        total = jnp.zeros(s_in.shape[1:], f32)
        sums = jnp.zeros(z_in.shape[1:], f32)
        for i in range(15, -1, -1) if backward else range(16):
            s_out[i] = total.astype(bf16)
            z_out[i] = sums
            total = total + s_in[i].astype(f32)
            sums = sums + z_in[i]
        for k in range(1, 16):
            other = lax.rem(n + k, 16)
            put(s_out.at[other], prior.at[int(backward), :, at(n * srows, srows, 16), :], scan_sem.at[sem0 + 2], peers[k])
            put(z_out.at[other], sums_in.at[int(backward), n], scan_sem.at[sem0 + 3], peers[k])
        one = fetch(s_out.at[n], prior.at[int(backward), :, at(n * srows, srows, 16), :], local_sem.at[0])
        two = fetch(z_out.at[n], sums_in.at[int(backward), n], local_sem.at[1])
        one.wait()
        two.wait()

    def scan_end(sem0):
        arrived(s_in.at[pl.ds(0, 15)], scan_sem.at[sem0 + 2])
        arrived(z_in.at[pl.ds(0, 15)], scan_sem.at[sem0 + 3])

    scan_out(0)
    relay(2, 2)
    for k in range(1, 4):
        forward(3, k)

    @pl.loop(0, 2 * pairs)
    def _(i):
        features_of(0, i)

    relay(2, 3)

    def mask_of(b, turn):
        row = lax.broadcasted_iota(jnp.int32, (half_rows, half_rows), 0)
        col = lax.broadcasted_iota(jnp.int32, (half_rows, half_rows), 1)
        causal = row <= col if turn else col <= row
        return jnp.where(causal, 1.0, flags[b, 0:1, :])

    @pl.loop(0, 2 * pairs)
    def _(i):
        b, p = i // pairs, lax.rem(i, pairs)
        rows = at(b * half_rows, half_rows, 16)
        values = qkv[2, rows, at(p * 128, 128, 128)]
        mask = mask_of(b, False)
        both = None
        for odd in range(2):
            cols = at(p * 256 + odd * 128, 128, 128)
            scores = (mm(feat[0, rows, cols], feat[1, rows, cols], NT) * mask).astype(bf16)
            right = jnp.concatenate(
                [own_half(values, first, odd), own_half(jnp.ones_like(values), first, odd)], 1
            )
            term = mm(scores, right)
            both = term if both is None else both + term
        num[rows, at(p * 128, 128, 128)] = both[:, :128]
        rden[rows, at(p * 128, 128, 128)] = both[:, 128:]

    scan_back(0, False)
    for k in range(1, 4):
        relay(3, k)
    complete(1)
    scan_end(0)

    def sums_pair(direction, b, p, odd):
        tile = sums_in[direction, 2 * p + odd]
        slot = lax.broadcasted_iota(jnp.int32, (8, 128), 0) == b
        return jnp.sum(jnp.where(slot, tile, 0.0), 0, keepdims=True)

    @pl.loop(0, 2 * pairs)
    def _(i):
        b, p = i // pairs, lax.rem(i, pairs)
        rows = at(b * half_rows, half_rows, 16)
        cols = at(p * 128, 128, 128)
        queries = feat[0, rows, at(p * 256, 256, 128)]
        before = pair_block(prior[0, b, at(p * 128, 128, 16), :], first)
        zero = jnp.zeros((64, 128), bf16)
        z_low = jnp.broadcast_to(sums_pair(0, b, p, 0), (64, 128)).astype(bf16)
        z_high = jnp.broadcast_to(sums_pair(0, b, p, 1), (64, 128)).astype(bf16)
        z_rows = jnp.concatenate(
            [jnp.concatenate([z_low, zero], 1), jnp.concatenate([zero, z_high], 1)], 0
        )
        inverse = 1.0 / (rden[rows, cols] + mm(queries, z_rows, NT))
        o[rows, cols] = ((num[rows, cols] + mm(queries, before)) * inverse).astype(bf16)
        rden[rows, cols] = inverse

    @pl.loop(0, 2)
    def _(i):
        rows = at(i * half_rows, half_rows, 16)
        mid[rows, :] = x[rows, :].astype(f32) + mm(o[rows, :], wo[...])

    across(2)

    @pl.loop(0, 4)
    def _(i):
        rows = at(i * step, step, 16)
        e, _unused = statistics(mid[rows, :])
        n2[rows, :] = (e * nrm[2:3, :] + nrm[3:4, :]).astype(bf16)

    complete(2)

    @pl.loop(0, ff // 256)
    def _(i):
        cols = at(i * 256, 256, 128)
        u = mm(n2[...], wu[:, cols])
        scale = 0.7978845608028654
        square = u * u
        tanh = jnp.tanh(scale * u * (1.0 + 0.044715 * square))
        cdf = 0.5 + 0.5 * tanh
        a[:, cols] = (u * cdf).astype(bf16)
        slope = cdf + (0.5 * scale) * u * (1.0 - tanh * tanh) * (1.0 + 0.134145 * square)
        gp[:, cols] = slope.astype(bf16)

    across(3)
    complete(3)

    @pl.loop(0, chunks)
    def _(i):
        cols = at(i * 256, 256, 128)
        rows_out[:, cols] = (mid[:, cols] + mm(a[...], wd[cols, :], NT)).astype(bf16)

    links = []

    def pass_on(i, b, way, hop, block):
        dst = (all_out, all_in)[i]
        src = (rows_out, rows_in)[i]
        origin = src.at[pl.ds(b * half_rows, half_rows)] if hop == 0 else dst.at[b, block]
        return pltpu.make_async_remote_copy(
            src_ref=origin, dst_ref=dst.at[b, block], send_sem=rows_sem.at[i, way, hop, b, 0],
            recv_sem=rows_sem.at[i, way, hop, b, 1], device_id=(f, c, t + 1 if way == 0 else t - 1),
            device_id_type=MESH,
        )

    def rows_hop(i, b, hop):
        dst = (all_out, all_in)[i]
        for way in range(2):
            block = t - hop if way == 0 else t + hop
            here = block >= 0 if way == 0 else block <= 3
            more = t < 3 if way == 0 else t > 0
            if hop > 0:
                @pl.when(here)
                def _():
                    arrived(dst.at[b, 0], rows_sem.at[i, way, hop - 1, b, 1])
            if hop < 3:
                @pl.when(jnp.logical_and(here, more))
                def _():
                    pass_on(i, b, way, hop, block).start()

    def rows_sent(i):
        for b in range(2):
            for hop in range(3):
                for way in range(2):
                    block = t - hop if way == 0 else t + hop
                    here = block >= 0 if way == 0 else block <= 3
                    more = t < 3 if way == 0 else t > 0

                    @pl.when(jnp.logical_and(here, more))
                    def _():
                        pass_on(i, b, way, hop, block).wait_send()

    own_rows = []
    for b in range(2):
        own_rows.append(fetch(rows_out.at[pl.ds(b * half_rows, half_rows)], all_out.at[b, t], local_sem.at[2 + b]))
        rows_hop(0, b, 0)

    def grad_pair(m):
        if m < 2:
            h = d // 4
            for tt in range(4):
                if m == 0:
                    src = w[m].at[:, pl.ds(tt * h, h), at((1 - f) * (d // 2), d // 2, 128)]
                    put(src, pair_in[m].at[:, tt], gpair_sem.at[m], partner)
                else:
                    src = w[m].at[pl.ds(tt * h, h), at((1 - f) * (d // 2), d // 2, 128)]
                    put(src, pair_in[m].at[tt], gpair_sem.at[m], partner)
        else:
            put(half(w[m], m, 1 - f), pair_in[m], gpair_sem.at[m], partner)

    def grad_xy(m):
        arrived(pair_in[m], gpair_sem.at[m])
        h = d // 4
        cols = at(f * (d // 2), d // 2, 128)
        if m == 0:
            @pl.loop(0, 12)
            def _(i):
                kind, tt = i // 4, lax.rem(i, 4)
                mine = wq[kind, at(tt * h, h, 16), cols].astype(f32)
                pair_in[0][kind, tt] = (mine + pair_in[0][kind, tt].astype(f32)).astype(bf16)
        elif m == 1:
            @pl.loop(0, 4)
            def _(tt):
                mine = wo[at(tt * h, h, 16), cols].astype(f32)
                pair_in[1][tt] = (mine + pair_in[1][tt].astype(f32)).astype(bf16)
        else:
            @pl.loop(0, 12)
            def _(i):
                rows = at(i * 32, 32, 16)
                mine = w[m][at(f * (d // 2) + i * 32, 32, 16), :].astype(f32)
                pair_in[m][rows, :] = (mine + pair_in[m][rows, :].astype(f32)).astype(bf16)
        for j in range(1, 4):
            put(context_part(pair_in[m], m, c ^ j), xy_in[m].at[j - 1], gxy_sem.at[m, j], (f, c ^ j, t))

    def grad_z(m):
        for j in range(1, 4):
            arrived(xy_in[m].at[j - 1], gxy_sem.at[m, j])
        if m == 0:
            h = d // 16

            @pl.loop(0, 12)
            def _(i):
                kind, tt = i // 4, lax.rem(i, 4)
                total = pair_in[0][kind, tt, at(c * h, h, 16), :].astype(f32)
                for j in range(3):
                    total = total + xy_in[0][j, kind, tt].astype(f32)
                part[0][kind, tt] = total.astype(bf16)
        elif m == 1:
            h = d // 16

            @pl.loop(0, 4)
            def _(tt):
                total = pair_in[1][tt, at(c * h, h, 16), :].astype(f32)
                for j in range(3):
                    total = total + xy_in[1][j, tt].astype(f32)
                part[1][tt] = total.astype(bf16)
        else:
            @pl.loop(0, d // 8 // 16)
            def _(i):
                rows = at(i * 16, 16, 16)
                total = pair_in[m][at(c * (d // 8) + i * 16, 16, 16), :].astype(f32)
                for j in range(3):
                    total = total + xy_in[m][j, rows, :].astype(f32)
                part[m][rows, :] = total.astype(bf16)
        for k in range(1, 4):
            other = lax.rem(t + k, 4)
            put(tensor_part(part[m], m, other), tz_in[m].at[k - 1], gz_sem.at[m, k], (f, c, other))

    def grad_last(m):
        for k in range(1, 4):
            arrived(tz_in[m].at[k - 1], gz_sem.at[m, k])
        if m == 0:
            for kind in range(3):
                total = part[0][kind, t].astype(f32)
                for k in range(3):
                    total = total + tz_in[0][k, kind].astype(f32)
                last[0][kind] = total.astype(bf16)
        elif m == 1:
            total = part[1][t].astype(f32)
            for k in range(3):
                total = total + tz_in[1][k].astype(f32)
            last[1][...] = total.astype(bf16)
        else:
            cols = at(t * (ff // 4), ff // 4, 128)

            @pl.loop(0, d // 8 // 16)
            def _(i):
                rows = at(i * 16, 16, 16)
                total = part[m][rows, cols].astype(f32)
                for k in range(3):
                    total = total + tz_in[m][k, rows, :].astype(f32)
                last[m][rows, :] = total.astype(bf16)
        for j in range(1, 4):
            put(last[m], quarter(outs[m], m, c), last_sem.at[m, j], (f, c ^ j, t))
        fetch(last[m], quarter(outs[m], m, c), local_sem.at[10 + m]).wait()

    for copy in started:
        copy.wait_send()
    started.clear()

    @pl.loop(0, ff // 256)
    def _(i):
        cols = at(i * 256, 256, 128)
        gp[:, cols] = (mm(g[...], wd[:, cols]) * gp[:, cols].astype(f32)).astype(bf16)

    def turn(src):
        @pl.loop(0, chunks)
        def _(i):
            cols = at(i * 256, 256, 128)
            turned[at(i * 256, 256, 16), :] = src[:, cols].astype(f32).T.astype(bf16)

    turn(g)

    @pl.loop(0, ff // 256)
    def _(i):
        cols = at(i * 256, 256, 128)
        wd[:, cols] = mm(turned[...], a[:, cols]).astype(bf16)

    grad_pair(3)
    rows_hop(0, 0, 1)

    @pl.loop(0, chunks)
    def _(i):
        cols = at(i * 256, 256, 128)
        num[:, cols] = mm(gp[...], wu[cols, :], NT)

    @pl.loop(0, 4)
    def _(i):
        rows = at(i * step, step, 16)
        e, rstd = statistics(mid[rows, :])
        grad = num[rows, :]
        vec[2:3, :] += jnp.sum(grad * e, 0, keepdims=True)
        vec[3:4, :] += jnp.sum(grad, 0, keepdims=True)
        total = g[rows, :].astype(f32) + norm_back(grad, e, rstd, nrm[2:3, :])
        mid[rows, :] = total
        gm[rows, :] = total.astype(bf16)

    grad_xy(3)

    @pl.loop(0, chunks)
    def _(i):
        cols = at(i * 256, 256, 128)
        back = mm(gm[...], wo[cols, :], NT)
        for side in range(2):
            cut = at(i * 256 + side * 128, 128, 128)
            grad = back[:, side * 128 : side * 128 + 128]
            inverse = rden[:, cut]
            dnum[:, cut] = (grad * inverse).astype(bf16)
            dden[:, cut] = -mm((grad * o[:, cut].astype(f32)).astype(bf16), ones64) * inverse

    @pl.loop(0, 2 * pairs)
    def _(i):
        b, p = i // pairs, lax.rem(i, pairs)
        rows = at(b * half_rows, half_rows, 16)
        cols = at(p * 128, 128, 128)
        queries = feat[0, rows, at(p * 256, 256, 128)]
        both = mm(queries, dnum[rows, cols], TN)
        states[b, at(p * 128, 128, 16), :] = near_far(first, both[:128], both[128:]).astype(bf16)
        slot = lax.broadcasted_iota(jnp.int32, (8, 128), 0) == b
        packed = dden[rows, cols]
        for odd in range(2):
            full = split_half(packed, first, odd)
            tall = jnp.sum(queries[:, odd * 128 : odd * 128 + 128].astype(f32) * full, 0, keepdims=True)
            z_buf[2 * p + odd] = jnp.where(slot, tall, z_buf[2 * p + odd])

    scan_out(4)

    turn(n2)

    @pl.loop(0, ff // 256)
    def _(i):
        cols = at(i * 256, 256, 128)
        wu[:, cols] = mm(turned[...], gp[:, cols]).astype(bf16)

    grad_pair(2)

    scan_back(4, True)
    rows_hop(0, 1, 1)

    @pl.loop(0, chunks)
    def _(i):
        cols = at(i * 256, 256, 128)
        wo[cols, :] = mm(o[:, cols].astype(f32).T.astype(bf16), gm[...]).astype(bf16)

    grad_pair(1)

    lane = lanes_of((1, 128))

    def extended(values, one, two, odd):
        base = 0 if odd else 64
        rest = jnp.where(lane == base, one, jnp.where(lane == base + 1, two, jnp.zeros_like(values)))
        return jnp.where(first, rest, values) if odd else jnp.where(first, values, rest)

    def block_maps(side, p):
        low_ = jnp.where(first, mx[side, 2 * p], jnp.zeros((64, 128), bf16))
        high_ = jnp.where(first, jnp.zeros((64, 128), bf16), -mx[side, 2 * p + 1])
        return jnp.concatenate([low_, high_], 0)

    def through_features(side, b, p, rows, cols, grads):
        logits = []
        for odd in range(2):
            prob = feat[side, rows, at(p * 256 + odd * 128, 128, 128)].astype(f32)
            grad = grads[odd]
            inner = mm((prob * grad).astype(bf16), ones64)
            both = prob * (grad - inner)
            other = pltpu.roll(both, 64, 1)
            logits.append(other - both if odd else both - other)
        packed = jnp.where(first, logits[0], logits[1]).astype(bf16)
        dproj[side, rows, cols] = mm(packed, block_maps(side, p), NT).astype(bf16)
        square = mm(qkv[side, rows, cols], packed, TN)
        small[side * pairs + p] += near_far(first, square[:64], square[64:])

    def exact(packed, odd):
        full = split_half(packed, first, odd)
        head = full.astype(bf16)
        return full, head, (full - head.astype(f32)).astype(bf16)

    @pl.loop(0, 2 * pairs)
    def _(i):
        b, p = i // pairs, lax.rem(i, pairs)
        rows = at(b * half_rows, half_rows, 16)
        cols = at(p * 128, 128, 128)
        values, grad_rows = qkv[2, rows, cols], dnum[rows, cols]
        packed = dden[rows, cols]
        before = prior[0, b, at(p * 128, 128, 16), :]
        mask = mask_of(b, False)
        unit = jnp.ones_like(values)
        grads = []
        for odd in range(2):
            full, head, tail = exact(packed, odd)
            left = extended(grad_rows, head, tail, odd)
            right = extended(values, unit, unit, odd)
            scores = (mm(left, right, NT) * mask).astype(bf16)
            total = mm(scores, feat[1, rows, at(p * 256 + odd * 128, 128, 128)])
            total = total + mm(own_half(grad_rows, first, odd), before, NT)
            grads.append(total + full * sums_pair(0, b, p, odd))
        through_features(0, b, p, rows, cols, grads)

    grad_xy(2)
    scan_end(4)
    rows_hop(0, 0, 2)

    def key_side(b, p):
        rows = pl.ds(b * half_rows, half_rows)
        cols = at(p * 128, 128, 128)
        values, grad_rows = qkv[2, rows, cols], dnum[rows, cols]
        packed = dden[rows, cols]
        after = prior[1, b, at(p * 128, 128, 16), :]
        mask = mask_of(b, True)
        unit = jnp.ones_like(values)
        value_grad = mm(feat[1, rows, at(p * 256, 256, 128)], pair_block(after, first))
        grads = []
        for odd in range(2):
            fcols = at(p * 256 + odd * 128, 128, 128)
            queries, keys = feat[0, rows, fcols], feat[1, rows, fcols]
            _full, head, tail = exact(packed, odd)
            left = extended(values, unit, unit, odd)
            right = extended(grad_rows, head, tail, odd)
            scores = (mm(left, right, NT) * mask).astype(bf16)
            total = mm(scores, queries) + mm(own_half(values, first, odd), after, NT)
            grads.append(total + sums_pair(1, b, p, odd))
            weights = (mm(keys, queries, NT) * mask).astype(bf16)
            value_grad = value_grad + mm(weights, own_half(grad_rows, first, odd))
        dproj[2, rows, cols] = value_grad.astype(bf16)
        through_features(1, b, p, rows, cols, grads)

    for b in range(2):
        @pl.loop(0, pairs)
        def _(p):
            key_side(b, p)

        if b == 0:
            grad_xy(1)
            rows_hop(0, 1, 2)

        @pl.loop(0, chunks)
        def _(i):
            cols = at(i * 256, 256, 128)
            rows = pl.ds(b * half_rows, half_rows)
            total = mm(dproj[0, rows, :], wq[0, :, cols])
            for kind in range(1, 3):
                total = total + mm(dproj[kind, rows, :], wq[kind, :, cols])
            num[rows, cols] = total

        @pl.loop(2 * b, 2 * b + 2)
        def _(i):
            rows = at(i * step, step, 16)
            e, rstd = statistics(x[rows, :].astype(f32))
            grad = num[rows, :]
            vec[0:1, :] += jnp.sum(grad * e, 0, keepdims=True)
            vec[1:2, :] += jnp.sum(grad, 0, keepdims=True)
            rows_in[rows, :] = (mid[rows, :] + norm_back(grad, e, rstd, nrm[0:1, :])).astype(bf16)

        own_rows.append(fetch(rows_in.at[pl.ds(b * half_rows, half_rows)], all_in.at[b, t], local_sem.at[4 + b]))
        rows_hop(1, b, 0)

    lo_map = head_rows // 2
    put(small.at[:, at((1 - f) * lo_map, lo_map, 16), :], small_pair, small_sem.at[0], partner)
    put(vec.at[:, at((1 - f) * lo_norm, lo_norm, 128)], vec_pair, small_sem.at[1], partner)

    @pl.loop(0, 3 * chunks)
    def _(i):
        kind, j = i // chunks, lax.rem(i, chunks)
        cols = at(j * 256, 256, 128)
        wq[kind, cols, :] = mm(dproj[kind, :, cols].astype(f32).T.astype(bf16), n1[...]).astype(bf16)

    grad_pair(0)
    arrived(small_pair, small_sem.at[0])
    arrived(vec_pair, small_sem.at[1])
    for tt in range(4):
        for side in range(2):
            for q in range(2):
                p = side * pairs + pairs_of[tt] + q
                mine = small[p, at(f * lo_map, lo_map, 16), :] + small_pair[p]
                small_own[tt, 2 * side + q] = mine.astype(bf16)
    vec_own[...] = vec[:, at(f * lo_norm, lo_norm, 128)] + vec_pair[...]
    for k in range(1, 4):
        other = lax.rem(t + k, 4)
        put(small_own.at[other], small_in.at[t], small_sem.at[2], (f, c, other))
        put(vec_own, vec_in.at[t], small_sem.at[3], (f, c, other))
    own_small = [
        fetch(small_own.at[t], small_in.at[t], local_sem.at[6]),
        fetch(vec_own, vec_in.at[t], local_sem.at[7]),
    ]
    grad_z(3)
    rows_hop(1, 0, 1)
    grad_xy(0)
    for copy in own_small:
        copy.wait()
    arrived(small_in.at[pl.ds(0, 3)], small_sem.at[2])
    arrived(vec_in.at[pl.ds(0, 3)], small_sem.at[3])
    total = small_in[0].astype(f32)
    sums = vec_in[0]
    for i in range(1, 4):
        total = total + small_in[i].astype(f32)
        sums = sums + vec_in[i]
    small_sum[...] = total.astype(bf16)
    vec_sum[...] = sums
    for j in range(1, 4):
        put(small_sum, small_all.at[c], small_sem.at[4], (f, c ^ j, t))
        put(vec_sum, vec_all.at[c], small_sem.at[5], (f, c ^ j, t))
    own_small = [
        fetch(small_sum, small_all.at[c], local_sem.at[6]),
        fetch(vec_sum, vec_all.at[c], local_sem.at[7]),
    ]
    rows_hop(1, 1, 1)
    grad_z(2)
    grad_z(1)
    grad_last(3)
    rows_hop(1, 0, 2)
    for copy in own_small:
        copy.wait()
    arrived(small_all.at[pl.ds(0, 3)], small_sem.at[4])
    arrived(vec_all.at[pl.ds(0, 3)], small_sem.at[5])
    total = small_all[0].astype(f32)
    sums = vec_all[0]
    for i in range(1, 4):
        total = total + small_all[i].astype(f32)
        sums = sums + vec_all[i]
    norms_out[...] = sums
    odd_slot = lax.rem(t, 2) == 1
    for side in range(2):
        near, far = total[2 * side], total[2 * side + 1]
        near_high, far_high = pltpu.roll(near, 64, 1), pltpu.roll(far, 64, 1)
        for j, (high, low) in enumerate(((near_high, near), (far, near_high), (far_high, far))):
            maps_out[side][j] = jnp.where(odd_slot, high, low)[:, :64]
    grad_last(2)
    grad_last(1)
    rows_hop(1, 1, 2)
    grad_z(0)
    rows_hop(0, 0, 3)
    rows_hop(0, 1, 3)
    grad_last(0)
    for m in range(4):
        for j in range(1, 4):
            arrived(last[m], last_sem.at[m, j])
    rows_hop(1, 0, 3)
    rows_hop(1, 1, 3)
    for copy in own_rows:
        copy.wait()
    for copy in started:
        copy.wait_send()
    rows_sent(0)
    rows_sent(1)

def mesh_device(
    inputs,
    cotangent,
    picture_starts,
    qkv_weight,
    out_weight,
    up_weight,
    down_weight,
    query_map,
    key_map,
    first_gain,
    first_bias,
    second_gain,
    second_bias,
):
    micro, seq_local, seq_len, d = inputs.shape
    span = seq_len // 4
    rows = micro * seq_local * span
    ff = up_weight.shape[1] * 4
    heads = query_map.shape[0] * 4
    head = query_map.shape[2]
    own_block = lax.axis_index("context") * 4 + lax.axis_index("tensor")
    flags = jnp.any(picture_starts.reshape(micro, -1) // BLK == own_block, 1).astype(f32)
    flags = jnp.broadcast_to(flags[:, None, None], (micro, 8, span))
    maps = jnp.stack([query_map, key_map])
    maps = jnp.concatenate([maps, -maps], -1)
    norms = jnp.stack([first_gain, first_bias, second_gain, second_bias]).astype(f32)
    norms = jnp.concatenate([norms, jnp.zeros_like(norms)])
    dma = pltpu.SemaphoreType.DMA
    own = [(3, 4, d // 4, d // 2), (4, d // 4, d // 2), (d // 2, ff), (d // 2, ff)]
    sums = [(3, 4, d // 16, d // 2), (4, d // 16, d // 2), (d // 8, ff), (d // 8, ff)]
    last = [(3, d // 16, d // 2), (d // 16, d // 2), (d // 8, ff // 4), (d // 8, ff // 4)]
    outs = [(3, d // 4, d // 2), (d // 4, d // 2), (d // 2, ff // 4), (d // 2, ff // 4)]
    low = [(3, d, d), (d, d), (d, ff), (d, ff), (2, heads, head, 128)]
    state_rows = heads // 2 * 128
    pieces = (16, micro, state_rows // 16, 128)
    tiny = [(2 * (heads // 2), head, 128), (2 * (heads // 2), head // 2, 128), (4, 4, head // 2, 128)]
    maps_shape = (heads // 4, head // 2, head)
    scratch = [pltpu.VMEM(s, bf16) for s in low]
    scratch += [pltpu.VMEM((8, d), f32)]
    scratch += [pltpu.VMEM((rows, d), bf16)] * 3
    scratch += [pltpu.VMEM((3, rows, d), bf16), pltpu.VMEM((2, rows, heads * 128), bf16)]
    scratch += [pltpu.VMEM((2, micro, state_rows, 128), bf16), pltpu.VMEM((2, 16, 8, 128), f32)]
    scratch += [pltpu.VMEM((micro, state_rows, 128), bf16), pltpu.VMEM((16, 8, 128), f32)]
    scratch += [pltpu.VMEM(pieces, bf16), pltpu.VMEM((16, 8, 128), f32)] * 2
    scratch += [pltpu.VMEM((rows, d), bf16)] + [pltpu.VMEM((rows, d), f32)] * 3
    scratch += [pltpu.VMEM((rows, d), bf16)] + [pltpu.VMEM((rows, ff), bf16)] * 2
    scratch += [pltpu.VMEM((rows, d), bf16)] * 3 + [pltpu.VMEM((rows, d), f32)]
    scratch += [pltpu.VMEM((3, rows, d), bf16), pltpu.VMEM((rows, d), bf16), pltpu.VMEM((d, rows), bf16)]
    scratch += [pltpu.VMEM(s, bf16) for s in own]
    scratch += [pltpu.VMEM((3,) + s, bf16) for s in sums]
    scratch += [pltpu.VMEM(s, bf16) for s in sums]
    scratch += [pltpu.VMEM((3,) + s, bf16) for s in last]
    scratch += [pltpu.VMEM(s, bf16) for s in last]
    scratch += [pltpu.VMEM(s, f32) for s in tiny[:2]] + [pltpu.VMEM(tiny[2], bf16)] * 2
    scratch += [pltpu.VMEM(tiny[2][1:], bf16), pltpu.VMEM(tiny[2], bf16)]
    scratch += [pltpu.VMEM(s, f32) for s in ((8, d), (8, d // 2), (8, d // 2), (4, 8, d // 2), (8, d // 2), (4, 8, d // 2))]
    scratch += [dma((14,)), dma(()), dma((8,)), dma((4, 4)), dma((4, 4, 4)), dma((4,))]
    scratch += [dma((8,)), dma((2, 2, 3, 2, 2)), dma((4,)), dma((4, 4)), dma((4, 4)), dma((4, 4)), dma((6,))]
    spread_rows = (micro, 4, span, d)
    anywhere = pl.BlockSpec(memory_space=pl.ANY)
    all_out, all_in, share_0, share_1, share_2, share_3, map_0, map_1, norm_grads = pl.pallas_call(
        layer_kernel,
        out_shape=[jax.ShapeDtypeStruct(spread_rows, bf16)] * 2
        + [jax.ShapeDtypeStruct(s, bf16) for s in outs]
        + [jax.ShapeDtypeStruct(maps_shape, f32)] * 2
        + [jax.ShapeDtypeStruct((8, d // 2), f32)],
        in_specs=[anywhere] * 2 + [pl.BlockSpec(memory_space=pltpu.VMEM)] + [anywhere] * 6,
        out_specs=[anywhere] * 6 + [pl.BlockSpec(memory_space=pltpu.VMEM)] * 3,
        scratch_shapes=scratch,
        compiler_params=pltpu.CompilerParams(collective_id=0, has_side_effects=True, vmem_limit_bytes=67043328),
        name="layer",
    )(inputs, cotangent, flags, maps, norms, qkv_weight.transpose(0, 2, 1), out_weight, up_weight, down_weight.T)
    return (
        all_out.reshape(inputs.shape),
        all_in.reshape(inputs.shape).astype(f32),
        share_0.astype(f32).transpose(0, 2, 1),
        share_1.astype(f32),
        share_2.astype(f32),
        share_3.astype(f32).T,
        map_0,
        map_1,
        norm_grads[0],
        norm_grads[1],
        norm_grads[2],
        norm_grads[3],
    )


def solution(mesh):
    in_specs = (
        P(None, "fsdp", "context", None),
        P(None, "fsdp", "context", None),
        P(None, "fsdp", None),
        P(None, "fsdp", "tensor"),
        P("tensor", "fsdp"),
        P("fsdp", "tensor"),
        P("tensor", "fsdp"),
        P("tensor", "fsdp", None),
        P("tensor", "fsdp", None),
        P("fsdp"),
        P("fsdp"),
        P("fsdp"),
        P("fsdp"),
    )
    out_specs = (
        P(None, "fsdp", "context", None),
        P(None, "fsdp", "context", None),
        P(None, "fsdp", "tensor"),
        P("tensor", "fsdp"),
        P("fsdp", "tensor"),
        P("tensor", "fsdp"),
        P("tensor", "fsdp", None),
        P("tensor", "fsdp", None),
        P("fsdp"),
        P("fsdp"),
        P("fsdp"),
        P("fsdp"),
    )
    sizes = tuple(mesh.shape[name] for name in EVERY)
    return jax.shard_map(
        mesh_device if sizes == (2, 4, 4) else per_device, mesh=mesh, in_specs=in_specs, out_specs=out_specs, check_vma=False
    )
```

```python
import jax
import jax.numpy as jnp
from jax import lax
from jax.experimental import pallas as pl
from jax.experimental.pallas import tpu as pltpu
from jax.sharding import PartitionSpec as P

BLK = 256
MICRO = 2


epsilon = 1e-05
highest = lax.Precision.HIGHEST


EVERY = ("fsdp", "context", "tensor")


def carried_in(value, backward):
    slot, mine = lax.axis_index("tensor"), lax.axis_index("context")
    near = lax.all_gather(value, "tensor")
    far = lax.all_gather(jnp.sum(near, 0).astype(value.dtype), "context")
    near_ids = jnp.arange(near.shape[0]).reshape((-1,) + (1,) * value.ndim)
    far_ids = jnp.arange(far.shape[0]).reshape((-1,) + (1,) * value.ndim)
    near_mask = near_ids > slot if backward else near_ids < slot
    far_mask = far_ids > mine if backward else far_ids < mine
    near, far = near.astype(jnp.float32), far.astype(jnp.float32)
    return jnp.sum(jnp.where(near_mask, near, 0.0), 0) + jnp.sum(jnp.where(far_mask, far, 0.0), 0)


def layer_norm(values, norm_gain, norm_bias):
    center = values - jnp.mean(values, -1, keepdims=True)
    spread = jnp.mean(center * center, -1, keepdims=True)
    return center * lax.rsqrt(spread + epsilon) * norm_gain + norm_bias


def features(logits):
    return jnp.concatenate([jax.nn.softmax(logits, -1), jax.nn.softmax(-logits, -1)], -1)


def gelu_tanh(values):
    return jax.nn.gelu(values, approximate=True)


def prefix_before(values):
    running = jnp.cumsum(values, 1)
    return jnp.concatenate([jnp.zeros_like(values[:, :1]), running[:, :-1]], 1)


def suffix_after(values):
    running = jnp.flip(jnp.cumsum(jnp.flip(values, 1), 1), 1)
    return jnp.concatenate([running[:, 1:], jnp.zeros_like(values[:, :1])], 1)


def spread(part, axis, parts):
    own = lax.axis_index("context")
    size = part.shape[axis] // parts
    mine = lax.dynamic_slice_in_dim(part, own * size, size, axis)
    return lax.all_gather(mine, EVERY)


def full_in(part):
    pieces = spread(part, 1, lax.axis_size("context"))
    fsdp, ctx, tens = (lax.axis_size(name) for name in EVERY)
    pieces = pieces.reshape((fsdp, ctx, tens) + pieces.shape[1:])
    pieces = pieces.transpose(3, 0, 1, 4, 2, 5)
    return pieces.reshape(pieces.shape[0], -1, pieces.shape[4] * pieces.shape[5])


def share_in(grad):
    fsdp, ctx, tens = (lax.axis_size(name) for name in EVERY)
    kinds, rows, cols = grad.shape
    pieces = grad.astype(jnp.bfloat16).reshape(kinds, fsdp, ctx, rows // fsdp // ctx, tens, cols // tens)
    pieces = pieces.transpose(1, 2, 4, 0, 3, 5).reshape((-1,) + (kinds, rows // fsdp // ctx, cols // tens))
    mine = lax.psum_scatter(pieces, EVERY, scatter_dimension=0)
    return lax.all_gather(mine, "context", axis=1, tiled=True).astype(jnp.float32)


def full_rows(part):
    pieces = spread(part, 0, lax.axis_size("context"))
    fsdp, ctx, tens = (lax.axis_size(name) for name in EVERY)
    pieces = pieces.reshape((fsdp, ctx, tens) + pieces.shape[1:])
    pieces = pieces.transpose(2, 1, 3, 0, 4)
    return pieces.reshape(tens * part.shape[0], -1)


def share_rows(grad):
    fsdp, ctx, tens = (lax.axis_size(name) for name in EVERY)
    rows, cols = grad.shape
    pieces = grad.astype(jnp.bfloat16).reshape(tens, ctx, rows // tens // ctx, fsdp, cols // fsdp)
    pieces = pieces.transpose(3, 1, 0, 2, 4).reshape(-1, rows // tens // ctx, cols // fsdp)
    mine = lax.psum_scatter(pieces, EVERY, scatter_dimension=0)
    return lax.all_gather(mine, "context", axis=0, tiled=True).astype(jnp.float32)


def full_maps(part):
    pieces = lax.all_gather(part, ("fsdp", "tensor"))
    fsdp, tens = lax.axis_size("fsdp"), lax.axis_size("tensor")
    pieces = pieces.reshape((fsdp, tens) + part.shape).transpose(1, 2, 0, 3, 4)
    return pieces.reshape(tens * part.shape[0], fsdp * part.shape[1], part.shape[2])


def own_maps(total):
    fsdp, tens = lax.axis_size("fsdp"), lax.axis_size("tensor")
    heads, rows, _ = total.shape
    mine = lax.dynamic_slice_in_dim(total, lax.axis_index("tensor") * (heads // tens), heads // tens, 0)
    return lax.dynamic_slice_in_dim(mine, lax.axis_index("fsdp") * (rows // fsdp), rows // fsdp, 1)


def per_device(
    inputs,
    cotangent,
    picture_starts,
    qkv_weight,
    out_weight,
    up_weight,
    down_weight,
    query_map,
    key_map,
    first_gain,
    first_bias,
    second_gain,
    second_bias,
):
    tensor_size = lax.axis_size("tensor")
    micro, seq_local, seq_len, model_width = inputs.shape
    span = seq_len // tensor_size
    slot = lax.axis_index("tensor")
    head_size = query_map.shape[2]
    feat_size = 2 * head_size
    blocks_local = span // BLK
    seq_count = micro * seq_local
    block_total = seq_count * blocks_local
    row_count = seq_count * span
    first_block = (lax.axis_index("context") * tensor_size + slot) * blocks_local
    block_ids = first_block + jnp.arange(blocks_local, dtype=jnp.int32)
    position = jnp.arange(BLK, dtype=jnp.int32)
    causal = position[None, :] <= position[:, None]

    in_full = full_in(qkv_weight)
    out_full = full_rows(out_weight)
    up_full = full_in(up_weight[None])[0]
    down_full = full_rows(down_weight)
    qmap_full, kmap_full = full_maps(query_map), full_maps(key_map)
    norms = lax.all_gather(jnp.stack([first_gain, first_bias, second_gain, second_bias]), "fsdp", axis=1, tiled=True)
    gain_first, bias_first, gain_second, bias_second = norms.astype(jnp.float32)

    def own(values):
        mine = lax.dynamic_slice_in_dim(values, slot * span, span, 2)
        return mine.reshape(row_count, model_width)

    source = own(inputs).astype(jnp.float32)
    starts_here = picture_starts.reshape(seq_count, -1)
    block_flags = (
        jnp.sum((starts_here[:, :, None] // BLK == block_ids[None, None, :]).astype(jnp.int32), 1)
        > 0
    )
    allowed = causal[None, None] | block_flags[:, :, None, None]
    allowed = allowed.reshape(block_total, 1, BLK, BLK)
    normed_one = layer_norm(source, gain_first, bias_first)
    normed_low = normed_one.astype(jnp.bfloat16)
    projected = jnp.einsum(
        "rd,cde->cre", normed_low, in_full, preferred_element_type=jnp.float32
    ).astype(jnp.bfloat16)
    heads_local = projected.shape[2] // head_size
    queries = projected[0].reshape(row_count, heads_local, head_size)
    key_rows = projected[1].reshape(row_count, heads_local, head_size)
    value_rows = projected[2].reshape(row_count, heads_local, head_size)
    query_logits = jnp.einsum(
        "rhi,hij->rhj", queries, qmap_full, preferred_element_type=jnp.float32
    )
    key_logits = jnp.einsum(
        "rhi,hij->rhj", key_rows, kmap_full, preferred_element_type=jnp.float32
    )
    query_blocks = (
        features(query_logits)
        .astype(jnp.bfloat16)
        .reshape(block_total, BLK, heads_local, feat_size)
    )
    key_blocks = (
        features(key_logits)
        .astype(jnp.bfloat16)
        .reshape(block_total, BLK, heads_local, feat_size)
    )
    value_blocks = value_rows.reshape(block_total, BLK, heads_local, head_size)
    scores = jnp.einsum(
        "nthf,nshf->nhts", query_blocks, key_blocks, preferred_element_type=jnp.float32
    )
    weights_low = jnp.where(allowed, scores, 0.0).astype(jnp.bfloat16)
    states = jnp.einsum(
        "nshf,nshe->nhfe", key_blocks, value_blocks, preferred_element_type=jnp.float32
    )
    states = states.reshape(seq_count, blocks_local, heads_local, feat_size, head_size)
    key_sums = jnp.sum(key_blocks.astype(jnp.float32), 1).reshape(
        seq_count, blocks_local, heads_local, feat_size
    )
    state_total = jnp.sum(states, 1)
    sums_total = jnp.sum(key_sums, 1)
    carried = carried_in(state_total.astype(jnp.bfloat16), False)
    carried_sums = carried_in(sums_total, False)
    prior_states = (carried[:, None] + prefix_before(states)).astype(jnp.bfloat16)
    prior_states = prior_states.reshape(block_total, heads_local, feat_size, head_size)
    prior_sums = (carried_sums[:, None] + prefix_before(key_sums)).reshape(
        block_total, heads_local, feat_size
    )
    numerator = jnp.einsum(
        "nhts,nshe->nthe", weights_low, value_blocks, preferred_element_type=jnp.float32
    )
    numerator = numerator + jnp.einsum(
        "nthf,nhfe->nthe", query_blocks, prior_states, preferred_element_type=jnp.float32
    )
    denominator = jnp.sum(weights_low.astype(jnp.float32), -1).transpose(0, 2, 1)
    denominator = denominator + jnp.einsum(
        "nthf,nhf->nth", query_blocks.astype(jnp.float32), prior_sums, precision=highest
    )
    mixed_heads = (
        (numerator / denominator[..., None])
        .astype(jnp.bfloat16)
        .reshape(row_count, heads_local * head_size)
    )
    attended = jnp.dot(mixed_heads, out_full, preferred_element_type=jnp.float32)
    middle = source + attended
    normed_two = layer_norm(middle, gain_second, bias_second)
    normed_two_low = normed_two.astype(jnp.bfloat16)
    hidden_pre = jnp.dot(normed_two_low, up_full, preferred_element_type=jnp.float32)
    hidden_low = gelu_tanh(hidden_pre).astype(jnp.bfloat16)
    branch = jnp.dot(hidden_low, down_full, preferred_element_type=jnp.float32)
    output = (middle + branch).astype(jnp.bfloat16).reshape(micro, seq_local, span, model_width)
    output = lax.all_gather(output, "tensor", axis=2, tiled=True)
    upstream_low = own(cotangent)
    upstream = upstream_low.astype(jnp.float32)
    grad_down = jnp.einsum(
        "rk,rd->kd", hidden_low, upstream_low, preferred_element_type=jnp.float32
    )
    hidden_grad = jnp.einsum(
        "rd,kd->rk", upstream_low, down_full, preferred_element_type=jnp.float32
    )
    gelu_result, gelu_pull = jax.vjp(gelu_tanh, hidden_pre)
    pre_grad = gelu_pull(hidden_grad)[0].astype(jnp.bfloat16)
    grad_up = jnp.einsum(
        "rd,rf->df", normed_two_low, pre_grad, preferred_element_type=jnp.float32
    )
    normed_two_grad = jnp.einsum(
        "rf,df->rd", pre_grad, up_full, preferred_element_type=jnp.float32
    )
    norm_result, second_pull = jax.vjp(layer_norm, middle, gain_second, bias_second)
    middle_part, grad_gain_second, grad_bias_second = second_pull(normed_two_grad)
    middle_grad = upstream + middle_part
    middle_low = middle_grad.astype(jnp.bfloat16)
    grad_out = jnp.einsum(
        "rk,rd->kd", mixed_heads, middle_low, preferred_element_type=jnp.float32
    )
    mixed_grad = jnp.einsum(
        "rd,kd->rk", middle_low, out_full, preferred_element_type=jnp.float32
    )
    mixed_grad = mixed_grad.reshape(block_total, BLK, heads_local, head_size)
    numer_grad = (mixed_grad / denominator[..., None]).astype(jnp.bfloat16)
    denom_grad = -jnp.sum(mixed_grad * numerator, -1) / (denominator * denominator)
    weight_grad = jnp.einsum(
        "nthe,nshe->nhts", numer_grad, value_blocks, preferred_element_type=jnp.float32
    )
    weight_grad = weight_grad + denom_grad.transpose(0, 2, 1)[..., None]
    weight_grad_low = jnp.where(allowed, weight_grad, 0.0).astype(jnp.bfloat16)
    value_grad = jnp.einsum(
        "nhts,nthe->nshe", weights_low, numer_grad, preferred_element_type=jnp.float32
    )
    query_grad = jnp.einsum(
        "nhts,nshf->nthf", weight_grad_low, key_blocks, preferred_element_type=jnp.float32
    )
    query_grad = query_grad + jnp.einsum(
        "nthe,nhfe->nthf", numer_grad, prior_states, preferred_element_type=jnp.float32
    )
    query_grad = query_grad + denom_grad[..., None] * prior_sums[:, None]
    key_grad = jnp.einsum(
        "nhts,nthf->nshf", weight_grad_low, query_blocks, preferred_element_type=jnp.float32
    )
    prior_grad = jnp.einsum(
        "nthf,nthe->nhfe", query_blocks, numer_grad, preferred_element_type=jnp.float32
    )
    prior_grad = prior_grad.reshape(seq_count, blocks_local, heads_local, feat_size, head_size)
    prior_sums_grad = jnp.einsum(
        "nthf,nth->nhf", query_blocks.astype(jnp.float32), denom_grad, precision=highest
    )
    prior_sums_grad = prior_sums_grad.reshape(seq_count, blocks_local, heads_local, feat_size)
    grad_total = jnp.sum(prior_grad, 1)
    grad_sums_total = jnp.sum(prior_sums_grad, 1)
    later_states = carried_in(grad_total.astype(jnp.bfloat16), True)
    later_sums = carried_in(grad_sums_total, True)
    state_grad = (later_states[:, None] + suffix_after(prior_grad)).astype(jnp.bfloat16)
    state_grad = state_grad.reshape(block_total, heads_local, feat_size, head_size)
    sums_grad = (later_sums[:, None] + suffix_after(prior_sums_grad)).reshape(
        block_total, heads_local, feat_size
    )
    key_grad = key_grad + jnp.einsum(
        "nshe,nhfe->nshf", value_blocks, state_grad, preferred_element_type=jnp.float32
    )
    key_grad = key_grad + sums_grad[:, None]
    value_grad = value_grad + jnp.einsum(
        "nshf,nhfe->nshe", key_blocks, state_grad, preferred_element_type=jnp.float32
    )
    query_feat_now, query_pull = jax.vjp(features, query_logits)
    query_logit_grad = query_pull(query_grad.reshape(row_count, heads_local, feat_size))[
        0
    ].astype(jnp.bfloat16)
    key_feat_now, key_pull = jax.vjp(features, key_logits)
    key_logit_grad = key_pull(key_grad.reshape(row_count, heads_local, feat_size))[0].astype(
        jnp.bfloat16
    )
    grad_qmap = jnp.einsum(
        "rhi,rhj->hij", queries, query_logit_grad, preferred_element_type=jnp.float32
    )
    grad_kmap = jnp.einsum(
        "rhi,rhj->hij", key_rows, key_logit_grad, preferred_element_type=jnp.float32
    )
    raw_query_grad = jnp.einsum(
        "rhj,hij->rhi", query_logit_grad, qmap_full, preferred_element_type=jnp.float32
    )
    raw_key_grad = jnp.einsum(
        "rhj,hij->rhi", key_logit_grad, kmap_full, preferred_element_type=jnp.float32
    )
    projected_grad = jnp.stack(
        [
            raw_query_grad.reshape(row_count, -1),
            raw_key_grad.reshape(row_count, -1),
            value_grad.reshape(row_count, -1),
        ]
    ).astype(jnp.bfloat16)
    grad_in = jnp.einsum(
        "rd,cre->cde", normed_low, projected_grad, preferred_element_type=jnp.float32
    )
    normed_one_grad = jnp.einsum(
        "cre,cde->rd", projected_grad, in_full, preferred_element_type=jnp.float32
    )
    first_result, first_pull = jax.vjp(layer_norm, source, gain_first, bias_first)
    source_part, grad_gain_first, grad_bias_first = first_pull(normed_one_grad)
    input_grad = (middle_grad + source_part).astype(jnp.bfloat16)
    input_grad = input_grad.reshape(micro, seq_local, span, model_width)
    input_grad = lax.all_gather(input_grad, "tensor", axis=2, tiled=True).astype(jnp.float32)
    norm_grads = jnp.stack([grad_gain_first, grad_bias_first, grad_gain_second, grad_bias_second])
    grad_qmap, grad_kmap, norm_grads = lax.psum((grad_qmap, grad_kmap, norm_grads), EVERY)
    share = first_gain.shape[0]
    norm_grads = lax.dynamic_slice_in_dim(norm_grads, lax.axis_index("fsdp") * share, share, 1)
    return (
        output,
        input_grad,
        share_in(grad_in),
        share_rows(grad_out),
        share_in(grad_up[None])[0],
        share_rows(grad_down),
        own_maps(grad_qmap),
        own_maps(grad_kmap),
        norm_grads[0],
        norm_grads[1],
        norm_grads[2],
        norm_grads[3],
    )


MESH = pl.DeviceIdType.MESH
bf16 = jnp.bfloat16
f32 = jnp.float32


def whereabouts():
    return tuple(lax.axis_index(name) for name in EVERY)


def neighbours(f, c, t):
    n = c * 4 + t
    peers = [(1 - f, c, t)]
    for k in range(1, 16):
        other = lax.rem(n + k, 16)
        peers.append((f, other // 4, lax.rem(other, 4)))
    for k in range(1, 4):
        peers.append((1 - f, c, lax.rem(t + k, 4)))
    return peers


def meet(f, c, t):
    barrier = pltpu.get_barrier_semaphore()
    peers = neighbours(f, c, t)
    for peer in peers:
        pl.semaphore_signal(barrier, inc=1, device_id=peer, device_id_type=MESH)
    pl.semaphore_wait(barrier, len(peers))


def send(src, dst, send_sem, recv_sem, peer):
    copy = pltpu.make_async_remote_copy(
        src_ref=src, dst_ref=dst, send_sem=send_sem, recv_sem=recv_sem,
        device_id=peer, device_id_type=MESH,
    )
    copy.start()
    return copy


def arrived(ref, sem):
    pltpu.make_async_copy(ref, ref, sem).wait()


def at(start, size, unit):
    return pl.ds(pl.multiple_of(start, unit), size)


def half(ref, m, f):
    if m == 0:
        w = ref.shape[2] // 2
        return ref.at[:, :, at(f * w, w, 128)]
    if m == 1:
        w = ref.shape[1] // 2
        return ref.at[:, at(f * w, w, 128)]
    w = ref.shape[0] // 2
    return ref.at[at(f * w, w, 16), :]


def shard(ref, m, f, t):
    if m == 0:
        w, h = ref.shape[2] // 2, ref.shape[1] // 4
        return ref.at[:, at(t * h, h, 16), at(f * w, w, 128)]
    if m == 1:
        w, h = ref.shape[1] // 2, ref.shape[0] // 4
        return ref.at[at(t * h, h, 16), at(f * w, w, 128)]
    h, w = ref.shape[0] // 2, ref.shape[1] // 4
    return ref.at[at(f * h, h, 16), at(t * w, w, 128)]


def piece(ref, m, f, c, t):
    if m == 0:
        w, h = ref.shape[2] // 2, ref.shape[1] // 16
        return ref.at[:, at(t * 4 * h + c * h, h, 16), at(f * w, w, 128)]
    if m == 1:
        w, h = ref.shape[1] // 2, ref.shape[0] // 16
        return ref.at[at(t * 4 * h + c * h, h, 16), at(f * w, w, 128)]
    h, w = ref.shape[0] // 8, ref.shape[1] // 4
    return ref.at[at(f * 4 * h + c * h, h, 16), at(t * w, w, 128)]


def quarter(ref, m, c):
    if m == 0:
        h = ref.shape[1] // 4
        return ref.at[:, at(c * h, h, 16), :]
    h = ref.shape[0] // 4
    return ref.at[at(c * h, h, 16), :]


def context_part(ref, m, c):
    if m == 0:
        h = ref.shape[2] // 4
        return ref.at[:, :, at(c * h, h, 16), :]
    if m == 1:
        h = ref.shape[1] // 4
        return ref.at[:, at(c * h, h, 16), :]
    h = ref.shape[0] // 4
    return ref.at[at(c * h, h, 16), :]


def two_of(ref, m, side):
    if m == 0:
        return ref.at[:, pl.ds(2 * side, 2)]
    if m == 1:
        return ref.at[pl.ds(2 * side, 2)]
    w = ref.shape[1] // 2
    return ref.at[:, pl.ds(side * w, w)]


def tensor_part(ref, m, t):
    if m == 0:
        return ref.at[:, t]
    if m == 1:
        return ref.at[t]
    w = ref.shape[1] // 4
    return ref.at[:, at(t * w, w, 128)]


NN = (((1,), (0,)), ((), ()))
NT = (((1,), (1,)), ((), ()))
TN = (((0,), (0,)), ((), ()))


def mm(a, b, dims=NN):
    return lax.dot_general(a, b, dims, preferred_element_type=f32)


def lanes_of(shape):
    return lax.broadcasted_iota(jnp.int32, shape, len(shape) - 1)


def block_ones(size, group):
    row = lax.broadcasted_iota(jnp.int32, (size, size), 0) // group
    col = lax.broadcasted_iota(jnp.int32, (size, size), 1) // group
    return jnp.where(row == col, 1.0, 0.0).astype(bf16)


def statistics(rows):
    center = rows - jnp.mean(rows, -1, keepdims=True)
    rstd = lax.rsqrt(jnp.mean(center * center, -1, keepdims=True) + epsilon)
    return center * rstd, rstd


def norm_back(grad, e, rstd, gain):
    w = grad * gain
    return rstd * (w - jnp.mean(w, -1, keepdims=True) - e * jnp.mean(w * e, -1, keepdims=True))


def near_far(first, low, high):
    return jnp.where(first, low, high)


def own_half(values, first, odd):
    zero = jnp.zeros_like(values)
    return jnp.where(first, zero, values) if odd else jnp.where(first, values, zero)


def pair_block(values, first):
    return jnp.concatenate([own_half(values, first, 0), own_half(values, first, 1)], 0)


def split_half(full, first, odd):
    other = pltpu.roll(full, 64, 1)
    return jnp.where(first, other, full) if odd else jnp.where(first, full, other)


def layer_kernel(*refs):
    inputs, cotangent, flags, maps, norms = refs[:5]
    shards = refs[5:9]
    all_out, all_in = refs[9:11]
    outs, maps_out, norms_out = refs[11:15], refs[15:17], refs[17]
    w, mx, nrm, x, g, n1, qkv, feat = refs[18:22], *refs[22:29]
    prior, sums_in, states, z_buf, s_in, z_in, s_out, z_out = refs[29:37]
    o, rden, num, mid, n2, a, gp, rows_out = refs[37:45]
    gm, dnum, dden, dproj, rows_in, turned = refs[45:51]
    pair_in, xy_in, part, tz_in, last = (refs[51 + 4 * i : 55 + 4 * i] for i in range(5))
    small, small_pair, small_own, small_in, small_sum, small_all = refs[71:77]
    vec, vec_pair, vec_own, vec_in, vec_sum, vec_all = refs[77:83]
    local_sem, send_sem, extra_sem, z_sem, xy_sem, pair_sem = refs[83:89]
    scan_sem, rows_sem, gpair_sem, gxy_sem, gz_sem, last_sem, small_sem = refs[89:96]
    wq, wo, wu, wd = w
    d = x.shape[1]
    ff = a.shape[1]
    half_rows = x.shape[0] // 2
    f, c, t = whereabouts()
    n = c * 4 + t
    peers = neighbours(f, c, t)
    partner = peers[0]
    started = []

    def put(src, dst, recv_sem, peer):
        started.append(send(src, dst, send_sem, recv_sem, peer))

    fetched = []

    def fetch(src, dst, sem):
        copy = pltpu.make_async_copy(src, dst, sem)
        copy.start()
        return copy

    for i in range(2):
        rows = pl.ds(i * half_rows, half_rows)
        fetched.append(fetch(inputs.at[i, 0, at(t * half_rows, half_rows, 16), :], x.at[rows], local_sem.at[i]))
        fetched.append(fetch(cotangent.at[i, 0, at(t * half_rows, half_rows, 16), :], g.at[rows], local_sem.at[2 + i]))
    h3 = maps.shape[1]
    head_rows = small.shape[1]
    pairs_of = (0, 1, 3, 4)
    lo_norm = d // 2

    def map_place(ff_, tt):
        return mx.at[:, pl.ds(tt * h3, h3), at(ff_ * 32, 32, 16), :]

    def norm_place(ff_):
        return nrm.at[:, at(ff_ * lo_norm, lo_norm, 128)]

    fetched.append(fetch(maps, map_place(f, t), local_sem.at[4]))
    fetched.append(fetch(norms, norm_place(f), local_sem.at[5]))
    shard_copies = [fetch(shards[m], shard(w[m], m, f, t), local_sem.at[6 + m]) for m in range(4)]
    z_buf[...] = jnp.zeros_like(z_buf)
    small[...] = jnp.zeros_like(small)
    vec[...] = jnp.zeros_like(vec)
    meet(f, c, t)

    order = (0, 1, 2, 3)
    put(norms, norm_place(f), extra_sem.at[0], partner)
    put(maps, map_place(f, t), extra_sem.at[4], partner)
    for m in order:
        for k in range(1, 4):
            put(quarter(shards[m], m, c), piece(w[m], m, f, c, t), z_sem.at[m, k], (f, c, lax.rem(t + k, 4)))
        if m == 0:
            for k in range(1, 4):
                put(maps, map_place(f, t), extra_sem.at[k], (f, c, lax.rem(t + k, 4)))
    for m in order:
        put(shards[m], shard(w[m], m, f, t), pair_sem.at[m], partner)

    def forward(m, k):
        got = piece(w[m], m, f, c, lax.rem(t + 4 - k, 4))
        arrived(got, z_sem.at[m, k])
        for j in range(1, 3):
            put(got, got, xy_sem.at[m, k, j], (f, c ^ j, t))
        put(got, got, pair_sem.at[m], partner)

    def relay(m, k):
        for j in range(1, 3):
            got = piece(w[m], m, f, c ^ j, lax.rem(t + 4 - k, 4))
            arrived(got, xy_sem.at[m, k, j])
            if (m + k + j) % 2:
                put(got, got, xy_sem.at[m, k, 3], (f, c ^ 3 ^ j, t))
            put(got, got, pair_sem.at[m], partner)

    def across(m):
        for k in range(1, 4):
            got = piece(w[m], m, f, c ^ 3, lax.rem(t + 4 - k, 4))
            arrived(got, xy_sem.at[m, k, 3])
            put(got, got, pair_sem.at[m], partner)

    def take_maps():
        for k in range(1, 4):
            got = map_place(f, lax.rem(t + 4 - k, 4))
            arrived(got, extra_sem.at[k])
            put(got, got, extra_sem.at[4 + k], partner)

    def maps_here():
        for k in range(4):
            arrived(map_place(1 - f, lax.rem(t + 4 - k, 4)), extra_sem.at[4 + k])

    def complete(m):
        shard_copies[m].wait()
        arrived(half(w[m], m, 1 - f), pair_sem.at[m])

    for k in range(1, 4):
        forward(0, k)
    for copy in fetched:
        copy.wait()
    arrived(norm_place(1 - f), extra_sem.at[0])
    first = lanes_of((1, 128)) < 64
    ones64 = block_ones(128, 64)
    step = half_rows // 2

    @pl.loop(0, 4)
    def _(i):
        rows = at(i * step, step, 16)
        e, _unused = statistics(x[rows, :].astype(f32))
        n1[rows, :] = (e * nrm[0:1, :] + nrm[1:2, :]).astype(bf16)

    take_maps()
    for k in range(1, 4):
        relay(0, k)
        forward(1, k)
    across(0)
    forward(2, 1)
    complete(0)

    chunks = d // 256

    @pl.loop(0, 3 * chunks)
    def _(i):
        kind, j = i // chunks, lax.rem(i, chunks)
        cols = at(j * 256, 256, 128)
        qkv[kind, :, cols] = mm(n1[...], wq[kind, cols, :], NT).astype(bf16)

    for k in range(1, 4):
        relay(1, k)
    forward(2, 2)
    maps_here()

    pairs = d // 128

    def pair_map(side, p):
        zero = jnp.zeros((64, 128), bf16)
        top = jnp.concatenate([mx[side, 2 * p], zero], 1)
        bottom = jnp.concatenate([zero, mx[side, 2 * p + 1]], 1)
        return jnp.concatenate([top, bottom], 0)

    def features_of(side, i):
        b, p = i // pairs, lax.rem(i, pairs)
        rows = at(b * half_rows, half_rows, 16)
        logits = mm(qkv[side, rows, at(p * 128, 128, 128)], pair_map(side, p))
        for odd in range(2):
            part_ = logits[:, odd * 128 : odd * 128 + 128]
            low_top = jnp.max(jnp.where(first, part_, -jnp.inf), -1, keepdims=True)
            high_top = jnp.max(jnp.where(first, -jnp.inf, part_), -1, keepdims=True)
            e = jnp.exp(part_ - jnp.where(first, low_top, high_top))
            total = mm(e.astype(bf16), ones64)
            feat[side, rows, at(p * 256 + odd * 128, 128, 128)] = (e / total).astype(bf16)

    @pl.loop(0, 2 * pairs)
    def _(i):
        features_of(1, i)

    forward(2, 3)
    across(1)
    relay(2, 1)

    @pl.loop(0, 2 * pairs)
    def _(i):
        b, p = i // pairs, lax.rem(i, pairs)
        rows = at(b * half_rows, half_rows, 16)
        keys = feat[1, rows, at(p * 256, 256, 128)]
        both = mm(keys, qkv[2, rows, at(p * 128, 128, 128)], TN)
        states[b, at(p * 128, 128, 16), :] = near_far(first, both[:128], both[128:]).astype(bf16)
        tall = mm(jnp.ones((8, half_rows), bf16), keys)
        slot = lax.broadcasted_iota(jnp.int32, (8, 128), 0) == b
        z_buf[2 * p] = jnp.where(slot, tall[:, :128], z_buf[2 * p])
        z_buf[2 * p + 1] = jnp.where(slot, tall[:, 128:], z_buf[2 * p + 1])

    srows = states.shape[1] // 16

    def scan_out(sem0):
        for k in range(1, 16):
            other = lax.rem(n + k, 16)
            put(states.at[:, at(other * srows, srows, 16), :], s_in.at[n], scan_sem.at[sem0], peers[k])
            put(z_buf.at[other], z_in.at[n], scan_sem.at[sem0 + 1], peers[k])
        one = fetch(states.at[:, at(n * srows, srows, 16), :], s_in.at[n], local_sem.at[0])
        two = fetch(z_buf.at[n], z_in.at[n], local_sem.at[1])
        one.wait()
        two.wait()

    def scan_back(sem0, backward):
        arrived(s_in.at[pl.ds(0, 15)], scan_sem.at[sem0])
        arrived(z_in.at[pl.ds(0, 15)], scan_sem.at[sem0 + 1])
        total = jnp.zeros(s_in.shape[1:], f32)
        sums = jnp.zeros(z_in.shape[1:], f32)
        for i in range(15, -1, -1) if backward else range(16):
            s_out[i] = total.astype(bf16)
            z_out[i] = sums
            total = total + s_in[i].astype(f32)
            sums = sums + z_in[i]
        for k in range(1, 16):
            other = lax.rem(n + k, 16)
            put(s_out.at[other], prior.at[int(backward), :, at(n * srows, srows, 16), :], scan_sem.at[sem0 + 2], peers[k])
            put(z_out.at[other], sums_in.at[int(backward), n], scan_sem.at[sem0 + 3], peers[k])
        one = fetch(s_out.at[n], prior.at[int(backward), :, at(n * srows, srows, 16), :], local_sem.at[0])
        two = fetch(z_out.at[n], sums_in.at[int(backward), n], local_sem.at[1])
        one.wait()
        two.wait()

    def scan_end(sem0):
        arrived(s_in.at[pl.ds(0, 15)], scan_sem.at[sem0 + 2])
        arrived(z_in.at[pl.ds(0, 15)], scan_sem.at[sem0 + 3])

    scan_out(0)
    relay(2, 2)
    for k in range(1, 4):
        forward(3, k)

    @pl.loop(0, 2 * pairs)
    def _(i):
        features_of(0, i)

    relay(2, 3)

    def mask_of(b, turn):
        row = lax.broadcasted_iota(jnp.int32, (half_rows, half_rows), 0)
        col = lax.broadcasted_iota(jnp.int32, (half_rows, half_rows), 1)
        causal = row <= col if turn else col <= row
        return jnp.where(causal, 1.0, flags[b, 0:1, :])

    @pl.loop(0, 2 * pairs)
    def _(i):
        b, p = i // pairs, lax.rem(i, pairs)
        rows = at(b * half_rows, half_rows, 16)
        values = qkv[2, rows, at(p * 128, 128, 128)]
        mask = mask_of(b, False)
        both = None
        for odd in range(2):
            cols = at(p * 256 + odd * 128, 128, 128)
            scores = (mm(feat[0, rows, cols], feat[1, rows, cols], NT) * mask).astype(bf16)
            right = jnp.concatenate(
                [own_half(values, first, odd), own_half(jnp.ones_like(values), first, odd)], 1
            )
            term = mm(scores, right)
            both = term if both is None else both + term
        num[rows, at(p * 128, 128, 128)] = both[:, :128]
        rden[rows, at(p * 128, 128, 128)] = both[:, 128:]

    scan_back(0, False)
    for k in range(1, 4):
        relay(3, k)
    complete(1)
    scan_end(0)

    def sums_pair(direction, b, p, odd):
        tile = sums_in[direction, 2 * p + odd]
        slot = lax.broadcasted_iota(jnp.int32, (8, 128), 0) == b
        return jnp.sum(jnp.where(slot, tile, 0.0), 0, keepdims=True)

    @pl.loop(0, 2 * pairs)
    def _(i):
        b, p = i // pairs, lax.rem(i, pairs)
        rows = at(b * half_rows, half_rows, 16)
        cols = at(p * 128, 128, 128)
        queries = feat[0, rows, at(p * 256, 256, 128)]
        before = pair_block(prior[0, b, at(p * 128, 128, 16), :], first)
        zero = jnp.zeros((64, 128), bf16)
        z_low = jnp.broadcast_to(sums_pair(0, b, p, 0), (64, 128)).astype(bf16)
        z_high = jnp.broadcast_to(sums_pair(0, b, p, 1), (64, 128)).astype(bf16)
        z_rows = jnp.concatenate(
            [jnp.concatenate([z_low, zero], 1), jnp.concatenate([zero, z_high], 1)], 0
        )
        inverse = 1.0 / (rden[rows, cols] + mm(queries, z_rows, NT))
        o[rows, cols] = ((num[rows, cols] + mm(queries, before)) * inverse).astype(bf16)
        rden[rows, cols] = inverse

    @pl.loop(0, 2)
    def _(i):
        rows = at(i * half_rows, half_rows, 16)
        mid[rows, :] = x[rows, :].astype(f32) + mm(o[rows, :], wo[...])

    across(2)

    @pl.loop(0, 4)
    def _(i):
        rows = at(i * step, step, 16)
        e, _unused = statistics(mid[rows, :])
        n2[rows, :] = (e * nrm[2:3, :] + nrm[3:4, :]).astype(bf16)

    complete(2)

    @pl.loop(0, ff // 256)
    def _(i):
        cols = at(i * 256, 256, 128)
        u = mm(n2[...], wu[:, cols])
        scale = 0.7978845608028654
        square = u * u
        tanh = jnp.tanh(scale * u * (1.0 + 0.044715 * square))
        cdf = 0.5 + 0.5 * tanh
        a[:, cols] = (u * cdf).astype(bf16)
        slope = cdf + (0.5 * scale) * u * (1.0 - tanh * tanh) * (1.0 + 0.134145 * square)
        gp[:, cols] = slope.astype(bf16)

    across(3)
    complete(3)

    @pl.loop(0, chunks)
    def _(i):
        cols = at(i * 256, 256, 128)
        rows_out[:, cols] = (mid[:, cols] + mm(a[...], wd[cols, :], NT)).astype(bf16)

    links = []

    def pass_on(i, b, way, hop, block):
        dst = (all_out, all_in)[i]
        src = (rows_out, rows_in)[i]
        origin = src.at[pl.ds(b * half_rows, half_rows)] if hop == 0 else dst.at[b, block]
        return pltpu.make_async_remote_copy(
            src_ref=origin, dst_ref=dst.at[b, block], send_sem=rows_sem.at[i, way, hop, b, 0],
            recv_sem=rows_sem.at[i, way, hop, b, 1], device_id=(f, c, t + 1 if way == 0 else t - 1),
            device_id_type=MESH,
        )

    def rows_hop(i, b, hop):
        dst = (all_out, all_in)[i]
        for way in range(2):
            block = t - hop if way == 0 else t + hop
            here = block >= 0 if way == 0 else block <= 3
            more = t < 3 if way == 0 else t > 0
            if hop > 0:
                @pl.when(here)
                def _():
                    arrived(dst.at[b, 0], rows_sem.at[i, way, hop - 1, b, 1])
            if hop < 3:
                @pl.when(jnp.logical_and(here, more))
                def _():
                    pass_on(i, b, way, hop, block).start()

    def rows_sent(i):
        for b in range(2):
            for hop in range(3):
                for way in range(2):
                    block = t - hop if way == 0 else t + hop
                    here = block >= 0 if way == 0 else block <= 3
                    more = t < 3 if way == 0 else t > 0

                    @pl.when(jnp.logical_and(here, more))
                    def _():
                        pass_on(i, b, way, hop, block).wait_send()

    own_rows = []
    for b in range(2):
        own_rows.append(fetch(rows_out.at[pl.ds(b * half_rows, half_rows)], all_out.at[b, t], local_sem.at[2 + b]))
        rows_hop(0, b, 0)

    def grad_pair(m):
        if m < 2:
            h = d // 4
            for tt in range(4):
                if m == 0:
                    src = w[m].at[:, pl.ds(tt * h, h), at((1 - f) * (d // 2), d // 2, 128)]
                    put(src, pair_in[m].at[:, tt], gpair_sem.at[m], partner)
                else:
                    src = w[m].at[pl.ds(tt * h, h), at((1 - f) * (d // 2), d // 2, 128)]
                    put(src, pair_in[m].at[tt], gpair_sem.at[m], partner)
        else:
            put(half(w[m], m, 1 - f), pair_in[m], gpair_sem.at[m], partner)

    def grad_xy(m):
        arrived(pair_in[m], gpair_sem.at[m])
        h = d // 4
        cols = at(f * (d // 2), d // 2, 128)
        if m == 0:
            @pl.loop(0, 12)
            def _(i):
                kind, tt = i // 4, lax.rem(i, 4)
                mine = wq[kind, at(tt * h, h, 16), cols].astype(f32)
                pair_in[0][kind, tt] = (mine + pair_in[0][kind, tt].astype(f32)).astype(bf16)
        elif m == 1:
            @pl.loop(0, 4)
            def _(tt):
                mine = wo[at(tt * h, h, 16), cols].astype(f32)
                pair_in[1][tt] = (mine + pair_in[1][tt].astype(f32)).astype(bf16)
        else:
            @pl.loop(0, 12)
            def _(i):
                rows = at(i * 32, 32, 16)
                mine = w[m][at(f * (d // 2) + i * 32, 32, 16), :].astype(f32)
                pair_in[m][rows, :] = (mine + pair_in[m][rows, :].astype(f32)).astype(bf16)
        for side in range(2):
            way = 1 + side
            for i, owner in ((1, 3), (0, way)):
                put(
                    two_of(context_part(pair_in[m], m, c ^ owner), m, side), two_of(xy_in[m].at[i], m, side),
                    gxy_sem.at[m, side, i], (f, c ^ way, t),
                )

    def grad_mid(m):
        for side in range(2):
            way = 1 + side
            rest = two_of(xy_in[m].at[1], m, side)
            mine = two_of(context_part(pair_in[m], m, c ^ 3 ^ way), m, side)
            arrived(rest, gxy_sem.at[m, side, 1])
            if m == 0:
                @pl.loop(0, 6)
                def _(i):
                    kind, tt = i // 2, lax.rem(i, 2)
                    rest[kind, tt] = (mine[kind, tt].astype(f32) + rest[kind, tt].astype(f32)).astype(bf16)
            elif m == 1:
                rest[...] = (mine[...].astype(f32) + rest[...].astype(f32)).astype(bf16)
            else:
                @pl.loop(0, d // 8 // 16)
                def _(i):
                    rows = at(i * 16, 16, 16)
                    rest[rows, :] = (mine[rows, :].astype(f32) + rest[rows, :].astype(f32)).astype(bf16)
            put(rest, two_of(xy_in[m].at[2], m, side), gxy_sem.at[m, side, 2], (f, c ^ 3 ^ way, t))

    def grad_z(m):
        for side in range(2):
            for i in (0, 2):
                arrived(two_of(xy_in[m].at[i], m, side), gxy_sem.at[m, side, i])
        if m == 0:
            h = d // 16

            @pl.loop(0, 12)
            def _(i):
                kind, tt = i // 4, lax.rem(i, 4)
                total = pair_in[0][kind, tt, at(c * h, h, 16), :].astype(f32)
                for j in (0, 2):
                    total = total + xy_in[0][j, kind, tt].astype(f32)
                part[0][kind, tt] = total.astype(bf16)
        elif m == 1:
            h = d // 16

            @pl.loop(0, 4)
            def _(tt):
                total = pair_in[1][tt, at(c * h, h, 16), :].astype(f32)
                for j in (0, 2):
                    total = total + xy_in[1][j, tt].astype(f32)
                part[1][tt] = total.astype(bf16)
        else:
            @pl.loop(0, d // 8 // 16)
            def _(i):
                rows = at(i * 16, 16, 16)
                total = pair_in[m][at(c * (d // 8) + i * 16, 16, 16), :].astype(f32)
                for j in (0, 2):
                    total = total + xy_in[m][j, rows, :].astype(f32)
                part[m][rows, :] = total.astype(bf16)
        for way, first_ in ((0, 0), (1, 3)):
            @pl.when(t == first_)
            def _():
                for owner in (3, 2, 1) if way == 0 else (0, 1, 2):
                    step_on(m, way, owner, True).start()

    def came(m, way, owner):
        return tz_in[m].at[owner - 1 if way == 0 else 3 + owner], gz_sem.at[m, owner - 1 if way == 0 else 3 + owner]

    def step_on(m, way, owner, from_end=False):
        dst, sem = came(m, way, owner)
        return pltpu.make_async_remote_copy(
            src_ref=tensor_part(part[m], m, owner) if from_end else dst, dst_ref=dst, send_sem=send_sem,
            recv_sem=sem, device_id=(f, c, t + 1 if way == 0 else t - 1), device_id_type=MESH,
        )

    def add_up(m, dst, own_part, others):
        if m == 0:
            for kind in range(3):
                total = own_part[kind].astype(f32)
                for other in others:
                    total = total + other[kind].astype(f32)
                dst[kind] = total.astype(bf16)
        elif m == 1:
            total = own_part[...].astype(f32)
            for other in others:
                total = total + other[...].astype(f32)
            dst[...] = total.astype(bf16)
        else:
            @pl.loop(0, d // 8 // 16)
            def _(i):
                rows = at(i * 16, 16, 16)
                total = own_part[rows, :].astype(f32)
                for other in others:
                    total = total + other[rows, :].astype(f32)
                dst[rows, :] = total.astype(bf16)

    def grad_chain(m, hop):
        for way, here in ((0, hop), (1, 3 - hop)):
            @pl.when(t == here)
            def _():
                for owner in range(3, here, -1) if way == 0 else range(here):
                    buf, sem = came(m, way, owner)
                    arrived(buf, sem)
                    add_up(m, buf, tensor_part(part[m], m, owner), [buf])
                    step_on(m, way, owner).start()

    def chains_sent():
        for m in range(4):
            for way in range(2):
                for owner in (1, 2, 3) if way == 0 else (0, 1, 2):
                    @pl.when(t < owner if way == 0 else t > owner)
                    def _():
                        step_on(m, way, owner).wait_send()

    def grad_last(m):
        for tt in range(4):
            @pl.when(t == tt)
            def _():
                others = []
                for way in range(2):
                    if (tt > 0, tt < 3)[way]:
                        buf, sem = came(m, way, tt)
                        arrived(buf, sem)
                        others.append(buf)
                add_up(m, last[m], tensor_part(part[m], m, tt), others)

        for j in range(1, 4):
            put(last[m], quarter(outs[m], m, c), last_sem.at[m, j], (f, c ^ j, t))
        fetch(last[m], quarter(outs[m], m, c), local_sem.at[10 + m]).wait()

    for copy in started:
        copy.wait_send()
    started.clear()

    @pl.loop(0, ff // 256)
    def _(i):
        cols = at(i * 256, 256, 128)
        gp[:, cols] = (mm(g[...], wd[:, cols]) * gp[:, cols].astype(f32)).astype(bf16)

    def turn(src):
        @pl.loop(0, chunks)
        def _(i):
            cols = at(i * 256, 256, 128)
            turned[at(i * 256, 256, 16), :] = src[:, cols].astype(f32).T.astype(bf16)

    turn(g)

    @pl.loop(0, ff // 256)
    def _(i):
        cols = at(i * 256, 256, 128)
        wd[:, cols] = mm(turned[...], a[:, cols]).astype(bf16)

    grad_pair(3)
    rows_hop(0, 0, 1)

    @pl.loop(0, chunks)
    def _(i):
        cols = at(i * 256, 256, 128)
        num[:, cols] = mm(gp[...], wu[cols, :], NT)

    @pl.loop(0, 4)
    def _(i):
        rows = at(i * step, step, 16)
        e, rstd = statistics(mid[rows, :])
        grad = num[rows, :]
        vec[2:3, :] += jnp.sum(grad * e, 0, keepdims=True)
        vec[3:4, :] += jnp.sum(grad, 0, keepdims=True)
        total = g[rows, :].astype(f32) + norm_back(grad, e, rstd, nrm[2:3, :])
        mid[rows, :] = total
        gm[rows, :] = total.astype(bf16)

    grad_xy(3)

    @pl.loop(0, chunks)
    def _(i):
        cols = at(i * 256, 256, 128)
        back = mm(gm[...], wo[cols, :], NT)
        for side in range(2):
            cut = at(i * 256 + side * 128, 128, 128)
            grad = back[:, side * 128 : side * 128 + 128]
            inverse = rden[:, cut]
            dnum[:, cut] = (grad * inverse).astype(bf16)
            dden[:, cut] = -mm((grad * o[:, cut].astype(f32)).astype(bf16), ones64) * inverse

    @pl.loop(0, 2 * pairs)
    def _(i):
        b, p = i // pairs, lax.rem(i, pairs)
        rows = at(b * half_rows, half_rows, 16)
        cols = at(p * 128, 128, 128)
        queries = feat[0, rows, at(p * 256, 256, 128)]
        both = mm(queries, dnum[rows, cols], TN)
        states[b, at(p * 128, 128, 16), :] = near_far(first, both[:128], both[128:]).astype(bf16)
        slot = lax.broadcasted_iota(jnp.int32, (8, 128), 0) == b
        packed = dden[rows, cols]
        for odd in range(2):
            full = split_half(packed, first, odd)
            tall = jnp.sum(queries[:, odd * 128 : odd * 128 + 128].astype(f32) * full, 0, keepdims=True)
            z_buf[2 * p + odd] = jnp.where(slot, tall, z_buf[2 * p + odd])

    scan_out(4)

    turn(n2)

    @pl.loop(0, ff // 256)
    def _(i):
        cols = at(i * 256, 256, 128)
        wu[:, cols] = mm(turned[...], gp[:, cols]).astype(bf16)

    grad_pair(2)

    scan_back(4, True)
    rows_hop(0, 1, 1)

    @pl.loop(0, chunks)
    def _(i):
        cols = at(i * 256, 256, 128)
        wo[cols, :] = mm(o[:, cols].astype(f32).T.astype(bf16), gm[...]).astype(bf16)

    grad_pair(1)
    grad_mid(3)

    lane = lanes_of((1, 128))

    def extended(values, one, two, odd):
        base = 0 if odd else 64
        rest = jnp.where(lane == base, one, jnp.where(lane == base + 1, two, jnp.zeros_like(values)))
        return jnp.where(first, rest, values) if odd else jnp.where(first, values, rest)

    def block_maps(side, p):
        low_ = jnp.where(first, mx[side, 2 * p], jnp.zeros((64, 128), bf16))
        high_ = jnp.where(first, jnp.zeros((64, 128), bf16), -mx[side, 2 * p + 1])
        return jnp.concatenate([low_, high_], 0)

    def through_features(side, b, p, rows, cols, grads):
        logits = []
        for odd in range(2):
            prob = feat[side, rows, at(p * 256 + odd * 128, 128, 128)].astype(f32)
            grad = grads[odd]
            inner = mm((prob * grad).astype(bf16), ones64)
            both = prob * (grad - inner)
            other = pltpu.roll(both, 64, 1)
            logits.append(other - both if odd else both - other)
        packed = jnp.where(first, logits[0], logits[1]).astype(bf16)
        dproj[side, rows, cols] = mm(packed, block_maps(side, p), NT).astype(bf16)
        square = mm(qkv[side, rows, cols], packed, TN)
        small[side * pairs + p] += near_far(first, square[:64], square[64:])

    def exact(packed, odd):
        full = split_half(packed, first, odd)
        head = full.astype(bf16)
        return full, head, (full - head.astype(f32)).astype(bf16)

    @pl.loop(0, 2 * pairs)
    def _(i):
        b, p = i // pairs, lax.rem(i, pairs)
        rows = at(b * half_rows, half_rows, 16)
        cols = at(p * 128, 128, 128)
        values, grad_rows = qkv[2, rows, cols], dnum[rows, cols]
        packed = dden[rows, cols]
        before = prior[0, b, at(p * 128, 128, 16), :]
        mask = mask_of(b, False)
        unit = jnp.ones_like(values)
        grads = []
        for odd in range(2):
            full, head, tail = exact(packed, odd)
            left = extended(grad_rows, head, tail, odd)
            right = extended(values, unit, unit, odd)
            scores = (mm(left, right, NT) * mask).astype(bf16)
            total = mm(scores, feat[1, rows, at(p * 256 + odd * 128, 128, 128)])
            total = total + mm(own_half(grad_rows, first, odd), before, NT)
            grads.append(total + full * sums_pair(0, b, p, odd))
        through_features(0, b, p, rows, cols, grads)

    grad_xy(2)
    scan_end(4)
    rows_hop(0, 0, 2)
    grad_z(3)

    def key_side(b, p):
        rows = pl.ds(b * half_rows, half_rows)
        cols = at(p * 128, 128, 128)
        values, grad_rows = qkv[2, rows, cols], dnum[rows, cols]
        packed = dden[rows, cols]
        after = prior[1, b, at(p * 128, 128, 16), :]
        mask = mask_of(b, True)
        unit = jnp.ones_like(values)
        value_grad = mm(feat[1, rows, at(p * 256, 256, 128)], pair_block(after, first))
        grads = []
        for odd in range(2):
            fcols = at(p * 256 + odd * 128, 128, 128)
            queries, keys = feat[0, rows, fcols], feat[1, rows, fcols]
            _full, head, tail = exact(packed, odd)
            left = extended(values, unit, unit, odd)
            right = extended(grad_rows, head, tail, odd)
            scores = (mm(left, right, NT) * mask).astype(bf16)
            total = mm(scores, queries) + mm(own_half(values, first, odd), after, NT)
            grads.append(total + sums_pair(1, b, p, odd))
            weights = (mm(keys, queries, NT) * mask).astype(bf16)
            value_grad = value_grad + mm(weights, own_half(grad_rows, first, odd))
        dproj[2, rows, cols] = value_grad.astype(bf16)
        through_features(1, b, p, rows, cols, grads)

    for b in range(2):
        @pl.loop(0, pairs)
        def _(p):
            key_side(b, p)

        if b == 0:
            grad_xy(1)
            rows_hop(0, 1, 2)
            grad_mid(2)
            grad_chain(3, 1)
        else:
            grad_mid(1)
            grad_z(2)
            grad_chain(3, 2)

        @pl.loop(0, chunks)
        def _(i):
            cols = at(i * 256, 256, 128)
            rows = pl.ds(b * half_rows, half_rows)
            total = mm(dproj[0, rows, :], wq[0, :, cols])
            for kind in range(1, 3):
                total = total + mm(dproj[kind, rows, :], wq[kind, :, cols])
            num[rows, cols] = total

        @pl.loop(2 * b, 2 * b + 2)
        def _(i):
            rows = at(i * step, step, 16)
            e, rstd = statistics(x[rows, :].astype(f32))
            grad = num[rows, :]
            vec[0:1, :] += jnp.sum(grad * e, 0, keepdims=True)
            vec[1:2, :] += jnp.sum(grad, 0, keepdims=True)
            rows_in[rows, :] = (mid[rows, :] + norm_back(grad, e, rstd, nrm[0:1, :])).astype(bf16)

        own_rows.append(fetch(rows_in.at[pl.ds(b * half_rows, half_rows)], all_in.at[b, t], local_sem.at[4 + b]))
        rows_hop(1, b, 0)

    lo_map = head_rows // 2
    put(small.at[:, at((1 - f) * lo_map, lo_map, 16), :], small_pair, small_sem.at[0], partner)
    put(vec.at[:, at((1 - f) * lo_norm, lo_norm, 128)], vec_pair, small_sem.at[1], partner)

    @pl.loop(0, 3 * chunks)
    def _(i):
        kind, j = i // chunks, lax.rem(i, chunks)
        cols = at(j * 256, 256, 128)
        wq[kind, cols, :] = mm(dproj[kind, :, cols].astype(f32).T.astype(bf16), n1[...]).astype(bf16)

    grad_pair(0)
    arrived(small_pair, small_sem.at[0])
    arrived(vec_pair, small_sem.at[1])
    for tt in range(4):
        for side in range(2):
            for q in range(2):
                p = side * pairs + pairs_of[tt] + q
                mine = small[p, at(f * lo_map, lo_map, 16), :] + small_pair[p]
                small_own[tt, 2 * side + q] = mine.astype(bf16)
    vec_own[...] = vec[:, at(f * lo_norm, lo_norm, 128)] + vec_pair[...]
    for k in range(1, 4):
        other = lax.rem(t + k, 4)
        put(small_own.at[other], small_in.at[t], small_sem.at[2], (f, c, other))
        put(vec_own, vec_in.at[t], small_sem.at[3], (f, c, other))
    own_small = [
        fetch(small_own.at[t], small_in.at[t], local_sem.at[6]),
        fetch(vec_own, vec_in.at[t], local_sem.at[7]),
    ]
    rows_hop(1, 0, 1)
    grad_last(3)
    grad_xy(0)
    grad_chain(2, 1)
    grad_z(1)
    for copy in own_small:
        copy.wait()
    arrived(small_in.at[pl.ds(0, 3)], small_sem.at[2])
    arrived(vec_in.at[pl.ds(0, 3)], small_sem.at[3])
    total = small_in[0].astype(f32)
    sums = vec_in[0]
    for i in range(1, 4):
        total = total + small_in[i].astype(f32)
        sums = sums + vec_in[i]
    small_sum[...] = total.astype(bf16)
    vec_sum[...] = sums
    for j in range(1, 4):
        put(small_sum, small_all.at[c], small_sem.at[4], (f, c ^ j, t))
        put(vec_sum, vec_all.at[c], small_sem.at[5], (f, c ^ j, t))
    own_small = [
        fetch(small_sum, small_all.at[c], local_sem.at[6]),
        fetch(vec_sum, vec_all.at[c], local_sem.at[7]),
    ]
    rows_hop(1, 1, 1)
    grad_chain(2, 2)
    grad_chain(1, 1)
    grad_mid(0)
    grad_last(2)
    grad_chain(1, 2)
    grad_z(0)
    rows_hop(1, 0, 2)
    for copy in own_small:
        copy.wait()
    arrived(small_all.at[pl.ds(0, 3)], small_sem.at[4])
    arrived(vec_all.at[pl.ds(0, 3)], small_sem.at[5])
    total = small_all[0].astype(f32)
    sums = vec_all[0]
    for i in range(1, 4):
        total = total + small_all[i].astype(f32)
        sums = sums + vec_all[i]
    norms_out[...] = sums
    odd_slot = lax.rem(t, 2) == 1
    for side in range(2):
        near, far = total[2 * side], total[2 * side + 1]
        near_high, far_high = pltpu.roll(near, 64, 1), pltpu.roll(far, 64, 1)
        for j, (high, low) in enumerate(((near_high, near), (far, near_high), (far_high, far))):
            maps_out[side][j] = jnp.where(odd_slot, high, low)[:, :64]
    grad_chain(0, 1)
    grad_last(1)
    rows_hop(1, 1, 2)
    grad_chain(0, 2)
    rows_hop(0, 0, 3)
    rows_hop(0, 1, 3)
    grad_last(0)
    for m in range(4):
        for j in range(1, 4):
            arrived(last[m], last_sem.at[m, j])
    rows_hop(1, 0, 3)
    rows_hop(1, 1, 3)
    for copy in own_rows:
        copy.wait()
    for copy in started:
        copy.wait_send()
    chains_sent()
    rows_sent(0)
    rows_sent(1)

def mesh_device(
    inputs,
    cotangent,
    picture_starts,
    qkv_weight,
    out_weight,
    up_weight,
    down_weight,
    query_map,
    key_map,
    first_gain,
    first_bias,
    second_gain,
    second_bias,
):
    micro, seq_local, seq_len, d = inputs.shape
    span = seq_len // 4
    rows = micro * seq_local * span
    ff = up_weight.shape[1] * 4
    heads = query_map.shape[0] * 4
    head = query_map.shape[2]
    own_block = lax.axis_index("context") * 4 + lax.axis_index("tensor")
    flags = jnp.any(picture_starts.reshape(micro, -1) // BLK == own_block, 1).astype(f32)
    flags = jnp.broadcast_to(flags[:, None, None], (micro, 8, span))
    maps = jnp.stack([query_map, key_map])
    maps = jnp.concatenate([maps, -maps], -1)
    norms = jnp.stack([first_gain, first_bias, second_gain, second_bias]).astype(f32)
    norms = jnp.concatenate([norms, jnp.zeros_like(norms)])
    dma = pltpu.SemaphoreType.DMA
    own = [(3, 4, d // 4, d // 2), (4, d // 4, d // 2), (d // 2, ff), (d // 2, ff)]
    sums = [(3, 4, d // 16, d // 2), (4, d // 16, d // 2), (d // 8, ff), (d // 8, ff)]
    last = [(3, d // 16, d // 2), (d // 16, d // 2), (d // 8, ff // 4), (d // 8, ff // 4)]
    outs = [(3, d // 4, d // 2), (d // 4, d // 2), (d // 2, ff // 4), (d // 2, ff // 4)]
    low = [(3, d, d), (d, d), (d, ff), (d, ff), (2, heads, head, 128)]
    state_rows = heads // 2 * 128
    pieces = (16, micro, state_rows // 16, 128)
    tiny = [(2 * (heads // 2), head, 128), (2 * (heads // 2), head // 2, 128), (4, 4, head // 2, 128)]
    maps_shape = (heads // 4, head // 2, head)
    scratch = [pltpu.VMEM(s, bf16) for s in low]
    scratch += [pltpu.VMEM((8, d), f32)]
    scratch += [pltpu.VMEM((rows, d), bf16)] * 3
    scratch += [pltpu.VMEM((3, rows, d), bf16), pltpu.VMEM((2, rows, heads * 128), bf16)]
    scratch += [pltpu.VMEM((2, micro, state_rows, 128), bf16), pltpu.VMEM((2, 16, 8, 128), f32)]
    scratch += [pltpu.VMEM((micro, state_rows, 128), bf16), pltpu.VMEM((16, 8, 128), f32)]
    scratch += [pltpu.VMEM(pieces, bf16), pltpu.VMEM((16, 8, 128), f32)] * 2
    scratch += [pltpu.VMEM((rows, d), bf16)] + [pltpu.VMEM((rows, d), f32)] * 3
    scratch += [pltpu.VMEM((rows, d), bf16)] + [pltpu.VMEM((rows, ff), bf16)] * 2
    scratch += [pltpu.VMEM((rows, d), bf16)] * 3 + [pltpu.VMEM((rows, d), f32)]
    scratch += [pltpu.VMEM((3, rows, d), bf16), pltpu.VMEM((rows, d), bf16), pltpu.VMEM((d, rows), bf16)]
    scratch += [pltpu.VMEM(s, bf16) for s in own]
    scratch += [pltpu.VMEM((3,) + s, bf16) for s in sums]
    scratch += [pltpu.VMEM(s, bf16) for s in sums]
    scratch += [pltpu.VMEM((6,) + s, bf16) for s in last]
    scratch += [pltpu.VMEM(s, bf16) for s in last]
    scratch += [pltpu.VMEM(s, f32) for s in tiny[:2]] + [pltpu.VMEM(tiny[2], bf16)] * 2
    scratch += [pltpu.VMEM(tiny[2][1:], bf16), pltpu.VMEM(tiny[2], bf16)]
    scratch += [pltpu.VMEM(s, f32) for s in ((8, d), (8, d // 2), (8, d // 2), (4, 8, d // 2), (8, d // 2), (4, 8, d // 2))]
    scratch += [dma((14,)), dma(()), dma((8,)), dma((4, 4)), dma((4, 4, 4)), dma((4,))]
    scratch += [dma((8,)), dma((2, 2, 3, 2, 2)), dma((4,)), dma((4, 2, 3)), dma((4, 6)), dma((4, 4)), dma((6,))]
    spread_rows = (micro, 4, span, d)
    anywhere = pl.BlockSpec(memory_space=pl.ANY)
    all_out, all_in, share_0, share_1, share_2, share_3, map_0, map_1, norm_grads = pl.pallas_call(
        layer_kernel,
        out_shape=[jax.ShapeDtypeStruct(spread_rows, bf16)] * 2
        + [jax.ShapeDtypeStruct(s, bf16) for s in outs]
        + [jax.ShapeDtypeStruct(maps_shape, f32)] * 2
        + [jax.ShapeDtypeStruct((8, d // 2), f32)],
        in_specs=[anywhere] * 2 + [pl.BlockSpec(memory_space=pltpu.VMEM)] + [anywhere] * 6,
        out_specs=[anywhere] * 6 + [pl.BlockSpec(memory_space=pltpu.VMEM)] * 3,
        scratch_shapes=scratch,
        compiler_params=pltpu.CompilerParams(collective_id=0, has_side_effects=True, vmem_limit_bytes=67043328),
        name="layer",
    )(inputs, cotangent, flags, maps, norms, qkv_weight.transpose(0, 2, 1), out_weight, up_weight, down_weight.T)
    return (
        all_out.reshape(inputs.shape),
        all_in.reshape(inputs.shape).astype(f32),
        share_0.astype(f32).transpose(0, 2, 1),
        share_1.astype(f32),
        share_2.astype(f32),
        share_3.astype(f32).T,
        map_0,
        map_1,
        norm_grads[0],
        norm_grads[1],
        norm_grads[2],
        norm_grads[3],
    )


def solution(mesh):
    in_specs = (
        P(None, "fsdp", "context", None),
        P(None, "fsdp", "context", None),
        P(None, "fsdp", None),
        P(None, "fsdp", "tensor"),
        P("tensor", "fsdp"),
        P("fsdp", "tensor"),
        P("tensor", "fsdp"),
        P("tensor", "fsdp", None),
        P("tensor", "fsdp", None),
        P("fsdp"),
        P("fsdp"),
        P("fsdp"),
        P("fsdp"),
    )
    out_specs = (
        P(None, "fsdp", "context", None),
        P(None, "fsdp", "context", None),
        P(None, "fsdp", "tensor"),
        P("tensor", "fsdp"),
        P("fsdp", "tensor"),
        P("tensor", "fsdp"),
        P("tensor", "fsdp", None),
        P("tensor", "fsdp", None),
        P("fsdp"),
        P("fsdp"),
        P("fsdp"),
        P("fsdp"),
    )
    sizes = tuple(mesh.shape[name] for name in EVERY)
    return jax.shard_map(
        mesh_device if sizes == (2, 4, 4) else per_device, mesh=mesh, in_specs=in_specs, out_specs=out_specs, check_vma=False
    )
```

```python
import jax
import jax.numpy as jnp
from jax import lax
from jax.experimental import pallas as pl
from jax.experimental.pallas import tpu as pltpu
from jax.sharding import PartitionSpec as P

BLK = 256
MICRO = 2


epsilon = 1e-05
highest = lax.Precision.HIGHEST


EVERY = ("fsdp", "context", "tensor")


def carried_in(value, backward):
    slot, mine = lax.axis_index("tensor"), lax.axis_index("context")
    near = lax.all_gather(value, "tensor")
    far = lax.all_gather(jnp.sum(near, 0).astype(value.dtype), "context")
    near_ids = jnp.arange(near.shape[0]).reshape((-1,) + (1,) * value.ndim)
    far_ids = jnp.arange(far.shape[0]).reshape((-1,) + (1,) * value.ndim)
    near_mask = near_ids > slot if backward else near_ids < slot
    far_mask = far_ids > mine if backward else far_ids < mine
    near, far = near.astype(jnp.float32), far.astype(jnp.float32)
    return jnp.sum(jnp.where(near_mask, near, 0.0), 0) + jnp.sum(jnp.where(far_mask, far, 0.0), 0)


def layer_norm(values, norm_gain, norm_bias):
    center = values - jnp.mean(values, -1, keepdims=True)
    spread = jnp.mean(center * center, -1, keepdims=True)
    return center * lax.rsqrt(spread + epsilon) * norm_gain + norm_bias


def features(logits):
    return jnp.concatenate([jax.nn.softmax(logits, -1), jax.nn.softmax(-logits, -1)], -1)


def gelu_tanh(values):
    return jax.nn.gelu(values, approximate=True)


def prefix_before(values):
    running = jnp.cumsum(values, 1)
    return jnp.concatenate([jnp.zeros_like(values[:, :1]), running[:, :-1]], 1)


def suffix_after(values):
    running = jnp.flip(jnp.cumsum(jnp.flip(values, 1), 1), 1)
    return jnp.concatenate([running[:, 1:], jnp.zeros_like(values[:, :1])], 1)


def spread(part, axis, parts):
    own = lax.axis_index("context")
    size = part.shape[axis] // parts
    mine = lax.dynamic_slice_in_dim(part, own * size, size, axis)
    return lax.all_gather(mine, EVERY)


def full_in(part):
    pieces = spread(part, 1, lax.axis_size("context"))
    fsdp, ctx, tens = (lax.axis_size(name) for name in EVERY)
    pieces = pieces.reshape((fsdp, ctx, tens) + pieces.shape[1:])
    pieces = pieces.transpose(3, 0, 1, 4, 2, 5)
    return pieces.reshape(pieces.shape[0], -1, pieces.shape[4] * pieces.shape[5])


def share_in(grad):
    fsdp, ctx, tens = (lax.axis_size(name) for name in EVERY)
    kinds, rows, cols = grad.shape
    pieces = grad.astype(jnp.bfloat16).reshape(kinds, fsdp, ctx, rows // fsdp // ctx, tens, cols // tens)
    pieces = pieces.transpose(1, 2, 4, 0, 3, 5).reshape((-1,) + (kinds, rows // fsdp // ctx, cols // tens))
    mine = lax.psum_scatter(pieces, EVERY, scatter_dimension=0)
    return lax.all_gather(mine, "context", axis=1, tiled=True).astype(jnp.float32)


def full_rows(part):
    pieces = spread(part, 0, lax.axis_size("context"))
    fsdp, ctx, tens = (lax.axis_size(name) for name in EVERY)
    pieces = pieces.reshape((fsdp, ctx, tens) + pieces.shape[1:])
    pieces = pieces.transpose(2, 1, 3, 0, 4)
    return pieces.reshape(tens * part.shape[0], -1)


def share_rows(grad):
    fsdp, ctx, tens = (lax.axis_size(name) for name in EVERY)
    rows, cols = grad.shape
    pieces = grad.astype(jnp.bfloat16).reshape(tens, ctx, rows // tens // ctx, fsdp, cols // fsdp)
    pieces = pieces.transpose(3, 1, 0, 2, 4).reshape(-1, rows // tens // ctx, cols // fsdp)
    mine = lax.psum_scatter(pieces, EVERY, scatter_dimension=0)
    return lax.all_gather(mine, "context", axis=0, tiled=True).astype(jnp.float32)


def full_maps(part):
    pieces = lax.all_gather(part, ("fsdp", "tensor"))
    fsdp, tens = lax.axis_size("fsdp"), lax.axis_size("tensor")
    pieces = pieces.reshape((fsdp, tens) + part.shape).transpose(1, 2, 0, 3, 4)
    return pieces.reshape(tens * part.shape[0], fsdp * part.shape[1], part.shape[2])


def own_maps(total):
    fsdp, tens = lax.axis_size("fsdp"), lax.axis_size("tensor")
    heads, rows, _ = total.shape
    mine = lax.dynamic_slice_in_dim(total, lax.axis_index("tensor") * (heads // tens), heads // tens, 0)
    return lax.dynamic_slice_in_dim(mine, lax.axis_index("fsdp") * (rows // fsdp), rows // fsdp, 1)


def per_device(
    inputs,
    cotangent,
    picture_starts,
    qkv_weight,
    out_weight,
    up_weight,
    down_weight,
    query_map,
    key_map,
    first_gain,
    first_bias,
    second_gain,
    second_bias,
):
    tensor_size = lax.axis_size("tensor")
    micro, seq_local, seq_len, model_width = inputs.shape
    span = seq_len // tensor_size
    slot = lax.axis_index("tensor")
    head_size = query_map.shape[2]
    feat_size = 2 * head_size
    blocks_local = span // BLK
    seq_count = micro * seq_local
    block_total = seq_count * blocks_local
    row_count = seq_count * span
    first_block = (lax.axis_index("context") * tensor_size + slot) * blocks_local
    block_ids = first_block + jnp.arange(blocks_local, dtype=jnp.int32)
    position = jnp.arange(BLK, dtype=jnp.int32)
    causal = position[None, :] <= position[:, None]

    in_full = full_in(qkv_weight)
    out_full = full_rows(out_weight)
    up_full = full_in(up_weight[None])[0]
    down_full = full_rows(down_weight)
    qmap_full, kmap_full = full_maps(query_map), full_maps(key_map)
    norms = lax.all_gather(jnp.stack([first_gain, first_bias, second_gain, second_bias]), "fsdp", axis=1, tiled=True)
    gain_first, bias_first, gain_second, bias_second = norms.astype(jnp.float32)

    def own(values):
        mine = lax.dynamic_slice_in_dim(values, slot * span, span, 2)
        return mine.reshape(row_count, model_width)

    source = own(inputs).astype(jnp.float32)
    starts_here = picture_starts.reshape(seq_count, -1)
    block_flags = (
        jnp.sum((starts_here[:, :, None] // BLK == block_ids[None, None, :]).astype(jnp.int32), 1)
        > 0
    )
    allowed = causal[None, None] | block_flags[:, :, None, None]
    allowed = allowed.reshape(block_total, 1, BLK, BLK)
    normed_one = layer_norm(source, gain_first, bias_first)
    normed_low = normed_one.astype(jnp.bfloat16)
    projected = jnp.einsum(
        "rd,cde->cre", normed_low, in_full, preferred_element_type=jnp.float32
    ).astype(jnp.bfloat16)
    heads_local = projected.shape[2] // head_size
    queries = projected[0].reshape(row_count, heads_local, head_size)
    key_rows = projected[1].reshape(row_count, heads_local, head_size)
    value_rows = projected[2].reshape(row_count, heads_local, head_size)
    query_logits = jnp.einsum(
        "rhi,hij->rhj", queries, qmap_full, preferred_element_type=jnp.float32
    )
    key_logits = jnp.einsum(
        "rhi,hij->rhj", key_rows, kmap_full, preferred_element_type=jnp.float32
    )
    query_blocks = (
        features(query_logits)
        .astype(jnp.bfloat16)
        .reshape(block_total, BLK, heads_local, feat_size)
    )
    key_blocks = (
        features(key_logits)
        .astype(jnp.bfloat16)
        .reshape(block_total, BLK, heads_local, feat_size)
    )
    value_blocks = value_rows.reshape(block_total, BLK, heads_local, head_size)
    scores = jnp.einsum(
        "nthf,nshf->nhts", query_blocks, key_blocks, preferred_element_type=jnp.float32
    )
    weights_low = jnp.where(allowed, scores, 0.0).astype(jnp.bfloat16)
    states = jnp.einsum(
        "nshf,nshe->nhfe", key_blocks, value_blocks, preferred_element_type=jnp.float32
    )
    states = states.reshape(seq_count, blocks_local, heads_local, feat_size, head_size)
    key_sums = jnp.sum(key_blocks.astype(jnp.float32), 1).reshape(
        seq_count, blocks_local, heads_local, feat_size
    )
    state_total = jnp.sum(states, 1)
    sums_total = jnp.sum(key_sums, 1)
    carried = carried_in(state_total.astype(jnp.bfloat16), False)
    carried_sums = carried_in(sums_total, False)
    prior_states = (carried[:, None] + prefix_before(states)).astype(jnp.bfloat16)
    prior_states = prior_states.reshape(block_total, heads_local, feat_size, head_size)
    prior_sums = (carried_sums[:, None] + prefix_before(key_sums)).reshape(
        block_total, heads_local, feat_size
    )
    numerator = jnp.einsum(
        "nhts,nshe->nthe", weights_low, value_blocks, preferred_element_type=jnp.float32
    )
    numerator = numerator + jnp.einsum(
        "nthf,nhfe->nthe", query_blocks, prior_states, preferred_element_type=jnp.float32
    )
    denominator = jnp.sum(weights_low.astype(jnp.float32), -1).transpose(0, 2, 1)
    denominator = denominator + jnp.einsum(
        "nthf,nhf->nth", query_blocks.astype(jnp.float32), prior_sums, precision=highest
    )
    mixed_heads = (
        (numerator / denominator[..., None])
        .astype(jnp.bfloat16)
        .reshape(row_count, heads_local * head_size)
    )
    attended = jnp.dot(mixed_heads, out_full, preferred_element_type=jnp.float32)
    middle = source + attended
    normed_two = layer_norm(middle, gain_second, bias_second)
    normed_two_low = normed_two.astype(jnp.bfloat16)
    hidden_pre = jnp.dot(normed_two_low, up_full, preferred_element_type=jnp.float32)
    hidden_low = gelu_tanh(hidden_pre).astype(jnp.bfloat16)
    branch = jnp.dot(hidden_low, down_full, preferred_element_type=jnp.float32)
    output = (middle + branch).astype(jnp.bfloat16).reshape(micro, seq_local, span, model_width)
    output = lax.all_gather(output, "tensor", axis=2, tiled=True)
    upstream_low = own(cotangent)
    upstream = upstream_low.astype(jnp.float32)
    grad_down = jnp.einsum(
        "rk,rd->kd", hidden_low, upstream_low, preferred_element_type=jnp.float32
    )
    hidden_grad = jnp.einsum(
        "rd,kd->rk", upstream_low, down_full, preferred_element_type=jnp.float32
    )
    gelu_result, gelu_pull = jax.vjp(gelu_tanh, hidden_pre)
    pre_grad = gelu_pull(hidden_grad)[0].astype(jnp.bfloat16)
    grad_up = jnp.einsum(
        "rd,rf->df", normed_two_low, pre_grad, preferred_element_type=jnp.float32
    )
    normed_two_grad = jnp.einsum(
        "rf,df->rd", pre_grad, up_full, preferred_element_type=jnp.float32
    )
    norm_result, second_pull = jax.vjp(layer_norm, middle, gain_second, bias_second)
    middle_part, grad_gain_second, grad_bias_second = second_pull(normed_two_grad)
    middle_grad = upstream + middle_part
    middle_low = middle_grad.astype(jnp.bfloat16)
    grad_out = jnp.einsum(
        "rk,rd->kd", mixed_heads, middle_low, preferred_element_type=jnp.float32
    )
    mixed_grad = jnp.einsum(
        "rd,kd->rk", middle_low, out_full, preferred_element_type=jnp.float32
    )
    mixed_grad = mixed_grad.reshape(block_total, BLK, heads_local, head_size)
    numer_grad = (mixed_grad / denominator[..., None]).astype(jnp.bfloat16)
    denom_grad = -jnp.sum(mixed_grad * numerator, -1) / (denominator * denominator)
    weight_grad = jnp.einsum(
        "nthe,nshe->nhts", numer_grad, value_blocks, preferred_element_type=jnp.float32
    )
    weight_grad = weight_grad + denom_grad.transpose(0, 2, 1)[..., None]
    weight_grad_low = jnp.where(allowed, weight_grad, 0.0).astype(jnp.bfloat16)
    value_grad = jnp.einsum(
        "nhts,nthe->nshe", weights_low, numer_grad, preferred_element_type=jnp.float32
    )
    query_grad = jnp.einsum(
        "nhts,nshf->nthf", weight_grad_low, key_blocks, preferred_element_type=jnp.float32
    )
    query_grad = query_grad + jnp.einsum(
        "nthe,nhfe->nthf", numer_grad, prior_states, preferred_element_type=jnp.float32
    )
    query_grad = query_grad + denom_grad[..., None] * prior_sums[:, None]
    key_grad = jnp.einsum(
        "nhts,nthf->nshf", weight_grad_low, query_blocks, preferred_element_type=jnp.float32
    )
    prior_grad = jnp.einsum(
        "nthf,nthe->nhfe", query_blocks, numer_grad, preferred_element_type=jnp.float32
    )
    prior_grad = prior_grad.reshape(seq_count, blocks_local, heads_local, feat_size, head_size)
    prior_sums_grad = jnp.einsum(
        "nthf,nth->nhf", query_blocks.astype(jnp.float32), denom_grad, precision=highest
    )
    prior_sums_grad = prior_sums_grad.reshape(seq_count, blocks_local, heads_local, feat_size)
    grad_total = jnp.sum(prior_grad, 1)
    grad_sums_total = jnp.sum(prior_sums_grad, 1)
    later_states = carried_in(grad_total.astype(jnp.bfloat16), True)
    later_sums = carried_in(grad_sums_total, True)
    state_grad = (later_states[:, None] + suffix_after(prior_grad)).astype(jnp.bfloat16)
    state_grad = state_grad.reshape(block_total, heads_local, feat_size, head_size)
    sums_grad = (later_sums[:, None] + suffix_after(prior_sums_grad)).reshape(
        block_total, heads_local, feat_size
    )
    key_grad = key_grad + jnp.einsum(
        "nshe,nhfe->nshf", value_blocks, state_grad, preferred_element_type=jnp.float32
    )
    key_grad = key_grad + sums_grad[:, None]
    value_grad = value_grad + jnp.einsum(
        "nshf,nhfe->nshe", key_blocks, state_grad, preferred_element_type=jnp.float32
    )
    query_feat_now, query_pull = jax.vjp(features, query_logits)
    query_logit_grad = query_pull(query_grad.reshape(row_count, heads_local, feat_size))[
        0
    ].astype(jnp.bfloat16)
    key_feat_now, key_pull = jax.vjp(features, key_logits)
    key_logit_grad = key_pull(key_grad.reshape(row_count, heads_local, feat_size))[0].astype(
        jnp.bfloat16
    )
    grad_qmap = jnp.einsum(
        "rhi,rhj->hij", queries, query_logit_grad, preferred_element_type=jnp.float32
    )
    grad_kmap = jnp.einsum(
        "rhi,rhj->hij", key_rows, key_logit_grad, preferred_element_type=jnp.float32
    )
    raw_query_grad = jnp.einsum(
        "rhj,hij->rhi", query_logit_grad, qmap_full, preferred_element_type=jnp.float32
    )
    raw_key_grad = jnp.einsum(
        "rhj,hij->rhi", key_logit_grad, kmap_full, preferred_element_type=jnp.float32
    )
    projected_grad = jnp.stack(
        [
            raw_query_grad.reshape(row_count, -1),
            raw_key_grad.reshape(row_count, -1),
            value_grad.reshape(row_count, -1),
        ]
    ).astype(jnp.bfloat16)
    grad_in = jnp.einsum(
        "rd,cre->cde", normed_low, projected_grad, preferred_element_type=jnp.float32
    )
    normed_one_grad = jnp.einsum(
        "cre,cde->rd", projected_grad, in_full, preferred_element_type=jnp.float32
    )
    first_result, first_pull = jax.vjp(layer_norm, source, gain_first, bias_first)
    source_part, grad_gain_first, grad_bias_first = first_pull(normed_one_grad)
    input_grad = (middle_grad + source_part).astype(jnp.bfloat16)
    input_grad = input_grad.reshape(micro, seq_local, span, model_width)
    input_grad = lax.all_gather(input_grad, "tensor", axis=2, tiled=True).astype(jnp.float32)
    norm_grads = jnp.stack([grad_gain_first, grad_bias_first, grad_gain_second, grad_bias_second])
    grad_qmap, grad_kmap, norm_grads = lax.psum((grad_qmap, grad_kmap, norm_grads), EVERY)
    share = first_gain.shape[0]
    norm_grads = lax.dynamic_slice_in_dim(norm_grads, lax.axis_index("fsdp") * share, share, 1)
    return (
        output,
        input_grad,
        share_in(grad_in),
        share_rows(grad_out),
        share_in(grad_up[None])[0],
        share_rows(grad_down),
        own_maps(grad_qmap),
        own_maps(grad_kmap),
        norm_grads[0],
        norm_grads[1],
        norm_grads[2],
        norm_grads[3],
    )


MESH = pl.DeviceIdType.MESH
bf16 = jnp.bfloat16
f32 = jnp.float32


def whereabouts():
    return tuple(lax.axis_index(name) for name in EVERY)


def neighbours(f, c, t):
    n = c * 4 + t
    peers = [(1 - f, c, t)]
    for k in range(1, 16):
        other = lax.rem(n + k, 16)
        peers.append((f, other // 4, lax.rem(other, 4)))
    for k in range(1, 4):
        peers.append((1 - f, c, lax.rem(t + k, 4)))
    return peers


def meet(f, c, t):
    barrier = pltpu.get_barrier_semaphore()
    peers = neighbours(f, c, t)
    for peer in peers:
        pl.semaphore_signal(barrier, inc=1, device_id=peer, device_id_type=MESH)
    pl.semaphore_wait(barrier, len(peers))


def send(src, dst, send_sem, recv_sem, peer):
    copy = pltpu.make_async_remote_copy(
        src_ref=src, dst_ref=dst, send_sem=send_sem, recv_sem=recv_sem,
        device_id=peer, device_id_type=MESH,
    )
    copy.start()
    return copy


def arrived(ref, sem):
    pltpu.make_async_copy(ref, ref, sem).wait()


def at(start, size, unit):
    return pl.ds(pl.multiple_of(start, unit), size)


GROUPS = (0, 4, 1, 2, 3)


def of(refs, m, *index):
    ref = refs[m % 4].at[index] if index else refs[m % 4]
    return ref.at[kinds(m)] if m % 4 == 0 else ref


def kinds(m):
    return pl.ds(1, 2) if m == 0 else pl.ds(0, 1)


def kind_count(m):
    return 2 if m == 0 else 1


def half(ref, m, f):
    if m % 4 == 0:
        w = ref.shape[2] // 2
        return ref.at[:, :, at(f * w, w, 128)]
    if m == 1:
        w = ref.shape[1] // 2
        return ref.at[:, at(f * w, w, 128)]
    w = ref.shape[0] // 2
    return ref.at[at(f * w, w, 16), :]


def shard(ref, m, f, t):
    if m % 4 == 0:
        w, h = ref.shape[2] // 2, ref.shape[1] // 4
        return ref.at[:, at(t * h, h, 16), at(f * w, w, 128)]
    if m == 1:
        w, h = ref.shape[1] // 2, ref.shape[0] // 4
        return ref.at[at(t * h, h, 16), at(f * w, w, 128)]
    h, w = ref.shape[0] // 2, ref.shape[1] // 4
    return ref.at[at(f * h, h, 16), at(t * w, w, 128)]


def piece(ref, m, f, c, t):
    if m % 4 == 0:
        w, h = ref.shape[2] // 2, ref.shape[1] // 16
        return ref.at[:, at(t * 4 * h + c * h, h, 16), at(f * w, w, 128)]
    if m == 1:
        w, h = ref.shape[1] // 2, ref.shape[0] // 16
        return ref.at[at(t * 4 * h + c * h, h, 16), at(f * w, w, 128)]
    h, w = ref.shape[0] // 8, ref.shape[1] // 4
    return ref.at[at(f * 4 * h + c * h, h, 16), at(t * w, w, 128)]


def quarter(ref, m, c):
    if m % 4 == 0:
        h = ref.shape[1] // 4
        return ref.at[:, at(c * h, h, 16), :]
    h = ref.shape[0] // 4
    return ref.at[at(c * h, h, 16), :]


def context_part(ref, m, c):
    if m % 4 == 0:
        h = ref.shape[2] // 4
        return ref.at[:, :, at(c * h, h, 16), :]
    if m == 1:
        h = ref.shape[1] // 4
        return ref.at[:, at(c * h, h, 16), :]
    h = ref.shape[0] // 4
    return ref.at[at(c * h, h, 16), :]


def two_of(ref, m, side):
    if m % 4 == 0:
        return ref.at[:, pl.ds(2 * side, 2)]
    if m == 1:
        return ref.at[pl.ds(2 * side, 2)]
    w = ref.shape[1] // 2
    return ref.at[:, pl.ds(side * w, w)]


def tensor_part(ref, m, t):
    if m % 4 == 0:
        return ref.at[:, t]
    if m == 1:
        return ref.at[t]
    w = ref.shape[1] // 4
    return ref.at[:, at(t * w, w, 128)]


NN = (((1,), (0,)), ((), ()))
NT = (((1,), (1,)), ((), ()))
TN = (((0,), (0,)), ((), ()))


def mm(a, b, dims=NN):
    return lax.dot_general(a, b, dims, preferred_element_type=f32)


def lanes_of(shape):
    return lax.broadcasted_iota(jnp.int32, shape, len(shape) - 1)


def block_ones(size, group):
    row = lax.broadcasted_iota(jnp.int32, (size, size), 0) // group
    col = lax.broadcasted_iota(jnp.int32, (size, size), 1) // group
    return jnp.where(row == col, 1.0, 0.0).astype(bf16)


def statistics(rows):
    center = rows - jnp.mean(rows, -1, keepdims=True)
    rstd = lax.rsqrt(jnp.mean(center * center, -1, keepdims=True) + epsilon)
    return center * rstd, rstd


def norm_back(grad, e, rstd, gain):
    w = grad * gain
    return rstd * (w - jnp.mean(w, -1, keepdims=True) - e * jnp.mean(w * e, -1, keepdims=True))


def near_far(first, low, high):
    return jnp.where(first, low, high)


def own_half(values, first, odd):
    zero = jnp.zeros_like(values)
    return jnp.where(first, zero, values) if odd else jnp.where(first, values, zero)


def pair_block(values, first):
    return jnp.concatenate([own_half(values, first, 0), own_half(values, first, 1)], 0)


def split_half(full, first, odd):
    other = pltpu.roll(full, 64, 1)
    return jnp.where(first, other, full) if odd else jnp.where(first, full, other)


def layer_kernel(*refs):
    inputs, cotangent, flags, maps, norms = refs[:5]
    shards = refs[5:9]
    all_out, all_in = refs[9:11]
    outs, maps_out, norms_out = refs[11:15], refs[15:17], refs[17]
    w, mx, nrm, x, g, n1, qkv, feat = refs[18:22], *refs[22:29]
    prior, sums_in, states, z_buf, s_in, z_in, s_out, z_out = refs[29:37]
    o, rden, num, mid, n2, a, gp, rows_out = refs[37:45]
    gm, dnum, dden, dproj, rows_in, turned = refs[45:51]
    pair_in, xy_in, part, tz_in, last = (refs[51 + 4 * i : 55 + 4 * i] for i in range(5))
    small, small_pair, small_own, small_in, small_sum, small_all = refs[71:77]
    vec, vec_pair, vec_own, vec_in, vec_sum, vec_all = refs[77:83]
    local_sem, send_sem, extra_sem, z_sem, xy_sem, pair_sem = refs[83:89]
    scan_sem, rows_sem, gpair_sem, gxy_sem, gz_sem, last_sem, small_sem = refs[89:96]
    wq, wo, wu, wd = w
    d = x.shape[1]
    ff = a.shape[1]
    half_rows = x.shape[0] // 2
    f, c, t = whereabouts()
    n = c * 4 + t
    peers = neighbours(f, c, t)
    partner = peers[0]
    started = []

    def put(src, dst, recv_sem, peer):
        started.append(send(src, dst, send_sem, recv_sem, peer))

    started_if = []

    def put_if(pred, src, dst, recv_sem, peer):
        def copy():
            return pltpu.make_async_remote_copy(
                src_ref=src, dst_ref=dst, send_sem=send_sem, recv_sem=recv_sem, device_id=peer, device_id_type=MESH,
            )

        @pl.when(pred)
        def _():
            copy().start()

        started_if.append((pred, copy))

    fetched = []

    def fetch(src, dst, sem):
        copy = pltpu.make_async_copy(src, dst, sem)
        copy.start()
        return copy

    for i in range(2):
        rows = pl.ds(i * half_rows, half_rows)
        fetched.append(fetch(inputs.at[i, 0, at(t * half_rows, half_rows, 16), :], x.at[rows], local_sem.at[i]))
        fetched.append(fetch(cotangent.at[i, 0, at(t * half_rows, half_rows, 16), :], g.at[rows], local_sem.at[2 + i]))
    h3 = maps.shape[1]
    head_rows = small.shape[1]
    pairs_of = (0, 1, 3, 4)
    lo_norm = d // 2

    def map_place(ff_, tt):
        return mx.at[:, pl.ds(tt * h3, h3), at(ff_ * 32, 32, 16), :]

    def norm_place(ff_):
        return nrm.at[:, at(ff_ * lo_norm, lo_norm, 128)]

    fetched.append(fetch(maps, map_place(f, t), local_sem.at[4]))
    fetched.append(fetch(norms, norm_place(f), local_sem.at[5]))
    shard_copies = [fetch(of(shards, m), shard(of(w, m), m, f, t), local_sem.at[6 + m]) for m in range(5)]
    z_buf[...] = jnp.zeros_like(z_buf)
    small[...] = jnp.zeros_like(small)
    vec[...] = jnp.zeros_like(vec)
    meet(f, c, t)

    put(norms, norm_place(f), extra_sem.at[0], partner)
    put(maps, map_place(f, t), extra_sem.at[4], partner)
    for m in GROUPS:
        for k, pred in ((2, None), (1, t != 3), (3, t != 0)):
            src, dst = quarter(of(shards, m), m, c), piece(of(w, m), m, f, c, t)
            peer = (f, c, lax.rem(t + k, 4))
            if pred is None:
                put(src, dst, z_sem.at[m, k], peer)
            else:
                put_if(pred, src, dst, z_sem.at[m, k], peer)
        if m == 0:
            for k in range(1, 4):
                put(maps, map_place(f, t), extra_sem.at[k], (f, c, lax.rem(t + k, 4)))
    for m in GROUPS:
        put(of(shards, m), shard(of(w, m), m, f, t), pair_sem.at[m], partner)

    def forward(m, k):
        got = piece(of(w, m), m, f, c, lax.rem(t + 4 - k, 4))
        arrived(got, z_sem.at[m, k])
        if k == 2:
            put_if(t == 2, got, got, z_sem.at[m, 3], (f, c, t + 1))
            put_if(t == 1, got, got, z_sem.at[m, 1], (f, c, t - 1))
        for j in range(1, 3):
            put(got, got, xy_sem.at[m, k, j], (f, c ^ j, t))
        put(got, got, pair_sem.at[m], partner)

    def relay(m, k):
        for j in range(1, 3):
            got = piece(of(w, m), m, f, c ^ j, lax.rem(t + 4 - k, 4))
            arrived(got, xy_sem.at[m, k, j])
            if ((0, 1, 2, 3, 1)[m] + k + j) % 2:
                put(got, got, xy_sem.at[m, k, 3], (f, c ^ 3 ^ j, t))
            put(got, got, pair_sem.at[m], partner)

    def across(m):
        for k in range(1, 4):
            got = piece(of(w, m), m, f, c ^ 3, lax.rem(t + 4 - k, 4))
            arrived(got, xy_sem.at[m, k, 3])
            put(got, got, pair_sem.at[m], partner)

    def take_maps():
        for k in range(1, 4):
            got = map_place(f, lax.rem(t + 4 - k, 4))
            arrived(got, extra_sem.at[k])
            put(got, got, extra_sem.at[4 + k], partner)

    def maps_here():
        for k in range(4):
            arrived(map_place(1 - f, lax.rem(t + 4 - k, 4)), extra_sem.at[4 + k])

    def complete(m):
        shard_copies[m].wait()
        arrived(half(of(w, m), m, 1 - f), pair_sem.at[m])

    for k in (2, 1, 3):
        forward(0, k)
    for copy in fetched:
        copy.wait()
    arrived(norm_place(1 - f), extra_sem.at[0])
    first = lanes_of((1, 128)) < 64
    ones64 = block_ones(128, 64)
    step = half_rows // 2

    @pl.loop(0, 4)
    def _(i):
        rows = at(i * step, step, 16)
        e, _unused = statistics(x[rows, :].astype(f32))
        n1[rows, :] = (e * nrm[0:1, :] + nrm[1:2, :]).astype(bf16)

    take_maps()
    for k in (2, 1, 3):
        relay(0, k)
        forward(4, k)
    for k in (2, 1, 3):
        forward(1, k)
    across(0)
    forward(2, 2)
    complete(0)

    chunks = d // 256

    def project(i):
        kind, j = i // chunks, lax.rem(i, chunks)
        cols = at(j * 256, 256, 128)
        qkv[kind, :, cols] = mm(n1[...], wq[kind, cols, :], NT).astype(bf16)

    pl.loop(chunks, 3 * chunks)(project)

    for k in (2, 1, 3):
        relay(4, k)
    forward(2, 1)
    maps_here()

    pairs = d // 128

    def pair_map(side, p):
        zero = jnp.zeros((64, 128), bf16)
        top = jnp.concatenate([mx[side, 2 * p], zero], 1)
        bottom = jnp.concatenate([zero, mx[side, 2 * p + 1]], 1)
        return jnp.concatenate([top, bottom], 0)

    def features_of(side, i):
        b, p = i // pairs, lax.rem(i, pairs)
        rows = at(b * half_rows, half_rows, 16)
        logits = mm(qkv[side, rows, at(p * 128, 128, 128)], pair_map(side, p))
        for odd in range(2):
            part_ = logits[:, odd * 128 : odd * 128 + 128]
            low_top = jnp.max(jnp.where(first, part_, -jnp.inf), -1, keepdims=True)
            high_top = jnp.max(jnp.where(first, -jnp.inf, part_), -1, keepdims=True)
            e = jnp.exp(part_ - jnp.where(first, low_top, high_top))
            total = mm(e.astype(bf16), ones64)
            feat[side, rows, at(p * 256 + odd * 128, 128, 128)] = (e / total).astype(bf16)

    @pl.loop(0, 2 * pairs)
    def _(i):
        features_of(1, i)

    across(4)
    for k in (2, 1, 3):
        relay(1, k)
    forward(2, 3)

    @pl.loop(0, 2 * pairs)
    def _(i):
        b, p = i // pairs, lax.rem(i, pairs)
        rows = at(b * half_rows, half_rows, 16)
        keys = feat[1, rows, at(p * 256, 256, 128)]
        both = mm(keys, qkv[2, rows, at(p * 128, 128, 128)], TN)
        states[b, at(p * 128, 128, 16), :] = near_far(first, both[:128], both[128:]).astype(bf16)
        tall = mm(jnp.ones((8, half_rows), bf16), keys)
        slot = lax.broadcasted_iota(jnp.int32, (8, 128), 0) == b
        z_buf[2 * p] = jnp.where(slot, tall[:, :128], z_buf[2 * p])
        z_buf[2 * p + 1] = jnp.where(slot, tall[:, 128:], z_buf[2 * p + 1])

    srows = states.shape[1] // 16

    def scan_out(sem0):
        for k in range(1, 16):
            other = lax.rem(n + k, 16)
            put(states.at[:, at(other * srows, srows, 16), :], s_in.at[n], scan_sem.at[sem0], peers[k])
            put(z_buf.at[other], z_in.at[n], scan_sem.at[sem0 + 1], peers[k])
        one = fetch(states.at[:, at(n * srows, srows, 16), :], s_in.at[n], local_sem.at[0])
        two = fetch(z_buf.at[n], z_in.at[n], local_sem.at[1])
        one.wait()
        two.wait()

    def scan_back(sem0, backward):
        arrived(s_in.at[pl.ds(0, 15)], scan_sem.at[sem0])
        arrived(z_in.at[pl.ds(0, 15)], scan_sem.at[sem0 + 1])
        total = jnp.zeros(s_in.shape[1:], f32)
        sums = jnp.zeros(z_in.shape[1:], f32)
        for i in range(15, -1, -1) if backward else range(16):
            s_out[i] = total.astype(bf16)
            z_out[i] = sums
            total = total + s_in[i].astype(f32)
            sums = sums + z_in[i]
        for k in range(1, 16):
            other = lax.rem(n + k, 16)
            put(s_out.at[other], prior.at[int(backward), :, at(n * srows, srows, 16), :], scan_sem.at[sem0 + 2], peers[k])
            put(z_out.at[other], sums_in.at[int(backward), n], scan_sem.at[sem0 + 3], peers[k])
        one = fetch(s_out.at[n], prior.at[int(backward), :, at(n * srows, srows, 16), :], local_sem.at[0])
        two = fetch(z_out.at[n], sums_in.at[int(backward), n], local_sem.at[1])
        one.wait()
        two.wait()

    def scan_end(sem0):
        arrived(s_in.at[pl.ds(0, 15)], scan_sem.at[sem0 + 2])
        arrived(z_in.at[pl.ds(0, 15)], scan_sem.at[sem0 + 3])

    scan_out(0)
    complete(4)
    pl.loop(0, chunks)(project)
    relay(2, 2)
    forward(3, 2)

    @pl.loop(0, 2 * pairs)
    def _(i):
        features_of(0, i)

    forward(3, 1)
    forward(3, 3)
    across(1)
    relay(2, 1)
    relay(2, 3)

    def mask_of(b, turn):
        row = lax.broadcasted_iota(jnp.int32, (half_rows, half_rows), 0)
        col = lax.broadcasted_iota(jnp.int32, (half_rows, half_rows), 1)
        causal = row <= col if turn else col <= row
        return jnp.where(causal, 1.0, flags[b, 0:1, :])

    @pl.loop(0, 2 * pairs)
    def _(i):
        b, p = i // pairs, lax.rem(i, pairs)
        rows = at(b * half_rows, half_rows, 16)
        values = qkv[2, rows, at(p * 128, 128, 128)]
        mask = mask_of(b, False)
        both = None
        for odd in range(2):
            cols = at(p * 256 + odd * 128, 128, 128)
            scores = (mm(feat[0, rows, cols], feat[1, rows, cols], NT) * mask).astype(bf16)
            right = jnp.concatenate(
                [own_half(values, first, odd), own_half(jnp.ones_like(values), first, odd)], 1
            )
            term = mm(scores, right)
            both = term if both is None else both + term
        num[rows, at(p * 128, 128, 128)] = both[:, :128]
        rden[rows, at(p * 128, 128, 128)] = both[:, 128:]

    scan_back(0, False)
    for k in (2, 1, 3):
        relay(3, k)
    across(2)
    complete(1)
    scan_end(0)

    def sums_pair(direction, b, p, odd):
        tile = sums_in[direction, 2 * p + odd]
        slot = lax.broadcasted_iota(jnp.int32, (8, 128), 0) == b
        return jnp.sum(jnp.where(slot, tile, 0.0), 0, keepdims=True)

    @pl.loop(0, 2 * pairs)
    def _(i):
        b, p = i // pairs, lax.rem(i, pairs)
        rows = at(b * half_rows, half_rows, 16)
        cols = at(p * 128, 128, 128)
        queries = feat[0, rows, at(p * 256, 256, 128)]
        before = pair_block(prior[0, b, at(p * 128, 128, 16), :], first)
        zero = jnp.zeros((64, 128), bf16)
        z_low = jnp.broadcast_to(sums_pair(0, b, p, 0), (64, 128)).astype(bf16)
        z_high = jnp.broadcast_to(sums_pair(0, b, p, 1), (64, 128)).astype(bf16)
        z_rows = jnp.concatenate(
            [jnp.concatenate([z_low, zero], 1), jnp.concatenate([zero, z_high], 1)], 0
        )
        inverse = 1.0 / (rden[rows, cols] + mm(queries, z_rows, NT))
        o[rows, cols] = ((num[rows, cols] + mm(queries, before)) * inverse).astype(bf16)
        rden[rows, cols] = inverse

    @pl.loop(0, 2)
    def _(i):
        rows = at(i * half_rows, half_rows, 16)
        mid[rows, :] = x[rows, :].astype(f32) + mm(o[rows, :], wo[...])

    @pl.loop(0, 4)
    def _(i):
        rows = at(i * step, step, 16)
        e, _unused = statistics(mid[rows, :])
        n2[rows, :] = (e * nrm[2:3, :] + nrm[3:4, :]).astype(bf16)

    complete(2)

    @pl.loop(0, ff // 256)
    def _(i):
        cols = at(i * 256, 256, 128)
        u = mm(n2[...], wu[:, cols])
        scale = 0.7978845608028654
        square = u * u
        tanh = jnp.tanh(scale * u * (1.0 + 0.044715 * square))
        cdf = 0.5 + 0.5 * tanh
        a[:, cols] = (u * cdf).astype(bf16)
        slope = cdf + (0.5 * scale) * u * (1.0 - tanh * tanh) * (1.0 + 0.134145 * square)
        gp[:, cols] = slope.astype(bf16)

    across(3)
    complete(3)

    def branch(b):
        @pl.loop(0, chunks)
        def _(i):
            rows = pl.ds(b * half_rows, half_rows)
            cols = at(i * 256, 256, 128)
            rows_out[rows, cols] = (mid[rows, cols] + mm(a[rows, :], wd[cols, :], NT)).astype(bf16)

    links = []

    def pass_on(i, b, way, hop, block):
        dst = (all_out, all_in)[i]
        src = (rows_out, rows_in)[i]
        origin = src.at[pl.ds(b * half_rows, half_rows)] if hop == 0 else dst.at[b, block]
        return pltpu.make_async_remote_copy(
            src_ref=origin, dst_ref=dst.at[b, block], send_sem=rows_sem.at[i, way, hop, b, 0],
            recv_sem=rows_sem.at[i, way, hop, b, 1], device_id=(f, c, t + 1 if way == 0 else t - 1),
            device_id_type=MESH,
        )

    def rows_hop(i, b, hop):
        dst = (all_out, all_in)[i]
        for way in range(2):
            block = t - hop if way == 0 else t + hop
            here = block >= 0 if way == 0 else block <= 3
            more = t < 3 if way == 0 else t > 0
            if hop > 0:
                @pl.when(here)
                def _():
                    arrived(dst.at[b, 0], rows_sem.at[i, way, hop - 1, b, 1])
            if hop < 3:
                @pl.when(jnp.logical_and(here, more))
                def _():
                    pass_on(i, b, way, hop, block).start()

    def rows_sent(i):
        for b in range(2):
            for hop in range(3):
                for way in range(2):
                    block = t - hop if way == 0 else t + hop
                    here = block >= 0 if way == 0 else block <= 3
                    more = t < 3 if way == 0 else t > 0

                    @pl.when(jnp.logical_and(here, more))
                    def _():
                        pass_on(i, b, way, hop, block).wait_send()

    own_rows = []
    for b in range(2):
        branch(b)
        own_rows.append(fetch(rows_out.at[pl.ds(b * half_rows, half_rows)], all_out.at[b, t], local_sem.at[2 + b]))
        rows_hop(0, b, 0)

    def grad_pair(m):
        if m % 4 < 2:
            h = d // 4
            for tt in range(4):
                if m % 4 == 0:
                    src = of(w, m).at[:, pl.ds(tt * h, h), at((1 - f) * (d // 2), d // 2, 128)]
                    put(src, of(pair_in, m).at[:, tt], gpair_sem.at[m], partner)
                else:
                    src = w[m].at[pl.ds(tt * h, h), at((1 - f) * (d // 2), d // 2, 128)]
                    put(src, pair_in[m].at[tt], gpair_sem.at[m], partner)
        else:
            put(half(w[m], m, 1 - f), pair_in[m], gpair_sem.at[m], partner)

    def grad_xy(m):
        arrived(of(pair_in, m), gpair_sem.at[m])
        h = d // 4
        cols = at(f * (d // 2), d // 2, 128)
        if m % 4 == 0:
            @pl.loop(0, 4 * kind_count(m))
            def _(i):
                kind, tt = i // 4 + (m == 0), lax.rem(i, 4)
                mine = wq[kind, at(tt * h, h, 16), cols].astype(f32)
                pair_in[0][kind, tt] = (mine + pair_in[0][kind, tt].astype(f32)).astype(bf16)
        elif m == 1:
            @pl.loop(0, 4)
            def _(tt):
                mine = wo[at(tt * h, h, 16), cols].astype(f32)
                pair_in[1][tt] = (mine + pair_in[1][tt].astype(f32)).astype(bf16)
        else:
            @pl.loop(0, 12)
            def _(i):
                rows = at(i * 32, 32, 16)
                mine = w[m][at(f * (d // 2) + i * 32, 32, 16), :].astype(f32)
                pair_in[m][rows, :] = (mine + pair_in[m][rows, :].astype(f32)).astype(bf16)
        for side in range(2):
            way = 1 + side
            for i, owner in ((1, 3), (0, way)):
                put(
                    two_of(context_part(of(pair_in, m), m, c ^ owner), m, side), two_of(of(xy_in, m, i), m, side),
                    gxy_sem.at[m, side, i], (f, c ^ way, t),
                )

    def grad_mid(m):
        for side in range(2):
            way = 1 + side
            rest = two_of(of(xy_in, m, 1), m, side)
            mine = two_of(context_part(of(pair_in, m), m, c ^ 3 ^ way), m, side)
            arrived(rest, gxy_sem.at[m, side, 1])
            if m % 4 == 0:
                @pl.loop(0, 2 * kind_count(m))
                def _(i):
                    kind, tt = i // 2, lax.rem(i, 2)
                    rest[kind, tt] = (mine[kind, tt].astype(f32) + rest[kind, tt].astype(f32)).astype(bf16)
            elif m == 1:
                rest[...] = (mine[...].astype(f32) + rest[...].astype(f32)).astype(bf16)
            else:
                @pl.loop(0, d // 8 // 16)
                def _(i):
                    rows = at(i * 16, 16, 16)
                    rest[rows, :] = (mine[rows, :].astype(f32) + rest[rows, :].astype(f32)).astype(bf16)
            put(rest, two_of(of(xy_in, m, 2), m, side), gxy_sem.at[m, side, 2], (f, c ^ 3 ^ way, t))

    def grad_z(m):
        for side in range(2):
            for i in (0, 2):
                arrived(two_of(of(xy_in, m, i), m, side), gxy_sem.at[m, side, i])
        if m % 4 == 0:
            h = d // 16

            @pl.loop(0, 4 * kind_count(m))
            def _(i):
                kind, tt = i // 4 + (m == 0), lax.rem(i, 4)
                total = pair_in[0][kind, tt, at(c * h, h, 16), :].astype(f32)
                for j in (0, 2):
                    total = total + xy_in[0][j, kind, tt].astype(f32)
                part[0][kind, tt] = total.astype(bf16)
        elif m == 1:
            h = d // 16

            @pl.loop(0, 4)
            def _(tt):
                total = pair_in[1][tt, at(c * h, h, 16), :].astype(f32)
                for j in (0, 2):
                    total = total + xy_in[1][j, tt].astype(f32)
                part[1][tt] = total.astype(bf16)
        else:
            @pl.loop(0, d // 8 // 16)
            def _(i):
                rows = at(i * 16, 16, 16)
                total = pair_in[m][at(c * (d // 8) + i * 16, 16, 16), :].astype(f32)
                for j in (0, 2):
                    total = total + xy_in[m][j, rows, :].astype(f32)
                part[m][rows, :] = total.astype(bf16)
        for way, first_ in ((0, 0), (1, 3)):
            @pl.when(t == first_)
            def _():
                for owner in (3, 2, 1) if way == 0 else (0, 1, 2):
                    step_on(m, way, owner, True).start()

    def came(m, way, owner):
        slot = owner - 1 if way == 0 else 3 + owner
        return of(tz_in, m, slot), gz_sem.at[m, slot]

    def step_on(m, way, owner, from_end=False):
        dst, sem = came(m, way, owner)
        return pltpu.make_async_remote_copy(
            src_ref=tensor_part(of(part, m), m, owner) if from_end else dst, dst_ref=dst, send_sem=send_sem,
            recv_sem=sem, device_id=(f, c, t + 1 if way == 0 else t - 1), device_id_type=MESH,
        )

    def add_up(m, dst, own_part, others):
        if m % 4 == 0:
            for kind in range(kind_count(m)):
                total = own_part[kind].astype(f32)
                for other in others:
                    total = total + other[kind].astype(f32)
                dst[kind] = total.astype(bf16)
        elif m == 1:
            total = own_part[...].astype(f32)
            for other in others:
                total = total + other[...].astype(f32)
            dst[...] = total.astype(bf16)
        else:
            @pl.loop(0, d // 8 // 16)
            def _(i):
                rows = at(i * 16, 16, 16)
                total = own_part[rows, :].astype(f32)
                for other in others:
                    total = total + other[rows, :].astype(f32)
                dst[rows, :] = total.astype(bf16)

    def grad_chain(m, hop):
        for way, here in ((0, hop), (1, 3 - hop)):
            @pl.when(t == here)
            def _():
                for owner in range(3, here, -1) if way == 0 else range(here):
                    buf, sem = came(m, way, owner)
                    arrived(buf, sem)
                    add_up(m, buf, tensor_part(of(part, m), m, owner), [buf])
                    step_on(m, way, owner).start()

    def chains_sent():
        for m in range(5):
            for way in range(2):
                for owner in (1, 2, 3) if way == 0 else (0, 1, 2):
                    @pl.when(t < owner if way == 0 else t > owner)
                    def _():
                        step_on(m, way, owner).wait_send()

    def grad_last(m):
        for tt in range(4):
            @pl.when(t == tt)
            def _():
                others = []
                for way in range(2):
                    if (tt > 0, tt < 3)[way]:
                        buf, sem = came(m, way, tt)
                        arrived(buf, sem)
                        others.append(buf)
                add_up(m, of(last, m), tensor_part(of(part, m), m, tt), others)

        for j in range(1, 4):
            put(of(last, m), quarter(of(outs, m), m, c), last_sem.at[m, j], (f, c ^ j, t))
        fetch(of(last, m), quarter(of(outs, m), m, c), local_sem.at[11 + m]).wait()

    for copy in started:
        copy.wait_send()
    started.clear()
    for pred, copy in started_if:
        @pl.when(pred)
        def _():
            copy().wait_send()

    @pl.loop(0, ff // 256)
    def _(i):
        cols = at(i * 256, 256, 128)
        gp[:, cols] = (mm(g[...], wd[:, cols]) * gp[:, cols].astype(f32)).astype(bf16)

    def turn(src):
        @pl.loop(0, chunks)
        def _(i):
            cols = at(i * 256, 256, 128)
            turned[at(i * 256, 256, 16), :] = src[:, cols].astype(f32).T.astype(bf16)

    turn(g)

    @pl.loop(0, ff // 256)
    def _(i):
        cols = at(i * 256, 256, 128)
        wd[:, cols] = mm(turned[...], a[:, cols]).astype(bf16)

    grad_pair(3)
    rows_hop(0, 0, 1)

    @pl.loop(0, chunks)
    def _(i):
        cols = at(i * 256, 256, 128)
        num[:, cols] = mm(gp[...], wu[cols, :], NT)

    @pl.loop(0, 4)
    def _(i):
        rows = at(i * step, step, 16)
        e, rstd = statistics(mid[rows, :])
        grad = num[rows, :]
        vec[2:3, :] += jnp.sum(grad * e, 0, keepdims=True)
        vec[3:4, :] += jnp.sum(grad, 0, keepdims=True)
        total = g[rows, :].astype(f32) + norm_back(grad, e, rstd, nrm[2:3, :])
        mid[rows, :] = total
        gm[rows, :] = total.astype(bf16)

    grad_xy(3)

    @pl.loop(0, chunks)
    def _(i):
        cols = at(i * 256, 256, 128)
        back = mm(gm[...], wo[cols, :], NT)
        for side in range(2):
            cut = at(i * 256 + side * 128, 128, 128)
            grad = back[:, side * 128 : side * 128 + 128]
            inverse = rden[:, cut]
            dnum[:, cut] = (grad * inverse).astype(bf16)
            dden[:, cut] = -mm((grad * o[:, cut].astype(f32)).astype(bf16), ones64) * inverse

    @pl.loop(0, 2 * pairs)
    def _(i):
        b, p = i // pairs, lax.rem(i, pairs)
        rows = at(b * half_rows, half_rows, 16)
        cols = at(p * 128, 128, 128)
        queries = feat[0, rows, at(p * 256, 256, 128)]
        both = mm(queries, dnum[rows, cols], TN)
        states[b, at(p * 128, 128, 16), :] = near_far(first, both[:128], both[128:]).astype(bf16)
        slot = lax.broadcasted_iota(jnp.int32, (8, 128), 0) == b
        packed = dden[rows, cols]
        for odd in range(2):
            full = split_half(packed, first, odd)
            tall = jnp.sum(queries[:, odd * 128 : odd * 128 + 128].astype(f32) * full, 0, keepdims=True)
            z_buf[2 * p + odd] = jnp.where(slot, tall, z_buf[2 * p + odd])

    scan_out(4)

    turn(n2)

    @pl.loop(0, ff // 256)
    def _(i):
        cols = at(i * 256, 256, 128)
        wu[:, cols] = mm(turned[...], gp[:, cols]).astype(bf16)

    grad_pair(2)

    scan_back(4, True)
    rows_hop(0, 1, 1)

    @pl.loop(0, chunks)
    def _(i):
        cols = at(i * 256, 256, 128)
        wo[cols, :] = mm(o[:, cols].astype(f32).T.astype(bf16), gm[...]).astype(bf16)

    grad_pair(1)
    grad_mid(3)

    lane = lanes_of((1, 128))

    def extended(values, one, two, odd):
        base = 0 if odd else 64
        rest = jnp.where(lane == base, one, jnp.where(lane == base + 1, two, jnp.zeros_like(values)))
        return jnp.where(first, rest, values) if odd else jnp.where(first, values, rest)

    def block_maps(side, p):
        low_ = jnp.where(first, mx[side, 2 * p], jnp.zeros((64, 128), bf16))
        high_ = jnp.where(first, jnp.zeros((64, 128), bf16), -mx[side, 2 * p + 1])
        return jnp.concatenate([low_, high_], 0)

    def through_features(side, b, p, rows, cols, grads):
        logits = []
        for odd in range(2):
            prob = feat[side, rows, at(p * 256 + odd * 128, 128, 128)].astype(f32)
            grad = grads[odd]
            inner = mm((prob * grad).astype(bf16), ones64)
            both = prob * (grad - inner)
            other = pltpu.roll(both, 64, 1)
            logits.append(other - both if odd else both - other)
        packed = jnp.where(first, logits[0], logits[1]).astype(bf16)
        dproj[side, rows, cols] = mm(packed, block_maps(side, p), NT).astype(bf16)
        square = mm(qkv[side, rows, cols], packed, TN)
        small[side * pairs + p] += near_far(first, square[:64], square[64:])

    def exact(packed, odd):
        full = split_half(packed, first, odd)
        head = full.astype(bf16)
        return full, head, (full - head.astype(f32)).astype(bf16)

    @pl.loop(0, 2 * pairs)
    def _(i):
        b, p = i // pairs, lax.rem(i, pairs)
        rows = at(b * half_rows, half_rows, 16)
        cols = at(p * 128, 128, 128)
        values, grad_rows = qkv[2, rows, cols], dnum[rows, cols]
        packed = dden[rows, cols]
        before = prior[0, b, at(p * 128, 128, 16), :]
        mask = mask_of(b, False)
        unit = jnp.ones_like(values)
        grads = []
        for odd in range(2):
            full, head, tail = exact(packed, odd)
            left = extended(grad_rows, head, tail, odd)
            right = extended(values, unit, unit, odd)
            scores = (mm(left, right, NT) * mask).astype(bf16)
            total = mm(scores, feat[1, rows, at(p * 256 + odd * 128, 128, 128)])
            total = total + mm(own_half(grad_rows, first, odd), before, NT)
            grads.append(total + full * sums_pair(0, b, p, odd))
        through_features(0, b, p, rows, cols, grads)

    grad_xy(2)

    @pl.loop(0, chunks)
    def _(i):
        cols = at(i * 256, 256, 128)
        num[:, cols] = mm(dproj[0], wq[0, :, cols])

    def grad_of(i):
        kind, j = i // chunks, lax.rem(i, chunks)
        cols = at(j * 256, 256, 128)
        wq[kind, cols, :] = mm(dproj[kind, :, cols].astype(f32).T.astype(bf16), n1[...]).astype(bf16)

    pl.loop(0, chunks)(grad_of)
    grad_pair(4)
    scan_end(4)
    rows_hop(0, 0, 2)
    grad_z(3)

    def key_side(b, p):
        rows = pl.ds(b * half_rows, half_rows)
        cols = at(p * 128, 128, 128)
        values, grad_rows = qkv[2, rows, cols], dnum[rows, cols]
        packed = dden[rows, cols]
        after = prior[1, b, at(p * 128, 128, 16), :]
        mask = mask_of(b, True)
        unit = jnp.ones_like(values)
        value_grad = mm(feat[1, rows, at(p * 256, 256, 128)], pair_block(after, first))
        grads = []
        for odd in range(2):
            fcols = at(p * 256 + odd * 128, 128, 128)
            queries, keys = feat[0, rows, fcols], feat[1, rows, fcols]
            _full, head, tail = exact(packed, odd)
            left = extended(values, unit, unit, odd)
            right = extended(grad_rows, head, tail, odd)
            scores = (mm(left, right, NT) * mask).astype(bf16)
            total = mm(scores, queries) + mm(own_half(values, first, odd), after, NT)
            grads.append(total + sums_pair(1, b, p, odd))
            weights = (mm(keys, queries, NT) * mask).astype(bf16)
            value_grad = value_grad + mm(weights, own_half(grad_rows, first, odd))
        dproj[2, rows, cols] = value_grad.astype(bf16)
        through_features(1, b, p, rows, cols, grads)

    for b in range(2):
        @pl.loop(0, pairs)
        def _(p):
            key_side(b, p)

        if b == 0:
            grad_xy(1)
            rows_hop(0, 1, 2)
            grad_mid(2)
            grad_chain(3, 1)
            grad_xy(4)
        else:
            grad_mid(1)
            grad_mid(4)
            grad_z(2)
            grad_chain(3, 2)

        @pl.loop(0, chunks)
        def _(i):
            cols = at(i * 256, 256, 128)
            rows = pl.ds(b * half_rows, half_rows)
            total = num[rows, cols]
            for kind in range(1, 3):
                total = total + mm(dproj[kind, rows, :], wq[kind, :, cols])
            num[rows, cols] = total

        @pl.loop(2 * b, 2 * b + 2)
        def _(i):
            rows = at(i * step, step, 16)
            e, rstd = statistics(x[rows, :].astype(f32))
            grad = num[rows, :]
            vec[0:1, :] += jnp.sum(grad * e, 0, keepdims=True)
            vec[1:2, :] += jnp.sum(grad, 0, keepdims=True)
            rows_in[rows, :] = (mid[rows, :] + norm_back(grad, e, rstd, nrm[0:1, :])).astype(bf16)

        own_rows.append(fetch(rows_in.at[pl.ds(b * half_rows, half_rows)], all_in.at[b, t], local_sem.at[4 + b]))
        rows_hop(1, b, 0)

    lo_map = head_rows // 2
    put(small.at[:, at((1 - f) * lo_map, lo_map, 16), :], small_pair, small_sem.at[0], partner)
    put(vec.at[:, at((1 - f) * lo_norm, lo_norm, 128)], vec_pair, small_sem.at[1], partner)

    pl.loop(chunks, 3 * chunks)(grad_of)
    grad_pair(0)
    arrived(small_pair, small_sem.at[0])
    arrived(vec_pair, small_sem.at[1])
    for tt in range(4):
        for side in range(2):
            for q in range(2):
                p = side * pairs + pairs_of[tt] + q
                mine = small[p, at(f * lo_map, lo_map, 16), :] + small_pair[p]
                small_own[tt, 2 * side + q] = mine.astype(bf16)
    vec_own[...] = vec[:, at(f * lo_norm, lo_norm, 128)] + vec_pair[...]
    for k in range(1, 4):
        other = lax.rem(t + k, 4)
        put(small_own.at[other], small_in.at[t], small_sem.at[2], (f, c, other))
        put(vec_own, vec_in.at[t], small_sem.at[3], (f, c, other))
    own_small = [
        fetch(small_own.at[t], small_in.at[t], local_sem.at[6]),
        fetch(vec_own, vec_in.at[t], local_sem.at[7]),
    ]
    rows_hop(1, 0, 1)
    grad_last(3)
    grad_xy(0)
    grad_chain(2, 1)
    grad_z(1)
    grad_z(4)
    for copy in own_small:
        copy.wait()
    arrived(small_in.at[pl.ds(0, 3)], small_sem.at[2])
    arrived(vec_in.at[pl.ds(0, 3)], small_sem.at[3])
    total = small_in[0].astype(f32)
    sums = vec_in[0]
    for i in range(1, 4):
        total = total + small_in[i].astype(f32)
        sums = sums + vec_in[i]
    small_sum[...] = total.astype(bf16)
    vec_sum[...] = sums
    for j in range(1, 4):
        put(small_sum, small_all.at[c], small_sem.at[4], (f, c ^ j, t))
        put(vec_sum, vec_all.at[c], small_sem.at[5], (f, c ^ j, t))
    own_small = [
        fetch(small_sum, small_all.at[c], local_sem.at[6]),
        fetch(vec_sum, vec_all.at[c], local_sem.at[7]),
    ]
    rows_hop(1, 1, 1)
    grad_chain(2, 2)
    grad_chain(1, 1)
    grad_chain(4, 1)
    grad_mid(0)
    grad_last(2)
    grad_chain(1, 2)
    grad_chain(4, 2)
    grad_z(0)
    rows_hop(1, 0, 2)
    for copy in own_small:
        copy.wait()
    arrived(small_all.at[pl.ds(0, 3)], small_sem.at[4])
    arrived(vec_all.at[pl.ds(0, 3)], small_sem.at[5])
    total = small_all[0].astype(f32)
    sums = vec_all[0]
    for i in range(1, 4):
        total = total + small_all[i].astype(f32)
        sums = sums + vec_all[i]
    norms_out[...] = sums
    odd_slot = lax.rem(t, 2) == 1
    for side in range(2):
        near, far = total[2 * side], total[2 * side + 1]
        near_high, far_high = pltpu.roll(near, 64, 1), pltpu.roll(far, 64, 1)
        for j, (high, low) in enumerate(((near_high, near), (far, near_high), (far_high, far))):
            maps_out[side][j] = jnp.where(odd_slot, high, low)[:, :64]
    grad_chain(0, 1)
    grad_last(1)
    grad_last(4)
    rows_hop(1, 1, 2)
    grad_chain(0, 2)
    rows_hop(0, 0, 3)
    rows_hop(0, 1, 3)
    grad_last(0)
    for m in range(5):
        for j in range(1, 4):
            arrived(of(last, m), last_sem.at[m, j])
    rows_hop(1, 0, 3)
    rows_hop(1, 1, 3)
    for copy in own_rows:
        copy.wait()
    for copy in started:
        copy.wait_send()
    chains_sent()
    rows_sent(0)
    rows_sent(1)

def mesh_device(
    inputs,
    cotangent,
    picture_starts,
    qkv_weight,
    out_weight,
    up_weight,
    down_weight,
    query_map,
    key_map,
    first_gain,
    first_bias,
    second_gain,
    second_bias,
):
    micro, seq_local, seq_len, d = inputs.shape
    span = seq_len // 4
    rows = micro * seq_local * span
    ff = up_weight.shape[1] * 4
    heads = query_map.shape[0] * 4
    head = query_map.shape[2]
    own_block = lax.axis_index("context") * 4 + lax.axis_index("tensor")
    flags = jnp.any(picture_starts.reshape(micro, -1) // BLK == own_block, 1).astype(f32)
    flags = jnp.broadcast_to(flags[:, None, None], (micro, 8, span))
    maps = jnp.stack([query_map, key_map])
    maps = jnp.concatenate([maps, -maps], -1)
    norms = jnp.stack([first_gain, first_bias, second_gain, second_bias]).astype(f32)
    norms = jnp.concatenate([norms, jnp.zeros_like(norms)])
    dma = pltpu.SemaphoreType.DMA
    own = [(3, 4, d // 4, d // 2), (4, d // 4, d // 2), (d // 2, ff), (d // 2, ff)]
    sums = [(3, 4, d // 16, d // 2), (4, d // 16, d // 2), (d // 8, ff), (d // 8, ff)]
    last = [(3, d // 16, d // 2), (d // 16, d // 2), (d // 8, ff // 4), (d // 8, ff // 4)]
    outs = [(3, d // 4, d // 2), (d // 4, d // 2), (d // 2, ff // 4), (d // 2, ff // 4)]
    low = [(3, d, d), (d, d), (d, ff), (d, ff), (2, heads, head, 128)]
    state_rows = heads // 2 * 128
    pieces = (16, micro, state_rows // 16, 128)
    tiny = [(2 * (heads // 2), head, 128), (2 * (heads // 2), head // 2, 128), (4, 4, head // 2, 128)]
    maps_shape = (heads // 4, head // 2, head)
    scratch = [pltpu.VMEM(s, bf16) for s in low]
    scratch += [pltpu.VMEM((8, d), f32)]
    scratch += [pltpu.VMEM((rows, d), bf16)] * 3
    scratch += [pltpu.VMEM((3, rows, d), bf16), pltpu.VMEM((2, rows, heads * 128), bf16)]
    scratch += [pltpu.VMEM((2, micro, state_rows, 128), bf16), pltpu.VMEM((2, 16, 8, 128), f32)]
    scratch += [pltpu.VMEM((micro, state_rows, 128), bf16), pltpu.VMEM((16, 8, 128), f32)]
    scratch += [pltpu.VMEM(pieces, bf16), pltpu.VMEM((16, 8, 128), f32)] * 2
    scratch += [pltpu.VMEM((rows, d), bf16)] + [pltpu.VMEM((rows, d), f32)] * 3
    scratch += [pltpu.VMEM((rows, d), bf16)] + [pltpu.VMEM((rows, ff), bf16)] * 2
    scratch += [pltpu.VMEM((rows, d), bf16)] * 3 + [pltpu.VMEM((rows, d), f32)]
    scratch += [pltpu.VMEM((3, rows, d), bf16), pltpu.VMEM((rows, d), bf16), pltpu.VMEM((d, rows), bf16)]
    scratch += [pltpu.VMEM(s, bf16) for s in own]
    scratch += [pltpu.VMEM((3,) + s, bf16) for s in sums]
    scratch += [pltpu.VMEM(s, bf16) for s in sums]
    scratch += [pltpu.VMEM((6,) + s, bf16) for s in last]
    scratch += [pltpu.VMEM(s, bf16) for s in last]
    scratch += [pltpu.VMEM(s, f32) for s in tiny[:2]] + [pltpu.VMEM(tiny[2], bf16)] * 2
    scratch += [pltpu.VMEM(tiny[2][1:], bf16), pltpu.VMEM(tiny[2], bf16)]
    scratch += [pltpu.VMEM(s, f32) for s in ((8, d), (8, d // 2), (8, d // 2), (4, 8, d // 2), (8, d // 2), (4, 8, d // 2))]
    scratch += [dma((16,)), dma(()), dma((8,)), dma((5, 4)), dma((5, 4, 4)), dma((5,))]
    scratch += [dma((8,)), dma((2, 2, 3, 2, 2)), dma((5,)), dma((5, 2, 3)), dma((5, 6)), dma((5, 4)), dma((6,))]
    spread_rows = (micro, 4, span, d)
    anywhere = pl.BlockSpec(memory_space=pl.ANY)
    all_out, all_in, share_0, share_1, share_2, share_3, map_0, map_1, norm_grads = pl.pallas_call(
        layer_kernel,
        out_shape=[jax.ShapeDtypeStruct(spread_rows, bf16)] * 2
        + [jax.ShapeDtypeStruct(s, bf16) for s in outs]
        + [jax.ShapeDtypeStruct(maps_shape, f32)] * 2
        + [jax.ShapeDtypeStruct((8, d // 2), f32)],
        in_specs=[anywhere] * 2 + [pl.BlockSpec(memory_space=pltpu.VMEM)] + [anywhere] * 6,
        out_specs=[anywhere] * 6 + [pl.BlockSpec(memory_space=pltpu.VMEM)] * 3,
        scratch_shapes=scratch,
        compiler_params=pltpu.CompilerParams(collective_id=0, has_side_effects=True, vmem_limit_bytes=67043328),
        name="layer",
    )(inputs, cotangent, flags, maps, norms, qkv_weight.transpose(0, 2, 1), out_weight, up_weight, down_weight.T)
    return (
        all_out.reshape(inputs.shape),
        all_in.reshape(inputs.shape).astype(f32),
        share_0.astype(f32).transpose(0, 2, 1),
        share_1.astype(f32),
        share_2.astype(f32),
        share_3.astype(f32).T,
        map_0,
        map_1,
        norm_grads[0],
        norm_grads[1],
        norm_grads[2],
        norm_grads[3],
    )


def solution(mesh):
    in_specs = (
        P(None, "fsdp", "context", None),
        P(None, "fsdp", "context", None),
        P(None, "fsdp", None),
        P(None, "fsdp", "tensor"),
        P("tensor", "fsdp"),
        P("fsdp", "tensor"),
        P("tensor", "fsdp"),
        P("tensor", "fsdp", None),
        P("tensor", "fsdp", None),
        P("fsdp"),
        P("fsdp"),
        P("fsdp"),
        P("fsdp"),
    )
    out_specs = (
        P(None, "fsdp", "context", None),
        P(None, "fsdp", "context", None),
        P(None, "fsdp", "tensor"),
        P("tensor", "fsdp"),
        P("fsdp", "tensor"),
        P("tensor", "fsdp"),
        P("tensor", "fsdp", None),
        P("tensor", "fsdp", None),
        P("fsdp"),
        P("fsdp"),
        P("fsdp"),
        P("fsdp"),
    )
    sizes = tuple(mesh.shape[name] for name in EVERY)
    return jax.shard_map(
        mesh_device if sizes == (2, 4, 4) else per_device, mesh=mesh, in_specs=in_specs, out_specs=out_specs, check_vma=False
    )
```

```python
import jax
import jax.numpy as jnp
from jax import lax
from jax.experimental import pallas as pl
from jax.experimental.pallas import tpu as pltpu
from jax.sharding import PartitionSpec as P

BLK = 256
MICRO = 2


epsilon = 1e-05
highest = lax.Precision.HIGHEST


EVERY = ("fsdp", "context", "tensor")


def carried_in(value, backward):
    slot, mine = lax.axis_index("tensor"), lax.axis_index("context")
    near = lax.all_gather(value, "tensor")
    far = lax.all_gather(jnp.sum(near, 0).astype(value.dtype), "context")
    near_ids = jnp.arange(near.shape[0]).reshape((-1,) + (1,) * value.ndim)
    far_ids = jnp.arange(far.shape[0]).reshape((-1,) + (1,) * value.ndim)
    near_mask = near_ids > slot if backward else near_ids < slot
    far_mask = far_ids > mine if backward else far_ids < mine
    near, far = near.astype(jnp.float32), far.astype(jnp.float32)
    return jnp.sum(jnp.where(near_mask, near, 0.0), 0) + jnp.sum(jnp.where(far_mask, far, 0.0), 0)


def layer_norm(values, norm_gain, norm_bias):
    center = values - jnp.mean(values, -1, keepdims=True)
    spread = jnp.mean(center * center, -1, keepdims=True)
    return center * lax.rsqrt(spread + epsilon) * norm_gain + norm_bias


def features(logits):
    return jnp.concatenate([jax.nn.softmax(logits, -1), jax.nn.softmax(-logits, -1)], -1)


def gelu_tanh(values):
    return jax.nn.gelu(values, approximate=True)


def prefix_before(values):
    running = jnp.cumsum(values, 1)
    return jnp.concatenate([jnp.zeros_like(values[:, :1]), running[:, :-1]], 1)


def suffix_after(values):
    running = jnp.flip(jnp.cumsum(jnp.flip(values, 1), 1), 1)
    return jnp.concatenate([running[:, 1:], jnp.zeros_like(values[:, :1])], 1)


def spread(part, axis, parts):
    own = lax.axis_index("context")
    size = part.shape[axis] // parts
    mine = lax.dynamic_slice_in_dim(part, own * size, size, axis)
    return lax.all_gather(mine, EVERY)


def full_in(part):
    pieces = spread(part, 1, lax.axis_size("context"))
    fsdp, ctx, tens = (lax.axis_size(name) for name in EVERY)
    pieces = pieces.reshape((fsdp, ctx, tens) + pieces.shape[1:])
    pieces = pieces.transpose(3, 0, 1, 4, 2, 5)
    return pieces.reshape(pieces.shape[0], -1, pieces.shape[4] * pieces.shape[5])


def share_in(grad):
    fsdp, ctx, tens = (lax.axis_size(name) for name in EVERY)
    kinds, rows, cols = grad.shape
    pieces = grad.astype(jnp.bfloat16).reshape(kinds, fsdp, ctx, rows // fsdp // ctx, tens, cols // tens)
    pieces = pieces.transpose(1, 2, 4, 0, 3, 5).reshape((-1,) + (kinds, rows // fsdp // ctx, cols // tens))
    mine = lax.psum_scatter(pieces, EVERY, scatter_dimension=0)
    return lax.all_gather(mine, "context", axis=1, tiled=True).astype(jnp.float32)


def full_rows(part):
    pieces = spread(part, 0, lax.axis_size("context"))
    fsdp, ctx, tens = (lax.axis_size(name) for name in EVERY)
    pieces = pieces.reshape((fsdp, ctx, tens) + pieces.shape[1:])
    pieces = pieces.transpose(2, 1, 3, 0, 4)
    return pieces.reshape(tens * part.shape[0], -1)


def share_rows(grad):
    fsdp, ctx, tens = (lax.axis_size(name) for name in EVERY)
    rows, cols = grad.shape
    pieces = grad.astype(jnp.bfloat16).reshape(tens, ctx, rows // tens // ctx, fsdp, cols // fsdp)
    pieces = pieces.transpose(3, 1, 0, 2, 4).reshape(-1, rows // tens // ctx, cols // fsdp)
    mine = lax.psum_scatter(pieces, EVERY, scatter_dimension=0)
    return lax.all_gather(mine, "context", axis=0, tiled=True).astype(jnp.float32)


def full_maps(part):
    pieces = lax.all_gather(part, ("fsdp", "tensor"))
    fsdp, tens = lax.axis_size("fsdp"), lax.axis_size("tensor")
    pieces = pieces.reshape((fsdp, tens) + part.shape).transpose(1, 2, 0, 3, 4)
    return pieces.reshape(tens * part.shape[0], fsdp * part.shape[1], part.shape[2])


def own_maps(total):
    fsdp, tens = lax.axis_size("fsdp"), lax.axis_size("tensor")
    heads, rows, _ = total.shape
    mine = lax.dynamic_slice_in_dim(total, lax.axis_index("tensor") * (heads // tens), heads // tens, 0)
    return lax.dynamic_slice_in_dim(mine, lax.axis_index("fsdp") * (rows // fsdp), rows // fsdp, 1)


def per_device(
    inputs,
    cotangent,
    picture_starts,
    qkv_weight,
    out_weight,
    up_weight,
    down_weight,
    query_map,
    key_map,
    first_gain,
    first_bias,
    second_gain,
    second_bias,
):
    tensor_size = lax.axis_size("tensor")
    micro, seq_local, seq_len, model_width = inputs.shape
    span = seq_len // tensor_size
    slot = lax.axis_index("tensor")
    head_size = query_map.shape[2]
    feat_size = 2 * head_size
    blocks_local = span // BLK
    seq_count = micro * seq_local
    block_total = seq_count * blocks_local
    row_count = seq_count * span
    first_block = (lax.axis_index("context") * tensor_size + slot) * blocks_local
    block_ids = first_block + jnp.arange(blocks_local, dtype=jnp.int32)
    position = jnp.arange(BLK, dtype=jnp.int32)
    causal = position[None, :] <= position[:, None]

    in_full = full_in(qkv_weight)
    out_full = full_rows(out_weight)
    up_full = full_in(up_weight[None])[0]
    down_full = full_rows(down_weight)
    qmap_full, kmap_full = full_maps(query_map), full_maps(key_map)
    norms = lax.all_gather(jnp.stack([first_gain, first_bias, second_gain, second_bias]), "fsdp", axis=1, tiled=True)
    gain_first, bias_first, gain_second, bias_second = norms.astype(jnp.float32)

    def own(values):
        mine = lax.dynamic_slice_in_dim(values, slot * span, span, 2)
        return mine.reshape(row_count, model_width)

    source = own(inputs).astype(jnp.float32)
    starts_here = picture_starts.reshape(seq_count, -1)
    block_flags = (
        jnp.sum((starts_here[:, :, None] // BLK == block_ids[None, None, :]).astype(jnp.int32), 1)
        > 0
    )
    allowed = causal[None, None] | block_flags[:, :, None, None]
    allowed = allowed.reshape(block_total, 1, BLK, BLK)
    normed_one = layer_norm(source, gain_first, bias_first)
    normed_low = normed_one.astype(jnp.bfloat16)
    projected = jnp.einsum(
        "rd,cde->cre", normed_low, in_full, preferred_element_type=jnp.float32
    ).astype(jnp.bfloat16)
    heads_local = projected.shape[2] // head_size
    queries = projected[0].reshape(row_count, heads_local, head_size)
    key_rows = projected[1].reshape(row_count, heads_local, head_size)
    value_rows = projected[2].reshape(row_count, heads_local, head_size)
    query_logits = jnp.einsum(
        "rhi,hij->rhj", queries, qmap_full, preferred_element_type=jnp.float32
    )
    key_logits = jnp.einsum(
        "rhi,hij->rhj", key_rows, kmap_full, preferred_element_type=jnp.float32
    )
    query_blocks = (
        features(query_logits)
        .astype(jnp.bfloat16)
        .reshape(block_total, BLK, heads_local, feat_size)
    )
    key_blocks = (
        features(key_logits)
        .astype(jnp.bfloat16)
        .reshape(block_total, BLK, heads_local, feat_size)
    )
    value_blocks = value_rows.reshape(block_total, BLK, heads_local, head_size)
    scores = jnp.einsum(
        "nthf,nshf->nhts", query_blocks, key_blocks, preferred_element_type=jnp.float32
    )
    weights_low = jnp.where(allowed, scores, 0.0).astype(jnp.bfloat16)
    states = jnp.einsum(
        "nshf,nshe->nhfe", key_blocks, value_blocks, preferred_element_type=jnp.float32
    )
    states = states.reshape(seq_count, blocks_local, heads_local, feat_size, head_size)
    key_sums = jnp.sum(key_blocks.astype(jnp.float32), 1).reshape(
        seq_count, blocks_local, heads_local, feat_size
    )
    state_total = jnp.sum(states, 1)
    sums_total = jnp.sum(key_sums, 1)
    carried = carried_in(state_total.astype(jnp.bfloat16), False)
    carried_sums = carried_in(sums_total, False)
    prior_states = (carried[:, None] + prefix_before(states)).astype(jnp.bfloat16)
    prior_states = prior_states.reshape(block_total, heads_local, feat_size, head_size)
    prior_sums = (carried_sums[:, None] + prefix_before(key_sums)).reshape(
        block_total, heads_local, feat_size
    )
    numerator = jnp.einsum(
        "nhts,nshe->nthe", weights_low, value_blocks, preferred_element_type=jnp.float32
    )
    numerator = numerator + jnp.einsum(
        "nthf,nhfe->nthe", query_blocks, prior_states, preferred_element_type=jnp.float32
    )
    denominator = jnp.sum(weights_low.astype(jnp.float32), -1).transpose(0, 2, 1)
    denominator = denominator + jnp.einsum(
        "nthf,nhf->nth", query_blocks.astype(jnp.float32), prior_sums, precision=highest
    )
    mixed_heads = (
        (numerator / denominator[..., None])
        .astype(jnp.bfloat16)
        .reshape(row_count, heads_local * head_size)
    )
    attended = jnp.dot(mixed_heads, out_full, preferred_element_type=jnp.float32)
    middle = source + attended
    normed_two = layer_norm(middle, gain_second, bias_second)
    normed_two_low = normed_two.astype(jnp.bfloat16)
    hidden_pre = jnp.dot(normed_two_low, up_full, preferred_element_type=jnp.float32)
    hidden_low = gelu_tanh(hidden_pre).astype(jnp.bfloat16)
    branch = jnp.dot(hidden_low, down_full, preferred_element_type=jnp.float32)
    output = (middle + branch).astype(jnp.bfloat16).reshape(micro, seq_local, span, model_width)
    output = lax.all_gather(output, "tensor", axis=2, tiled=True)
    upstream_low = own(cotangent)
    upstream = upstream_low.astype(jnp.float32)
    grad_down = jnp.einsum(
        "rk,rd->kd", hidden_low, upstream_low, preferred_element_type=jnp.float32
    )
    hidden_grad = jnp.einsum(
        "rd,kd->rk", upstream_low, down_full, preferred_element_type=jnp.float32
    )
    gelu_result, gelu_pull = jax.vjp(gelu_tanh, hidden_pre)
    pre_grad = gelu_pull(hidden_grad)[0].astype(jnp.bfloat16)
    grad_up = jnp.einsum(
        "rd,rf->df", normed_two_low, pre_grad, preferred_element_type=jnp.float32
    )
    normed_two_grad = jnp.einsum(
        "rf,df->rd", pre_grad, up_full, preferred_element_type=jnp.float32
    )
    norm_result, second_pull = jax.vjp(layer_norm, middle, gain_second, bias_second)
    middle_part, grad_gain_second, grad_bias_second = second_pull(normed_two_grad)
    middle_grad = upstream + middle_part
    middle_low = middle_grad.astype(jnp.bfloat16)
    grad_out = jnp.einsum(
        "rk,rd->kd", mixed_heads, middle_low, preferred_element_type=jnp.float32
    )
    mixed_grad = jnp.einsum(
        "rd,kd->rk", middle_low, out_full, preferred_element_type=jnp.float32
    )
    mixed_grad = mixed_grad.reshape(block_total, BLK, heads_local, head_size)
    numer_grad = (mixed_grad / denominator[..., None]).astype(jnp.bfloat16)
    denom_grad = -jnp.sum(mixed_grad * numerator, -1) / (denominator * denominator)
    weight_grad = jnp.einsum(
        "nthe,nshe->nhts", numer_grad, value_blocks, preferred_element_type=jnp.float32
    )
    weight_grad = weight_grad + denom_grad.transpose(0, 2, 1)[..., None]
    weight_grad_low = jnp.where(allowed, weight_grad, 0.0).astype(jnp.bfloat16)
    value_grad = jnp.einsum(
        "nhts,nthe->nshe", weights_low, numer_grad, preferred_element_type=jnp.float32
    )
    query_grad = jnp.einsum(
        "nhts,nshf->nthf", weight_grad_low, key_blocks, preferred_element_type=jnp.float32
    )
    query_grad = query_grad + jnp.einsum(
        "nthe,nhfe->nthf", numer_grad, prior_states, preferred_element_type=jnp.float32
    )
    query_grad = query_grad + denom_grad[..., None] * prior_sums[:, None]
    key_grad = jnp.einsum(
        "nhts,nthf->nshf", weight_grad_low, query_blocks, preferred_element_type=jnp.float32
    )
    prior_grad = jnp.einsum(
        "nthf,nthe->nhfe", query_blocks, numer_grad, preferred_element_type=jnp.float32
    )
    prior_grad = prior_grad.reshape(seq_count, blocks_local, heads_local, feat_size, head_size)
    prior_sums_grad = jnp.einsum(
        "nthf,nth->nhf", query_blocks.astype(jnp.float32), denom_grad, precision=highest
    )
    prior_sums_grad = prior_sums_grad.reshape(seq_count, blocks_local, heads_local, feat_size)
    grad_total = jnp.sum(prior_grad, 1)
    grad_sums_total = jnp.sum(prior_sums_grad, 1)
    later_states = carried_in(grad_total.astype(jnp.bfloat16), True)
    later_sums = carried_in(grad_sums_total, True)
    state_grad = (later_states[:, None] + suffix_after(prior_grad)).astype(jnp.bfloat16)
    state_grad = state_grad.reshape(block_total, heads_local, feat_size, head_size)
    sums_grad = (later_sums[:, None] + suffix_after(prior_sums_grad)).reshape(
        block_total, heads_local, feat_size
    )
    key_grad = key_grad + jnp.einsum(
        "nshe,nhfe->nshf", value_blocks, state_grad, preferred_element_type=jnp.float32
    )
    key_grad = key_grad + sums_grad[:, None]
    value_grad = value_grad + jnp.einsum(
        "nshf,nhfe->nshe", key_blocks, state_grad, preferred_element_type=jnp.float32
    )
    query_feat_now, query_pull = jax.vjp(features, query_logits)
    query_logit_grad = query_pull(query_grad.reshape(row_count, heads_local, feat_size))[
        0
    ].astype(jnp.bfloat16)
    key_feat_now, key_pull = jax.vjp(features, key_logits)
    key_logit_grad = key_pull(key_grad.reshape(row_count, heads_local, feat_size))[0].astype(
        jnp.bfloat16
    )
    grad_qmap = jnp.einsum(
        "rhi,rhj->hij", queries, query_logit_grad, preferred_element_type=jnp.float32
    )
    grad_kmap = jnp.einsum(
        "rhi,rhj->hij", key_rows, key_logit_grad, preferred_element_type=jnp.float32
    )
    raw_query_grad = jnp.einsum(
        "rhj,hij->rhi", query_logit_grad, qmap_full, preferred_element_type=jnp.float32
    )
    raw_key_grad = jnp.einsum(
        "rhj,hij->rhi", key_logit_grad, kmap_full, preferred_element_type=jnp.float32
    )
    projected_grad = jnp.stack(
        [
            raw_query_grad.reshape(row_count, -1),
            raw_key_grad.reshape(row_count, -1),
            value_grad.reshape(row_count, -1),
        ]
    ).astype(jnp.bfloat16)
    grad_in = jnp.einsum(
        "rd,cre->cde", normed_low, projected_grad, preferred_element_type=jnp.float32
    )
    normed_one_grad = jnp.einsum(
        "cre,cde->rd", projected_grad, in_full, preferred_element_type=jnp.float32
    )
    first_result, first_pull = jax.vjp(layer_norm, source, gain_first, bias_first)
    source_part, grad_gain_first, grad_bias_first = first_pull(normed_one_grad)
    input_grad = (middle_grad + source_part).astype(jnp.bfloat16)
    input_grad = input_grad.reshape(micro, seq_local, span, model_width)
    input_grad = lax.all_gather(input_grad, "tensor", axis=2, tiled=True).astype(jnp.float32)
    norm_grads = jnp.stack([grad_gain_first, grad_bias_first, grad_gain_second, grad_bias_second])
    grad_qmap, grad_kmap, norm_grads = lax.psum((grad_qmap, grad_kmap, norm_grads), EVERY)
    share = first_gain.shape[0]
    norm_grads = lax.dynamic_slice_in_dim(norm_grads, lax.axis_index("fsdp") * share, share, 1)
    return (
        output,
        input_grad,
        share_in(grad_in),
        share_rows(grad_out),
        share_in(grad_up[None])[0],
        share_rows(grad_down),
        own_maps(grad_qmap),
        own_maps(grad_kmap),
        norm_grads[0],
        norm_grads[1],
        norm_grads[2],
        norm_grads[3],
    )


MESH = pl.DeviceIdType.MESH
bf16 = jnp.bfloat16
f32 = jnp.float32


def whereabouts():
    return tuple(lax.axis_index(name) for name in EVERY)


def neighbours(f, c, t):
    n = c * 4 + t
    peers = [(1 - f, c, t)]
    for k in range(1, 16):
        other = lax.rem(n + k, 16)
        peers.append((f, other // 4, lax.rem(other, 4)))
    for k in range(1, 4):
        peers.append((1 - f, c, lax.rem(t + k, 4)))
    return peers


def meet(f, c, t):
    barrier = pltpu.get_barrier_semaphore()
    peers = neighbours(f, c, t)
    for peer in peers:
        pl.semaphore_signal(barrier, inc=1, device_id=peer, device_id_type=MESH)
    pl.semaphore_wait(barrier, len(peers))


def send(src, dst, send_sem, recv_sem, peer):
    copy = pltpu.make_async_remote_copy(
        src_ref=src, dst_ref=dst, send_sem=send_sem, recv_sem=recv_sem,
        device_id=peer, device_id_type=MESH,
    )
    copy.start()
    return copy


def arrived(ref, sem):
    pltpu.make_async_copy(ref, ref, sem).wait()


def at(start, size, unit):
    return pl.ds(pl.multiple_of(start, unit), size)


GROUPS = (0, 4, 1, 2, 3)


def of(refs, m, *index):
    ref = refs[m % 4].at[index] if index else refs[m % 4]
    return ref.at[kinds(m)] if m % 4 == 0 else ref


def kinds(m):
    return pl.ds(1, 2) if m == 0 else pl.ds(0, 1)


def kind_count(m):
    return 2 if m == 0 else 1


def half(ref, m, f):
    if m % 4 == 0:
        w = ref.shape[2] // 2
        return ref.at[:, :, at(f * w, w, 128)]
    if m == 1:
        w = ref.shape[1] // 2
        return ref.at[:, at(f * w, w, 128)]
    w = ref.shape[0] // 2
    return ref.at[at(f * w, w, 16), :]


def shard(ref, m, f, t):
    if m % 4 == 0:
        w, h = ref.shape[2] // 2, ref.shape[1] // 4
        return ref.at[:, at(t * h, h, 16), at(f * w, w, 128)]
    if m == 1:
        w, h = ref.shape[1] // 2, ref.shape[0] // 4
        return ref.at[at(t * h, h, 16), at(f * w, w, 128)]
    h, w = ref.shape[0] // 2, ref.shape[1] // 4
    return ref.at[at(f * h, h, 16), at(t * w, w, 128)]


def piece(ref, m, f, c, t):
    if m % 4 == 0:
        w, h = ref.shape[2] // 2, ref.shape[1] // 16
        return ref.at[:, at(t * 4 * h + c * h, h, 16), at(f * w, w, 128)]
    if m == 1:
        w, h = ref.shape[1] // 2, ref.shape[0] // 16
        return ref.at[at(t * 4 * h + c * h, h, 16), at(f * w, w, 128)]
    h, w = ref.shape[0] // 8, ref.shape[1] // 4
    return ref.at[at(f * 4 * h + c * h, h, 16), at(t * w, w, 128)]


def quarter(ref, m, c):
    if m % 4 == 0:
        h = ref.shape[1] // 4
        return ref.at[:, at(c * h, h, 16), :]
    h = ref.shape[0] // 4
    return ref.at[at(c * h, h, 16), :]


def context_part(ref, m, c):
    if m % 4 == 0:
        h = ref.shape[2] // 4
        return ref.at[:, :, at(c * h, h, 16), :]
    if m == 1:
        h = ref.shape[1] // 4
        return ref.at[:, at(c * h, h, 16), :]
    h = ref.shape[0] // 4
    return ref.at[at(c * h, h, 16), :]


def two_of(ref, m, side):
    if m % 4 == 0:
        return ref.at[:, pl.ds(2 * side, 2)]
    if m == 1:
        return ref.at[pl.ds(2 * side, 2)]
    w = ref.shape[1] // 2
    return ref.at[:, pl.ds(side * w, w)]


def tensor_part(ref, m, t):
    if m % 4 == 0:
        return ref.at[:, t]
    if m == 1:
        return ref.at[t]
    w = ref.shape[1] // 4
    return ref.at[:, at(t * w, w, 128)]


NN = (((1,), (0,)), ((), ()))
NT = (((1,), (1,)), ((), ()))
TN = (((0,), (0,)), ((), ()))


def mm(a, b, dims=NN):
    return lax.dot_general(a, b, dims, preferred_element_type=f32)


def lanes_of(shape):
    return lax.broadcasted_iota(jnp.int32, shape, len(shape) - 1)


def block_ones(size, group):
    row = lax.broadcasted_iota(jnp.int32, (size, size), 0) // group
    col = lax.broadcasted_iota(jnp.int32, (size, size), 1) // group
    return jnp.where(row == col, 1.0, 0.0).astype(bf16)


def statistics(rows):
    center = rows - jnp.mean(rows, -1, keepdims=True)
    rstd = lax.rsqrt(jnp.mean(center * center, -1, keepdims=True) + epsilon)
    return center * rstd, rstd


def norm_back(grad, e, rstd, gain):
    w = grad * gain
    return rstd * (w - jnp.mean(w, -1, keepdims=True) - e * jnp.mean(w * e, -1, keepdims=True))


def near_far(first, low, high):
    return jnp.where(first, low, high)


def own_half(values, first, odd):
    zero = jnp.zeros_like(values)
    return jnp.where(first, zero, values) if odd else jnp.where(first, values, zero)


def pair_block(values, first):
    return jnp.concatenate([own_half(values, first, 0), own_half(values, first, 1)], 0)


def split_half(full, first, odd):
    other = pltpu.roll(full, 64, 1)
    return jnp.where(first, other, full) if odd else jnp.where(first, full, other)


def layer_kernel(*refs):
    inputs, cotangent, starts, own_maps_in = *refs[:3], refs[3:5]
    norms_in, shards, down = refs[5:9], refs[9:12], refs[12]
    flags, maps, norms = refs[-3:]
    refs = refs[4:-3]
    all_out, all_in = refs[9:11]
    outs, maps_out, norms_out = refs[11:15], refs[15:17], refs[17]
    w, mx, nrm, x, g, n1, qkv, feat = refs[18:22], *refs[22:29]
    prior, sums_in, states, z_buf, s_in, z_in, s_out, z_out = refs[29:37]
    o, rden, num, mid, n2, a, gp, rows_out = refs[37:45]
    gm, dnum, dden, dproj, rows_in, turned = refs[45:51]
    pair_in, xy_in, part, tz_in, last = (refs[51 + 4 * i : 55 + 4 * i] for i in range(5))
    small, small_pair, small_own, small_in, small_sum, small_all = refs[71:77]
    vec, vec_pair, vec_own, vec_in, vec_sum, vec_all = refs[77:83]
    local_sem, send_sem, extra_sem, z_sem, xy_sem, pair_sem = refs[83:89]
    scan_sem, rows_sem, gpair_sem, gxy_sem, gz_sem, last_sem, small_sem = refs[89:96]
    wq, wo, wu, wd = w
    d = x.shape[1]
    ff = a.shape[1]
    half_rows = x.shape[0] // 2
    shards = (*shards, gm.at[pl.ds(0, d // 2)])
    f, c, t = whereabouts()
    n = c * 4 + t
    peers = neighbours(f, c, t)
    partner = peers[0]
    started = []

    def put(src, dst, recv_sem, peer):
        started.append(send(src, dst, send_sem, recv_sem, peer))

    started_if = []

    def put_if(pred, src, dst, recv_sem, peer):
        def copy():
            return pltpu.make_async_remote_copy(
                src_ref=src, dst_ref=dst, send_sem=send_sem, recv_sem=recv_sem, device_id=peer, device_id_type=MESH,
            )

        @pl.when(pred)
        def _():
            copy().start()

        started_if.append((pred, copy))

    fetched = []

    def fetch(src, dst, sem):
        copy = pltpu.make_async_copy(src, dst, sem)
        copy.start()
        return copy

    for i in range(2):
        rows = pl.ds(i * half_rows, half_rows)
        fetched.append(fetch(inputs.at[i, 0, at(t * half_rows, half_rows, 16), :], x.at[rows], local_sem.at[i]))
        fetched.append(fetch(cotangent.at[i, 0, at(t * half_rows, half_rows, 16), :], g.at[rows], local_sem.at[2 + i]))
    h3 = maps.shape[1]
    head_rows = small.shape[1]
    pairs_of = (0, 1, 3, 4)
    lo_norm = d // 2

    def map_place(ff_, tt):
        return mx.at[:, pl.ds(tt * h3, h3), at(ff_ * 32, 32, 16), :]

    def norm_place(ff_):
        return nrm.at[:, at(ff_ * lo_norm, lo_norm, 128)]

    for side in range(2):
        own_map = own_maps_in[side][...]
        maps[side] = jnp.concatenate([own_map, -own_map], -1)
    norms[...] = jnp.zeros_like(norms)
    for i in range(4):
        norms[i : i + 1, :] = norms_in[i][...].astype(f32).reshape(1, -1)
    fetched.append(fetch(maps, map_place(f, t), local_sem.at[4]))
    fetched.append(fetch(norms, norm_place(f), local_sem.at[5]))
    shard_copies = {m: fetch(of(shards, m), shard(of(w, m), m, f, t), local_sem.at[6 + m]) for m in (0, 4, 1, 2)}
    down_rows = turned.at[:, pl.ds(0, d // 2)]
    down_copy = fetch(down, down_rows, local_sem.at[11])
    z_buf[...] = jnp.zeros_like(z_buf)
    for b in range(2):
        hits = jnp.where(starts[b] == n * BLK, 1.0, 0.0)
        flags[b] = jnp.broadcast_to(jnp.max(hits, -1, keepdims=True), flags.shape[1:])
    small[...] = jnp.zeros_like(small)
    vec[...] = jnp.zeros_like(vec)
    meet(f, c, t)

    put(norms, norm_place(f), extra_sem.at[0], partner)
    put(maps, map_place(f, t), extra_sem.at[4], partner)
    for m in GROUPS:
        if m == 3:
            down_copy.wait()
            for i in range(0, ff // 4, 256):
                gm[0 : d // 2, i : i + 256] = turned[i : i + 256, 0 : d // 2].astype(f32).T.astype(bf16)
            shard_copies[3] = fetch(shards[3], shard(w[3], 3, f, t), local_sem.at[9])
        for k, pred in ((2, None), (1, t != 3), (3, t != 0)):
            src, dst = quarter(of(shards, m), m, c), piece(of(w, m), m, f, c, t)
            peer = (f, c, lax.rem(t + k, 4))
            if pred is None:
                put(src, dst, z_sem.at[m, k], peer)
            else:
                put_if(pred, src, dst, z_sem.at[m, k], peer)
        if m == 0:
            for k in range(1, 4):
                put(maps, map_place(f, t), extra_sem.at[k], (f, c, lax.rem(t + k, 4)))
    for m in GROUPS:
        put(of(shards, m), shard(of(w, m), m, f, t), pair_sem.at[m], partner)

    def forward(m, k):
        got = piece(of(w, m), m, f, c, lax.rem(t + 4 - k, 4))
        arrived(got, z_sem.at[m, k])
        if k == 2:
            put_if(t == 2, got, got, z_sem.at[m, 3], (f, c, t + 1))
            put_if(t == 1, got, got, z_sem.at[m, 1], (f, c, t - 1))
        for j in range(1, 3):
            put(got, got, xy_sem.at[m, k, j], (f, c ^ j, t))
        put(got, got, pair_sem.at[m], partner)

    def relay(m, k):
        for j in range(1, 3):
            got = piece(of(w, m), m, f, c ^ j, lax.rem(t + 4 - k, 4))
            arrived(got, xy_sem.at[m, k, j])
            if ((0, 1, 2, 3, 1)[m] + k + j) % 2:
                put(got, got, xy_sem.at[m, k, 3], (f, c ^ 3 ^ j, t))
            put(got, got, pair_sem.at[m], partner)

    def across(m):
        for k in range(1, 4):
            got = piece(of(w, m), m, f, c ^ 3, lax.rem(t + 4 - k, 4))
            arrived(got, xy_sem.at[m, k, 3])
            put(got, got, pair_sem.at[m], partner)

    def take_maps():
        for k in range(1, 4):
            got = map_place(f, lax.rem(t + 4 - k, 4))
            arrived(got, extra_sem.at[k])
            put(got, got, extra_sem.at[4 + k], partner)

    def maps_here():
        for k in range(4):
            arrived(map_place(1 - f, lax.rem(t + 4 - k, 4)), extra_sem.at[4 + k])

    def complete(m):
        shard_copies[m].wait()
        arrived(half(of(w, m), m, 1 - f), pair_sem.at[m])

    for k in (2, 1, 3):
        forward(0, k)
    for copy in fetched:
        copy.wait()
    arrived(norm_place(1 - f), extra_sem.at[0])
    first = lanes_of((1, 128)) < 64
    ones64 = block_ones(128, 64)
    step = half_rows // 2

    @pl.loop(0, 4)
    def _(i):
        rows = at(i * step, step, 16)
        e, _unused = statistics(x[rows, :].astype(f32))
        n1[rows, :] = (e * nrm[0:1, :] + nrm[1:2, :]).astype(bf16)

    take_maps()
    for k in (2, 1, 3):
        relay(0, k)
        forward(4, k)
    for k in (2, 1, 3):
        forward(1, k)
    across(0)
    forward(2, 2)
    complete(0)

    chunks = d // 256

    def project(i):
        kind, j = i // chunks, lax.rem(i, chunks)
        cols = at(j * 256, 256, 128)
        qkv[kind, :, cols] = mm(n1[...], wq[kind, cols, :], NT).astype(bf16)

    pl.loop(chunks, 3 * chunks)(project)

    for k in (2, 1, 3):
        relay(4, k)
    forward(2, 1)
    maps_here()

    pairs = d // 128

    def pair_map(side, p):
        zero = jnp.zeros((64, 128), bf16)
        top = jnp.concatenate([mx[side, 2 * p], zero], 1)
        bottom = jnp.concatenate([zero, mx[side, 2 * p + 1]], 1)
        return jnp.concatenate([top, bottom], 0)

    def features_of(side, i):
        b, p = i // pairs, lax.rem(i, pairs)
        rows = at(b * half_rows, half_rows, 16)
        logits = mm(qkv[side, rows, at(p * 128, 128, 128)], pair_map(side, p))
        for odd in range(2):
            part_ = logits[:, odd * 128 : odd * 128 + 128]
            low_top = jnp.max(jnp.where(first, part_, -jnp.inf), -1, keepdims=True)
            high_top = jnp.max(jnp.where(first, -jnp.inf, part_), -1, keepdims=True)
            e = jnp.exp(part_ - jnp.where(first, low_top, high_top))
            total = mm(e.astype(bf16), ones64)
            feat[side, rows, at(p * 256 + odd * 128, 128, 128)] = (e / total).astype(bf16)

    @pl.loop(0, 2 * pairs)
    def _(i):
        features_of(1, i)

    across(4)
    for k in (2, 1, 3):
        relay(1, k)
    forward(2, 3)

    @pl.loop(0, 2 * pairs)
    def _(i):
        b, p = i // pairs, lax.rem(i, pairs)
        rows = at(b * half_rows, half_rows, 16)
        keys = feat[1, rows, at(p * 256, 256, 128)]
        both = mm(keys, qkv[2, rows, at(p * 128, 128, 128)], TN)
        states[b, at(p * 128, 128, 16), :] = near_far(first, both[:128], both[128:]).astype(bf16)
        tall = mm(jnp.ones((8, half_rows), bf16), keys)
        slot = lax.broadcasted_iota(jnp.int32, (8, 128), 0) == b
        z_buf[2 * p] = jnp.where(slot, tall[:, :128], z_buf[2 * p])
        z_buf[2 * p + 1] = jnp.where(slot, tall[:, 128:], z_buf[2 * p + 1])

    srows = states.shape[1] // 16

    def scan_out(sem0):
        for k in range(1, 16):
            other = lax.rem(n + k, 16)
            put(states.at[:, at(other * srows, srows, 16), :], s_in.at[n], scan_sem.at[sem0], peers[k])
            put(z_buf.at[other], z_in.at[n], scan_sem.at[sem0 + 1], peers[k])
        one = fetch(states.at[:, at(n * srows, srows, 16), :], s_in.at[n], local_sem.at[0])
        two = fetch(z_buf.at[n], z_in.at[n], local_sem.at[1])
        one.wait()
        two.wait()

    def scan_back(sem0, backward):
        arrived(s_in.at[pl.ds(0, 15)], scan_sem.at[sem0])
        arrived(z_in.at[pl.ds(0, 15)], scan_sem.at[sem0 + 1])
        total = jnp.zeros(s_in.shape[1:], f32)
        sums = jnp.zeros(z_in.shape[1:], f32)
        for i in range(15, -1, -1) if backward else range(16):
            s_out[i] = total.astype(bf16)
            z_out[i] = sums
            total = total + s_in[i].astype(f32)
            sums = sums + z_in[i]
        for k in range(1, 16):
            other = lax.rem(n + k, 16)
            put(s_out.at[other], prior.at[int(backward), :, at(n * srows, srows, 16), :], scan_sem.at[sem0 + 2], peers[k])
            put(z_out.at[other], sums_in.at[int(backward), n], scan_sem.at[sem0 + 3], peers[k])
        one = fetch(s_out.at[n], prior.at[int(backward), :, at(n * srows, srows, 16), :], local_sem.at[0])
        two = fetch(z_out.at[n], sums_in.at[int(backward), n], local_sem.at[1])
        one.wait()
        two.wait()

    def scan_end(sem0):
        arrived(s_in.at[pl.ds(0, 15)], scan_sem.at[sem0 + 2])
        arrived(z_in.at[pl.ds(0, 15)], scan_sem.at[sem0 + 3])

    scan_out(0)
    complete(4)
    pl.loop(0, chunks)(project)
    relay(2, 2)
    forward(3, 2)

    @pl.loop(0, 2 * pairs)
    def _(i):
        features_of(0, i)

    forward(3, 1)
    forward(3, 3)
    across(1)
    relay(2, 1)
    relay(2, 3)

    def mask_of(b, turn):
        row = lax.broadcasted_iota(jnp.int32, (half_rows, half_rows), 0)
        col = lax.broadcasted_iota(jnp.int32, (half_rows, half_rows), 1)
        causal = row <= col if turn else col <= row
        return jnp.where(causal, 1.0, flags[b, 0:1, :])

    @pl.loop(0, 2 * pairs)
    def _(i):
        b, p = i // pairs, lax.rem(i, pairs)
        rows = at(b * half_rows, half_rows, 16)
        values = qkv[2, rows, at(p * 128, 128, 128)]
        mask = mask_of(b, False)
        both = None
        for odd in range(2):
            cols = at(p * 256 + odd * 128, 128, 128)
            scores = (mm(feat[0, rows, cols], feat[1, rows, cols], NT) * mask).astype(bf16)
            right = jnp.concatenate(
                [own_half(values, first, odd), own_half(jnp.ones_like(values), first, odd)], 1
            )
            term = mm(scores, right)
            both = term if both is None else both + term
        num[rows, at(p * 128, 128, 128)] = both[:, :128]
        rden[rows, at(p * 128, 128, 128)] = both[:, 128:]

    scan_back(0, False)
    for k in (2, 1, 3):
        relay(3, k)
    across(2)
    complete(1)
    scan_end(0)

    def sums_pair(direction, b, p, odd):
        tile = sums_in[direction, 2 * p + odd]
        slot = lax.broadcasted_iota(jnp.int32, (8, 128), 0) == b
        return jnp.sum(jnp.where(slot, tile, 0.0), 0, keepdims=True)

    @pl.loop(0, 2 * pairs)
    def _(i):
        b, p = i // pairs, lax.rem(i, pairs)
        rows = at(b * half_rows, half_rows, 16)
        cols = at(p * 128, 128, 128)
        queries = feat[0, rows, at(p * 256, 256, 128)]
        before = pair_block(prior[0, b, at(p * 128, 128, 16), :], first)
        zero = jnp.zeros((64, 128), bf16)
        z_low = jnp.broadcast_to(sums_pair(0, b, p, 0), (64, 128)).astype(bf16)
        z_high = jnp.broadcast_to(sums_pair(0, b, p, 1), (64, 128)).astype(bf16)
        z_rows = jnp.concatenate(
            [jnp.concatenate([z_low, zero], 1), jnp.concatenate([zero, z_high], 1)], 0
        )
        inverse = 1.0 / (rden[rows, cols] + mm(queries, z_rows, NT))
        o[rows, cols] = ((num[rows, cols] + mm(queries, before)) * inverse).astype(bf16)
        rden[rows, cols] = inverse

    @pl.loop(0, 2)
    def _(i):
        rows = at(i * half_rows, half_rows, 16)
        mid[rows, :] = x[rows, :].astype(f32) + mm(o[rows, :], wo[...])

    @pl.loop(0, 4)
    def _(i):
        rows = at(i * step, step, 16)
        e, _unused = statistics(mid[rows, :])
        n2[rows, :] = (e * nrm[2:3, :] + nrm[3:4, :]).astype(bf16)

    complete(2)

    @pl.loop(0, ff // 256)
    def _(i):
        cols = at(i * 256, 256, 128)
        u = mm(n2[...], wu[:, cols])
        scale = 0.7978845608028654
        square = u * u
        tanh = jnp.tanh(scale * u * (1.0 + 0.044715 * square))
        cdf = 0.5 + 0.5 * tanh
        a[:, cols] = (u * cdf).astype(bf16)
        slope = cdf + (0.5 * scale) * u * (1.0 - tanh * tanh) * (1.0 + 0.134145 * square)
        gp[:, cols] = slope.astype(bf16)

    across(3)
    complete(3)

    def branch(b):
        @pl.loop(0, chunks)
        def _(i):
            rows = pl.ds(b * half_rows, half_rows)
            cols = at(i * 256, 256, 128)
            rows_out[rows, cols] = (mid[rows, cols] + mm(a[rows, :], wd[cols, :], NT)).astype(bf16)

    links = []

    def pass_on(i, b, way, hop, block):
        dst = (all_out, all_in)[i]
        src = (rows_out, rows_in)[i]
        origin = src.at[pl.ds(b * half_rows, half_rows)] if hop == 0 else dst.at[b, block]
        return pltpu.make_async_remote_copy(
            src_ref=origin, dst_ref=dst.at[b, block], send_sem=rows_sem.at[i, way, hop, b, 0],
            recv_sem=rows_sem.at[i, way, hop, b, 1], device_id=(f, c, t + 1 if way == 0 else t - 1),
            device_id_type=MESH,
        )

    def rows_hop(i, b, hop):
        dst = (all_out, all_in)[i]
        for way in range(2):
            block = t - hop if way == 0 else t + hop
            here = block >= 0 if way == 0 else block <= 3
            more = t < 3 if way == 0 else t > 0
            if hop > 0:
                @pl.when(here)
                def _():
                    arrived(dst.at[b, 0], rows_sem.at[i, way, hop - 1, b, 1])
            if hop < 3:
                @pl.when(jnp.logical_and(here, more))
                def _():
                    pass_on(i, b, way, hop, block).start()

    def rows_sent(i):
        for b in range(2):
            for hop in range(3):
                for way in range(2):
                    block = t - hop if way == 0 else t + hop
                    here = block >= 0 if way == 0 else block <= 3
                    more = t < 3 if way == 0 else t > 0

                    @pl.when(jnp.logical_and(here, more))
                    def _():
                        pass_on(i, b, way, hop, block).wait_send()

    own_rows = []
    for b in range(2):
        branch(b)
        own_rows.append(fetch(rows_out.at[pl.ds(b * half_rows, half_rows)], all_out.at[b, t], local_sem.at[2 + b]))
        rows_hop(0, b, 0)

    def grad_pair(m):
        if m % 4 < 2:
            h = d // 4
            for tt in range(4):
                if m % 4 == 0:
                    src = of(w, m).at[:, pl.ds(tt * h, h), at((1 - f) * (d // 2), d // 2, 128)]
                    put(src, of(pair_in, m).at[:, tt], gpair_sem.at[m], partner)
                else:
                    src = w[m].at[pl.ds(tt * h, h), at((1 - f) * (d // 2), d // 2, 128)]
                    put(src, pair_in[m].at[tt], gpair_sem.at[m], partner)
        else:
            put(half(w[m], m, 1 - f), pair_in[m], gpair_sem.at[m], partner)

    def grad_xy(m):
        arrived(of(pair_in, m), gpair_sem.at[m])
        h = d // 4
        cols = at(f * (d // 2), d // 2, 128)
        if m % 4 == 0:
            @pl.loop(0, 4 * kind_count(m))
            def _(i):
                kind, tt = i // 4 + (m == 0), lax.rem(i, 4)
                mine = wq[kind, at(tt * h, h, 16), cols].astype(f32)
                pair_in[0][kind, tt] = (mine + pair_in[0][kind, tt].astype(f32)).astype(bf16)
        elif m == 1:
            @pl.loop(0, 4)
            def _(tt):
                mine = wo[at(tt * h, h, 16), cols].astype(f32)
                pair_in[1][tt] = (mine + pair_in[1][tt].astype(f32)).astype(bf16)
        else:
            @pl.loop(0, 12)
            def _(i):
                rows = at(i * 32, 32, 16)
                mine = w[m][at(f * (d // 2) + i * 32, 32, 16), :].astype(f32)
                pair_in[m][rows, :] = (mine + pair_in[m][rows, :].astype(f32)).astype(bf16)
        for side in range(2):
            way = 1 + side
            for i, owner in ((1, 3), (0, way)):
                put(
                    two_of(context_part(of(pair_in, m), m, c ^ owner), m, side), two_of(of(xy_in, m, i), m, side),
                    gxy_sem.at[m, side, i], (f, c ^ way, t),
                )

    def grad_mid(m):
        for side in range(2):
            way = 1 + side
            rest = two_of(of(xy_in, m, 1), m, side)
            mine = two_of(context_part(of(pair_in, m), m, c ^ 3 ^ way), m, side)
            arrived(rest, gxy_sem.at[m, side, 1])
            if m % 4 == 0:
                @pl.loop(0, 2 * kind_count(m))
                def _(i):
                    kind, tt = i // 2, lax.rem(i, 2)
                    rest[kind, tt] = (mine[kind, tt].astype(f32) + rest[kind, tt].astype(f32)).astype(bf16)
            elif m == 1:
                rest[...] = (mine[...].astype(f32) + rest[...].astype(f32)).astype(bf16)
            else:
                @pl.loop(0, d // 8 // 16)
                def _(i):
                    rows = at(i * 16, 16, 16)
                    rest[rows, :] = (mine[rows, :].astype(f32) + rest[rows, :].astype(f32)).astype(bf16)
            put(rest, two_of(of(xy_in, m, 2), m, side), gxy_sem.at[m, side, 2], (f, c ^ 3 ^ way, t))

    def grad_z(m):
        for side in range(2):
            for i in (0, 2):
                arrived(two_of(of(xy_in, m, i), m, side), gxy_sem.at[m, side, i])
        if m % 4 == 0:
            h = d // 16

            @pl.loop(0, 4 * kind_count(m))
            def _(i):
                kind, tt = i // 4 + (m == 0), lax.rem(i, 4)
                total = pair_in[0][kind, tt, at(c * h, h, 16), :].astype(f32)
                for j in (0, 2):
                    total = total + xy_in[0][j, kind, tt].astype(f32)
                part[0][kind, tt] = total.astype(bf16)
        elif m == 1:
            h = d // 16

            @pl.loop(0, 4)
            def _(tt):
                total = pair_in[1][tt, at(c * h, h, 16), :].astype(f32)
                for j in (0, 2):
                    total = total + xy_in[1][j, tt].astype(f32)
                part[1][tt] = total.astype(bf16)
        else:
            @pl.loop(0, d // 8 // 16)
            def _(i):
                rows = at(i * 16, 16, 16)
                total = pair_in[m][at(c * (d // 8) + i * 16, 16, 16), :].astype(f32)
                for j in (0, 2):
                    total = total + xy_in[m][j, rows, :].astype(f32)
                part[m][rows, :] = total.astype(bf16)
        for way, first_ in ((0, 0), (1, 3)):
            @pl.when(t == first_)
            def _():
                for owner in (3, 2, 1) if way == 0 else (0, 1, 2):
                    step_on(m, way, owner, True).start()

    def came(m, way, owner):
        slot = owner - 1 if way == 0 else 3 + owner
        return of(tz_in, m, slot), gz_sem.at[m, slot]

    def step_on(m, way, owner, from_end=False):
        dst, sem = came(m, way, owner)
        return pltpu.make_async_remote_copy(
            src_ref=tensor_part(of(part, m), m, owner) if from_end else dst, dst_ref=dst, send_sem=send_sem,
            recv_sem=sem, device_id=(f, c, t + 1 if way == 0 else t - 1), device_id_type=MESH,
        )

    def add_up(m, dst, own_part, others):
        if m % 4 == 0:
            for kind in range(kind_count(m)):
                total = own_part[kind].astype(f32)
                for other in others:
                    total = total + other[kind].astype(f32)
                dst[kind] = total.astype(bf16)
        elif m == 1:
            total = own_part[...].astype(f32)
            for other in others:
                total = total + other[...].astype(f32)
            dst[...] = total.astype(bf16)
        else:
            @pl.loop(0, d // 8 // 16)
            def _(i):
                rows = at(i * 16, 16, 16)
                total = own_part[rows, :].astype(f32)
                for other in others:
                    total = total + other[rows, :].astype(f32)
                dst[rows, :] = total.astype(bf16)

    def grad_chain(m, hop):
        for way, here in ((0, hop), (1, 3 - hop)):
            @pl.when(t == here)
            def _():
                for owner in range(3, here, -1) if way == 0 else range(here):
                    buf, sem = came(m, way, owner)
                    arrived(buf, sem)
                    add_up(m, buf, tensor_part(of(part, m), m, owner), [buf])
                    step_on(m, way, owner).start()

    def chains_sent():
        for m in range(5):
            for way in range(2):
                for owner in (1, 2, 3) if way == 0 else (0, 1, 2):
                    @pl.when(t < owner if way == 0 else t > owner)
                    def _():
                        step_on(m, way, owner).wait_send()

    def grad_last(m):
        for tt in range(4):
            @pl.when(t == tt)
            def _():
                others = []
                for way in range(2):
                    if (tt > 0, tt < 3)[way]:
                        buf, sem = came(m, way, tt)
                        arrived(buf, sem)
                        others.append(buf)
                add_up(m, of(last, m), tensor_part(of(part, m), m, tt), others)

        for j in range(1, 4):
            put(of(last, m), quarter(of(outs, m), m, c), last_sem.at[m, j], (f, c ^ j, t))
        fetch(of(last, m), quarter(of(outs, m), m, c), local_sem.at[11 + m]).wait()

    for copy in started:
        copy.wait_send()
    started.clear()
    for pred, copy in started_if:
        @pl.when(pred)
        def _():
            copy().wait_send()

    @pl.loop(0, ff // 256)
    def _(i):
        cols = at(i * 256, 256, 128)
        gp[:, cols] = (mm(g[...], wd[:, cols]) * gp[:, cols].astype(f32)).astype(bf16)

    def turn(src):
        @pl.loop(0, chunks)
        def _(i):
            cols = at(i * 256, 256, 128)
            turned[at(i * 256, 256, 16), :] = src[:, cols].astype(f32).T.astype(bf16)

    turn(g)

    @pl.loop(0, ff // 256)
    def _(i):
        cols = at(i * 256, 256, 128)
        wd[:, cols] = mm(turned[...], a[:, cols]).astype(bf16)

    grad_pair(3)
    rows_hop(0, 0, 1)

    @pl.loop(0, chunks)
    def _(i):
        cols = at(i * 256, 256, 128)
        num[:, cols] = mm(gp[...], wu[cols, :], NT)

    @pl.loop(0, 4)
    def _(i):
        rows = at(i * step, step, 16)
        e, rstd = statistics(mid[rows, :])
        grad = num[rows, :]
        vec[2:3, :] += jnp.sum(grad * e, 0, keepdims=True)
        vec[3:4, :] += jnp.sum(grad, 0, keepdims=True)
        total = g[rows, :].astype(f32) + norm_back(grad, e, rstd, nrm[2:3, :])
        mid[rows, :] = total
        gm[rows, :] = total.astype(bf16)

    grad_xy(3)

    @pl.loop(0, chunks)
    def _(i):
        cols = at(i * 256, 256, 128)
        back = mm(gm[...], wo[cols, :], NT)
        for side in range(2):
            cut = at(i * 256 + side * 128, 128, 128)
            grad = back[:, side * 128 : side * 128 + 128]
            inverse = rden[:, cut]
            dnum[:, cut] = (grad * inverse).astype(bf16)
            dden[:, cut] = -mm((grad * o[:, cut].astype(f32)).astype(bf16), ones64) * inverse

    @pl.loop(0, 2 * pairs)
    def _(i):
        b, p = i // pairs, lax.rem(i, pairs)
        rows = at(b * half_rows, half_rows, 16)
        cols = at(p * 128, 128, 128)
        queries = feat[0, rows, at(p * 256, 256, 128)]
        both = mm(queries, dnum[rows, cols], TN)
        states[b, at(p * 128, 128, 16), :] = near_far(first, both[:128], both[128:]).astype(bf16)
        slot = lax.broadcasted_iota(jnp.int32, (8, 128), 0) == b
        packed = dden[rows, cols]
        for odd in range(2):
            full = split_half(packed, first, odd)
            tall = jnp.sum(queries[:, odd * 128 : odd * 128 + 128].astype(f32) * full, 0, keepdims=True)
            z_buf[2 * p + odd] = jnp.where(slot, tall, z_buf[2 * p + odd])

    scan_out(4)

    turn(n2)

    @pl.loop(0, ff // 256)
    def _(i):
        cols = at(i * 256, 256, 128)
        wu[:, cols] = mm(turned[...], gp[:, cols]).astype(bf16)

    grad_pair(2)

    scan_back(4, True)
    rows_hop(0, 1, 1)

    @pl.loop(0, chunks)
    def _(i):
        cols = at(i * 256, 256, 128)
        wo[cols, :] = mm(o[:, cols].astype(f32).T.astype(bf16), gm[...]).astype(bf16)

    grad_pair(1)
    grad_mid(3)

    lane = lanes_of((1, 128))

    def extended(values, one, two, odd):
        base = 0 if odd else 64
        rest = jnp.where(lane == base, one, jnp.where(lane == base + 1, two, jnp.zeros_like(values)))
        return jnp.where(first, rest, values) if odd else jnp.where(first, values, rest)

    def block_maps(side, p):
        low_ = jnp.where(first, mx[side, 2 * p], jnp.zeros((64, 128), bf16))
        high_ = jnp.where(first, jnp.zeros((64, 128), bf16), -mx[side, 2 * p + 1])
        return jnp.concatenate([low_, high_], 0)

    def through_features(side, b, p, rows, cols, grads):
        logits = []
        for odd in range(2):
            prob = feat[side, rows, at(p * 256 + odd * 128, 128, 128)].astype(f32)
            grad = grads[odd]
            inner = mm((prob * grad).astype(bf16), ones64)
            both = prob * (grad - inner)
            other = pltpu.roll(both, 64, 1)
            logits.append(other - both if odd else both - other)
        packed = jnp.where(first, logits[0], logits[1]).astype(bf16)
        dproj[side, rows, cols] = mm(packed, block_maps(side, p), NT).astype(bf16)
        square = mm(qkv[side, rows, cols], packed, TN)
        small[side * pairs + p] += near_far(first, square[:64], square[64:])

    def exact(packed, odd):
        full = split_half(packed, first, odd)
        head = full.astype(bf16)
        return full, head, (full - head.astype(f32)).astype(bf16)

    @pl.loop(0, 2 * pairs)
    def _(i):
        b, p = i // pairs, lax.rem(i, pairs)
        rows = at(b * half_rows, half_rows, 16)
        cols = at(p * 128, 128, 128)
        values, grad_rows = qkv[2, rows, cols], dnum[rows, cols]
        packed = dden[rows, cols]
        before = prior[0, b, at(p * 128, 128, 16), :]
        mask = mask_of(b, False)
        unit = jnp.ones_like(values)
        grads = []
        for odd in range(2):
            full, head, tail = exact(packed, odd)
            left = extended(grad_rows, head, tail, odd)
            right = extended(values, unit, unit, odd)
            scores = (mm(left, right, NT) * mask).astype(bf16)
            total = mm(scores, feat[1, rows, at(p * 256 + odd * 128, 128, 128)])
            total = total + mm(own_half(grad_rows, first, odd), before, NT)
            grads.append(total + full * sums_pair(0, b, p, odd))
        through_features(0, b, p, rows, cols, grads)

    grad_xy(2)

    @pl.loop(0, chunks)
    def _(i):
        cols = at(i * 256, 256, 128)
        num[:, cols] = mm(dproj[0], wq[0, :, cols])

    def grad_of(i):
        kind, j = i // chunks, lax.rem(i, chunks)
        cols = at(j * 256, 256, 128)
        wq[kind, cols, :] = mm(dproj[kind, :, cols].astype(f32).T.astype(bf16), n1[...]).astype(bf16)

    pl.loop(0, chunks)(grad_of)
    grad_pair(4)
    scan_end(4)
    rows_hop(0, 0, 2)
    grad_z(3)

    def key_side(b, p):
        rows = pl.ds(b * half_rows, half_rows)
        cols = at(p * 128, 128, 128)
        values, grad_rows = qkv[2, rows, cols], dnum[rows, cols]
        packed = dden[rows, cols]
        after = prior[1, b, at(p * 128, 128, 16), :]
        mask = mask_of(b, True)
        unit = jnp.ones_like(values)
        value_grad = mm(feat[1, rows, at(p * 256, 256, 128)], pair_block(after, first))
        grads = []
        for odd in range(2):
            fcols = at(p * 256 + odd * 128, 128, 128)
            queries, keys = feat[0, rows, fcols], feat[1, rows, fcols]
            _full, head, tail = exact(packed, odd)
            left = extended(values, unit, unit, odd)
            right = extended(grad_rows, head, tail, odd)
            scores = (mm(left, right, NT) * mask).astype(bf16)
            total = mm(scores, queries) + mm(own_half(values, first, odd), after, NT)
            grads.append(total + sums_pair(1, b, p, odd))
            weights = (mm(keys, queries, NT) * mask).astype(bf16)
            value_grad = value_grad + mm(weights, own_half(grad_rows, first, odd))
        dproj[2, rows, cols] = value_grad.astype(bf16)
        through_features(1, b, p, rows, cols, grads)

    for b in range(2):
        @pl.loop(0, pairs)
        def _(p):
            key_side(b, p)

        if b == 0:
            grad_xy(1)
            rows_hop(0, 1, 2)
            grad_mid(2)
            grad_chain(3, 1)
            grad_xy(4)
        else:
            grad_mid(1)
            grad_mid(4)
            grad_z(2)
            grad_chain(3, 2)

        @pl.loop(0, chunks)
        def _(i):
            cols = at(i * 256, 256, 128)
            rows = pl.ds(b * half_rows, half_rows)
            total = num[rows, cols]
            for kind in range(1, 3):
                total = total + mm(dproj[kind, rows, :], wq[kind, :, cols])
            num[rows, cols] = total

        @pl.loop(2 * b, 2 * b + 2)
        def _(i):
            rows = at(i * step, step, 16)
            e, rstd = statistics(x[rows, :].astype(f32))
            grad = num[rows, :]
            vec[0:1, :] += jnp.sum(grad * e, 0, keepdims=True)
            vec[1:2, :] += jnp.sum(grad, 0, keepdims=True)
            rows_in[rows, :] = (mid[rows, :] + norm_back(grad, e, rstd, nrm[0:1, :])).astype(bf16)

        own_rows.append(fetch(rows_in.at[pl.ds(b * half_rows, half_rows)], all_in.at[b, t], local_sem.at[4 + b]))
        rows_hop(1, b, 0)

    lo_map = head_rows // 2
    put(small.at[:, at((1 - f) * lo_map, lo_map, 16), :], small_pair, small_sem.at[0], partner)
    put(vec.at[:, at((1 - f) * lo_norm, lo_norm, 128)], vec_pair, small_sem.at[1], partner)

    pl.loop(chunks, 3 * chunks)(grad_of)
    grad_pair(0)
    arrived(small_pair, small_sem.at[0])
    arrived(vec_pair, small_sem.at[1])
    for tt in range(4):
        for side in range(2):
            for q in range(2):
                p = side * pairs + pairs_of[tt] + q
                mine = small[p, at(f * lo_map, lo_map, 16), :] + small_pair[p]
                small_own[tt, 2 * side + q] = mine.astype(bf16)
    vec_own[...] = vec[:, at(f * lo_norm, lo_norm, 128)] + vec_pair[...]
    for k in range(1, 4):
        other = lax.rem(t + k, 4)
        put(small_own.at[other], small_in.at[t], small_sem.at[2], (f, c, other))
        put(vec_own, vec_in.at[t], small_sem.at[3], (f, c, other))
    own_small = [
        fetch(small_own.at[t], small_in.at[t], local_sem.at[6]),
        fetch(vec_own, vec_in.at[t], local_sem.at[7]),
    ]
    rows_hop(1, 0, 1)
    grad_last(3)
    grad_xy(0)
    grad_chain(2, 1)
    grad_z(1)
    grad_z(4)
    for copy in own_small:
        copy.wait()
    arrived(small_in.at[pl.ds(0, 3)], small_sem.at[2])
    arrived(vec_in.at[pl.ds(0, 3)], small_sem.at[3])
    total = small_in[0].astype(f32)
    sums = vec_in[0]
    for i in range(1, 4):
        total = total + small_in[i].astype(f32)
        sums = sums + vec_in[i]
    small_sum[...] = total.astype(bf16)
    vec_sum[...] = sums
    for j in range(1, 4):
        put(small_sum, small_all.at[c], small_sem.at[4], (f, c ^ j, t))
        put(vec_sum, vec_all.at[c], small_sem.at[5], (f, c ^ j, t))
    own_small = [
        fetch(small_sum, small_all.at[c], local_sem.at[6]),
        fetch(vec_sum, vec_all.at[c], local_sem.at[7]),
    ]
    rows_hop(1, 1, 1)
    grad_chain(2, 2)
    grad_chain(1, 1)
    grad_chain(4, 1)
    grad_mid(0)
    grad_last(2)
    grad_chain(1, 2)
    grad_chain(4, 2)
    grad_z(0)
    rows_hop(1, 0, 2)
    for copy in own_small:
        copy.wait()
    arrived(small_all.at[pl.ds(0, 3)], small_sem.at[4])
    arrived(vec_all.at[pl.ds(0, 3)], small_sem.at[5])
    total = small_all[0].astype(f32)
    sums = vec_all[0]
    for i in range(1, 4):
        total = total + small_all[i].astype(f32)
        sums = sums + vec_all[i]
    norms_out[...] = sums
    odd_slot = lax.rem(t, 2) == 1
    for side in range(2):
        near, far = total[2 * side], total[2 * side + 1]
        near_high, far_high = pltpu.roll(near, 64, 1), pltpu.roll(far, 64, 1)
        for j, (high, low) in enumerate(((near_high, near), (far, near_high), (far_high, far))):
            maps_out[side][j] = jnp.where(odd_slot, high, low)[:, :64]
    grad_chain(0, 1)
    grad_last(1)
    grad_last(4)
    rows_hop(1, 1, 2)
    grad_chain(0, 2)
    rows_hop(0, 0, 3)
    rows_hop(0, 1, 3)
    grad_last(0)
    for m in range(5):
        for j in range(1, 4):
            arrived(of(last, m), last_sem.at[m, j])
    rows_hop(1, 0, 3)
    rows_hop(1, 1, 3)
    for copy in own_rows:
        copy.wait()
    for copy in started:
        copy.wait_send()
    chains_sent()
    rows_sent(0)
    rows_sent(1)

def mesh_device(
    inputs,
    cotangent,
    picture_starts,
    qkv_weight,
    out_weight,
    up_weight,
    down_weight,
    query_map,
    key_map,
    first_gain,
    first_bias,
    second_gain,
    second_bias,
):
    micro, seq_local, seq_len, d = inputs.shape
    span = seq_len // 4
    rows = micro * seq_local * span
    ff = up_weight.shape[1] * 4
    heads = query_map.shape[0] * 4
    head = query_map.shape[2]
    dma = pltpu.SemaphoreType.DMA
    own = [(3, 4, d // 4, d // 2), (4, d // 4, d // 2), (d // 2, ff), (d // 2, ff)]
    sums = [(3, 4, d // 16, d // 2), (4, d // 16, d // 2), (d // 8, ff), (d // 8, ff)]
    last = [(3, d // 16, d // 2), (d // 16, d // 2), (d // 8, ff // 4), (d // 8, ff // 4)]
    outs = [(3, d // 4, d // 2), (d // 4, d // 2), (d // 2, ff // 4), (d // 2, ff // 4)]
    low = [(3, d, d), (d, d), (d, ff), (d, ff), (2, heads, head, 128)]
    state_rows = heads // 2 * 128
    pieces = (16, micro, state_rows // 16, 128)
    tiny = [(2 * (heads // 2), head, 128), (2 * (heads // 2), head // 2, 128), (4, 4, head // 2, 128)]
    maps_shape = (heads // 4, head // 2, head)
    scratch = [pltpu.VMEM(s, bf16) for s in low]
    scratch += [pltpu.VMEM((8, d), f32)]
    scratch += [pltpu.VMEM((rows, d), bf16)] * 3
    scratch += [pltpu.VMEM((3, rows, d), bf16), pltpu.VMEM((2, rows, heads * 128), bf16)]
    scratch += [pltpu.VMEM((2, micro, state_rows, 128), bf16), pltpu.VMEM((2, 16, 8, 128), f32)]
    scratch += [pltpu.VMEM((micro, state_rows, 128), bf16), pltpu.VMEM((16, 8, 128), f32)]
    scratch += [pltpu.VMEM(pieces, bf16), pltpu.VMEM((16, 8, 128), f32)] * 2
    scratch += [pltpu.VMEM((rows, d), bf16)] + [pltpu.VMEM((rows, d), f32)] * 3
    scratch += [pltpu.VMEM((rows, d), bf16)] + [pltpu.VMEM((rows, ff), bf16)] * 2
    scratch += [pltpu.VMEM((rows, d), bf16)] * 3 + [pltpu.VMEM((rows, d), f32)]
    scratch += [pltpu.VMEM((3, rows, d), bf16), pltpu.VMEM((rows, d), bf16), pltpu.VMEM((d, rows), bf16)]
    scratch += [pltpu.VMEM(s, bf16) for s in own]
    scratch += [pltpu.VMEM((3,) + s, bf16) for s in sums]
    scratch += [pltpu.VMEM(s, bf16) for s in sums]
    scratch += [pltpu.VMEM((6,) + s, bf16) for s in last]
    scratch += [pltpu.VMEM(s, bf16) for s in last]
    scratch += [pltpu.VMEM(s, f32) for s in tiny[:2]] + [pltpu.VMEM(tiny[2], bf16)] * 2
    scratch += [pltpu.VMEM(tiny[2][1:], bf16), pltpu.VMEM(tiny[2], bf16)]
    scratch += [pltpu.VMEM(s, f32) for s in ((8, d), (8, d // 2), (8, d // 2), (4, 8, d // 2), (8, d // 2), (4, 8, d // 2))]
    scratch += [dma((16,)), dma(()), dma((8,)), dma((5, 4)), dma((5, 4, 4)), dma((5,))]
    scratch += [dma((8,)), dma((2, 2, 3, 2, 2)), dma((5,)), dma((5, 2, 3)), dma((5, 6)), dma((5, 4)), dma((6,))]
    scratch += [pltpu.VMEM((micro, 8, span), f32), pltpu.VMEM((2, heads // 4, head // 2, 128), bf16)]
    scratch += [pltpu.VMEM((8, d // 2), f32)]
    vmem = pl.BlockSpec(memory_space=pltpu.VMEM)
    spread_rows = (micro, 4, span, d)
    anywhere = pl.BlockSpec(memory_space=pl.ANY)
    all_out, all_in, share_0, share_1, share_2, share_3, map_0, map_1, norm_grads = pl.pallas_call(
        layer_kernel,
        out_shape=[jax.ShapeDtypeStruct(spread_rows, bf16)] * 2
        + [jax.ShapeDtypeStruct(s, bf16) for s in outs]
        + [jax.ShapeDtypeStruct(maps_shape, f32)] * 2
        + [jax.ShapeDtypeStruct((8, d // 2), f32)],
        in_specs=[anywhere] * 2 + [vmem] * 7 + [anywhere] * 4,
        out_specs=[anywhere] * 6 + [vmem] * 3,
        scratch_shapes=scratch,
        compiler_params=pltpu.CompilerParams(collective_id=0, has_side_effects=True, vmem_limit_bytes=67043328),
        name="layer",
    )(
        inputs, cotangent, picture_starts, query_map, key_map, first_gain, first_bias, second_gain, second_bias,
        qkv_weight.transpose(0, 2, 1), out_weight, up_weight, down_weight,
    )
    return (
        all_out.reshape(inputs.shape),
        all_in.reshape(inputs.shape).astype(f32),
        share_0.astype(f32).transpose(0, 2, 1),
        share_1.astype(f32),
        share_2.astype(f32),
        share_3.astype(f32).T,
        map_0,
        map_1,
        norm_grads[0],
        norm_grads[1],
        norm_grads[2],
        norm_grads[3],
    )


def solution(mesh):
    in_specs = (
        P(None, "fsdp", "context", None),
        P(None, "fsdp", "context", None),
        P(None, "fsdp", None),
        P(None, "fsdp", "tensor"),
        P("tensor", "fsdp"),
        P("fsdp", "tensor"),
        P("tensor", "fsdp"),
        P("tensor", "fsdp", None),
        P("tensor", "fsdp", None),
        P("fsdp"),
        P("fsdp"),
        P("fsdp"),
        P("fsdp"),
    )
    out_specs = (
        P(None, "fsdp", "context", None),
        P(None, "fsdp", "context", None),
        P(None, "fsdp", "tensor"),
        P("tensor", "fsdp"),
        P("fsdp", "tensor"),
        P("tensor", "fsdp"),
        P("tensor", "fsdp", None),
        P("tensor", "fsdp", None),
        P("fsdp"),
        P("fsdp"),
        P("fsdp"),
        P("fsdp"),
    )
    sizes = tuple(mesh.shape[name] for name in EVERY)
    return jax.shard_map(
        mesh_device if sizes == (2, 4, 4) else per_device, mesh=mesh, in_specs=in_specs, out_specs=out_specs, check_vma=False
    )
```

```python
import jax
import jax.numpy as jnp
from jax import lax
from jax.experimental import pallas as pl
from jax.experimental.pallas import tpu as pltpu
from jax.sharding import PartitionSpec as P

BLK = 256
MICRO = 2


epsilon = 1e-05
highest = lax.Precision.HIGHEST


EVERY = ("fsdp", "context", "tensor")


def carried_in(value, backward):
    slot, mine = lax.axis_index("tensor"), lax.axis_index("context")
    near = lax.all_gather(value, "tensor")
    far = lax.all_gather(jnp.sum(near, 0).astype(value.dtype), "context")
    near_ids = jnp.arange(near.shape[0]).reshape((-1,) + (1,) * value.ndim)
    far_ids = jnp.arange(far.shape[0]).reshape((-1,) + (1,) * value.ndim)
    near_mask = near_ids > slot if backward else near_ids < slot
    far_mask = far_ids > mine if backward else far_ids < mine
    near, far = near.astype(jnp.float32), far.astype(jnp.float32)
    return jnp.sum(jnp.where(near_mask, near, 0.0), 0) + jnp.sum(jnp.where(far_mask, far, 0.0), 0)


def layer_norm(values, norm_gain, norm_bias):
    center = values - jnp.mean(values, -1, keepdims=True)
    spread = jnp.mean(center * center, -1, keepdims=True)
    return center * lax.rsqrt(spread + epsilon) * norm_gain + norm_bias


def features(logits):
    return jnp.concatenate([jax.nn.softmax(logits, -1), jax.nn.softmax(-logits, -1)], -1)


def gelu_tanh(values):
    return jax.nn.gelu(values, approximate=True)


def prefix_before(values):
    running = jnp.cumsum(values, 1)
    return jnp.concatenate([jnp.zeros_like(values[:, :1]), running[:, :-1]], 1)


def suffix_after(values):
    running = jnp.flip(jnp.cumsum(jnp.flip(values, 1), 1), 1)
    return jnp.concatenate([running[:, 1:], jnp.zeros_like(values[:, :1])], 1)


def spread(part, axis, parts):
    own = lax.axis_index("context")
    size = part.shape[axis] // parts
    mine = lax.dynamic_slice_in_dim(part, own * size, size, axis)
    return lax.all_gather(mine, EVERY)


def full_in(part):
    pieces = spread(part, 1, lax.axis_size("context"))
    fsdp, ctx, tens = (lax.axis_size(name) for name in EVERY)
    pieces = pieces.reshape((fsdp, ctx, tens) + pieces.shape[1:])
    pieces = pieces.transpose(3, 0, 1, 4, 2, 5)
    return pieces.reshape(pieces.shape[0], -1, pieces.shape[4] * pieces.shape[5])


def share_in(grad):
    fsdp, ctx, tens = (lax.axis_size(name) for name in EVERY)
    kinds, rows, cols = grad.shape
    pieces = grad.astype(jnp.bfloat16).reshape(kinds, fsdp, ctx, rows // fsdp // ctx, tens, cols // tens)
    pieces = pieces.transpose(1, 2, 4, 0, 3, 5).reshape((-1,) + (kinds, rows // fsdp // ctx, cols // tens))
    mine = lax.psum_scatter(pieces, EVERY, scatter_dimension=0)
    return lax.all_gather(mine, "context", axis=1, tiled=True).astype(jnp.float32)


def full_rows(part):
    pieces = spread(part, 0, lax.axis_size("context"))
    fsdp, ctx, tens = (lax.axis_size(name) for name in EVERY)
    pieces = pieces.reshape((fsdp, ctx, tens) + pieces.shape[1:])
    pieces = pieces.transpose(2, 1, 3, 0, 4)
    return pieces.reshape(tens * part.shape[0], -1)


def share_rows(grad):
    fsdp, ctx, tens = (lax.axis_size(name) for name in EVERY)
    rows, cols = grad.shape
    pieces = grad.astype(jnp.bfloat16).reshape(tens, ctx, rows // tens // ctx, fsdp, cols // fsdp)
    pieces = pieces.transpose(3, 1, 0, 2, 4).reshape(-1, rows // tens // ctx, cols // fsdp)
    mine = lax.psum_scatter(pieces, EVERY, scatter_dimension=0)
    return lax.all_gather(mine, "context", axis=0, tiled=True).astype(jnp.float32)


def full_maps(part):
    pieces = lax.all_gather(part, ("fsdp", "tensor"))
    fsdp, tens = lax.axis_size("fsdp"), lax.axis_size("tensor")
    pieces = pieces.reshape((fsdp, tens) + part.shape).transpose(1, 2, 0, 3, 4)
    return pieces.reshape(tens * part.shape[0], fsdp * part.shape[1], part.shape[2])


def own_maps(total):
    fsdp, tens = lax.axis_size("fsdp"), lax.axis_size("tensor")
    heads, rows, _ = total.shape
    mine = lax.dynamic_slice_in_dim(total, lax.axis_index("tensor") * (heads // tens), heads // tens, 0)
    return lax.dynamic_slice_in_dim(mine, lax.axis_index("fsdp") * (rows // fsdp), rows // fsdp, 1)


def per_device(
    inputs,
    cotangent,
    picture_starts,
    qkv_weight,
    out_weight,
    up_weight,
    down_weight,
    query_map,
    key_map,
    first_gain,
    first_bias,
    second_gain,
    second_bias,
):
    tensor_size = lax.axis_size("tensor")
    micro, seq_local, seq_len, model_width = inputs.shape
    span = seq_len // tensor_size
    slot = lax.axis_index("tensor")
    head_size = query_map.shape[2]
    feat_size = 2 * head_size
    blocks_local = span // BLK
    seq_count = micro * seq_local
    block_total = seq_count * blocks_local
    row_count = seq_count * span
    first_block = (lax.axis_index("context") * tensor_size + slot) * blocks_local
    block_ids = first_block + jnp.arange(blocks_local, dtype=jnp.int32)
    position = jnp.arange(BLK, dtype=jnp.int32)
    causal = position[None, :] <= position[:, None]

    in_full = full_in(qkv_weight)
    out_full = full_rows(out_weight)
    up_full = full_in(up_weight[None])[0]
    down_full = full_rows(down_weight)
    qmap_full, kmap_full = full_maps(query_map), full_maps(key_map)
    norms = lax.all_gather(jnp.stack([first_gain, first_bias, second_gain, second_bias]), "fsdp", axis=1, tiled=True)
    gain_first, bias_first, gain_second, bias_second = norms.astype(jnp.float32)

    def own(values):
        mine = lax.dynamic_slice_in_dim(values, slot * span, span, 2)
        return mine.reshape(row_count, model_width)

    source = own(inputs).astype(jnp.float32)
    starts_here = picture_starts.reshape(seq_count, -1)
    block_flags = (
        jnp.sum((starts_here[:, :, None] // BLK == block_ids[None, None, :]).astype(jnp.int32), 1)
        > 0
    )
    allowed = causal[None, None] | block_flags[:, :, None, None]
    allowed = allowed.reshape(block_total, 1, BLK, BLK)
    normed_one = layer_norm(source, gain_first, bias_first)
    normed_low = normed_one.astype(jnp.bfloat16)
    projected = jnp.einsum(
        "rd,cde->cre", normed_low, in_full, preferred_element_type=jnp.float32
    ).astype(jnp.bfloat16)
    heads_local = projected.shape[2] // head_size
    queries = projected[0].reshape(row_count, heads_local, head_size)
    key_rows = projected[1].reshape(row_count, heads_local, head_size)
    value_rows = projected[2].reshape(row_count, heads_local, head_size)
    query_logits = jnp.einsum(
        "rhi,hij->rhj", queries, qmap_full, preferred_element_type=jnp.float32
    )
    key_logits = jnp.einsum(
        "rhi,hij->rhj", key_rows, kmap_full, preferred_element_type=jnp.float32
    )
    query_blocks = (
        features(query_logits)
        .astype(jnp.bfloat16)
        .reshape(block_total, BLK, heads_local, feat_size)
    )
    key_blocks = (
        features(key_logits)
        .astype(jnp.bfloat16)
        .reshape(block_total, BLK, heads_local, feat_size)
    )
    value_blocks = value_rows.reshape(block_total, BLK, heads_local, head_size)
    scores = jnp.einsum(
        "nthf,nshf->nhts", query_blocks, key_blocks, preferred_element_type=jnp.float32
    )
    weights_low = jnp.where(allowed, scores, 0.0).astype(jnp.bfloat16)
    states = jnp.einsum(
        "nshf,nshe->nhfe", key_blocks, value_blocks, preferred_element_type=jnp.float32
    )
    states = states.reshape(seq_count, blocks_local, heads_local, feat_size, head_size)
    key_sums = jnp.sum(key_blocks.astype(jnp.float32), 1).reshape(
        seq_count, blocks_local, heads_local, feat_size
    )
    state_total = jnp.sum(states, 1)
    sums_total = jnp.sum(key_sums, 1)
    carried = carried_in(state_total.astype(jnp.bfloat16), False)
    carried_sums = carried_in(sums_total, False)
    prior_states = (carried[:, None] + prefix_before(states)).astype(jnp.bfloat16)
    prior_states = prior_states.reshape(block_total, heads_local, feat_size, head_size)
    prior_sums = (carried_sums[:, None] + prefix_before(key_sums)).reshape(
        block_total, heads_local, feat_size
    )
    numerator = jnp.einsum(
        "nhts,nshe->nthe", weights_low, value_blocks, preferred_element_type=jnp.float32
    )
    numerator = numerator + jnp.einsum(
        "nthf,nhfe->nthe", query_blocks, prior_states, preferred_element_type=jnp.float32
    )
    denominator = jnp.sum(weights_low.astype(jnp.float32), -1).transpose(0, 2, 1)
    denominator = denominator + jnp.einsum(
        "nthf,nhf->nth", query_blocks.astype(jnp.float32), prior_sums, precision=highest
    )
    mixed_heads = (
        (numerator / denominator[..., None])
        .astype(jnp.bfloat16)
        .reshape(row_count, heads_local * head_size)
    )
    attended = jnp.dot(mixed_heads, out_full, preferred_element_type=jnp.float32)
    middle = source + attended
    normed_two = layer_norm(middle, gain_second, bias_second)
    normed_two_low = normed_two.astype(jnp.bfloat16)
    hidden_pre = jnp.dot(normed_two_low, up_full, preferred_element_type=jnp.float32)
    hidden_low = gelu_tanh(hidden_pre).astype(jnp.bfloat16)
    branch = jnp.dot(hidden_low, down_full, preferred_element_type=jnp.float32)
    output = (middle + branch).astype(jnp.bfloat16).reshape(micro, seq_local, span, model_width)
    output = lax.all_gather(output, "tensor", axis=2, tiled=True)
    upstream_low = own(cotangent)
    upstream = upstream_low.astype(jnp.float32)
    grad_down = jnp.einsum(
        "rk,rd->kd", hidden_low, upstream_low, preferred_element_type=jnp.float32
    )
    hidden_grad = jnp.einsum(
        "rd,kd->rk", upstream_low, down_full, preferred_element_type=jnp.float32
    )
    gelu_result, gelu_pull = jax.vjp(gelu_tanh, hidden_pre)
    pre_grad = gelu_pull(hidden_grad)[0].astype(jnp.bfloat16)
    grad_up = jnp.einsum(
        "rd,rf->df", normed_two_low, pre_grad, preferred_element_type=jnp.float32
    )
    normed_two_grad = jnp.einsum(
        "rf,df->rd", pre_grad, up_full, preferred_element_type=jnp.float32
    )
    norm_result, second_pull = jax.vjp(layer_norm, middle, gain_second, bias_second)
    middle_part, grad_gain_second, grad_bias_second = second_pull(normed_two_grad)
    middle_grad = upstream + middle_part
    middle_low = middle_grad.astype(jnp.bfloat16)
    grad_out = jnp.einsum(
        "rk,rd->kd", mixed_heads, middle_low, preferred_element_type=jnp.float32
    )
    mixed_grad = jnp.einsum(
        "rd,kd->rk", middle_low, out_full, preferred_element_type=jnp.float32
    )
    mixed_grad = mixed_grad.reshape(block_total, BLK, heads_local, head_size)
    numer_grad = (mixed_grad / denominator[..., None]).astype(jnp.bfloat16)
    denom_grad = -jnp.sum(mixed_grad * numerator, -1) / (denominator * denominator)
    weight_grad = jnp.einsum(
        "nthe,nshe->nhts", numer_grad, value_blocks, preferred_element_type=jnp.float32
    )
    weight_grad = weight_grad + denom_grad.transpose(0, 2, 1)[..., None]
    weight_grad_low = jnp.where(allowed, weight_grad, 0.0).astype(jnp.bfloat16)
    value_grad = jnp.einsum(
        "nhts,nthe->nshe", weights_low, numer_grad, preferred_element_type=jnp.float32
    )
    query_grad = jnp.einsum(
        "nhts,nshf->nthf", weight_grad_low, key_blocks, preferred_element_type=jnp.float32
    )
    query_grad = query_grad + jnp.einsum(
        "nthe,nhfe->nthf", numer_grad, prior_states, preferred_element_type=jnp.float32
    )
    query_grad = query_grad + denom_grad[..., None] * prior_sums[:, None]
    key_grad = jnp.einsum(
        "nhts,nthf->nshf", weight_grad_low, query_blocks, preferred_element_type=jnp.float32
    )
    prior_grad = jnp.einsum(
        "nthf,nthe->nhfe", query_blocks, numer_grad, preferred_element_type=jnp.float32
    )
    prior_grad = prior_grad.reshape(seq_count, blocks_local, heads_local, feat_size, head_size)
    prior_sums_grad = jnp.einsum(
        "nthf,nth->nhf", query_blocks.astype(jnp.float32), denom_grad, precision=highest
    )
    prior_sums_grad = prior_sums_grad.reshape(seq_count, blocks_local, heads_local, feat_size)
    grad_total = jnp.sum(prior_grad, 1)
    grad_sums_total = jnp.sum(prior_sums_grad, 1)
    later_states = carried_in(grad_total.astype(jnp.bfloat16), True)
    later_sums = carried_in(grad_sums_total, True)
    state_grad = (later_states[:, None] + suffix_after(prior_grad)).astype(jnp.bfloat16)
    state_grad = state_grad.reshape(block_total, heads_local, feat_size, head_size)
    sums_grad = (later_sums[:, None] + suffix_after(prior_sums_grad)).reshape(
        block_total, heads_local, feat_size
    )
    key_grad = key_grad + jnp.einsum(
        "nshe,nhfe->nshf", value_blocks, state_grad, preferred_element_type=jnp.float32
    )
    key_grad = key_grad + sums_grad[:, None]
    value_grad = value_grad + jnp.einsum(
        "nshf,nhfe->nshe", key_blocks, state_grad, preferred_element_type=jnp.float32
    )
    query_feat_now, query_pull = jax.vjp(features, query_logits)
    query_logit_grad = query_pull(query_grad.reshape(row_count, heads_local, feat_size))[
        0
    ].astype(jnp.bfloat16)
    key_feat_now, key_pull = jax.vjp(features, key_logits)
    key_logit_grad = key_pull(key_grad.reshape(row_count, heads_local, feat_size))[0].astype(
        jnp.bfloat16
    )
    grad_qmap = jnp.einsum(
        "rhi,rhj->hij", queries, query_logit_grad, preferred_element_type=jnp.float32
    )
    grad_kmap = jnp.einsum(
        "rhi,rhj->hij", key_rows, key_logit_grad, preferred_element_type=jnp.float32
    )
    raw_query_grad = jnp.einsum(
        "rhj,hij->rhi", query_logit_grad, qmap_full, preferred_element_type=jnp.float32
    )
    raw_key_grad = jnp.einsum(
        "rhj,hij->rhi", key_logit_grad, kmap_full, preferred_element_type=jnp.float32
    )
    projected_grad = jnp.stack(
        [
            raw_query_grad.reshape(row_count, -1),
            raw_key_grad.reshape(row_count, -1),
            value_grad.reshape(row_count, -1),
        ]
    ).astype(jnp.bfloat16)
    grad_in = jnp.einsum(
        "rd,cre->cde", normed_low, projected_grad, preferred_element_type=jnp.float32
    )
    normed_one_grad = jnp.einsum(
        "cre,cde->rd", projected_grad, in_full, preferred_element_type=jnp.float32
    )
    first_result, first_pull = jax.vjp(layer_norm, source, gain_first, bias_first)
    source_part, grad_gain_first, grad_bias_first = first_pull(normed_one_grad)
    input_grad = (middle_grad + source_part).astype(jnp.bfloat16)
    input_grad = input_grad.reshape(micro, seq_local, span, model_width)
    input_grad = lax.all_gather(input_grad, "tensor", axis=2, tiled=True).astype(jnp.float32)
    norm_grads = jnp.stack([grad_gain_first, grad_bias_first, grad_gain_second, grad_bias_second])
    grad_qmap, grad_kmap, norm_grads = lax.psum((grad_qmap, grad_kmap, norm_grads), EVERY)
    share = first_gain.shape[0]
    norm_grads = lax.dynamic_slice_in_dim(norm_grads, lax.axis_index("fsdp") * share, share, 1)
    return (
        output,
        input_grad,
        share_in(grad_in),
        share_rows(grad_out),
        share_in(grad_up[None])[0],
        share_rows(grad_down),
        own_maps(grad_qmap),
        own_maps(grad_kmap),
        norm_grads[0],
        norm_grads[1],
        norm_grads[2],
        norm_grads[3],
    )


MESH = pl.DeviceIdType.MESH
bf16 = jnp.bfloat16
f32 = jnp.float32


def whereabouts():
    return tuple(lax.axis_index(name) for name in EVERY)


def neighbours(f, c, t):
    n = c * 4 + t
    peers = [(1 - f, c, t)]
    for k in range(1, 16):
        other = lax.rem(n + k, 16)
        peers.append((f, other // 4, lax.rem(other, 4)))
    for k in range(1, 4):
        peers.append((1 - f, c, lax.rem(t + k, 4)))
    return peers


def meet(f, c, t):
    barrier = pltpu.get_barrier_semaphore()
    peers = neighbours(f, c, t)
    for peer in peers:
        pl.semaphore_signal(barrier, inc=1, device_id=peer, device_id_type=MESH)
    pl.semaphore_wait(barrier, len(peers))


def send(src, dst, send_sem, recv_sem, peer):
    copy = pltpu.make_async_remote_copy(
        src_ref=src, dst_ref=dst, send_sem=send_sem, recv_sem=recv_sem,
        device_id=peer, device_id_type=MESH,
    )
    copy.start()
    return copy


def arrived(ref, sem):
    pltpu.make_async_copy(ref, ref, sem).wait()


def at(start, size, unit):
    return pl.ds(pl.multiple_of(start, unit), size)


GROUPS = (0, 4, 1, 2, 3)


def of(refs, m, *index):
    ref = refs[m % 4].at[index] if index else refs[m % 4]
    return ref.at[kinds(m)] if m % 4 == 0 else ref


def kinds(m):
    return pl.ds(1, 2) if m == 0 else pl.ds(0, 1)


def kind_count(m):
    return 2 if m == 0 else 1


def half(ref, m, f):
    if m % 4 == 0:
        w = ref.shape[2] // 2
        return ref.at[:, :, at(f * w, w, 128)]
    if m == 1:
        w = ref.shape[1] // 2
        return ref.at[:, at(f * w, w, 128)]
    w = ref.shape[0] // 2
    return ref.at[at(f * w, w, 16), :]


def shard(ref, m, f, t):
    if m % 4 == 0:
        w, h = ref.shape[2] // 2, ref.shape[1] // 4
        return ref.at[:, at(t * h, h, 16), at(f * w, w, 128)]
    if m == 1:
        w, h = ref.shape[1] // 2, ref.shape[0] // 4
        return ref.at[at(t * h, h, 16), at(f * w, w, 128)]
    h, w = ref.shape[0] // 2, ref.shape[1] // 4
    return ref.at[at(f * h, h, 16), at(t * w, w, 128)]


def piece(ref, m, f, c, t):
    if m % 4 == 0:
        w, h = ref.shape[2] // 2, ref.shape[1] // 16
        return ref.at[:, at(t * 4 * h + c * h, h, 16), at(f * w, w, 128)]
    if m == 1:
        w, h = ref.shape[1] // 2, ref.shape[0] // 16
        return ref.at[at(t * 4 * h + c * h, h, 16), at(f * w, w, 128)]
    h, w = ref.shape[0] // 8, ref.shape[1] // 4
    return ref.at[at(f * 4 * h + c * h, h, 16), at(t * w, w, 128)]


def quarter(ref, m, c):
    if m % 4 == 0:
        h = ref.shape[1] // 4
        return ref.at[:, at(c * h, h, 16), :]
    h = ref.shape[0] // 4
    return ref.at[at(c * h, h, 16), :]


def context_part(ref, m, c):
    if m % 4 == 0:
        h = ref.shape[2] // 4
        return ref.at[:, :, at(c * h, h, 16), :]
    if m == 1:
        h = ref.shape[1] // 4
        return ref.at[:, at(c * h, h, 16), :]
    h = ref.shape[0] // 4
    return ref.at[at(c * h, h, 16), :]


def two_of(ref, m, side):
    if m % 4 == 0:
        return ref.at[:, pl.ds(2 * side, 2)]
    if m == 1:
        return ref.at[pl.ds(2 * side, 2)]
    w = ref.shape[1] // 2
    return ref.at[:, pl.ds(side * w, w)]


def tensor_part(ref, m, t):
    if m % 4 == 0:
        return ref.at[:, t]
    if m == 1:
        return ref.at[t]
    w = ref.shape[1] // 4
    return ref.at[:, at(t * w, w, 128)]


NN = (((1,), (0,)), ((), ()))
NT = (((1,), (1,)), ((), ()))
TN = (((0,), (0,)), ((), ()))


def mm(a, b, dims=NN):
    return lax.dot_general(a, b, dims, preferred_element_type=f32)


def lanes_of(shape):
    return lax.broadcasted_iota(jnp.int32, shape, len(shape) - 1)


def block_ones(size, group):
    row = lax.broadcasted_iota(jnp.int32, (size, size), 0) // group
    col = lax.broadcasted_iota(jnp.int32, (size, size), 1) // group
    return jnp.where(row == col, 1.0, 0.0).astype(bf16)


def statistics(rows):
    center = rows - jnp.mean(rows, -1, keepdims=True)
    rstd = lax.rsqrt(jnp.mean(center * center, -1, keepdims=True) + epsilon)
    return center * rstd, rstd


def norm_back(grad, e, rstd, gain):
    w = grad * gain
    return rstd * (w - jnp.mean(w, -1, keepdims=True) - e * jnp.mean(w * e, -1, keepdims=True))


def near_far(first, low, high):
    return jnp.where(first, low, high)


def own_half(values, first, odd):
    zero = jnp.zeros_like(values)
    return jnp.where(first, zero, values) if odd else jnp.where(first, values, zero)


def pair_block(values, first):
    return jnp.concatenate([own_half(values, first, 0), own_half(values, first, 1)], 0)


def split_half(full, first, odd):
    other = pltpu.roll(full, 64, 1)
    return jnp.where(first, other, full) if odd else jnp.where(first, full, other)


def layer_kernel(*refs):
    inputs, cotangent, starts, own_maps_in = *refs[:3], refs[3:5]
    norms_in, shards, down = refs[5:9], refs[9:12], refs[12]
    flags, maps, norms = refs[-3:]
    refs = refs[4:-3]
    all_out, all_in = refs[9:11]
    outs, maps_out, norms_out = refs[11:15], refs[15:17], refs[17]
    w, mx, nrm, x, g, n1, qkv, feat = refs[18:22], *refs[22:29]
    prior, sums_in, states, z_buf, s_in, z_in, s_out, z_out = refs[29:37]
    o, rden, num, mid, n2, a, gp, rows_out = refs[37:45]
    gm, dnum, dden, dproj, rows_in, turned = refs[45:51]
    pair_in, xy_in, part, tz_in, last = (refs[51 + 4 * i : 55 + 4 * i] for i in range(5))
    small, small_pair, small_own, small_in, small_sum, small_all = refs[71:77]
    vec, vec_pair, vec_own, vec_in, vec_sum, vec_all = refs[77:83]
    local_sem, send_sem, extra_sem, z_sem, xy_sem, pair_sem = refs[83:89]
    scan_sem, rows_sem, gpair_sem, gxy_sem, gz_sem, last_sem, small_sem = refs[89:96]
    wq, wo, wu, wd = w
    d = x.shape[1]
    ff = a.shape[1]
    half_rows = x.shape[0] // 2
    shards = (*shards, gm.at[pl.ds(0, d // 2)])
    f, c, t = whereabouts()
    n = c * 4 + t
    peers = neighbours(f, c, t)
    partner = peers[0]
    started = []

    def put(src, dst, recv_sem, peer):
        started.append(send(src, dst, send_sem, recv_sem, peer))

    started_if = []

    def put_if(pred, src, dst, recv_sem, peer):
        def copy():
            return pltpu.make_async_remote_copy(
                src_ref=src, dst_ref=dst, send_sem=send_sem, recv_sem=recv_sem, device_id=peer, device_id_type=MESH,
            )

        @pl.when(pred)
        def _():
            copy().start()

        started_if.append((pred, copy))

    fetched = []

    def fetch(src, dst, sem):
        copy = pltpu.make_async_copy(src, dst, sem)
        copy.start()
        return copy

    for i in range(2):
        rows = pl.ds(i * half_rows, half_rows)
        fetched.append(fetch(inputs.at[i, 0, at(t * half_rows, half_rows, 16), :], x.at[rows], local_sem.at[i]))
        fetched.append(fetch(cotangent.at[i, 0, at(t * half_rows, half_rows, 16), :], g.at[rows], local_sem.at[2 + i]))
    h3 = maps.shape[1]
    head_rows = small.shape[1]
    pairs_of = (0, 1, 3, 4)
    lo_norm = d // 2

    def map_place(ff_, tt):
        return mx.at[:, pl.ds(tt * h3, h3), at(ff_ * 32, 32, 16), :]

    def norm_place(ff_):
        return nrm.at[:, at(ff_ * lo_norm, lo_norm, 128)]

    for side in range(2):
        own_map = own_maps_in[side][...]
        maps[side] = jnp.concatenate([own_map, -own_map], -1)
    norms[...] = jnp.zeros_like(norms)
    for i in range(4):
        norms[i : i + 1, :] = norms_in[i][...].astype(f32).reshape(1, -1)
    fetched.append(fetch(maps, map_place(f, t), local_sem.at[4]))
    fetched.append(fetch(norms, norm_place(f), local_sem.at[5]))
    shard_copies = {m: fetch(of(shards, m), shard(of(w, m), m, f, t), local_sem.at[6 + m]) for m in (0, 4, 1, 2)}
    down_rows = turned.at[:, pl.ds(0, d // 2)]
    down_copy = fetch(down, down_rows, local_sem.at[11])
    z_buf[...] = jnp.zeros_like(z_buf)
    for b in range(2):
        hits = jnp.where(starts[b] == n * BLK, 1.0, 0.0)
        flags[b] = jnp.broadcast_to(jnp.max(hits, -1, keepdims=True), flags.shape[1:])
    small[...] = jnp.zeros_like(small)
    vec[...] = jnp.zeros_like(vec)
    meet(f, c, t)

    put(norms, norm_place(f), extra_sem.at[0], partner)
    put(maps, map_place(f, t), extra_sem.at[4], partner)
    for m in GROUPS:
        if m == 3:
            down_copy.wait()
            for i in range(0, ff // 4, 256):
                gm[0 : d // 2, i : i + 256] = turned[i : i + 256, 0 : d // 2].astype(f32).T.astype(bf16)
            shard_copies[3] = fetch(shards[3], shard(w[3], 3, f, t), local_sem.at[9])
        for k, pred in ((2, None), (1, t != 3), (3, t != 0)):
            src, dst = quarter(of(shards, m), m, c), piece(of(w, m), m, f, c, t)
            peer = (f, c, lax.rem(t + k, 4))
            if pred is None:
                put(src, dst, z_sem.at[m, k], peer)
            else:
                put_if(pred, src, dst, z_sem.at[m, k], peer)
        if m == 0:
            for k in range(1, 4):
                put(maps, map_place(f, t), extra_sem.at[k], (f, c, lax.rem(t + k, 4)))
    for m in GROUPS:
        put(of(shards, m), shard(of(w, m), m, f, t), pair_sem.at[m], partner)

    def forward(m, k):
        got = piece(of(w, m), m, f, c, lax.rem(t + 4 - k, 4))
        arrived(got, z_sem.at[m, k])
        if k == 2:
            put_if(t == 2, got, got, z_sem.at[m, 3], (f, c, t + 1))
            put_if(t == 1, got, got, z_sem.at[m, 1], (f, c, t - 1))
        for j in range(1, 3):
            put(got, got, xy_sem.at[m, k, j], (f, c ^ j, t))
        put(got, got, pair_sem.at[m], partner)

    def relay(m, k):
        for j in range(1, 3):
            got = piece(of(w, m), m, f, c ^ j, lax.rem(t + 4 - k, 4))
            arrived(got, xy_sem.at[m, k, j])
            if ((0, 1, 2, 3, 1)[m] + k + j) % 2:
                put(got, got, xy_sem.at[m, k, 3], (f, c ^ 3 ^ j, t))
            put(got, got, pair_sem.at[m], partner)

    def across(m):
        for k in range(1, 4):
            got = piece(of(w, m), m, f, c ^ 3, lax.rem(t + 4 - k, 4))
            arrived(got, xy_sem.at[m, k, 3])
            put(got, got, pair_sem.at[m], partner)

    def take_maps():
        for k in range(1, 4):
            got = map_place(f, lax.rem(t + 4 - k, 4))
            arrived(got, extra_sem.at[k])
            put(got, got, extra_sem.at[4 + k], partner)

    def maps_here():
        for k in range(4):
            arrived(map_place(1 - f, lax.rem(t + 4 - k, 4)), extra_sem.at[4 + k])

    def complete(m):
        shard_copies[m].wait()
        arrived(half(of(w, m), m, 1 - f), pair_sem.at[m])

    for k in (2, 1, 3):
        forward(0, k)
    for copy in fetched:
        copy.wait()
    arrived(norm_place(1 - f), extra_sem.at[0])
    first = lanes_of((1, 128)) < 64
    ones64 = block_ones(128, 64)
    step = half_rows // 2

    @pl.loop(0, 4)
    def _(i):
        rows = at(i * step, step, 16)
        e, _unused = statistics(x[rows, :].astype(f32))
        n1[rows, :] = (e * nrm[0:1, :] + nrm[1:2, :]).astype(bf16)

    def turn(src):
        @pl.loop(0, d // 256)
        def _(i):
            cols = at(i * 256, 256, 128)
            turned[at(i * 256, 256, 16), :] = src[:, cols].astype(f32).T.astype(bf16)

    turn(g)
    take_maps()
    for k in (2, 1, 3):
        relay(0, k)
        forward(4, k)
    for k in (2, 1, 3):
        forward(1, k)
    across(0)
    forward(2, 2)
    complete(0)

    chunks = d // 256

    def project(i):
        kind, j = i // chunks, lax.rem(i, chunks)
        cols = at(j * 256, 256, 128)
        qkv[kind, :, cols] = mm(n1[...], wq[kind, cols, :], NT).astype(bf16)

    pl.loop(chunks, 3 * chunks)(project)

    for k in (2, 1, 3):
        relay(4, k)
    forward(2, 1)
    maps_here()

    pairs = d // 128

    def pair_map(side, p):
        zero = jnp.zeros((64, 128), bf16)
        top = jnp.concatenate([mx[side, 2 * p], zero], 1)
        bottom = jnp.concatenate([zero, mx[side, 2 * p + 1]], 1)
        return jnp.concatenate([top, bottom], 0)

    def features_of(side, i):
        b, p = i // pairs, lax.rem(i, pairs)
        rows = at(b * half_rows, half_rows, 16)
        logits = mm(qkv[side, rows, at(p * 128, 128, 128)], pair_map(side, p))
        for odd in range(2):
            part_ = logits[:, odd * 128 : odd * 128 + 128]
            low_top = jnp.max(jnp.where(first, part_, -jnp.inf), -1, keepdims=True)
            high_top = jnp.max(jnp.where(first, -jnp.inf, part_), -1, keepdims=True)
            e = jnp.exp(part_ - jnp.where(first, low_top, high_top))
            total = mm(e.astype(bf16), ones64)
            feat[side, rows, at(p * 256 + odd * 128, 128, 128)] = (e / total).astype(bf16)

    @pl.loop(0, 2 * pairs)
    def _(i):
        features_of(1, i)

    across(4)
    for k in (2, 1, 3):
        relay(1, k)
    forward(2, 3)

    @pl.loop(0, 2 * pairs)
    def _(i):
        b, p = i // pairs, lax.rem(i, pairs)
        rows = at(b * half_rows, half_rows, 16)
        keys = feat[1, rows, at(p * 256, 256, 128)]
        both = mm(keys, qkv[2, rows, at(p * 128, 128, 128)], TN)
        states[b, at(p * 128, 128, 16), :] = near_far(first, both[:128], both[128:]).astype(bf16)
        tall = mm(jnp.ones((8, half_rows), bf16), keys)
        slot = lax.broadcasted_iota(jnp.int32, (8, 128), 0) == b
        z_buf[2 * p] = jnp.where(slot, tall[:, :128], z_buf[2 * p])
        z_buf[2 * p + 1] = jnp.where(slot, tall[:, 128:], z_buf[2 * p + 1])

    srows = states.shape[1] // 16

    def scan_out(sem0):
        for k in range(1, 16):
            other = lax.rem(n + k, 16)
            put(states.at[:, at(other * srows, srows, 16), :], s_in.at[n], scan_sem.at[sem0], peers[k])
            put(z_buf.at[other], z_in.at[n], scan_sem.at[sem0 + 1], peers[k])
        one = fetch(states.at[:, at(n * srows, srows, 16), :], s_in.at[n], local_sem.at[0])
        two = fetch(z_buf.at[n], z_in.at[n], local_sem.at[1])
        one.wait()
        two.wait()

    def scan_back(sem0, backward):
        arrived(s_in.at[pl.ds(0, 15)], scan_sem.at[sem0])
        arrived(z_in.at[pl.ds(0, 15)], scan_sem.at[sem0 + 1])
        total = jnp.zeros(s_in.shape[1:], f32)
        sums = jnp.zeros(z_in.shape[1:], f32)
        for i in range(15, -1, -1) if backward else range(16):
            s_out[i] = total.astype(bf16)
            z_out[i] = sums
            total = total + s_in[i].astype(f32)
            sums = sums + z_in[i]
        for k in range(1, 16):
            other = lax.rem(n + k, 16)
            put(s_out.at[other], prior.at[int(backward), :, at(n * srows, srows, 16), :], scan_sem.at[sem0 + 2], peers[k])
            put(z_out.at[other], sums_in.at[int(backward), n], scan_sem.at[sem0 + 3], peers[k])
        one = fetch(s_out.at[n], prior.at[int(backward), :, at(n * srows, srows, 16), :], local_sem.at[0])
        two = fetch(z_out.at[n], sums_in.at[int(backward), n], local_sem.at[1])
        one.wait()
        two.wait()

    def scan_end(sem0):
        arrived(s_in.at[pl.ds(0, 15)], scan_sem.at[sem0 + 2])
        arrived(z_in.at[pl.ds(0, 15)], scan_sem.at[sem0 + 3])

    scan_out(0)
    complete(4)
    pl.loop(0, chunks)(project)
    relay(2, 2)
    forward(3, 2)

    @pl.loop(0, 2 * pairs)
    def _(i):
        features_of(0, i)

    forward(3, 1)
    forward(3, 3)
    across(1)
    relay(2, 1)
    relay(2, 3)

    def mask_of(b, turn):
        row = lax.broadcasted_iota(jnp.int32, (half_rows, half_rows), 0)
        col = lax.broadcasted_iota(jnp.int32, (half_rows, half_rows), 1)
        causal = row <= col if turn else col <= row
        return jnp.where(causal, 1.0, flags[b, 0:1, :])

    @pl.loop(0, 2 * pairs)
    def _(i):
        b, p = i // pairs, lax.rem(i, pairs)
        rows = at(b * half_rows, half_rows, 16)
        values = qkv[2, rows, at(p * 128, 128, 128)]
        mask = mask_of(b, False)
        both = None
        for odd in range(2):
            cols = at(p * 256 + odd * 128, 128, 128)
            scores = (mm(feat[0, rows, cols], feat[1, rows, cols], NT) * mask).astype(bf16)
            right = jnp.concatenate(
                [own_half(values, first, odd), own_half(jnp.ones_like(values), first, odd)], 1
            )
            term = mm(scores, right)
            both = term if both is None else both + term
        num[rows, at(p * 128, 128, 128)] = both[:, :128]
        rden[rows, at(p * 128, 128, 128)] = both[:, 128:]

    scan_back(0, False)
    for k in (2, 1, 3):
        relay(3, k)
    across(2)
    complete(1)
    scan_end(0)

    def sums_pair(direction, b, p, odd):
        tile = sums_in[direction, 2 * p + odd]
        slot = lax.broadcasted_iota(jnp.int32, (8, 128), 0) == b
        return jnp.sum(jnp.where(slot, tile, 0.0), 0, keepdims=True)

    @pl.loop(0, 2 * pairs)
    def _(i):
        b, p = i // pairs, lax.rem(i, pairs)
        rows = at(b * half_rows, half_rows, 16)
        cols = at(p * 128, 128, 128)
        queries = feat[0, rows, at(p * 256, 256, 128)]
        before = pair_block(prior[0, b, at(p * 128, 128, 16), :], first)
        zero = jnp.zeros((64, 128), bf16)
        z_low = jnp.broadcast_to(sums_pair(0, b, p, 0), (64, 128)).astype(bf16)
        z_high = jnp.broadcast_to(sums_pair(0, b, p, 1), (64, 128)).astype(bf16)
        z_rows = jnp.concatenate(
            [jnp.concatenate([z_low, zero], 1), jnp.concatenate([zero, z_high], 1)], 0
        )
        inverse = 1.0 / (rden[rows, cols] + mm(queries, z_rows, NT))
        o[rows, cols] = ((num[rows, cols] + mm(queries, before)) * inverse).astype(bf16)
        rden[rows, cols] = inverse

    @pl.loop(0, 2)
    def _(i):
        rows = at(i * half_rows, half_rows, 16)
        mid[rows, :] = x[rows, :].astype(f32) + mm(o[rows, :], wo[...])

    @pl.loop(0, 4)
    def _(i):
        rows = at(i * step, step, 16)
        e, _unused = statistics(mid[rows, :])
        n2[rows, :] = (e * nrm[2:3, :] + nrm[3:4, :]).astype(bf16)

    complete(2)

    @pl.loop(0, ff // 256)
    def _(i):
        cols = at(i * 256, 256, 128)
        u = mm(n2[...], wu[:, cols])
        scale = 0.7978845608028654
        square = u * u
        tanh = jnp.tanh(scale * u * (1.0 + 0.044715 * square))
        cdf = 0.5 + 0.5 * tanh
        a[:, cols] = (u * cdf).astype(bf16)
        slope = cdf + (0.5 * scale) * u * (1.0 - tanh * tanh) * (1.0 + 0.134145 * square)
        gp[:, cols] = slope.astype(bf16)

    across(3)
    complete(3)

    def branch(b):
        @pl.loop(0, chunks)
        def _(i):
            rows = pl.ds(b * half_rows, half_rows)
            cols = at(i * 256, 256, 128)
            rows_out[rows, cols] = (mid[rows, cols] + mm(a[rows, :], wd[cols, :], NT)).astype(bf16)

    links = []

    def pass_on(i, b, way, hop, block):
        dst = (all_out, all_in)[i]
        src = (rows_out, rows_in)[i]
        origin = src.at[pl.ds(b * half_rows, half_rows)] if hop == 0 else dst.at[b, block]
        return pltpu.make_async_remote_copy(
            src_ref=origin, dst_ref=dst.at[b, block], send_sem=rows_sem.at[i, way, hop, b, 0],
            recv_sem=rows_sem.at[i, way, hop, b, 1], device_id=(f, c, t + 1 if way == 0 else t - 1),
            device_id_type=MESH,
        )

    def rows_hop(i, b, hop):
        dst = (all_out, all_in)[i]
        for way in range(2):
            block = t - hop if way == 0 else t + hop
            here = block >= 0 if way == 0 else block <= 3
            more = t < 3 if way == 0 else t > 0
            if hop > 0:
                @pl.when(here)
                def _():
                    arrived(dst.at[b, 0], rows_sem.at[i, way, hop - 1, b, 1])
            if hop < 3:
                @pl.when(jnp.logical_and(here, more))
                def _():
                    pass_on(i, b, way, hop, block).start()

    def rows_sent(i):
        for b in range(2):
            for hop in range(3):
                for way in range(2):
                    block = t - hop if way == 0 else t + hop
                    here = block >= 0 if way == 0 else block <= 3
                    more = t < 3 if way == 0 else t > 0

                    @pl.when(jnp.logical_and(here, more))
                    def _():
                        pass_on(i, b, way, hop, block).wait_send()

    own_rows = []
    for b in range(2):
        branch(b)
        own_rows.append(fetch(rows_out.at[pl.ds(b * half_rows, half_rows)], all_out.at[b, t], local_sem.at[2 + b]))
        rows_hop(0, b, 0)

    def grad_pair(m):
        if m % 4 < 2:
            h = d // 4
            for tt in range(4):
                if m % 4 == 0:
                    src = of(w, m).at[:, pl.ds(tt * h, h), at((1 - f) * (d // 2), d // 2, 128)]
                    put(src, of(pair_in, m).at[:, tt], gpair_sem.at[m], partner)
                else:
                    src = w[m].at[pl.ds(tt * h, h), at((1 - f) * (d // 2), d // 2, 128)]
                    put(src, pair_in[m].at[tt], gpair_sem.at[m], partner)
        else:
            put(half(w[m], m, 1 - f), pair_in[m], gpair_sem.at[m], partner)

    def grad_xy(m):
        arrived(of(pair_in, m), gpair_sem.at[m])
        h = d // 4
        cols = at(f * (d // 2), d // 2, 128)
        if m % 4 == 0:
            @pl.loop(0, 4 * kind_count(m))
            def _(i):
                kind, tt = i // 4 + (m == 0), lax.rem(i, 4)
                mine = wq[kind, at(tt * h, h, 16), cols].astype(f32)
                pair_in[0][kind, tt] = (mine + pair_in[0][kind, tt].astype(f32)).astype(bf16)
        elif m == 1:
            @pl.loop(0, 4)
            def _(tt):
                mine = wo[at(tt * h, h, 16), cols].astype(f32)
                pair_in[1][tt] = (mine + pair_in[1][tt].astype(f32)).astype(bf16)
        else:
            @pl.loop(0, 12)
            def _(i):
                rows = at(i * 32, 32, 16)
                mine = w[m][at(f * (d // 2) + i * 32, 32, 16), :].astype(f32)
                pair_in[m][rows, :] = (mine + pair_in[m][rows, :].astype(f32)).astype(bf16)
        for side in range(2):
            way = 1 + side
            for i, owner in ((1, 3), (0, way)):
                put(
                    two_of(context_part(of(pair_in, m), m, c ^ owner), m, side), two_of(of(xy_in, m, i), m, side),
                    gxy_sem.at[m, side, i], (f, c ^ way, t),
                )

    def grad_mid(m):
        for side in range(2):
            way = 1 + side
            rest = two_of(of(xy_in, m, 1), m, side)
            mine = two_of(context_part(of(pair_in, m), m, c ^ 3 ^ way), m, side)
            arrived(rest, gxy_sem.at[m, side, 1])
            if m % 4 == 0:
                @pl.loop(0, 2 * kind_count(m))
                def _(i):
                    kind, tt = i // 2, lax.rem(i, 2)
                    rest[kind, tt] = (mine[kind, tt].astype(f32) + rest[kind, tt].astype(f32)).astype(bf16)
            elif m == 1:
                rest[...] = (mine[...].astype(f32) + rest[...].astype(f32)).astype(bf16)
            else:
                @pl.loop(0, d // 8 // 16)
                def _(i):
                    rows = at(i * 16, 16, 16)
                    rest[rows, :] = (mine[rows, :].astype(f32) + rest[rows, :].astype(f32)).astype(bf16)
            put(rest, two_of(of(xy_in, m, 2), m, side), gxy_sem.at[m, side, 2], (f, c ^ 3 ^ way, t))

    def grad_z(m):
        for side in range(2):
            for i in (0, 2):
                arrived(two_of(of(xy_in, m, i), m, side), gxy_sem.at[m, side, i])
        if m % 4 == 0:
            h = d // 16

            @pl.loop(0, 4 * kind_count(m))
            def _(i):
                kind, tt = i // 4 + (m == 0), lax.rem(i, 4)
                total = pair_in[0][kind, tt, at(c * h, h, 16), :].astype(f32)
                for j in (0, 2):
                    total = total + xy_in[0][j, kind, tt].astype(f32)
                part[0][kind, tt] = total.astype(bf16)
        elif m == 1:
            h = d // 16

            @pl.loop(0, 4)
            def _(tt):
                total = pair_in[1][tt, at(c * h, h, 16), :].astype(f32)
                for j in (0, 2):
                    total = total + xy_in[1][j, tt].astype(f32)
                part[1][tt] = total.astype(bf16)
        else:
            @pl.loop(0, d // 8 // 16)
            def _(i):
                rows = at(i * 16, 16, 16)
                total = pair_in[m][at(c * (d // 8) + i * 16, 16, 16), :].astype(f32)
                for j in (0, 2):
                    total = total + xy_in[m][j, rows, :].astype(f32)
                part[m][rows, :] = total.astype(bf16)
        for way, first_ in ((0, 0), (1, 3)):
            @pl.when(t == first_)
            def _():
                for owner in (3, 2, 1) if way == 0 else (0, 1, 2):
                    step_on(m, way, owner, True).start()

    def came(m, way, owner):
        slot = owner - 1 if way == 0 else 3 + owner
        return of(tz_in, m, slot), gz_sem.at[m, slot]

    def step_on(m, way, owner, from_end=False):
        dst, sem = came(m, way, owner)
        return pltpu.make_async_remote_copy(
            src_ref=tensor_part(of(part, m), m, owner) if from_end else dst, dst_ref=dst, send_sem=send_sem,
            recv_sem=sem, device_id=(f, c, t + 1 if way == 0 else t - 1), device_id_type=MESH,
        )

    def add_up(m, dst, own_part, others):
        if m % 4 == 0:
            for kind in range(kind_count(m)):
                total = own_part[kind].astype(f32)
                for other in others:
                    total = total + other[kind].astype(f32)
                dst[kind] = total.astype(bf16)
        elif m == 1:
            total = own_part[...].astype(f32)
            for other in others:
                total = total + other[...].astype(f32)
            dst[...] = total.astype(bf16)
        else:
            @pl.loop(0, d // 8 // 16)
            def _(i):
                rows = at(i * 16, 16, 16)
                total = own_part[rows, :].astype(f32)
                for other in others:
                    total = total + other[rows, :].astype(f32)
                dst[rows, :] = total.astype(bf16)

    def grad_chain(m, hop):
        for way, here in ((0, hop), (1, 3 - hop)):
            @pl.when(t == here)
            def _():
                for owner in range(3, here, -1) if way == 0 else range(here):
                    buf, sem = came(m, way, owner)
                    arrived(buf, sem)
                    add_up(m, buf, tensor_part(of(part, m), m, owner), [buf])
                    step_on(m, way, owner).start()

    def chains_sent():
        for m in range(5):
            for way in range(2):
                for owner in (1, 2, 3) if way == 0 else (0, 1, 2):
                    @pl.when(t < owner if way == 0 else t > owner)
                    def _():
                        step_on(m, way, owner).wait_send()

    def grad_last(m):
        for tt in range(4):
            @pl.when(t == tt)
            def _():
                others = []
                for way in range(2):
                    if (tt > 0, tt < 3)[way]:
                        buf, sem = came(m, way, tt)
                        arrived(buf, sem)
                        others.append(buf)
                add_up(m, of(last, m), tensor_part(of(part, m), m, tt), others)

        for j in range(1, 4):
            put(of(last, m), quarter(of(outs, m), m, c), last_sem.at[m, j], (f, c ^ j, t))
        fetch(of(last, m), quarter(of(outs, m), m, c), local_sem.at[11 + m]).wait()

    for copy in started:
        copy.wait_send()
    started.clear()
    for pred, copy in started_if:
        @pl.when(pred)
        def _():
            copy().wait_send()

    @pl.loop(0, ff // 256)
    def _(i):
        cols = at(i * 256, 256, 128)
        gp[:, cols] = (mm(g[...], wd[:, cols]) * gp[:, cols].astype(f32)).astype(bf16)

    @pl.loop(0, ff // 256)
    def _(i):
        cols = at(i * 256, 256, 128)
        wd[:, cols] = mm(turned[...], a[:, cols]).astype(bf16)

    grad_pair(3)
    rows_hop(0, 0, 1)

    @pl.loop(0, chunks)
    def _(i):
        cols = at(i * 256, 256, 128)
        num[:, cols] = mm(gp[...], wu[cols, :], NT)

    @pl.loop(0, 4)
    def _(i):
        rows = at(i * step, step, 16)
        e, rstd = statistics(mid[rows, :])
        grad = num[rows, :]
        vec[2:3, :] += jnp.sum(grad * e, 0, keepdims=True)
        vec[3:4, :] += jnp.sum(grad, 0, keepdims=True)
        total = g[rows, :].astype(f32) + norm_back(grad, e, rstd, nrm[2:3, :])
        mid[rows, :] = total
        gm[rows, :] = total.astype(bf16)

    grad_xy(3)

    @pl.loop(0, chunks)
    def _(i):
        cols = at(i * 256, 256, 128)
        back = mm(gm[...], wo[cols, :], NT)
        for side in range(2):
            cut = at(i * 256 + side * 128, 128, 128)
            grad = back[:, side * 128 : side * 128 + 128]
            inverse = rden[:, cut]
            dnum[:, cut] = (grad * inverse).astype(bf16)
            dden[:, cut] = -mm((grad * o[:, cut].astype(f32)).astype(bf16), ones64) * inverse

    @pl.loop(0, 2 * pairs)
    def _(i):
        b, p = i // pairs, lax.rem(i, pairs)
        rows = at(b * half_rows, half_rows, 16)
        cols = at(p * 128, 128, 128)
        queries = feat[0, rows, at(p * 256, 256, 128)]
        both = mm(queries, dnum[rows, cols], TN)
        states[b, at(p * 128, 128, 16), :] = near_far(first, both[:128], both[128:]).astype(bf16)
        slot = lax.broadcasted_iota(jnp.int32, (8, 128), 0) == b
        packed = dden[rows, cols]
        for odd in range(2):
            full = split_half(packed, first, odd)
            tall = jnp.sum(queries[:, odd * 128 : odd * 128 + 128].astype(f32) * full, 0, keepdims=True)
            z_buf[2 * p + odd] = jnp.where(slot, tall, z_buf[2 * p + odd])

    scan_out(4)

    turn(n2)

    @pl.loop(0, ff // 256)
    def _(i):
        cols = at(i * 256, 256, 128)
        wu[:, cols] = mm(turned[...], gp[:, cols]).astype(bf16)

    grad_pair(2)

    scan_back(4, True)
    rows_hop(0, 1, 1)

    @pl.loop(0, chunks)
    def _(i):
        cols = at(i * 256, 256, 128)
        wo[cols, :] = mm(o[:, cols].astype(f32).T.astype(bf16), gm[...]).astype(bf16)

    grad_pair(1)
    grad_mid(3)

    lane = lanes_of((1, 128))

    def extended(values, one, two, odd):
        base = 0 if odd else 64
        rest = jnp.where(lane == base, one, jnp.where(lane == base + 1, two, jnp.zeros_like(values)))
        return jnp.where(first, rest, values) if odd else jnp.where(first, values, rest)

    def block_maps(side, p):
        low_ = jnp.where(first, mx[side, 2 * p], jnp.zeros((64, 128), bf16))
        high_ = jnp.where(first, jnp.zeros((64, 128), bf16), -mx[side, 2 * p + 1])
        return jnp.concatenate([low_, high_], 0)

    def through_features(side, b, p, rows, cols, grads):
        logits = []
        for odd in range(2):
            prob = feat[side, rows, at(p * 256 + odd * 128, 128, 128)].astype(f32)
            grad = grads[odd]
            inner = mm((prob * grad).astype(bf16), ones64)
            both = prob * (grad - inner)
            other = pltpu.roll(both, 64, 1)
            logits.append(other - both if odd else both - other)
        packed = jnp.where(first, logits[0], logits[1]).astype(bf16)
        dproj[side, rows, cols] = mm(packed, block_maps(side, p), NT).astype(bf16)
        square = mm(qkv[side, rows, cols], packed, TN)
        small[side * pairs + p] += near_far(first, square[:64], square[64:])

    def exact(packed, odd):
        full = split_half(packed, first, odd)
        head = full.astype(bf16)
        return full, head, (full - head.astype(f32)).astype(bf16)

    @pl.loop(0, 2 * pairs)
    def _(i):
        b, p = i // pairs, lax.rem(i, pairs)
        rows = at(b * half_rows, half_rows, 16)
        cols = at(p * 128, 128, 128)
        values, grad_rows = qkv[2, rows, cols], dnum[rows, cols]
        packed = dden[rows, cols]
        before = prior[0, b, at(p * 128, 128, 16), :]
        mask = mask_of(b, False)
        unit = jnp.ones_like(values)
        grads = []
        for odd in range(2):
            full, head, tail = exact(packed, odd)
            left = extended(grad_rows, head, tail, odd)
            right = extended(values, unit, unit, odd)
            scores = (mm(left, right, NT) * mask).astype(bf16)
            total = mm(scores, feat[1, rows, at(p * 256 + odd * 128, 128, 128)])
            total = total + mm(own_half(grad_rows, first, odd), before, NT)
            grads.append(total + full * sums_pair(0, b, p, odd))
        through_features(0, b, p, rows, cols, grads)

    grad_xy(2)

    @pl.loop(0, chunks)
    def _(i):
        cols = at(i * 256, 256, 128)
        num[:, cols] = mm(dproj[0], wq[0, :, cols])

    def grad_of(i):
        kind, j = i // chunks, lax.rem(i, chunks)
        cols = at(j * 256, 256, 128)
        wq[kind, cols, :] = mm(dproj[kind, :, cols].astype(f32).T.astype(bf16), n1[...]).astype(bf16)

    pl.loop(0, chunks)(grad_of)
    grad_pair(4)
    scan_end(4)
    rows_hop(0, 0, 2)
    grad_z(3)

    def key_side(b, p):
        rows = pl.ds(b * half_rows, half_rows)
        cols = at(p * 128, 128, 128)
        values, grad_rows = qkv[2, rows, cols], dnum[rows, cols]
        packed = dden[rows, cols]
        after = prior[1, b, at(p * 128, 128, 16), :]
        mask = mask_of(b, True)
        unit = jnp.ones_like(values)
        value_grad = mm(feat[1, rows, at(p * 256, 256, 128)], pair_block(after, first))
        grads = []
        for odd in range(2):
            fcols = at(p * 256 + odd * 128, 128, 128)
            queries, keys = feat[0, rows, fcols], feat[1, rows, fcols]
            _full, head, tail = exact(packed, odd)
            left = extended(values, unit, unit, odd)
            right = extended(grad_rows, head, tail, odd)
            scores = (mm(left, right, NT) * mask).astype(bf16)
            total = mm(scores, queries) + mm(own_half(values, first, odd), after, NT)
            grads.append(total + sums_pair(1, b, p, odd))
            weights = (mm(keys, queries, NT) * mask).astype(bf16)
            value_grad = value_grad + mm(weights, own_half(grad_rows, first, odd))
        dproj[2, rows, cols] = value_grad.astype(bf16)
        through_features(1, b, p, rows, cols, grads)

    for b in range(2):
        @pl.loop(0, pairs)
        def _(p):
            key_side(b, p)

        if b == 0:
            grad_xy(1)
            rows_hop(0, 1, 2)
            grad_mid(2)
            grad_chain(3, 1)
            grad_xy(4)
        else:
            grad_mid(1)
            grad_mid(4)
            grad_z(2)
            grad_chain(3, 2)

        @pl.loop(0, chunks)
        def _(i):
            cols = at(i * 256, 256, 128)
            rows = pl.ds(b * half_rows, half_rows)
            total = num[rows, cols]
            for kind in range(1, 3):
                total = total + mm(dproj[kind, rows, :], wq[kind, :, cols])
            num[rows, cols] = total

        @pl.loop(2 * b, 2 * b + 2)
        def _(i):
            rows = at(i * step, step, 16)
            e, rstd = statistics(x[rows, :].astype(f32))
            grad = num[rows, :]
            vec[0:1, :] += jnp.sum(grad * e, 0, keepdims=True)
            vec[1:2, :] += jnp.sum(grad, 0, keepdims=True)
            rows_in[rows, :] = (mid[rows, :] + norm_back(grad, e, rstd, nrm[0:1, :])).astype(bf16)

        own_rows.append(fetch(rows_in.at[pl.ds(b * half_rows, half_rows)], all_in.at[b, t], local_sem.at[4 + b]))
        rows_hop(1, b, 0)

    lo_map = head_rows // 2
    put(small.at[:, at((1 - f) * lo_map, lo_map, 16), :], small_pair, small_sem.at[0], partner)
    put(vec.at[:, at((1 - f) * lo_norm, lo_norm, 128)], vec_pair, small_sem.at[1], partner)

    pl.loop(chunks, 3 * chunks)(grad_of)
    grad_pair(0)
    arrived(small_pair, small_sem.at[0])
    arrived(vec_pair, small_sem.at[1])
    for tt in range(4):
        for side in range(2):
            for q in range(2):
                p = side * pairs + pairs_of[tt] + q
                mine = small[p, at(f * lo_map, lo_map, 16), :] + small_pair[p]
                small_own[tt, 2 * side + q] = mine.astype(bf16)
    vec_own[...] = vec[:, at(f * lo_norm, lo_norm, 128)] + vec_pair[...]
    for k in range(1, 4):
        other = lax.rem(t + k, 4)
        put(small_own.at[other], small_in.at[t], small_sem.at[2], (f, c, other))
        put(vec_own, vec_in.at[t], small_sem.at[3], (f, c, other))
    own_small = [
        fetch(small_own.at[t], small_in.at[t], local_sem.at[6]),
        fetch(vec_own, vec_in.at[t], local_sem.at[7]),
    ]
    rows_hop(1, 0, 1)
    grad_last(3)
    grad_xy(0)
    rows_hop(1, 1, 1)
    grad_chain(2, 1)
    grad_z(1)
    grad_z(4)
    for copy in own_small:
        copy.wait()
    arrived(small_in.at[pl.ds(0, 3)], small_sem.at[2])
    arrived(vec_in.at[pl.ds(0, 3)], small_sem.at[3])
    total = small_in[0].astype(f32)
    sums = vec_in[0]
    for i in range(1, 4):
        total = total + small_in[i].astype(f32)
        sums = sums + vec_in[i]
    small_sum[...] = total.astype(bf16)
    vec_sum[...] = sums
    for j in range(1, 4):
        put(small_sum, small_all.at[c], small_sem.at[4], (f, c ^ j, t))
        put(vec_sum, vec_all.at[c], small_sem.at[5], (f, c ^ j, t))
    own_small = [
        fetch(small_sum, small_all.at[c], local_sem.at[6]),
        fetch(vec_sum, vec_all.at[c], local_sem.at[7]),
    ]
    grad_chain(2, 2)
    grad_chain(1, 1)
    grad_chain(4, 1)
    grad_mid(0)
    rows_hop(1, 0, 2)
    grad_last(2)
    grad_chain(1, 2)
    grad_chain(4, 2)
    grad_z(0)
    for copy in own_small:
        copy.wait()
    arrived(small_all.at[pl.ds(0, 3)], small_sem.at[4])
    arrived(vec_all.at[pl.ds(0, 3)], small_sem.at[5])
    total = small_all[0].astype(f32)
    sums = vec_all[0]
    for i in range(1, 4):
        total = total + small_all[i].astype(f32)
        sums = sums + vec_all[i]
    norms_out[...] = sums
    odd_slot = lax.rem(t, 2) == 1
    for side in range(2):
        near, far = total[2 * side], total[2 * side + 1]
        near_high, far_high = pltpu.roll(near, 64, 1), pltpu.roll(far, 64, 1)
        for j, (high, low) in enumerate(((near_high, near), (far, near_high), (far_high, far))):
            maps_out[side][j] = jnp.where(odd_slot, high, low)[:, :64]
    grad_chain(0, 1)
    grad_last(1)
    grad_last(4)
    rows_hop(1, 1, 2)
    grad_chain(0, 2)
    rows_hop(0, 0, 3)
    rows_hop(0, 1, 3)
    grad_last(0)
    for m in range(5):
        for j in range(1, 4):
            arrived(of(last, m), last_sem.at[m, j])
    rows_hop(1, 0, 3)
    rows_hop(1, 1, 3)
    for copy in own_rows:
        copy.wait()
    for copy in started:
        copy.wait_send()
    chains_sent()
    rows_sent(0)
    rows_sent(1)

def mesh_device(
    inputs,
    cotangent,
    picture_starts,
    qkv_weight,
    out_weight,
    up_weight,
    down_weight,
    query_map,
    key_map,
    first_gain,
    first_bias,
    second_gain,
    second_bias,
):
    micro, seq_local, seq_len, d = inputs.shape
    span = seq_len // 4
    rows = micro * seq_local * span
    ff = up_weight.shape[1] * 4
    heads = query_map.shape[0] * 4
    head = query_map.shape[2]
    dma = pltpu.SemaphoreType.DMA
    own = [(3, 4, d // 4, d // 2), (4, d // 4, d // 2), (d // 2, ff), (d // 2, ff)]
    sums = [(3, 4, d // 16, d // 2), (4, d // 16, d // 2), (d // 8, ff), (d // 8, ff)]
    last = [(3, d // 16, d // 2), (d // 16, d // 2), (d // 8, ff // 4), (d // 8, ff // 4)]
    outs = [(3, d // 4, d // 2), (d // 4, d // 2), (d // 2, ff // 4), (d // 2, ff // 4)]
    low = [(3, d, d), (d, d), (d, ff), (d, ff), (2, heads, head, 128)]
    state_rows = heads // 2 * 128
    pieces = (16, micro, state_rows // 16, 128)
    tiny = [(2 * (heads // 2), head, 128), (2 * (heads // 2), head // 2, 128), (4, 4, head // 2, 128)]
    maps_shape = (heads // 4, head // 2, head)
    scratch = [pltpu.VMEM(s, bf16) for s in low]
    scratch += [pltpu.VMEM((8, d), f32)]
    scratch += [pltpu.VMEM((rows, d), bf16)] * 3
    scratch += [pltpu.VMEM((3, rows, d), bf16), pltpu.VMEM((2, rows, heads * 128), bf16)]
    scratch += [pltpu.VMEM((2, micro, state_rows, 128), bf16), pltpu.VMEM((2, 16, 8, 128), f32)]
    scratch += [pltpu.VMEM((micro, state_rows, 128), bf16), pltpu.VMEM((16, 8, 128), f32)]
    scratch += [pltpu.VMEM(pieces, bf16), pltpu.VMEM((16, 8, 128), f32)] * 2
    scratch += [pltpu.VMEM((rows, d), bf16)] + [pltpu.VMEM((rows, d), f32)] * 3
    scratch += [pltpu.VMEM((rows, d), bf16)] + [pltpu.VMEM((rows, ff), bf16)] * 2
    scratch += [pltpu.VMEM((rows, d), bf16)] * 3 + [pltpu.VMEM((rows, d), f32)]
    scratch += [pltpu.VMEM((3, rows, d), bf16), pltpu.VMEM((rows, d), bf16), pltpu.VMEM((d, rows), bf16)]
    scratch += [pltpu.VMEM(s, bf16) for s in own]
    scratch += [pltpu.VMEM((3,) + s, bf16) for s in sums]
    scratch += [pltpu.VMEM(s, bf16) for s in sums]
    scratch += [pltpu.VMEM((6,) + s, bf16) for s in last]
    scratch += [pltpu.VMEM(s, bf16) for s in last]
    scratch += [pltpu.VMEM(s, f32) for s in tiny[:2]] + [pltpu.VMEM(tiny[2], bf16)] * 2
    scratch += [pltpu.VMEM(tiny[2][1:], bf16), pltpu.VMEM(tiny[2], bf16)]
    scratch += [pltpu.VMEM(s, f32) for s in ((8, d), (8, d // 2), (8, d // 2), (4, 8, d // 2), (8, d // 2), (4, 8, d // 2))]
    scratch += [dma((16,)), dma(()), dma((8,)), dma((5, 4)), dma((5, 4, 4)), dma((5,))]
    scratch += [dma((8,)), dma((2, 2, 3, 2, 2)), dma((5,)), dma((5, 2, 3)), dma((5, 6)), dma((5, 4)), dma((6,))]
    scratch += [pltpu.VMEM((micro, 8, span), f32), pltpu.VMEM((2, heads // 4, head // 2, 128), bf16)]
    scratch += [pltpu.VMEM((8, d // 2), f32)]
    vmem = pl.BlockSpec(memory_space=pltpu.VMEM)
    spread_rows = (micro, 4, span, d)
    anywhere = pl.BlockSpec(memory_space=pl.ANY)
    all_out, all_in, share_0, share_1, share_2, share_3, map_0, map_1, norm_grads = pl.pallas_call(
        layer_kernel,
        out_shape=[jax.ShapeDtypeStruct(spread_rows, bf16)] * 2
        + [jax.ShapeDtypeStruct(s, bf16) for s in outs]
        + [jax.ShapeDtypeStruct(maps_shape, f32)] * 2
        + [jax.ShapeDtypeStruct((8, d // 2), f32)],
        in_specs=[anywhere] * 2 + [vmem] * 7 + [anywhere] * 4,
        out_specs=[anywhere] * 6 + [vmem] * 3,
        scratch_shapes=scratch,
        compiler_params=pltpu.CompilerParams(collective_id=0, has_side_effects=True, vmem_limit_bytes=67043328),
        name="layer",
    )(
        inputs, cotangent, picture_starts, query_map, key_map, first_gain, first_bias, second_gain, second_bias,
        qkv_weight.transpose(0, 2, 1), out_weight, up_weight, down_weight,
    )
    return (
        all_out.reshape(inputs.shape),
        all_in.reshape(inputs.shape).astype(f32),
        share_0.astype(f32).transpose(0, 2, 1),
        share_1.astype(f32),
        share_2.astype(f32),
        share_3.astype(f32).T,
        map_0,
        map_1,
        norm_grads[0],
        norm_grads[1],
        norm_grads[2],
        norm_grads[3],
    )


def solution(mesh):
    in_specs = (
        P(None, "fsdp", "context", None),
        P(None, "fsdp", "context", None),
        P(None, "fsdp", None),
        P(None, "fsdp", "tensor"),
        P("tensor", "fsdp"),
        P("fsdp", "tensor"),
        P("tensor", "fsdp"),
        P("tensor", "fsdp", None),
        P("tensor", "fsdp", None),
        P("fsdp"),
        P("fsdp"),
        P("fsdp"),
        P("fsdp"),
    )
    out_specs = (
        P(None, "fsdp", "context", None),
        P(None, "fsdp", "context", None),
        P(None, "fsdp", "tensor"),
        P("tensor", "fsdp"),
        P("fsdp", "tensor"),
        P("tensor", "fsdp"),
        P("tensor", "fsdp", None),
        P("tensor", "fsdp", None),
        P("fsdp"),
        P("fsdp"),
        P("fsdp"),
        P("fsdp"),
    )
    sizes = tuple(mesh.shape[name] for name in EVERY)
    return jax.shard_map(
        mesh_device if sizes == (2, 4, 4) else per_device, mesh=mesh, in_specs=in_specs, out_specs=out_specs, check_vma=False
    )
```
